32 devices in a mesh: clip: 8 (over y, x, core), tm: 4 (over z).
Axes of the slice: x: 2, y: 2, z: 4, core: 2. Of those that a mesh axis runs over, the one named last changes fastest.
Arguments:
- slow_in: bfloat16 [96, 4, 1024, 256], P('clip', 'tm')
- fast_in: bfloat16 [96, 16, 128, 256], P('clip', 'tm')
- clip_group: int32 [96], P('clip'), may hold values from 0 to 2, as said below
- reducer: bfloat16 [3, 256, 1280], replicated, may hold values from -0.09375 to 0.09375
- spatial: bfloat16 [9, 256, 256], replicated, may hold values from -0.125 to 0.125
- expand: bfloat16 [1024, 256], replicated, may hold values from -0.375 to 0.375
- lateral: bfloat16 [5, 256, 128], replicated, may hold values from -0.25 to 0.25
- squeeze: bfloat16 [3, 32, 128], replicated, may hold values from -0.3125 to 0.3125
- narrow: bfloat16 [9, 32, 32], replicated, may hold values from -0.375 to 0.375
- widening: bfloat16 [128, 32], replicated, may hold values from -1 to 1
- reducer_norm: bfloat16 [2, 256], replicated, may hold values from -0.5 to 3
- spatial_norm: bfloat16 [2, 256], replicated, may hold values from 0.5 to 1.5
- expand_norm: bfloat16 [2, 1024], replicated, may hold values from 0.5 to 1.5
- lateral_norm: bfloat16 [2, 256], replicated, may hold values from -0.5 to 4
- squeeze_norm: bfloat16 [2, 32], replicated, may hold values from -0.5 to 3
- narrow_norm: bfloat16 [2, 32], replicated, may hold values from 0.5 to 1.5
- widening_norm: bfloat16 [2, 128], replicated, may hold values from 0.5 to 1.5
- slow_cot: bfloat16 [96, 4, 1024, 256], P('clip', 'tm'), may hold values from -6 to 6
- fast_cot: bfloat16 [96, 16, 128, 256], P('clip', 'tm'), may hold values from -6 to 6
Outputs:
- slow_out: bfloat16 [96, 4, 1024, 256], P('clip', 'tm')
- fast_out: bfloat16 [96, 16, 128, 256], P('clip', 'tm')
- slow_grad: bfloat16 [96, 4, 1024, 256], P('clip', 'tm')
- fast_grad: bfloat16 [96, 16, 128, 256], P('clip', 'tm')
- reducer_grad: float32 [3, 256, 1280], replicated
- spatial_grad: float32 [9, 256, 256], replicated
- expand_grad: float32 [1024, 256], replicated
- lateral_grad: float32 [5, 256, 128], replicated
- squeeze_grad: float32 [3, 32, 128], replicated
- narrow_grad: float32 [9, 32, 32], replicated
- widening_grad: float32 [128, 32], replicated
- reducer_norm_grad: float32 [2, 256], replicated
- spatial_norm_grad: float32 [2, 256], replicated
- expand_norm_grad: float32 [2, 1024], replicated
- lateral_norm_grad: float32 [2, 256], replicated
- squeeze_norm_grad: float32 [2, 32], replicated
- narrow_norm_grad: float32 [2, 32], replicated
- widening_norm_grad: float32 [2, 128], replicated
The draws below stay inside these ranges and needn't reach their ends.
Inputs may be any that keep to these rules, and one draw needn't show every extreme that they name: `clip_group`: each of the groups 0, 1, 2 is held by two or more clips; groups 0 and 1 each hold 24 to 47 clips.
All inputs are finite; a program needn't handle non-finite values.
Results may differ from the reference program's by a relative error of at most 0.01.
Values may be sent and summed in bfloat16 or wider, within the bound.
A program may use at most 320 MiB of HBM per device.

```python
import jax
import jax.numpy as jnp
from jax import lax

C_SLOW = 1024
CL = 256
BS = 256
CF = 128
BF = 32
ALPHA = 4
SIDE = 16
CIN = 1280
CELLS = 256
CLIPS = 96
TS = 4
TF = 16


def draw_clip_group(key, part):
    shared = jax.random.fold_in(key, 7)
    key_low, key_mid, key_perm = jax.random.split(shared, 3)
    low_count = jax.random.randint(key_low, (), CLIPS // 4, CLIPS // 2).astype(jnp.int32)
    mid_count = jax.random.randint(key_mid, (), CLIPS // 4, CLIPS // 2).astype(jnp.int32)
    shuffle = jax.random.permutation(key_perm, CLIPS).astype(jnp.int32)
    above_low = (shuffle >= low_count).astype(jnp.int32)
    above_mid = (shuffle >= low_count + mid_count).astype(jnp.int32)
    return above_low + above_mid


def scaled_field(key, shape):
    key_base, key_scale = jax.random.split(key, 2)
    values = jax.random.normal(key_base, shape, jnp.float32)
    scales = jnp.exp(jax.random.uniform(key_scale, (shape[0], shape[1], 1, 1), jnp.float32, -0.7, 1.6))
    return (values * scales).astype(jnp.bfloat16)


def draw_slow_in(key, part):
    return scaled_field(key, (CLIPS, TS, C_SLOW, CELLS))


def draw_fast_in(key, part):
    return scaled_field(key, (CLIPS, TF, CF, CELLS))


def gain_pair(key, width, lowest, highest):
    key_gain, key_bias = jax.random.split(jax.random.fold_in(key, 11))
    gains = jax.random.uniform(key_gain, (1, width), jnp.float32, lowest, highest)
    biases = jax.random.uniform(key_bias, (1, width), jnp.float32, -0.5, 0.5)
    return jnp.concatenate([gains, biases], axis=0).astype(jnp.bfloat16)


def draw_reducer_norm(key, part):
    return gain_pair(key, BS, 1.5, 3.0)


def draw_lateral_norm(key, part):
    return gain_pair(key, CL, 2.0, 4.0)


def draw_squeeze_norm(key, part):
    return gain_pair(key, BF, 1.5, 3.0)


def level_of(rng, extent, cuts, low, largest):
    def one(dim, shards_of):
        steps = jax.random.uniform(jax.random.fold_in(jax.random.fold_in(rng, 6), dim), (shards_of,), jnp.float32, low / len(cuts), largest / len(cuts))
        return jnp.repeat(jnp.exp(steps), extent[dim] // shards_of).reshape((-1,) + (1,) * (len(extent) - dim - 1))

    level = one(*cuts[0])
    for cut in cuts[1:]:
        level = level * one(*cut)
    return level


def normal_values(own_key, extent, scale, most, cuts=(), kind=jnp.bfloat16):
    values = jax.random.normal(own_key, extent, jnp.float32) * scale
    if len(cuts) > 0:
        values = level_of(own_key, extent, cuts, -0.22, 0.18) * values
    return jnp.clip(values, min=-most, max=most).astype(kind)


def setup_inputs(seed: int = 0) -> dict:
    streams_of = jax.random.split(jax.random.key(seed), 20)
    slow_in = draw_slow_in(jax.random.fold_in(streams_of[19], 71), 0)
    fast_in = draw_fast_in(jax.random.fold_in(streams_of[19], 71), 0)
    clip_group = draw_clip_group(jax.random.fold_in(streams_of[19], 71), 0)
    reducer = normal_values(streams_of[3], (3, BS, CIN), (3 * CIN) ** -0.5, 0.09375)
    spatial = normal_values(streams_of[4], (9, BS, BS), (9 * BS) ** -0.5, 0.125)
    expand = normal_values(streams_of[5], (C_SLOW, BS), BS ** -0.5, 0.375)
    lateral = normal_values(streams_of[6], (5, CL, CF), (5 * CF) ** -0.5, 0.25)
    squeeze = normal_values(streams_of[7], (3, BF, CF), (3 * CF) ** -0.5, 0.3125)
    narrow = normal_values(streams_of[8], (9, BF, BF), (9 * BF) ** -0.5, 0.375)
    widening = normal_values(streams_of[9], (CF, BF), BF ** -0.5, 1.0)
    reducer_norm = draw_reducer_norm(jax.random.fold_in(streams_of[19], 71), 0)
    spatial_norm = jnp.clip(jax.random.uniform(streams_of[11], (2, BS), jnp.float32, 0.5, 1.5), 0.5, 1.5).astype(jnp.bfloat16)
    expand_norm = jnp.clip(jax.random.uniform(streams_of[12], (2, C_SLOW), jnp.float32, 0.5, 1.5), 0.5, 1.5).astype(jnp.bfloat16)
    lateral_norm = draw_lateral_norm(jax.random.fold_in(streams_of[19], 71), 0)
    squeeze_norm = draw_squeeze_norm(jax.random.fold_in(streams_of[19], 71), 0)
    narrow_norm = jnp.clip(jax.random.uniform(streams_of[15], (2, BF), jnp.float32, 0.5, 1.5), 0.5, 1.5).astype(jnp.bfloat16)
    widening_norm = jnp.clip(jax.random.uniform(streams_of[16], (2, CF), jnp.float32, 0.5, 1.5), 0.5, 1.5).astype(jnp.bfloat16)
    slow_cot = normal_values(streams_of[17], (CLIPS, TS, C_SLOW, CELLS), 1.0, 6.0, ((0, 8), (1, 4)))
    fast_cot = normal_values(streams_of[18], (CLIPS, TF, CF, CELLS), 1.0, 6.0, ((0, 8), (1, 4)))
    return dict(slow_in=slow_in, fast_in=fast_in, clip_group=clip_group, reducer=reducer, spatial=spatial, expand=expand, lateral=lateral, squeeze=squeeze, narrow=narrow, widening=widening, reducer_norm=reducer_norm, spatial_norm=spatial_norm, expand_norm=expand_norm, lateral_norm=lateral_norm, squeeze_norm=squeeze_norm, narrow_norm=narrow_norm, widening_norm=widening_norm, slow_cot=slow_cot, fast_cot=fast_cot)


EPS = 1e-05
HIGHEST = lax.Precision.HIGHEST

@jax.custom_vjp
def low(v):
    return lax.optimization_barrier(v.astype(jnp.bfloat16)).astype(jnp.float32)

@jax.custom_vjp
def low_back(v):
    return v

def low_keep(v):
    return (low(v), None)

def low_pass(kept, grad):
    return (grad,)

def back_keep(v):
    return (v, None)

def back_low(kept, grad):
    return (low(grad),)
low.defvjp(low_keep, low_pass)
low_back.defvjp(back_keep, back_low)

def tables(clip_group):
    onehot = (clip_group[:, None] == jnp.arange(3, dtype=jnp.int32)[None, :]).astype(jnp.float32)
    side_table = jnp.array([SIDE * 5 // 8, SIDE * 7 // 8, SIDE], jnp.float32)
    side_clip = jnp.dot(onehot, side_table, precision=HIGHEST)
    cell_ids = jnp.arange(SIDE * SIDE, dtype=jnp.int32)
    row_index = (cell_ids // SIDE).astype(jnp.float32)
    col_index = (cell_ids % SIDE).astype(jnp.float32)
    inside = (row_index[None, :] < side_clip[:, None]) & (col_index[None, :] < side_clip[:, None])
    group_cells = jnp.dot(onehot.T, side_clip * side_clip, precision=HIGHEST)
    return (onehot, inside.astype(jnp.float32)[:, None, None, :], group_cells)

def channel_mix(weight, field):
    return jnp.einsum('oc,ntcp->ntop', weight, field, precision=HIGHEST)

def time_conv(field, weight):
    frames = field.shape[1]
    padded = jnp.pad(field, ((0, 0), (1, 1), (0, 0), (0, 0)))
    total = channel_mix(weight[0], padded[:, 0:frames])
    for position in range(1, 3):
        total = total + channel_mix(weight[position], padded[:, position:position + frames])
    return total

def space_conv(field, weight):
    clip_count, frame_count, chan_count, cell_count = field.shape
    grid = field.reshape(clip_count, frame_count, chan_count, SIDE, SIDE)
    padded = jnp.pad(grid, ((0, 0), (0, 0), (0, 0), (1, 1), (1, 1)))
    total = None
    for row_shift in range(3):
        for col_shift in range(3):
            window = padded[..., row_shift:row_shift + SIDE, col_shift:col_shift + SIDE]
            window = window.reshape(clip_count, frame_count, chan_count, cell_count)
            term = channel_mix(weight[3 * row_shift + col_shift], window)
            total = term if total is None else total + term
    return total

def lateral_conv(field, weight):
    slow_frames = field.shape[1] // ALPHA
    padded = jnp.pad(field, ((0, 0), (2, 2), (0, 0), (0, 0)))
    total = channel_mix(weight[0], padded[:, 0:ALPHA * slow_frames:ALPHA])
    for position in range(1, 5):
        total = total + channel_mix(weight[position], padded[:, position:position + ALPHA * slow_frames:ALPHA])
    return total

def norm(conv_out, pair, onehot, inside, count):
    masked = conv_out * inside
    per_sum = lax.optimization_barrier(jnp.sum(masked, axis=(1, 3)))
    per_square = lax.optimization_barrier(jnp.sum(masked * conv_out, axis=(1, 3)))
    group_sum = jnp.dot(onehot.T, per_sum, precision=HIGHEST)
    group_square = jnp.dot(onehot.T, per_square, precision=HIGHEST)
    mean = group_sum / count[:, None]
    spread = group_square / count[:, None] - mean * mean
    inverse = lax.rsqrt(spread + EPS)
    clip_mean = jnp.dot(onehot, mean, precision=HIGHEST)[:, None, :, None]
    clip_inverse = jnp.dot(onehot, inverse, precision=HIGHEST)[:, None, :, None]
    normed = (conv_out - clip_mean) * clip_inverse
    return normed * pair[0][None, None, :, None] + pair[1][None, None, :, None]

def reference(slow_in, fast_in, clip_group, reducer, spatial, expand, lateral, squeeze, narrow, widening, reducer_norm, spatial_norm, expand_norm, lateral_norm, squeeze_norm, narrow_norm, widening_norm, slow_cot, fast_cot):
    onehot, inside, group_cells = tables(clip_group)
    slow_count = group_cells * slow_in.shape[1]
    fast_count = group_cells * fast_in.shape[1]

    def forward(slow_in, fast_in, reducer, spatial, expand, lateral, squeeze, narrow, widening, reducer_norm, spatial_norm, expand_norm, lateral_norm, squeeze_norm, narrow_norm, widening_norm):
        slow_field = slow_in * inside
        fast_field = fast_in * inside
        fast_one = low_back(time_conv(fast_field, squeeze))
        fast_act = low(jax.nn.silu(norm(fast_one, squeeze_norm, onehot, inside, fast_count)) * inside)
        fast_two = low_back(space_conv(fast_act, narrow))
        fast_act = low(jax.nn.silu(norm(fast_two, narrow_norm, onehot, inside, fast_count)) * inside)
        fast_three = low_back(channel_mix(widening, fast_act))
        fast_pre = norm(fast_three, widening_norm, onehot, inside, fast_count) + fast_field
        fast_out = jax.nn.silu(fast_pre) * inside
        side_conv = low_back(lateral_conv(fast_field, lateral))
        side_act = low(jax.nn.silu(norm(side_conv, lateral_norm, onehot, inside, slow_count)) * inside)
        combined = jnp.concatenate([slow_field, side_act], axis=2)
        slow_one = low_back(time_conv(combined, reducer))
        slow_act = low(jax.nn.silu(norm(slow_one, reducer_norm, onehot, inside, slow_count)) * inside)
        slow_two = low_back(space_conv(slow_act, spatial))
        slow_act = low(jax.nn.silu(norm(slow_two, spatial_norm, onehot, inside, slow_count)) * inside)
        slow_three = low_back(channel_mix(expand, slow_act))
        slow_pre = norm(slow_three, expand_norm, onehot, inside, slow_count) + slow_field
        slow_out = jax.nn.silu(slow_pre) * inside
        return (slow_out, fast_out)
    primal = tuple((value.astype(jnp.float32) for value in (slow_in, fast_in, reducer, spatial, expand, lateral, squeeze, narrow, widening, reducer_norm, spatial_norm, expand_norm, lateral_norm, squeeze_norm, narrow_norm, widening_norm)))
    outputs, pullback = jax.vjp(forward, *primal)
    grads = pullback((slow_cot.astype(jnp.float32), fast_cot.astype(jnp.float32)))
    return (outputs[0].astype(jnp.bfloat16), outputs[1].astype(jnp.bfloat16), grads[0].astype(jnp.bfloat16), grads[1].astype(jnp.bfloat16), grads[2], grads[3], grads[4], grads[5], grads[6], grads[7], grads[8], grads[9], grads[10], grads[11], grads[12], grads[13], grads[14], grads[15])
```

```python
import functools

import jax
import jax.numpy as jnp
from jax import lax
from jax.experimental import pallas as pl
from jax.experimental.pallas import tpu as pltpu
from jax.sharding import PartitionSpec as P

MESH = pl.DeviceIdType.MESH
F32, BF16 = jnp.float32, jnp.bfloat16
SIDE = 16
CELLS = SIDE * SIDE
EPS = 1e-05
VM = pltpu.VMEM
LIMIT = 56 * 1024 * 1024


def dot(a, b):
    return lax.dot_general(a, b, (((1,), (0,)), ((), ())), preferred_element_type=F32)


def dot_nt(a, b):
    return lax.dot_general(a, b, (((1,), (1,)), ((), ())), preferred_element_type=F32)


def side_of(g):
    return jnp.where(g == 0, SIDE * 5 // 8, jnp.where(g == 1, SIDE * 7 // 8, SIDE))


def mask_of(g):
    cell = lax.broadcasted_iota(jnp.int32, (1, CELLS), 1)
    side = side_of(g)
    return jnp.where(((cell >> 4) < side) & ((cell & 15) < side), 1.0, 0.0).astype(F32)


def counts_row(grp):
    lane = lax.broadcasted_iota(jnp.int32, (1, 128), 1)
    total = jnp.zeros((1, 128), F32)
    for c in range(grp.shape[0]):
        side = side_of(grp[c])
        total = total + jnp.where(lane == grp[c], (side * side).astype(F32), 0.0)
    return total


def add_stats(acc, lo, rows, first, second, g):
    lane = lax.broadcasted_iota(jnp.int32, (1, 128), 1)
    one = jnp.sum(first[:, :128] + first[:, 128:], axis=1, keepdims=True)
    two = jnp.sum(second[:, :128] + second[:, 128:], axis=1, keepdims=True)
    acc[lo : lo + rows, :] += jnp.where(lane == g, one, 0.0) + jnp.where(lane == g + 3, two, 0.0)


def ar_scratch(na, nb, width):
    dma = pltpu.SemaphoreType.DMA
    return [
        VM((8, width), F32),
        VM((na, 8, width), F32),
        VM((8, width), F32),
        VM((nb, 8, width), F32),
        dma((na - 1,)),
        dma((na - 1,)),
        dma((nb - 1,)),
        dma((nb - 1,)),
    ]


class Sum:
    def __init__(self, na, nb, refs):
        self.na, self.nb = na, nb
        self.mine, self.bufa, self.part, self.bufb, self.sa, self.ra, self.sb, self.rb = refs
        self.a, self.b = lax.axis_index("clip"), lax.axis_index("tm")
        bar = pltpu.get_barrier_semaphore()
        for peer in self.peers_a() + self.peers_b():
            pl.semaphore_signal(bar, inc=1, device_id=peer, device_id_type=MESH)
        self.bar = bar

    def peers_a(self):
        return [(lax.rem(self.a + d, self.na), self.b) for d in range(1, self.na)]

    def peers_b(self):
        return [(self.a, lax.rem(self.b + d, self.nb)) for d in range(1, self.nb)]

    def greet(self):
        pl.semaphore_wait(self.bar, self.na - 1 + self.nb - 1)

    def copies(self, src, buf, slot, ss, rs, peers):
        return [
            pltpu.make_async_remote_copy(
                src, buf.at[slot], ss.at[i], rs.at[i], device_id=peer, device_id_type=MESH
            )
            for i, peer in enumerate(peers)
        ]

    def start(self, acc, grp):
        width = self.mine.shape[1]
        rows = jnp.transpose(acc[...])[:8, :]
        row = lax.broadcasted_iota(jnp.int32, (8, 128), 0)
        head = jnp.where(row == 6, counts_row(grp), rows[:, :128])
        value = head if width == 128 else jnp.concatenate([head, rows[:, 128:]], axis=1)
        self.mine[...] = value
        self.bufa[self.a] = value
        self.first = self.copies(self.mine, self.bufa, self.a, self.sa, self.ra, self.peers_a())
        for c in self.first:
            c.start()

    def middle(self):
        for c in self.first:
            c.wait()
        total = self.bufa[0]
        for i in range(1, self.na):
            total = total + self.bufa[i]
        self.part[...] = total
        self.bufb[self.b] = total
        self.second = self.copies(self.part, self.bufb, self.b, self.sb, self.rb, self.peers_b())
        for c in self.second:
            c.start()

    def finish(self):
        for c in self.second:
            c.wait()
        total = self.bufb[0]
        for i in range(1, self.nb):
            total = total + self.bufb[i]
        return total


class Halo:
    def __init__(self, nb, step, parts, ss, rs):
        self.a, self.b = lax.axis_index("clip"), lax.axis_index("tm")
        to = self.b + step
        self.sends = (to >= 0) & (to < nb)
        source = self.b - step
        self.gets = (source >= 0) & (source < nb)
        peer = (self.a, lax.rem(to + nb, nb))
        self.copies = [
            pltpu.make_async_remote_copy(
                src, dst, ss.at[i], rs.at[i], device_id=peer, device_id_type=MESH
            )
            for i, (src, dst) in enumerate(parts)
        ]

    def start(self, i):
        @pl.when(self.sends)
        def _():
            self.copies[i].start()

    def arrive(self, i):
        @pl.when(self.gets)
        def _():
            self.copies[i].wait_recv()

    def sent(self):
        @pl.when(self.sends)
        def _():
            for c in self.copies:
                c.wait_send()


def fold_frames(total, chans):
    width = total.shape[1]
    if chans < 128:
        out = total
        shift = chans
        while shift < 128:
            out = out + pltpu.roll(out, shift, 1)
            shift *= 2
        return out
    out = total[:, :128]
    for f in range(1, width // 128):
        out = out + total[:, 128 * f : 128 * (f + 1)]
    return jnp.concatenate([out] * (width // 128), axis=1)


def moments(total, counts, frames):
    out = []
    for g in range(3):
        n = counts[6:7, g : g + 1] * float(frames)
        mean = total[g : g + 1, :] / n
        var = total[g + 3 : g + 4, :] / n - mean * mean
        out.append((n, mean, lax.rsqrt(var + EPS)))
    return out


def fill_tables(tab, base, rows_list):
    width = rows_list[0][0].shape[1]
    count = len(rows_list[0])
    rows = [rows_list[g][k] for g in range(3) for k in range(count)]
    rows = rows + [jnp.zeros((1, width), F32)] * (128 - len(rows))
    cols = jnp.transpose(jnp.concatenate(rows, axis=0))
    for g in range(3):
        for k in range(count):
            i = g * count + k
            tab[g, k, base : base + width, :] = jnp.broadcast_to(cols[:, i : i + 1], (width, 128))


def forward_rows(total, counts, frames, pair):
    out = []
    for n, mean, r in moments(total, counts, frames):
        gain = pair[0:1, :] * r
        out.append((gain, pair[1:2, :] - mean * gain))
    return out


def backward_rows(total, grads, counts, frames, pair):
    out, two_all, one_all = [], 0.0, 0.0
    for g, (n, mean, r) in enumerate(moments(total, counts, frames)):
        one = grads[g : g + 1, :]
        two = r * (grads[g + 3 : g + 4, :] - mean * one)
        c0 = pair[0:1, :] * r
        slope = c0 * r * two / n
        out.append((c0, -slope, slope * mean - c0 * one / n))
        two_all, one_all = two_all + two, one_all + one
    return out, jnp.concatenate([two_all, one_all], axis=0)


def wide(v):
    return jnp.concatenate([v, v], axis=1)


def coef(tab, g, k, lo, rows):
    return wide(tab[g, k, lo : lo + rows, :])


def sigmoid(v):
    return 0.5 * jnp.tanh(0.5 * v) + 0.5


def slope_of(v):
    s = sigmoid(v)
    return s * (1.0 + v * (1.0 - s))


def taps(x, dst, rows, sign):
    cell = lax.broadcasted_iota(jnp.int32, (1, CELLS), 1)
    row, col = cell >> 4, cell & 15
    for k in range(9):
        di, dl = sign * (k // 3 - 1), sign * (k % 3 - 1)
        step = SIDE * di + dl
        if step == 0:
            dst[k * rows : (k + 1) * rows, :] = x.astype(BF16)
            continue
        moved = pltpu.roll(x, (-step) % CELLS, 1)
        ok = (row + di >= 0) & (row + di < SIDE) & (col + dl >= 0) & (col + dl < SIDE)
        dst[k * rows : (k + 1) * rows, :] = jnp.where(ok, moved, 0.0).astype(BF16)


def loop(lo, hi):
    return pl.loop(lo, hi)


def parts_of(nc):
    for p in (3, 4, 2):
        if nc % p == 0:
            return p
    return 1


def k1(na, nb, grp, fast, wa, xe, y1, tot, acc, os, us, ur, ds, dr, *ar):
    s = Sum(na, nb, ar)
    nc = fast.shape[0]
    b = lax.axis_index("tm")
    np_ = parts_of(nc)
    size = nc // np_
    rows = [slice(i * size, (i + 1) * size) for i in range(np_)]
    own = [pltpu.make_async_copy(fast.at[r], xe.at[r, 256:768], os.at[i]) for i, r in enumerate(rows)]
    for c in own:
        c.start()
    up = Halo(nb, 1, [(fast.at[r, 256:512], xe.at[r, 0:256]) for r in rows], us, ur)
    down = Halo(nb, -1, [(fast.at[r, 0:128], xe.at[r, 768:896]) for r in rows], ds, dr)
    acc[...] = jnp.zeros_like(acc)

    @pl.when(b == 0)
    def _():
        xe[:, 0:256, :] = jnp.zeros((nc, 256, CELLS), BF16)

    @pl.when(b == nb - 1)
    def _():
        xe[:, 768:896, :] = jnp.zeros((nc, 128, CELLS), BF16)

    s.greet()
    for i in range(np_):
        up.start(i)
        down.start(i)
    for i in range(np_):
        own[i].wait()
        up.arrive(i)
        down.arrive(i)

        @loop(i * size, (i + 1) * size)
        def _(c):
            g = grp[c]
            m = mask_of(g)
            for lo in range(0, 384, 128):
                y = dot(wa[lo : lo + 128, :], xe[c])
                y1[c, lo : lo + 128, :] = y
                ym = y * m
                add_stats(acc, lo, 128, ym, ym * y, g)

    s.start(acc, grp)
    s.middle()
    up.sent()
    down.sent()
    tot[...] = s.finish()


def k2(na, nb, grp, y1, tot1, par1, slow, wr, wn, act1, y2, tot, tab, acc, x9, su, sd, ru, rd, us, ur, ds, dr, *ar):
    s = Sum(na, nb, ar)
    nc = y1.shape[0]
    b = lax.axis_index("tm")
    np_ = parts_of(nc)
    size = nc // np_
    acc[...] = jnp.zeros_like(acc)
    t = tot1[...]
    fill_tables(tab, 0, forward_rows(t[:, :256], t, 1, par1[:, :256]))
    fill_tables(tab, 256, forward_rows(fold_frames(t[:, 256:], 32), t, 4, par1[:, 256:]))
    rows = [slice(i * size, (i + 1) * size) for i in range(np_)]
    up = Halo(nb, 1, [(su.at[r], ru.at[r]) for r in rows], us, ur)
    down = Halo(nb, -1, [(sd.at[r], rd.at[r]) for r in rows], ds, dr)

    @pl.when(b == 0)
    def _():
        ru[...] = jnp.zeros_like(ru)

    @pl.when(b == nb - 1)
    def _():
        rd[...] = jnp.zeros_like(rd)

    for i in range(np_):

        @loop(i * size, (i + 1) * size)
        def _(c):
            g = grp[c]
            m = mask_of(g)
            for lo in range(0, 256, 128):
                u = y1[c, lo : lo + 128, :] * coef(tab, g, 0, lo, 128) + coef(tab, g, 1, lo, 128)
                act1[c, lo : lo + 128, :] = (u * sigmoid(u) * m).astype(BF16)
            for j, dst in enumerate((su, y2, sd)):
                for lo in range(0, 256, 128):
                    r0 = 256 * j + lo
                    p = dot(wr[r0 : r0 + 128, :1024], slow[c]) + dot(
                        wr[r0 : r0 + 128, 1024:], act1[c, 0:256, :]
                    )
                    dst[c, lo : lo + 128, :] = p.astype(dst.dtype)

        if i == 0:
            s.greet()
        up.start(i)
        down.start(i)

    @loop(0, nc)
    def _(c):
        g = grp[c]
        m = mask_of(g)
        u = y1[c, 256:384, :] * coef(tab, g, 0, 256, 128) + coef(tab, g, 1, 256, 128)
        act = u * sigmoid(u) * m
        act1[c, 256:384, :] = act.astype(BF16)
        taps(act, x9, 128, 1)
        y = dot(wn[...], x9[...])
        y2[c, 256:384, :] = y
        ym = y * m
        add_stats(acc, 256, 128, ym, ym * y, g)

    for i in range(np_):
        up.arrive(i)
        down.arrive(i)

        @loop(i * size, (i + 1) * size)
        def _(c):
            g = grp[c]
            m = mask_of(g)
            for lo in range(0, 256, 128):
                y = (
                    y2[c, lo : lo + 128, :]
                    + ru[c, lo : lo + 128, :].astype(F32)
                    + rd[c, lo : lo + 128, :].astype(F32)
                )
                y2[c, lo : lo + 128, :] = y
                ym = y * m
                add_stats(acc, lo, 128, ym, ym * y, g)

    s.start(acc, grp)
    s.middle()
    up.sent()
    down.sent()
    tot[...] = s.finish()


def k3(na, nb, grp, y2, tot2, par2, ws, ww, act2, y3, tot, tab, acc, x9, *ar):
    s = Sum(na, nb, ar)
    nc = y2.shape[0]
    acc[...] = jnp.zeros_like(acc)
    t = tot2[...]
    fill_tables(tab, 0, forward_rows(t[:, :256], t, 1, par2[:, :256]))
    fill_tables(tab, 256, forward_rows(fold_frames(t[:, 256:], 32), t, 4, par2[:, 256:]))

    @loop(0, nc)
    def _(c):
        g = grp[c]
        m = mask_of(g)
        u = y2[c, 256:384, :] * coef(tab, g, 0, 256, 128) + coef(tab, g, 1, 256, 128)
        act2[c, 256:384, :] = (u * sigmoid(u) * m).astype(BF16)
        u = y2[c, 0:256, :] * coef(tab, g, 0, 0, 256) + coef(tab, g, 1, 0, 256)
        act = u * sigmoid(u) * m
        act2[c, 0:256, :] = act.astype(BF16)
        taps(act, x9, 256, 1)
        for lo in range(0, 512, 128):
            y = dot(ww[lo : lo + 128, :], act2[c, 256:384, :])
            ym = y * m
            add_stats(acc, 256 + lo, 128, ym, ym * y, g)
        for lo in range(0, 256, 128):
            y = dot(ws[lo : lo + 128, :], x9[...])
            y3[c, lo : lo + 128, :] = y
            ym = y * m
            add_stats(acc, lo, 128, ym, ym * y, g)

    s.greet()
    s.start(acc, grp)
    s.middle()
    tot[...] = s.finish()


def k4(
    na, nb, grp, y3, tot3, par3, parw, we, ww, act2, xe, fcot,
    acts, tot, fout, dzw, accw,
    tab, tabw, acc, cbuf, obuf, cs, osem, *ar,
):
    s = Sum(na, nb, ar)
    nc = y3.shape[0]
    acc[...] = jnp.zeros_like(acc)
    accw[...] = jnp.zeros_like(accw)
    t = tot3[...]
    fill_tables(tab, 0, forward_rows(t[:, :256], t, 1, par3))
    fill_tables(tabw, 0, forward_rows(fold_frames(t[:, 256:], 128), t, 4, parw))

    def load(c, slot):
        return pltpu.make_async_copy(fcot.at[c], cbuf.at[slot], cs.at[slot])

    def store(c, slot):
        return pltpu.make_async_copy(obuf.at[slot], fout.at[c], osem.at[slot])

    load(0, 0).start()

    @loop(0, nc)
    def _(c):
        g = grp[c]
        m = mask_of(g)
        for lo in range(0, 256, 128):
            u = y3[c, lo : lo + 128, :] * coef(tab, g, 0, lo, 128) + coef(tab, g, 1, lo, 128)
            acts[c, lo : lo + 128, :] = (u * sigmoid(u) * m).astype(BF16)
        for lo in range(0, 1024, 128):
            y = dot(we[lo : lo + 128, :], acts[c])
            ym = y * m
            add_stats(acc, lo, 128, ym, ym * y, g)

    s.greet()
    s.start(acc, grp)

    @loop(0, nc)
    def _(c):
        slot = lax.rem(c, 2)
        g = grp[c]
        m = mask_of(g)

        @pl.when(c + 1 < nc)
        def _():
            load(c + 1, 1 - slot).start()

        load(c, slot).wait()

        @pl.when(c >= 2)
        def _():
            store(c - 2, slot).wait()

        for lo in range(0, 512, 128):
            y = dot(ww[lo : lo + 128, :], act2[c, 256:384, :])
            v = y * coef(tabw, g, 0, lo, 128) + coef(tabw, g, 1, lo, 128)
            v = v + xe[c, 256 + lo : 384 + lo, :].astype(F32)
            sg = sigmoid(v)
            obuf[slot, lo : lo + 128, :] = (v * sg * m).astype(BF16)
            dz = cbuf[slot, lo : lo + 128, :].astype(F32) * m * (sg * (1.0 + v * (1.0 - sg)))
            dzw[c, lo : lo + 128, :] = dz
            add_stats(accw, lo, 128, dz, dz * y, g)
        store(c, slot).start()

    s.middle()
    for c in range(max(0, nc - 2), nc):
        store(c, c % 2).wait()
    tot[...] = s.finish()


def k5(
    na, nb, grp, acts, tot4, pare, we, accw, slow, cot,
    sout, dze, tot,
    tab, acc, xbuf, cbuf, obuf, xs, cs, osem, *ar,
):
    s = Sum(na, nb, ar)
    nc = acts.shape[0]
    width = we.shape[0]

    def loads(c, slot):
        return (
            pltpu.make_async_copy(slow.at[c], xbuf.at[slot], xs.at[slot]),
            pltpu.make_async_copy(cot.at[c], cbuf.at[slot], cs.at[slot]),
        )

    def stores(c, slot):
        return (pltpu.make_async_copy(obuf.at[slot], sout.at[c], osem.at[slot]),)

    for d in loads(0, 0):
        d.start()
    acc[0:width, :] = jnp.zeros((width, 128), F32)
    acc[width:, :] = accw[...]
    t = tot4[...]
    fill_tables(tab, 0, forward_rows(t, t, 1, pare))

    @loop(0, nc)
    def _(c):
        slot = lax.rem(c, 2)
        g = grp[c]
        m = mask_of(g)

        @pl.when(c + 1 < nc)
        def _():
            for d in loads(c + 1, 1 - slot):
                d.start()

        for d in loads(c, slot):
            d.wait()

        @pl.when(c >= 2)
        def _():
            for d in stores(c - 2, slot):
                d.wait()

        for lo in range(0, width, 128):
            y = dot(we[lo : lo + 128, :], acts[c])
            v = y * coef(tab, g, 0, lo, 128) + coef(tab, g, 1, lo, 128)
            v = v + xbuf[slot, lo : lo + 128, :].astype(F32)
            sg = sigmoid(v)
            obuf[slot, lo : lo + 128, :] = (v * sg * m).astype(BF16)
            dz = cbuf[slot, lo : lo + 128, :].astype(F32) * m * (sg * (1.0 + v * (1.0 - sg)))
            dze[c, lo : lo + 128, :] = dz
            add_stats(acc, lo, 128, dz, dz * y, g)
        for d in stores(c, slot):
            d.start()

    s.greet()
    s.start(acc, grp)
    s.middle()
    for c in range(max(0, nc - 2), nc):
        for d in stores(c, c % 2):
            d.wait()
    tot[...] = s.finish()


def k6(
    na, nb, grp, acts, act2, y3, y2, dze, dzw, tot5, tot4, tot3, tot2, pare, parw, par3, par2, we, wet, ww, wwt,
    dzs, dzn, tot, accn, eg, wg, epair, wpair,
    tab, tabs, tabw, tabn, acc, dye, *ar,
):
    s = Sum(na, nb, ar)
    nc = acts.shape[0]
    width = we.shape[0]

    acc[...] = jnp.zeros_like(acc)
    accn[...] = jnp.zeros_like(accn)
    t4, t5, t3 = tot4[...], tot5[...], tot3[...]
    rows, pair = backward_rows(t4, t5[:, :width], t4, 1, pare)
    fill_tables(tab, 0, rows)
    epair[...] = pair
    fill_tables(tabs, 0, forward_rows(t3[:, :256], t3, 1, par3))

    @loop(0, nc)
    def _(c):
        g = grp[c]
        m = mask_of(g)

        for lo in range(0, width, 128):
            y = dot(we[lo : lo + 128, :], acts[c])
            dy = dze[c, lo : lo + 128, :] * coef(tab, g, 0, lo, 128)
            dy = dy + y * coef(tab, g, 1, lo, 128) + coef(tab, g, 2, lo, 128)
            dye[c, lo : lo + 128, :] = (dy * m).astype(BF16)
        for lo in range(0, 256, 128):
            dx = dot(wet[lo : lo + 128, :], dye[c])
            y = y3[c, lo : lo + 128, :]
            u = y * coef(tabs, g, 0, lo, 128) + coef(tabs, g, 1, lo, 128)
            dz = m * slope_of(u) * dx
            dzs[c, lo : lo + 128, :] = dz
            add_stats(acc, lo, 128, dz, dz * y, g)

    s.greet()
    s.start(acc, grp)
    rows, pair = backward_rows(
        fold_frames(t3[:, 256:], 128), fold_frames(t5[:, width:], 128), t3, 4, parw
    )
    fill_tables(tabw, 0, rows)
    wpair[...] = pair[:, :128]
    t2 = tot2[...]
    fill_tables(tabn, 0, forward_rows(fold_frames(t2[:, 256:], 32), t2, 4, par2[:, 256:]))
    wg[...] = jnp.zeros_like(wg)
    eg[...] = jnp.zeros_like(eg)

    @loop(0, nc)
    def _(c):
        for lo in range(0, width, 256):
            eg[lo : lo + 256, :] += dot_nt(dye[c, lo : lo + 256, :], acts[c])

    s.middle()

    @loop(0, nc)
    def _(c):
        g = grp[c]
        m = mask_of(g)
        dx = jnp.zeros((128, CELLS), F32)
        act = act2[c, 256:384, :]
        for lo in range(0, 512, 128):
            y = dot(ww[lo : lo + 128, :], act)
            dy = dzw[c, lo : lo + 128, :].astype(F32) * coef(tabw, g, 0, lo, 128)
            dy = dy + y * coef(tabw, g, 1, lo, 128) + coef(tabw, g, 2, lo, 128)
            dy = (dy * m).astype(BF16)
            dx = dx + dot(wwt[:, lo : lo + 128], dy)
            wg[lo : lo + 128, :] += dot_nt(dy, act)
        y = y2[c, 256:384, :]
        u = y * coef(tabn, g, 0, 0, 128) + coef(tabn, g, 1, 0, 128)
        dz = m * slope_of(u) * dx
        dzn[c] = dz
        add_stats(accn, 0, 128, dz, dz * y, g)

    tot[...] = s.finish()


def k7(
    na, nb, grp, dzs, y3, y2, tot6, tot3, tot2, par3, par2, wst, accn,
    dzr, dys, tot, spair,
    tab, tabr, acc, d9, *ar,
):
    s = Sum(na, nb, ar)
    nc = dzs.shape[0]
    acc[0:256, :] = jnp.zeros((256, 128), F32)
    acc[256:, :] = accn[...]
    t3, t2 = tot3[...], tot2[...]
    rows, pair = backward_rows(t3[:, :256], tot6[...], t3, 1, par3)
    fill_tables(tab, 0, rows)
    spair[...] = pair
    fill_tables(tabr, 0, forward_rows(t2[:, :256], t2, 1, par2[:, :256]))

    @loop(0, nc)
    def _(c):
        g = grp[c]
        m = mask_of(g)
        dy = dzs[c] * coef(tab, g, 0, 0, 256) + y3[c] * coef(tab, g, 1, 0, 256)
        dy = (dy + coef(tab, g, 2, 0, 256)) * m
        dys[c] = dy.astype(BF16)
        taps(dy, d9, 256, -1)
        for lo in range(0, 256, 128):
            dx = dot(wst[lo : lo + 128, :], d9[...])
            y = y2[c, lo : lo + 128, :]
            u = y * coef(tabr, g, 0, lo, 128) + coef(tabr, g, 1, lo, 128)
            dz = m * slope_of(u) * dx
            dzr[c, lo : lo + 128, :] = dz
            add_stats(acc, lo, 128, dz, dz * y, g)

    s.greet()
    s.start(acc, grp)
    s.middle()
    tot[...] = s.finish()


def k8(
    na, nb, grp, dzr, dzn, dys, y2, y1, act1, act2, tot7, tot2, tot1, par2, par1, wrt, wnt,
    dyr, dz1, tot, sg, ng, rpair, npair,
    tab, tabn, tabl, acc, d9, d9n, us, ur, ds, dr, *ar,
):
    s = Sum(na, nb, ar)
    nc = dzr.shape[0]
    b = lax.axis_index("tm")
    np_ = parts_of(nc)
    size = nc // np_
    acc[...] = jnp.zeros_like(acc)
    t7, t2, t1 = tot7[...], tot2[...], tot1[...]
    rows, pair = backward_rows(t2[:, :256], t7[:, :256], t2, 1, par2[:, :256])
    fill_tables(tab, 0, rows)
    rpair[...] = pair
    rng = [slice(i * size, (i + 1) * size) for i in range(np_)]
    up = Halo(nb, 1, [(dyr.at[r, 256:512], dyr.at[r, 512:768]) for r in rng], us, ur)
    down = Halo(nb, -1, [(dyr.at[r, 256:512], dyr.at[r, 0:256]) for r in rng], ds, dr)

    @pl.when(b == 0)
    def _():
        dyr[:, 512:768, :] = jnp.zeros((nc, 256, CELLS), BF16)

    @pl.when(b == nb - 1)
    def _():
        dyr[:, 0:256, :] = jnp.zeros((nc, 256, CELLS), BF16)

    for i in range(np_):

        @loop(i * size, (i + 1) * size)
        def _(c):
            g = grp[c]
            m = mask_of(g)
            for lo in range(0, 256, 128):
                dy = dzr[c, lo : lo + 128, :] * coef(tab, g, 0, lo, 128)
                dy = dy + y2[c, lo : lo + 128, :] * coef(tab, g, 1, lo, 128)
                dy = (dy + coef(tab, g, 2, lo, 128)) * m
                dyr[c, 256 + lo : 384 + lo, :] = dy.astype(BF16)

        if i == 0:
            s.greet()
        up.start(i)
        down.start(i)

    rows, pair = backward_rows(
        fold_frames(t2[:, 256:], 32), fold_frames(t7[:, 256:], 32), t2, 4, par2[:, 256:]
    )
    fill_tables(tabn, 0, rows)
    npair[...] = pair
    fill_tables(tabl, 0, forward_rows(t1[:, :256], t1, 1, par1[:, :256]))
    fill_tables(tabl, 256, forward_rows(fold_frames(t1[:, 256:], 32), t1, 4, par1[:, 256:]))
    ng[...] = jnp.zeros_like(ng)
    sg[...] = jnp.zeros_like(sg)

    @loop(0, nc)
    def _(c):
        g = grp[c]
        m = mask_of(g)
        dy = dzn[c] * coef(tabn, g, 0, 0, 128) + y2[c, 256:384, :] * coef(tabn, g, 1, 0, 128)
        dy = (dy + coef(tabn, g, 2, 0, 128)) * m
        taps(dy, d9n, 128, -1)
        dx = dot(wnt[...], d9n[...])
        y = y1[c, 256:384, :]
        u = y * coef(tabl, g, 0, 256, 128) + coef(tabl, g, 1, 256, 128)
        dz = m * slope_of(u) * dx
        dz1[c, 256:384, :] = dz
        add_stats(acc, 256, 128, dz, dz * y, g)
        for lo in range(0, 1152, 384):
            ng[lo : lo + 384, :] += dot_nt(d9n[lo : lo + 384, :], act1[c, 256:384, :])
        taps(dys[c].astype(F32), d9, 256, -1)
        for lo in range(0, 2304, 256):
            sg[lo : lo + 256, :] += dot_nt(d9[lo : lo + 256, :], act2[c, 0:256, :])

    for i in range(np_):
        up.arrive(i)
        down.arrive(i)

        @loop(i * size, (i + 1) * size)
        def _(c):
            g = grp[c]
            m = mask_of(g)
            for lo in range(0, 256, 128):
                dx = dot(wrt[1024 + lo : 1152 + lo, :], dyr[c])
                y = y1[c, lo : lo + 128, :]
                u = y * coef(tabl, g, 0, lo, 128) + coef(tabl, g, 1, lo, 128)
                dz = m * slope_of(u) * dx
                dz1[c, lo : lo + 128, :] = dz
                add_stats(acc, lo, 128, dz, dz * y, g)

    s.start(acc, grp)
    s.middle()
    up.sent()
    down.sent()
    tot[...] = s.finish()


def k9(
    na, nb, grp, dz1, y1, xe, act1, dyr, dzw, tot8, tot1, par1, wrt, wf, slow, dze,
    sgrad, fgrad, rg, lg, qg, lpair, qpair,
    tab, dyl, dyq, xbuf, zbuf, obuf, fbuf, xs, zs, osem, fs, ls, lr, us, ur, ds, dr, *ar,
):
    s = Sum(na, nb, ar)
    nc = dz1.shape[0]
    b = lax.axis_index("tm")
    np_ = parts_of(nc)
    size = nc // np_

    def loads(c, slot):
        return (
            pltpu.make_async_copy(slow.at[c], xbuf.at[slot], xs.at[slot]),
            pltpu.make_async_copy(dze.at[c], zbuf.at[slot], zs.at[slot]),
        )

    def store(c, slot):
        return pltpu.make_async_copy(obuf.at[slot], sgrad.at[c], osem.at[slot])

    def fstore(c, slot):
        return pltpu.make_async_copy(fbuf.at[slot], fgrad.at[c], fs.at[slot])

    for d in loads(0, 0):
        d.start()
    t8, t1 = tot8[...], tot1[...]
    rows, pair = backward_rows(t1[:, :256], t8[:, :256], t1, 1, par1[:, :256])
    fill_tables(tab, 0, rows)
    lpair[...] = pair
    rows, pair = backward_rows(
        fold_frames(t1[:, 256:], 32), fold_frames(t8[:, 256:], 32), t1, 4, par1[:, 256:]
    )
    fill_tables(tab, 256, rows)
    qpair[...] = pair
    rng = [slice(i * size, (i + 1) * size) for i in range(np_)]
    lat = Halo(nb, -1, [(dyl.at[r, 0:256], dyl.at[r, 256:512]) for r in rng], ls, lr)
    up = Halo(nb, 1, [(dyq.at[r, 160:192], dyq.at[r, 0:32]) for r in rng], us, ur)
    down = Halo(nb, -1, [(dyq.at[r, 64:96], dyq.at[r, 192:224]) for r in rng], ds, dr)
    dyq[:, 32:64, :] = jnp.zeros((nc, 32, CELLS), BF16)
    dyq[:, 224:256, :] = jnp.zeros((nc, 32, CELLS), BF16)

    @pl.when(b == 0)
    def _():
        dyq[:, 0:32, :] = jnp.zeros((nc, 32, CELLS), BF16)

    @pl.when(b == nb - 1)
    def _():
        dyq[:, 192:224, :] = jnp.zeros((nc, 32, CELLS), BF16)
        dyl[:, 256:512, :] = jnp.zeros((nc, 256, CELLS), BF16)

    for i in range(np_):

        @loop(i * size, (i + 1) * size)
        def _(c):
            g = grp[c]
            m = mask_of(g)
            for lo in range(0, 384, 128):
                dy = dz1[c, lo : lo + 128, :] * coef(tab, g, 0, lo, 128)
                dy = dy + y1[c, lo : lo + 128, :] * coef(tab, g, 1, lo, 128)
                dy = ((dy + coef(tab, g, 2, lo, 128)) * m).astype(BF16)
                if lo < 256:
                    dyl[c, lo : lo + 128, :] = dy
                else:
                    dyq[c, 64:192, :] = dy

        if i == 0:
            s.greet()
        lat.start(i)
        up.start(i)
        down.start(i)

    rg[...] = jnp.zeros_like(rg)
    lg[...] = jnp.zeros_like(lg)
    qg[...] = jnp.zeros_like(qg)

    @loop(0, nc)
    def _(c):
        slot = lax.rem(c, 2)
        m = mask_of(grp[c])

        @pl.when(c + 1 < nc)
        def _():
            for d in loads(c + 1, 1 - slot):
                d.start()

        for d in loads(c, slot):
            d.wait()

        @pl.when(c >= 2)
        def _():
            store(c - 2, slot).wait()

        for lo in range(0, 1024, 128):
            dx = dot(wrt[lo : lo + 128, :], dyr[c]) + zbuf[slot, lo : lo + 128, :]
            obuf[slot, lo : lo + 128, :] = (dx * m).astype(BF16)
        store(c, slot).start()
        for lo in range(0, 768, 256):
            dy = dyr[c, lo : lo + 256, :]
            rg[lo : lo + 256, 0:1024] += dot_nt(dy, xbuf[slot])
            rg[lo : lo + 256, 1024:1280] += dot_nt(dy, act1[c, 0:256, :])
        lg[...] += dot_nt(dyl[c, 0:256, :], xe[c, 0:640, :])
        qg[...] += dot_nt(dyq[c, 64:192, :], xe[c, 128:896, :])

    for i in range(np_):
        lat.arrive(i)
        up.arrive(i)
        down.arrive(i)

        @loop(i * size, (i + 1) * size)
        def _(c):
            slot = lax.rem(c, 2)
            m = mask_of(grp[c])

            @pl.when(c >= 2)
            def _():
                fstore(c - 2, slot).wait()

            for lo in range(0, 512, 128):
                dx = dot(wf[lo : lo + 128, 0:512], dyl[c]) + dot(wf[lo : lo + 128, 512:768], dyq[c])
                dx = dx + dzw[c, lo : lo + 128, :].astype(F32)
                fbuf[slot, lo : lo + 128, :] = (dx * m).astype(BF16)
            fstore(c, slot).start()

    for c in range(max(0, nc - 2), nc):
        store(c, c % 2).wait()
        fstore(c, c % 2).wait()
    lat.sent()
    up.sent()
    down.sent()


def weights_of(reducer, spatial, expand, lateral, squeeze, narrow, widening):
    eye = jnp.eye(4, dtype=BF16)
    band = jnp.asarray(
        [[[1.0 if e == f + 1 + j else 0.0 for j in range(3)] for e in range(7)] for f in range(4)], BF16
    )
    lat = jnp.transpose(lateral, (1, 0, 2)).reshape(256, 640)
    lat = jnp.pad(lat, ((0, 0), (0, 256)))
    sq = jnp.einsum("fej,jop->foep", band, squeeze).reshape(128, 896)
    wa = jnp.concatenate([lat, sq], axis=0)
    wr = reducer.reshape(768, 1280)
    wrt = jnp.transpose(wr)
    wn = jnp.einsum("fg,koc->fokgc", eye, narrow).reshape(128, 1152)
    wnt = jnp.einsum("fg,koc->fckgo", eye, narrow).reshape(128, 1152)
    ws = jnp.transpose(spatial, (1, 0, 2)).reshape(256, 2304)
    wst = jnp.transpose(spatial, (2, 0, 1)).reshape(256, 2304)
    ww = jnp.einsum("fg,oc->fogc", eye, widening).reshape(512, 128)
    wwt = jnp.transpose(ww)
    back = jnp.asarray(
        [
            [[1.0 if e == (0, 2, 3, 4, 5, 6)[f + 2 - j] else 0.0 for j in range(3)] for e in range(8)]
            for f in range(4)
        ],
        BF16,
    )
    sqb = jnp.einsum("fej,jop->fpeo", back, squeeze).reshape(512, 256)
    late = jnp.asarray(
        [
            [[1.0 if (s, k) in pairs else 0.0 for k in range(5)] for s in range(2)]
            for pairs in (((0, 2),), ((0, 3),), ((0, 4), (1, 0)), ((1, 1),))
        ],
        BF16,
    )
    latb = jnp.einsum("fsk,kop->fpso", late, lateral).reshape(512, 512)
    wf = jnp.concatenate([latb, sqb], axis=1)
    return wa, wr, wrt, wn, wnt, ws, wst, expand, jnp.transpose(expand), ww, wwt, wf


def sds(shape, dtype):
    return jax.ShapeDtypeStruct(shape, dtype)


def build(na, nb):
    def call(body, cid, ins, outs, scratch, args, arw, flops=0):
        spec = {"v": VM, "h": pl.ANY, "s": pltpu.SMEM}
        moved = sum(a.size * a.dtype.itemsize for a in args) + sum(
            o.size * o.dtype.itemsize for o in outs[1]
        )
        return pl.pallas_call(
            functools.partial(body, na, nb),
            name=body.__name__,
            out_shape=tuple(outs[1]),
            in_specs=[pl.BlockSpec(memory_space=spec[k]) for k in ins],
            out_specs=tuple(pl.BlockSpec(memory_space=spec[k]) for k in outs[0]),
            scratch_shapes=scratch + ar_scratch(na, nb, arw),
            compiler_params=pltpu.CompilerParams(
                collective_id=cid, has_side_effects=True, vmem_limit_bytes=LIMIT
            ),
            cost_estimate=pl.CostEstimate(flops=flops, bytes_accessed=moved, transcendentals=0),
        )(*args)

    def body(
        slow_in, fast_in, clip_group, reducer, spatial, expand, lateral, squeeze, narrow, widening,
        reducer_norm, spatial_norm, expand_norm, lateral_norm, squeeze_norm, narrow_norm, widening_norm,
        slow_cot, fast_cot,
    ):
        nc = slow_in.shape[0]
        dma = pltpu.SemaphoreType.DMA
        grp = clip_group
        slow = slow_in.reshape(nc, 1024, CELLS)
        fast = fast_in.reshape(nc, 512, CELLS)
        scot = slow_cot.reshape(nc, 1024, CELLS)
        fcot = fast_cot.reshape(nc, 512, CELLS)
        wa, wr, wrt, wn, wnt, ws, wst, we, wet, ww, wwt, wf = weights_of(
            reducer, spatial, expand, lateral, squeeze, narrow, widening
        )

        def four(pair):
            return jnp.concatenate([pair] * 4, axis=1)

        par1 = jnp.concatenate([lateral_norm, four(squeeze_norm)], axis=1).astype(F32)
        par2 = jnp.concatenate([reducer_norm, four(narrow_norm)], axis=1).astype(F32)
        par3 = spatial_norm.astype(F32)
        pare = expand_norm.astype(F32)
        parw = four(widening_norm).astype(F32)
        np_ = parts_of(nc)
        sems = [dma((np_,))] * 4

        def act(c, dtype):
            return sds((nc, c, CELLS), dtype)

        def tab(k, c):
            return VM((3, k, c, 128), F32)

        xe, y1, tot1 = call(
            k1, 1, "shv", ("vvv", [act(896, BF16), act(384, F32), sds((8, 384), F32)]),
            [VM((384, 128), F32), dma((np_,))] + sems, (grp, fast, wa), 384,
        )
        half = VM((nc, 256, CELLS), BF16)
        act1, y2, tot2 = call(
            k2, 2, "svvvvvv", ("vvv", [act(384, BF16), act(384, F32), sds((8, 384), F32)]),
            [tab(2, 384), VM((384, 128), F32), VM((1152, CELLS), BF16), half, half, half, half] + sems,
            (grp, y1, tot1, par1, slow, wr, wn), 384,
        )
        act2, y3, tot3 = call(
            k3, 3, "svvvvv", ("vvv", [act(384, BF16), act(256, F32), sds((8, 768), F32)]),
            [tab(2, 384), VM((768, 128), F32), VM((2304, CELLS), BF16)],
            (grp, y2, tot2, par2, ws, ww), 768,
        )
        two = VM((2, 512, CELLS), BF16)
        acts, tot4, fast_out, dzw, accw = call(
            k4, 4, "svvvvvvvvh",
            ("vvhvv", [act(256, BF16), sds((8, 1024), F32), act(512, BF16), act(512, F32), sds((512, 128), F32)]),
            [tab(2, 256), tab(2, 512), VM((1024, 128), F32), two, two, dma((2,)), dma((2,))],
            (grp, y3, tot3, par3, parw, we, ww, act2, xe, fcot), 1024,
        )
        big = VM((2, 1024, CELLS), BF16)
        slow_out, dze, tot5 = call(
            k5, 5, "svvvvvhh", ("hvv", [act(1024, BF16), act(1024, F32), sds((8, 1536), F32)]),
            [tab(2, 1024), VM((1536, 128), F32), big, big, big] + [dma((2,))] * 3,
            (grp, acts, tot4, pare, we, accw, slow, scot), 1536,
        )
        dzs, dzn, tot6, accn, eg, wg, epair, wpair = call(
            k6, 6, "svvvvvv" + "v" * 12,
            (
                "v" * 8,
                [
                    act(256, F32), act(128, F32), sds((8, 256), F32), sds((128, 128), F32),
                    sds((1024, 256), F32), sds((512, 128), F32), sds((2, 1024), F32), sds((2, 128), F32),
                ],
            ),
            [
                tab(3, 1024), tab(2, 256), tab(3, 512), tab(2, 128), VM((256, 128), F32),
                VM((nc, 1024, CELLS), BF16),
            ],
            (grp, acts, act2, y3, y2, dze, dzw, tot5, tot4, tot3, tot2, pare, parw, par3, par2, we, wet, ww, wwt),
            256,
        )
        dzr, dys, tot7, spair = call(
            k7, 7, "s" + "v" * 10,
            ("v" * 4, [act(256, F32), act(256, BF16), sds((8, 384), F32), sds((2, 256), F32)]),
            [tab(3, 256), tab(2, 256), VM((384, 128), F32), VM((2304, CELLS), BF16)],
            (grp, dzs, y3, y2, tot6, tot3, tot2, par3, par2, wst, accn), 384,
        )
        dyr, dz1, tot8, sg, ng, rpair, npair = call(
            k8, 8, "s" + "v" * 14,
            (
                "v" * 7,
                [
                    act(768, BF16), act(384, F32), sds((8, 384), F32), sds((2304, 256), F32),
                    sds((1152, 128), F32), sds((2, 256), F32), sds((2, 128), F32),
                ],
            ),
            [
                tab(3, 256), tab(3, 128), tab(2, 384), VM((384, 128), F32),
                VM((2304, CELLS), BF16), VM((1152, CELLS), BF16),
            ] + sems,
            (grp, dzr, dzn, dys, y2, y1, act1, act2, tot7, tot2, tot1, par2, par1, wrt, wnt), 384,
        )
        slow_grad, fast_grad, rg, lg, qg, lpair, qpair = call(
            k9, 9, "s" + "v" * 11 + "hh",
            (
                "hhvvvvv",
                [
                    act(1024, BF16), act(512, BF16), sds((768, 1280), F32), sds((256, 640), F32),
                    sds((128, 768), F32), sds((2, 256), F32), sds((2, 128), F32),
                ],
            ),
            [
                tab(3, 384), VM((nc, 512, CELLS), BF16), VM((nc, 256, CELLS), BF16), big, VM((2, 1024, CELLS), F32), big, two,
                dma((2,)), dma((2,)), dma((2,)), dma((2,)),
            ] + sems + [dma((np_,))] * 2,
            (grp, dz1, y1, xe, act1, dyr, dzw, tot8, tot1, par1, wrt, wf, slow, dze), 128,
        )
        eye = jnp.eye(4, dtype=F32)
        reducer_grad = rg.reshape(3, 256, 1280)
        spatial_grad = sg.reshape(9, 256, 256)
        lateral_grad = jnp.transpose(lg.reshape(256, 5, 128), (1, 0, 2))
        q6 = qg.reshape(4, 32, 6, 128)
        squeeze_grad = jnp.stack([sum(q6[f, :, f + j, :] for f in range(4)) for j in range(3)])
        n6 = ng.reshape(9, 4, 32, 4, 32)
        narrow_grad = sum(n6[:, f, :, f, :] for f in range(4))
        w6 = wg.reshape(4, 128, 4, 32)
        widening_grad = sum(w6[f, :, f, :] for f in range(4))
        grads = lax.psum(
            (reducer_grad, spatial_grad, eg, lateral_grad, squeeze_grad, narrow_grad, widening_grad),
            ("clip", "tm"),
        )
        return (
            slow_out.reshape(slow_in.shape), fast_out.reshape(fast_in.shape),
            slow_grad.reshape(slow_in.shape), fast_grad.reshape(fast_in.shape),
            *grads,
            rpair, spair, epair, lpair, qpair[:, :32], npair[:, :32], wpair,
        )

    return body


def solution(mesh):
    body = build(mesh.shape["clip"], mesh.shape["tm"])
    big = P("clip", "tm", None, None)
    return jax.shard_map(
        body,
        mesh=mesh,
        in_specs=(big, big, P("clip")) + (P(),) * 14 + (big, big),
        out_specs=(big,) * 4 + (P(),) * 14,
        check_vma=False,
    )
```

```python
import functools

import jax
import jax.numpy as jnp
from jax import lax
from jax.experimental import pallas as pl
from jax.experimental.pallas import tpu as pltpu
from jax.sharding import PartitionSpec as P

MESH = pl.DeviceIdType.MESH
F32, BF16 = jnp.float32, jnp.bfloat16
SIDE = 16
CELLS = SIDE * SIDE
EPS = 1e-05
VM = pltpu.VMEM
LIMIT = 56 * 1024 * 1024


def dot(a, b):
    return lax.dot_general(a, b, (((1,), (0,)), ((), ())), preferred_element_type=F32)


def dot_nt(a, b):
    return lax.dot_general(a, b, (((1,), (1,)), ((), ())), preferred_element_type=F32)


def side_of(g):
    return jnp.where(g == 0, SIDE * 5 // 8, jnp.where(g == 1, SIDE * 7 // 8, SIDE))


def mask_of(g):
    cell = lax.broadcasted_iota(jnp.int32, (1, CELLS), 1)
    side = side_of(g)
    return jnp.where(((cell >> 4) < side) & ((cell & 15) < side), 1.0, 0.0).astype(F32)


def counts_row(grp):
    lane = lax.broadcasted_iota(jnp.int32, (1, 128), 1)
    total = jnp.zeros((1, 128), F32)
    for c in range(grp.shape[0]):
        side = side_of(grp[c])
        total = total + jnp.where(lane == grp[c], (side * side).astype(F32), 0.0)
    return total


def add_stats(acc, lo, rows, first, second, g):
    lane = lax.broadcasted_iota(jnp.int32, (1, 128), 1)
    one = jnp.sum(first[:, :128] + first[:, 128:], axis=1, keepdims=True)
    two = jnp.sum(second[:, :128] + second[:, 128:], axis=1, keepdims=True)
    acc[lo : lo + rows, :] += jnp.where(lane == g, one, 0.0) + jnp.where(lane == g + 3, two, 0.0)


def ar_scratch(na, nb, width):
    dma = pltpu.SemaphoreType.DMA
    return [
        VM((8, width), F32),
        VM((na, 8, width), F32),
        VM((8, width), F32),
        VM((nb, 8, width), F32),
        dma((na - 1,)),
        dma((na - 1,)),
        dma((nb - 1,)),
        dma((nb - 1,)),
    ]


class Sum:
    def __init__(self, na, nb, refs):
        self.na, self.nb = na, nb
        if refs is not None:
            self.mine, self.bufa, self.part, self.bufb, self.sa, self.ra, self.sb, self.rb = refs
        self.a, self.b = lax.axis_index("clip"), lax.axis_index("tm")
        bar = pltpu.get_barrier_semaphore()
        for peer in self.peers_a() + self.peers_b():
            pl.semaphore_signal(bar, inc=1, device_id=peer, device_id_type=MESH)
        self.bar = bar

    def peers_a(self):
        return [(lax.rem(self.a + d, self.na), self.b) for d in range(1, self.na)]

    def peers_b(self):
        return [(self.a, lax.rem(self.b + d, self.nb)) for d in range(1, self.nb)]

    def greet(self):
        pl.semaphore_wait(self.bar, self.na - 1 + self.nb - 1)

    def copies(self, src, buf, slot, ss, rs, peers):
        return [
            pltpu.make_async_remote_copy(
                src, buf.at[slot], ss.at[i], rs.at[i], device_id=peer, device_id_type=MESH
            )
            for i, peer in enumerate(peers)
        ]

    def start(self, acc, grp):
        width = self.mine.shape[1]
        rows = jnp.transpose(acc[...])[:8, :]
        row = lax.broadcasted_iota(jnp.int32, (8, 128), 0)
        head = jnp.where(row == 6, counts_row(grp), rows[:, :128])
        value = head if width == 128 else jnp.concatenate([head, rows[:, 128:]], axis=1)
        self.mine[...] = value
        self.bufa[self.a] = value
        self.first = self.copies(self.mine, self.bufa, self.a, self.sa, self.ra, self.peers_a())
        for c in self.first:
            c.start()

    def middle(self):
        for c in self.first:
            c.wait()
        total = self.bufa[0]
        for i in range(1, self.na):
            total = total + self.bufa[i]
        self.part[...] = total
        self.bufb[self.b] = total
        self.second = self.copies(self.part, self.bufb, self.b, self.sb, self.rb, self.peers_b())
        for c in self.second:
            c.start()

    def finish(self):
        for c in self.second:
            c.wait()
        total = self.bufb[0]
        for i in range(1, self.nb):
            total = total + self.bufb[i]
        return total


class Halo:
    def __init__(self, nb, step, parts, ss, rs):
        self.a, self.b = lax.axis_index("clip"), lax.axis_index("tm")
        to = self.b + step
        self.sends = (to >= 0) & (to < nb)
        source = self.b - step
        self.gets = (source >= 0) & (source < nb)
        peer = (self.a, lax.rem(to + nb, nb))
        self.copies = [
            pltpu.make_async_remote_copy(
                src, dst, ss.at[i], rs.at[i], device_id=peer, device_id_type=MESH
            )
            for i, (src, dst) in enumerate(parts)
        ]

    def start(self, i):
        @pl.when(self.sends)
        def _():
            self.copies[i].start()

    def arrive(self, i):
        @pl.when(self.gets)
        def _():
            self.copies[i].wait_recv()

    def sent(self):
        @pl.when(self.sends)
        def _():
            for c in self.copies:
                c.wait_send()


def fold_frames(total, chans):
    width = total.shape[1]
    if chans < 128:
        out = total
        shift = chans
        while shift < 128:
            out = out + pltpu.roll(out, shift, 1)
            shift *= 2
        return out
    out = total[:, :128]
    for f in range(1, width // 128):
        out = out + total[:, 128 * f : 128 * (f + 1)]
    return jnp.concatenate([out] * (width // 128), axis=1)


def moments(total, counts, frames):
    out = []
    for g in range(3):
        n = counts[6:7, g : g + 1] * float(frames)
        mean = total[g : g + 1, :] / n
        var = total[g + 3 : g + 4, :] / n - mean * mean
        out.append((n, mean, lax.rsqrt(var + EPS)))
    return out


def fill_tables(tab, base, rows_list):
    width = rows_list[0][0].shape[1]
    count = len(rows_list[0])
    rows = [rows_list[g][k] for g in range(3) for k in range(count)]
    rows = rows + [jnp.zeros((1, width), F32)] * (128 - len(rows))
    cols = jnp.transpose(jnp.concatenate(rows, axis=0))
    for g in range(3):
        for k in range(count):
            i = g * count + k
            tab[g, k, base : base + width, :] = jnp.broadcast_to(cols[:, i : i + 1], (width, 128))


def forward_rows(total, counts, frames, pair):
    out = []
    for n, mean, r in moments(total, counts, frames):
        gain = pair[0:1, :] * r
        out.append((gain, pair[1:2, :] - mean * gain))
    return out


def backward_rows(total, grads, counts, frames, pair):
    out, two_all, one_all = [], 0.0, 0.0
    for g, (n, mean, r) in enumerate(moments(total, counts, frames)):
        one = grads[g : g + 1, :]
        two = r * (grads[g + 3 : g + 4, :] - mean * one)
        c0 = pair[0:1, :] * r
        slope = c0 * r * two / n
        out.append((c0, -slope, slope * mean - c0 * one / n))
        two_all, one_all = two_all + two, one_all + one
    return out, jnp.concatenate([two_all, one_all], axis=0)


def wide(v):
    return jnp.concatenate([v, v], axis=1)


def coef(tab, g, k, lo, rows):
    return wide(tab[g, k, lo : lo + rows, :])


def sigmoid(v):
    return 0.5 * jnp.tanh(0.5 * v) + 0.5


def slope_of(v):
    s = sigmoid(v)
    return s * (1.0 + v * (1.0 - s))


def taps(x, dst, rows, sign, at=0):
    cell = lax.broadcasted_iota(jnp.int32, (1, CELLS), 1)
    row, col = cell >> 4, cell & 15
    for k in range(9):
        di, dl = sign * (k // 3 - 1), sign * (k % 3 - 1)
        step = SIDE * di + dl
        if step == 0:
            dst[k * rows : (k + 1) * rows, at : at + CELLS] = x.astype(BF16)
            continue
        moved = pltpu.roll(x, (-step) % CELLS, 1)
        ok = (row + di >= 0) & (row + di < SIDE) & (col + dl >= 0) & (col + dl < SIDE)
        dst[k * rows : (k + 1) * rows, at : at + CELLS] = jnp.where(ok, moved, 0.0).astype(BF16)


def loop(lo, hi):
    return pl.loop(lo, hi)


def parts_of(nc):
    for p in (3, 4, 2):
        if nc % p == 0:
            return p
    return 1


def k1(na, nb, grp, fast, wa, xe, y1, tot, acc, os, us, ur, ds, dr, *ar):
    s = Sum(na, nb, ar)
    nc = fast.shape[0]
    b = lax.axis_index("tm")
    np_ = parts_of(nc)
    size = nc // np_
    rows = [slice(i * size, (i + 1) * size) for i in range(np_)]
    own = [pltpu.make_async_copy(fast.at[r], xe.at[r, 256:768], os.at[i]) for i, r in enumerate(rows)]
    for c in own:
        c.start()
    up = Halo(nb, 1, [(fast.at[r, 256:512], xe.at[r, 0:256]) for r in rows], us, ur)
    down = Halo(nb, -1, [(fast.at[r, 0:128], xe.at[r, 768:896]) for r in rows], ds, dr)
    acc[...] = jnp.zeros_like(acc)

    @pl.when(b == 0)
    def _():
        xe[:, 0:256, :] = jnp.zeros((nc, 256, CELLS), BF16)

    @pl.when(b == nb - 1)
    def _():
        xe[:, 768:896, :] = jnp.zeros((nc, 128, CELLS), BF16)

    s.greet()
    for i in range(np_):
        up.start(i)
        down.start(i)
    for i in range(np_):
        own[i].wait()
        up.arrive(i)
        down.arrive(i)

        @loop(i * size, (i + 1) * size)
        def _(c):
            g = grp[c]
            m = mask_of(g)
            for lo in range(0, 384, 128):
                y = dot(wa[lo : lo + 128, :], xe[c])
                y1[c, lo : lo + 128, :] = y
                ym = y * m
                add_stats(acc, lo, 128, ym, ym * y, g)

    s.start(acc, grp)
    s.middle()
    up.sent()
    down.sent()
    tot[...] = s.finish()


def k2(na, nb, grp, y1, tot1, par1, slow, wr, wn, act1, y2, tot, tab, acc, x9, su, sd, ru, rd, us, ur, ds, dr, *ar):
    s = Sum(na, nb, ar)
    nc = y1.shape[0]
    b = lax.axis_index("tm")
    np_ = parts_of(nc)
    size = nc // np_
    acc[...] = jnp.zeros_like(acc)
    t = tot1[...]
    fill_tables(tab, 0, forward_rows(t[:, :256], t, 1, par1[:, :256]))
    fill_tables(tab, 256, forward_rows(fold_frames(t[:, 256:], 32), t, 4, par1[:, 256:]))
    rows = [slice(i * size, (i + 1) * size) for i in range(np_)]
    up = Halo(nb, 1, [(su.at[r], ru.at[r]) for r in rows], us, ur)
    down = Halo(nb, -1, [(sd.at[r], rd.at[r]) for r in rows], ds, dr)

    @pl.when(b == 0)
    def _():
        ru[...] = jnp.zeros_like(ru)

    @pl.when(b == nb - 1)
    def _():
        rd[...] = jnp.zeros_like(rd)

    for i in range(np_):

        @loop(i * size, (i + 1) * size)
        def _(c):
            g = grp[c]
            m = mask_of(g)
            for lo in range(0, 256, 128):
                u = y1[c, lo : lo + 128, :] * coef(tab, g, 0, lo, 128) + coef(tab, g, 1, lo, 128)
                act1[c, lo : lo + 128, :] = (u * sigmoid(u) * m).astype(BF16)
            for j, dst in enumerate((su, y2, sd)):
                for lo in range(0, 256, 128):
                    r0 = 256 * j + lo
                    p = dot(wr[r0 : r0 + 128, :1024], slow[c]) + dot(
                        wr[r0 : r0 + 128, 1024:], act1[c, 0:256, :]
                    )
                    dst[c, lo : lo + 128, :] = p.astype(dst.dtype)

        if i == 0:
            s.greet()
        up.start(i)
        down.start(i)

    @loop(0, nc)
    def _(c):
        g = grp[c]
        m = mask_of(g)
        u = y1[c, 256:384, :] * coef(tab, g, 0, 256, 128) + coef(tab, g, 1, 256, 128)
        act = u * sigmoid(u) * m
        act1[c, 256:384, :] = act.astype(BF16)
        taps(act, x9, 128, 1)
        y = dot(wn[...], x9[...])
        y2[c, 256:384, :] = y
        ym = y * m
        add_stats(acc, 256, 128, ym, ym * y, g)

    for i in range(np_):
        up.arrive(i)
        down.arrive(i)

        @loop(i * size, (i + 1) * size)
        def _(c):
            g = grp[c]
            m = mask_of(g)
            for lo in range(0, 256, 128):
                y = (
                    y2[c, lo : lo + 128, :]
                    + ru[c, lo : lo + 128, :].astype(F32)
                    + rd[c, lo : lo + 128, :].astype(F32)
                )
                y2[c, lo : lo + 128, :] = y
                ym = y * m
                add_stats(acc, lo, 128, ym, ym * y, g)

    s.start(acc, grp)
    s.middle()
    up.sent()
    down.sent()
    tot[...] = s.finish()


def k3(na, nb, grp, y2, tot2, par2, ws, ww, act2, y3, tot, tab, acc, x9, *ar):
    s = Sum(na, nb, ar)
    nc = y2.shape[0]
    acc[...] = jnp.zeros_like(acc)
    t = tot2[...]
    fill_tables(tab, 0, forward_rows(t[:, :256], t, 1, par2[:, :256]))
    fill_tables(tab, 256, forward_rows(fold_frames(t[:, 256:], 32), t, 4, par2[:, 256:]))

    @loop(0, nc)
    def _(c):
        g = grp[c]
        m = mask_of(g)
        u = y2[c, 256:384, :] * coef(tab, g, 0, 256, 128) + coef(tab, g, 1, 256, 128)
        act2[c, 256:384, :] = (u * sigmoid(u) * m).astype(BF16)
        u = y2[c, 0:256, :] * coef(tab, g, 0, 0, 256) + coef(tab, g, 1, 0, 256)
        act = u * sigmoid(u) * m
        act2[c, 0:256, :] = act.astype(BF16)
        taps(act, x9, 256, 1)
        for lo in range(0, 512, 128):
            y = dot(ww[lo : lo + 128, :], act2[c, 256:384, :])
            ym = y * m
            add_stats(acc, 256 + lo, 128, ym, ym * y, g)
        for lo in range(0, 256, 128):
            y = dot(ws[lo : lo + 128, :], x9[...])
            y3[c, lo : lo + 128, :] = y
            ym = y * m
            add_stats(acc, lo, 128, ym, ym * y, g)

    s.greet()
    s.start(acc, grp)
    s.middle()
    tot[...] = s.finish()


def k4(
    na, nb, grp, y3, tot3, par3, parw, we, ww, act2, xe, fcot,
    acts, tot, fout, dzw, accw,
    tab, tabw, acc, cbuf, obuf, cs, osem, *ar,
):
    s = Sum(na, nb, ar)
    nc = y3.shape[0]
    acc[...] = jnp.zeros_like(acc)
    accw[...] = jnp.zeros_like(accw)
    t = tot3[...]
    fill_tables(tab, 0, forward_rows(t[:, :256], t, 1, par3))
    fill_tables(tabw, 0, forward_rows(fold_frames(t[:, 256:], 128), t, 4, parw))

    def load(c, slot):
        return pltpu.make_async_copy(fcot.at[c], cbuf.at[slot], cs.at[slot])

    def store(c, slot):
        return pltpu.make_async_copy(obuf.at[slot], fout.at[c], osem.at[slot])

    load(0, 0).start()

    @loop(0, nc)
    def _(c):
        g = grp[c]
        m = mask_of(g)
        for lo in range(0, 256, 128):
            u = y3[c, lo : lo + 128, :] * coef(tab, g, 0, lo, 128) + coef(tab, g, 1, lo, 128)
            acts[c, lo : lo + 128, :] = (u * sigmoid(u) * m).astype(BF16)
        for lo in range(0, 1024, 128):
            y = dot(we[lo : lo + 128, :], acts[c])
            ym = y * m
            add_stats(acc, lo, 128, ym, ym * y, g)

    s.greet()
    s.start(acc, grp)

    @loop(0, nc)
    def _(c):
        slot = lax.rem(c, 2)
        g = grp[c]
        m = mask_of(g)

        @pl.when(c + 1 < nc)
        def _():
            load(c + 1, 1 - slot).start()

        load(c, slot).wait()

        @pl.when(c >= 2)
        def _():
            store(c - 2, slot).wait()

        for lo in range(0, 512, 128):
            y = dot(ww[lo : lo + 128, :], act2[c, 256:384, :])
            v = y * coef(tabw, g, 0, lo, 128) + coef(tabw, g, 1, lo, 128)
            v = v + xe[c, 256 + lo : 384 + lo, :].astype(F32)
            sg = sigmoid(v)
            obuf[slot, lo : lo + 128, :] = (v * sg * m).astype(BF16)
            dz = cbuf[slot, lo : lo + 128, :].astype(F32) * m * (sg * (1.0 + v * (1.0 - sg)))
            dzw[c, lo : lo + 128, :] = dz
            add_stats(accw, lo, 128, dz, dz * y, g)
        store(c, slot).start()

    s.middle()
    for c in range(max(0, nc - 2), nc):
        store(c, c % 2).wait()
    tot[...] = s.finish()


def k5(
    na, nb, grp, acts, tot4, pare, we, accw, slow, cot,
    sout, dze, tot,
    tab, acc, xbuf, cbuf, obuf, xs, cs, osem, *ar,
):
    s = Sum(na, nb, ar)
    nc = acts.shape[0]
    width = we.shape[0]

    def loads(c, slot):
        return (
            pltpu.make_async_copy(slow.at[c], xbuf.at[slot], xs.at[slot]),
            pltpu.make_async_copy(cot.at[c], cbuf.at[slot], cs.at[slot]),
        )

    def stores(c, slot):
        return (pltpu.make_async_copy(obuf.at[slot], sout.at[c], osem.at[slot]),)

    for d in loads(0, 0):
        d.start()
    acc[0:width, :] = jnp.zeros((width, 128), F32)
    acc[width:, :] = accw[...]
    t = tot4[...]
    fill_tables(tab, 0, forward_rows(t, t, 1, pare))

    @loop(0, nc)
    def _(c):
        slot = lax.rem(c, 2)
        g = grp[c]
        m = mask_of(g)

        @pl.when(c + 1 < nc)
        def _():
            for d in loads(c + 1, 1 - slot):
                d.start()

        for d in loads(c, slot):
            d.wait()

        @pl.when(c >= 2)
        def _():
            for d in stores(c - 2, slot):
                d.wait()

        for lo in range(0, width, 128):
            y = dot(we[lo : lo + 128, :], acts[c])
            v = y * coef(tab, g, 0, lo, 128) + coef(tab, g, 1, lo, 128)
            v = v + xbuf[slot, lo : lo + 128, :].astype(F32)
            sg = sigmoid(v)
            obuf[slot, lo : lo + 128, :] = (v * sg * m).astype(BF16)
            dz = cbuf[slot, lo : lo + 128, :].astype(F32) * m * (sg * (1.0 + v * (1.0 - sg)))
            dze[c, lo : lo + 128, :] = dz
            add_stats(acc, lo, 128, dz, dz * y, g)
        for d in stores(c, slot):
            d.start()

    s.greet()
    s.start(acc, grp)
    s.middle()
    for c in range(max(0, nc - 2), nc):
        for d in stores(c, c % 2):
            d.wait()
    tot[...] = s.finish()


def k6(
    na, nb, grp, acts, act2, y3, y2, dze, dzw, tot5, tot4, tot3, tot2, pare, parw, par3, par2, we, wet, ww, wwt,
    dzs, dzn, tot, accn, eg, wg, epair, wpair,
    tab, tabs, tabw, tabn, acc, dye, *ar,
):
    s = Sum(na, nb, ar)
    nc = acts.shape[0]
    width = we.shape[0]

    acc[...] = jnp.zeros_like(acc)
    accn[...] = jnp.zeros_like(accn)
    t4, t5, t3 = tot4[...], tot5[...], tot3[...]
    rows, pair = backward_rows(t4, t5[:, :width], t4, 1, pare)
    fill_tables(tab, 0, rows)
    epair[...] = pair
    fill_tables(tabs, 0, forward_rows(t3[:, :256], t3, 1, par3))

    @loop(0, nc)
    def _(c):
        g = grp[c]
        m = mask_of(g)

        for lo in range(0, width, 128):
            y = dot(we[lo : lo + 128, :], acts[c])
            dy = dze[c, lo : lo + 128, :] * coef(tab, g, 0, lo, 128)
            dy = dy + y * coef(tab, g, 1, lo, 128) + coef(tab, g, 2, lo, 128)
            dye[c, lo : lo + 128, :] = (dy * m).astype(BF16)
        for lo in range(0, 256, 128):
            dx = dot(wet[lo : lo + 128, :], dye[c])
            y = y3[c, lo : lo + 128, :]
            u = y * coef(tabs, g, 0, lo, 128) + coef(tabs, g, 1, lo, 128)
            dz = m * slope_of(u) * dx
            dzs[c, lo : lo + 128, :] = dz
            add_stats(acc, lo, 128, dz, dz * y, g)

    s.greet()
    s.start(acc, grp)
    rows, pair = backward_rows(
        fold_frames(t3[:, 256:], 128), fold_frames(t5[:, width:], 128), t3, 4, parw
    )
    fill_tables(tabw, 0, rows)
    wpair[...] = pair[:, :128]
    t2 = tot2[...]
    fill_tables(tabn, 0, forward_rows(fold_frames(t2[:, 256:], 32), t2, 4, par2[:, 256:]))
    wg[...] = jnp.zeros_like(wg)
    eg[...] = jnp.zeros_like(eg)

    @loop(0, nc)
    def _(c):
        for lo in range(0, width, 256):
            eg[lo : lo + 256, :] += dot_nt(dye[c, lo : lo + 256, :], acts[c])

    s.middle()

    @loop(0, nc)
    def _(c):
        g = grp[c]
        m = mask_of(g)
        dx = jnp.zeros((128, CELLS), F32)
        act = act2[c, 256:384, :]
        for lo in range(0, 512, 128):
            y = dot(ww[lo : lo + 128, :], act)
            dy = dzw[c, lo : lo + 128, :].astype(F32) * coef(tabw, g, 0, lo, 128)
            dy = dy + y * coef(tabw, g, 1, lo, 128) + coef(tabw, g, 2, lo, 128)
            dy = (dy * m).astype(BF16)
            dx = dx + dot(wwt[:, lo : lo + 128], dy)
            wg[lo : lo + 128, :] += dot_nt(dy, act)
        y = y2[c, 256:384, :]
        u = y * coef(tabn, g, 0, 0, 128) + coef(tabn, g, 1, 0, 128)
        dz = m * slope_of(u) * dx
        dzn[c] = dz
        add_stats(accn, 0, 128, dz, dz * y, g)

    tot[...] = s.finish()


def k7(
    na, nb, grp, dzs, y3, y2, tot6, tot3, tot2, par3, par2, wst, accn,
    dzr, dys, tot, spair,
    tab, tabr, acc, d9, *ar,
):
    s = Sum(na, nb, ar)
    nc = dzs.shape[0]
    acc[0:256, :] = jnp.zeros((256, 128), F32)
    acc[256:, :] = accn[...]
    t3, t2 = tot3[...], tot2[...]
    rows, pair = backward_rows(t3[:, :256], tot6[...], t3, 1, par3)
    fill_tables(tab, 0, rows)
    spair[...] = pair
    fill_tables(tabr, 0, forward_rows(t2[:, :256], t2, 1, par2[:, :256]))

    @loop(0, nc)
    def _(c):
        g = grp[c]
        m = mask_of(g)
        dy = dzs[c] * coef(tab, g, 0, 0, 256) + y3[c] * coef(tab, g, 1, 0, 256)
        dy = (dy + coef(tab, g, 2, 0, 256)) * m
        dys[c] = dy.astype(BF16)
        taps(dy, d9, 256, -1)
        for lo in range(0, 256, 128):
            dx = dot(wst[lo : lo + 128, :], d9[...])
            y = y2[c, lo : lo + 128, :]
            u = y * coef(tabr, g, 0, lo, 128) + coef(tabr, g, 1, lo, 128)
            dz = m * slope_of(u) * dx
            dzr[c, lo : lo + 128, :] = dz
            add_stats(acc, lo, 128, dz, dz * y, g)

    s.greet()
    s.start(acc, grp)
    s.middle()
    tot[...] = s.finish()


def k8(
    na, nb, grp, dzr, dzn, dys, y2, y1, act1, act2, tot7, tot2, tot1, par2, par1, wrt, wnt, eg, slow,
    dyr, dz1, tot, gg, ng, rpair, npair,
    tab, tabn, tabl, acc, d9, d9n, xbuf, xs, us, ur, ds, dr, *ar,
):
    s = Sum(na, nb, ar)
    nc = dzr.shape[0]
    b = lax.axis_index("tm")
    np_ = parts_of(nc)
    size = nc // np_
    pairs = nc // 2

    def load(i, slot):
        return pltpu.make_async_copy(slow.at[pl.ds(2 * i, 2)], xbuf.at[slot], xs.at[slot])

    def reducer_terms(taps_of):
        @loop(0, pairs)
        def _(i):
            slot = lax.rem(i, 2)

            @pl.when(i + 1 < pairs)
            def _():
                load(i + 1, 1 - slot).start()

            load(i, slot).wait()
            for j in taps_of:
                dy = jnp.concatenate(
                    [dyr[2 * i + h, 256 * j : 256 * (j + 1), :] for h in range(2)], axis=1
                )
                for cb in range(5):
                    if cb < 4:
                        x = [xbuf[slot, h, 256 * cb : 256 * (cb + 1), :] for h in range(2)]
                    else:
                        x = [act1[2 * i + h, 0:256, :] for h in range(2)]
                    lo = 768 * cb + 256 * j
                    gg[lo : lo + 256, :] += dot_nt(dy, jnp.concatenate(x, axis=1))

    load(0, 0).start()
    acc[...] = jnp.zeros_like(acc)
    t7, t2, t1 = tot7[...], tot2[...], tot1[...]
    rows, pair = backward_rows(t2[:, :256], t7[:, :256], t2, 1, par2[:, :256])
    fill_tables(tab, 0, rows)
    rpair[...] = pair
    rng = [slice(i * size, (i + 1) * size) for i in range(np_)]
    up = Halo(nb, 1, [(dyr.at[r, 256:512], dyr.at[r, 512:768]) for r in rng], us, ur)
    down = Halo(nb, -1, [(dyr.at[r, 256:512], dyr.at[r, 0:256]) for r in rng], ds, dr)

    @pl.when(b == 0)
    def _():
        dyr[:, 512:768, :] = jnp.zeros((nc, 256, CELLS), BF16)

    @pl.when(b == nb - 1)
    def _():
        dyr[:, 0:256, :] = jnp.zeros((nc, 256, CELLS), BF16)

    for i in range(np_):

        @loop(i * size, (i + 1) * size)
        def _(c):
            g = grp[c]
            m = mask_of(g)
            for lo in range(0, 256, 128):
                dy = dzr[c, lo : lo + 128, :] * coef(tab, g, 0, lo, 128)
                dy = dy + y2[c, lo : lo + 128, :] * coef(tab, g, 1, lo, 128)
                dy = (dy + coef(tab, g, 2, lo, 128)) * m
                dyr[c, 256 + lo : 384 + lo, :] = dy.astype(BF16)

        if i == 0:
            s.greet()
        up.start(i)
        down.start(i)

    rows, pair = backward_rows(
        fold_frames(t2[:, 256:], 32), fold_frames(t7[:, 256:], 32), t2, 4, par2[:, 256:]
    )
    fill_tables(tabn, 0, rows)
    npair[...] = pair
    fill_tables(tabl, 0, forward_rows(t1[:, :256], t1, 1, par1[:, :256]))
    fill_tables(tabl, 256, forward_rows(fold_frames(t1[:, 256:], 32), t1, 4, par1[:, 256:]))
    ng[...] = jnp.zeros_like(ng)
    gg[0:6144, :] = jnp.zeros((6144, 256), F32)
    gg[6144:7168, :] = eg[...]

    @loop(0, pairs)
    def _(i):
        for h in range(2):
            c = 2 * i + h
            g = grp[c]
            m = mask_of(g)
            dy = dzn[c] * coef(tabn, g, 0, 0, 128) + y2[c, 256:384, :] * coef(tabn, g, 1, 0, 128)
            dy = (dy + coef(tabn, g, 2, 0, 128)) * m
            taps(dy, d9n, 128, -1)
            dx = dot(wnt[...], d9n[...])
            y = y1[c, 256:384, :]
            u = y * coef(tabl, g, 0, 256, 128) + coef(tabl, g, 1, 256, 128)
            dz = m * slope_of(u) * dx
            dz1[c, 256:384, :] = dz
            add_stats(acc, 256, 128, dz, dz * y, g)
            for lo in range(0, 1152, 384):
                ng[lo : lo + 384, :] += dot_nt(d9n[lo : lo + 384, :], act1[c, 256:384, :])
            taps(dys[c].astype(F32), d9, 256, -1, h * CELLS)
        act = jnp.concatenate([act2[2 * i + h, 0:256, :] for h in range(2)], axis=1)
        for lo in range(0, 2304, 256):
            gg[3840 + lo : 4096 + lo, :] += dot_nt(d9[lo : lo + 256, :], act)

    reducer_terms((1,))
    load(0, 0).start()
    for i in range(np_):
        up.arrive(i)
        down.arrive(i)

        @loop(i * size, (i + 1) * size)
        def _(c):
            g = grp[c]
            m = mask_of(g)
            for lo in range(0, 256, 128):
                dx = dot(wrt[1024 + lo : 1152 + lo, :], dyr[c])
                y = y1[c, lo : lo + 128, :]
                u = y * coef(tabl, g, 0, lo, 128) + coef(tabl, g, 1, lo, 128)
                dz = m * slope_of(u) * dx
                dz1[c, lo : lo + 128, :] = dz
                add_stats(acc, lo, 128, dz, dz * y, g)

    s.start(acc, grp)
    reducer_terms((0,))
    s.middle()
    load(0, 0).start()
    reducer_terms((2,))
    up.sent()
    down.sent()
    tot[...] = s.finish()


class Spread:
    def __init__(self, na, nb, refs):
        self.na, self.nb = na, nb
        (self.own, self.out, self.stage, self.rc, self.rx, self.cs, self.cr, self.ss, self.sr, self.zs, self.zr,
         self.gs, self.gr, self.hs, self.hr, self.ks, self.kr) = refs
        self.a, self.b = lax.axis_index("clip"), lax.axis_index("tm")
        self.bits = [i for i in range(1, 16) if (1 << i) < na]
        self.order = (self.bits, self.bits[::-1])
        self.half = self.own.shape[0]
        self.h = lax.rem(self.a, 2)

    def peer(self, bit):
        step = 1 << bit
        mine = lax.rem(self.a // step, 2)
        return (self.a + step * (1 - 2 * mine), self.b), mine

    def rows(self, start, count):
        return pl.ds(pl.multiple_of(start, 16), count)

    def copy(self, src, dst, ss, rs, peer):
        return pltpu.make_async_remote_copy(
            src, dst, ss, rs, device_id=peer, device_id_type=MESH
        )

    def first(self, block_of, chunks):
        self.chunks = chunks
        size = self.half // chunks
        peer, _ = self.peer(0)
        self.first_copies = []
        for j in range(chunks):
            rows = slice(j * size, (j + 1) * size)
            for i in range(j * size // 256, (j + 1) * size // 256):
                at = slice(256 * i, 256 * (i + 1))
                for mine in range(2):

                    @pl.when(self.h == mine)
                    def _():
                        self.own[at, :] = block_of(mine, i)
                        self.stage[at, :] = block_of(1 - mine, i).astype(BF16)

            c = self.copy(self.stage.at[rows], self.rc.at[rows], self.cs.at[j], self.cr.at[j], peer)
            c.start()
            self.first_copies.append(c)

    def first_done(self):
        size = self.half // self.chunks
        for j, c in enumerate(self.first_copies):
            c.wait()

            @pl.loop(j * size // 256, (j + 1) * size // 256)
            def _(i):
                at = pl.ds(pl.multiple_of(i * 256, 256), 256)
                self.own[at, :] = self.own[at, :] + self.rc[at, :].astype(F32)

        self.at = [0, self.half // 2]
        self.count = self.half // 2
        self.base = 0

    def cast(self, start, count):
        step = min(count, 256)

        @pl.loop(0, count // step)
        def _(i):
            at = self.rows(start + i * step, step)
            self.rc[at, :] = self.own[at, :].astype(BF16)

    def halve(self, n):
        half = self.count // 2
        self.pending = []
        for p in range(2):
            peer, mine = self.peer(self.order[p][n])
            away = self.at[p] + (1 - mine) * half
            self.at[p] = self.at[p] + mine * half
            self.cast(away, half)
            c = self.copy(
                self.rc.at[self.rows(away, half)], self.rx.at[p, self.base : self.base + half],
                self.ss.at[p, n], self.sr.at[p, n], peer,
            )
            c.start()
            self.pending.append(c)
        self.count = half

    def halved(self):
        half = self.count
        step = min(half, 256)
        for p in range(2):
            self.pending[p].wait()

            @pl.loop(0, half // step)
            def _(i):
                at = self.rows(self.at[p] + i * step, step)
                got = self.rx[p, self.rows(self.base + i * step, step), :]
                self.own[at, :] = self.own[at, :] + got.astype(F32)

        self.base += half

    def along(self):
        self.piece = self.count // self.nb
        self.pending = []
        for p in range(2):
            self.cast(self.at[p], self.count)
            for d in range(1, self.nb):
                to = lax.rem(self.b + d, self.nb)
                c = self.copy(
                    self.rc.at[self.rows(self.at[p] + to * self.piece, self.piece)],
                    self.rx.at[p, self.rows(self.base + self.b * self.piece, self.piece)],
                    self.zs.at[p, d - 1], self.zr.at[p, d - 1], (self.a, to),
                )
                c.start()
                self.pending.append(c)

    def place(self, p, start):
        return self.h * self.half + start

    def summed(self):
        pending, self.pending = self.pending, []
        for p in range(2):
            for c in pending[p * (self.nb - 1) : (p + 1) * (self.nb - 1)]:
                c.wait()
            start = self.at[p] + self.b * self.piece
            total = self.own[self.rows(start, self.piece), :]
            for d in range(1, self.nb):
                source = lax.rem(self.b + d, self.nb)
                total = total + self.rx[
                    p, self.rows(self.base + source * self.piece, self.piece), :
                ].astype(F32)
            at = self.rows(self.place(p, start), self.piece)
            self.out[at, :] = total.astype(BF16)
            for d in range(1, self.nb):
                c = self.copy(
                    self.out.at[at], self.out.at[at], self.gs.at[p, d - 1], self.gr.at[p, d - 1],
                    (self.a, lax.rem(self.b + d, self.nb)),
                )
                c.start()
                self.pending.append(c)

    def gather(self, n):
        for c in self.pending:
            c.wait()
        self.pending = []
        for p in range(2):
            peer, mine = self.peer(self.order[p][n])
            at = self.rows(self.place(p, self.at[p]), self.count)
            c = self.copy(self.out.at[at], self.out.at[at], self.hs.at[p, n], self.hr.at[p, n], peer)
            c.start()
            self.pending.append(c)
            self.at[p] = self.at[p] - mine * self.count
        self.count *= 2

    def last(self):
        pending, self.pending = self.pending, []
        peer, _ = self.peer(0)
        for p in range(2):
            pending[p].wait()
            at = self.rows(self.place(p, self.at[p]), self.count)
            c = self.copy(self.out.at[at], self.out.at[at], self.ks.at[p], self.kr.at[p], peer)
            c.start()
            self.pending.append(c)

    def done(self):
        for c in self.pending:
            c.wait()


def spread_scratch(na, nb, half, chunks):
    dma = pltpu.SemaphoreType.DMA
    stages = max(1, na.bit_length() - 2)
    pairs = [(chunks,), (2, stages), (2, nb - 1), (2, nb - 1), (2, stages), (2,)]
    return [VM((half, 256), BF16), VM((half, 256), BF16), VM((2, half // 2, 256), BF16)] + [
        dma(shape) for shape in pairs for _ in range(2)
    ]


def k9(
    na, nb, grp, dz1, y1, xe, dyr, dzw, tot8, tot1, par1, wrt, wf, dze, gg, ng, wg,
    sgrad, fgrad, out, lpair, qpair,
    tab, dyl, dyq, zbuf, obuf, fbuf, ebuf, wbuf, lg, qg, own, zs, osem, fs, es, wsem, ls, lr, us, ur, ds, dr, *ar,
):
    s = Sum(na, nb, None)
    sp = Spread(na, nb, (own, out) + ar)
    nc = dz1.shape[0]
    b = lax.axis_index("tm")
    np_ = parts_of(nc)
    size = nc // np_

    def load(c, slot):
        return pltpu.make_async_copy(dze.at[c], zbuf.at[slot], zs.at[slot])

    def eload(c, slot):
        return pltpu.make_async_copy(xe.at[c], ebuf.at[slot], es.at[slot])

    def wload(c, slot):
        return pltpu.make_async_copy(dzw.at[c], wbuf.at[slot], wsem.at[slot])

    def store(c, slot):
        return pltpu.make_async_copy(obuf.at[slot], sgrad.at[c], osem.at[slot])

    def fstore(c, slot):
        return pltpu.make_async_copy(fbuf.at[slot], fgrad.at[c], fs.at[slot])

    load(0, 0).start()
    eload(0, 0).start()
    wload(0, 0).start()
    t8, t1 = tot8[...], tot1[...]
    rows, pair = backward_rows(t1[:, :256], t8[:, :256], t1, 1, par1[:, :256])
    fill_tables(tab, 0, rows)
    lpair[...] = pair
    rows, pair = backward_rows(
        fold_frames(t1[:, 256:], 32), fold_frames(t8[:, 256:], 32), t1, 4, par1[:, 256:]
    )
    fill_tables(tab, 256, rows)
    qpair[...] = pair
    rng = [slice(i * size, (i + 1) * size) for i in range(np_)]
    lat = Halo(nb, -1, [(dyl.at[r, 0:256], dyl.at[r, 256:512]) for r in rng], ls, lr)
    up = Halo(nb, 1, [(dyq.at[r, 160:192], dyq.at[r, 0:32]) for r in rng], us, ur)
    down = Halo(nb, -1, [(dyq.at[r, 64:96], dyq.at[r, 192:224]) for r in rng], ds, dr)
    dyq[:, 32:64, :] = jnp.zeros((nc, 32, CELLS), BF16)
    dyq[:, 224:256, :] = jnp.zeros((nc, 32, CELLS), BF16)

    @pl.when(b == 0)
    def _():
        dyq[:, 0:32, :] = jnp.zeros((nc, 32, CELLS), BF16)

    @pl.when(b == nb - 1)
    def _():
        dyq[:, 192:224, :] = jnp.zeros((nc, 32, CELLS), BF16)
        dyl[:, 256:512, :] = jnp.zeros((nc, 256, CELLS), BF16)

    for i in range(np_):

        @loop(i * size, (i + 1) * size)
        def _(c):
            g = grp[c]
            m = mask_of(g)
            for lo in range(0, 384, 128):
                dy = dz1[c, lo : lo + 128, :] * coef(tab, g, 0, lo, 128)
                dy = dy + y1[c, lo : lo + 128, :] * coef(tab, g, 1, lo, 128)
                dy = ((dy + coef(tab, g, 2, lo, 128)) * m).astype(BF16)
                if lo < 256:
                    dyl[c, lo : lo + 128, :] = dy
                else:
                    dyq[c, 64:192, :] = dy

        if i == 0:
            s.greet()
        lat.start(i)
        up.start(i)
        down.start(i)

    lg[...] = jnp.zeros_like(lg)
    qg[...] = jnp.zeros_like(qg)

    @loop(0, nc)
    def _(c):
        slot = lax.rem(c, 2)

        @pl.when(c + 1 < nc)
        def _():
            eload(c + 1, 1 - slot).start()

        eload(c, slot).wait()
        dy = dyl[c, 0:256, :]
        lg[0:256, :] += dot_nt(dy, ebuf[slot, 0:256, :])
        lg[256:512, :] += dot_nt(dy, ebuf[slot, 256:512, :])
        lg[512:768, 0:128] += dot_nt(dy, ebuf[slot, 512:640, :])
        qg[...] += dot_nt(dyq[c, 64:192, :], ebuf[slot, 128:896, :])

    for j in range(3):
        lg[800 + 32 * j : 832 + 32 * j, 128:256] = sum(
            qg[32 * f : 32 * (f + 1), 128 * (f + j) : 128 * (f + j + 1)] for f in range(4)
        )
    for k in range(9):
        term = sum(
            ng[128 * k + 32 * f : 128 * k + 32 * (f + 1), 32 * f : 32 * (f + 1)] for f in range(4)
        )
        if k < 8:
            lg[768 + 32 * k : 800 + 32 * k, 0:32] = term
        else:
            lg[768:800, 128:160] = term
    lg[896:1024, 128:160] = sum(wg[128 * f : 128 * (f + 1), 32 * f : 32 * (f + 1)] for f in range(4))

    def block_of(half, i):
        if half == 0:
            return gg[256 * i : 256 * (i + 1), :]
        if i < 12:
            return gg[4096 + 256 * i : 4352 + 256 * i, :]
        return lg[256 * (i - 12) : 256 * (i - 11), :]

    sp.first(block_of, 4)

    @loop(0, nc)
    def _(c):
        slot = lax.rem(c, 2)
        m = mask_of(grp[c])

        @pl.when(c + 1 < nc)
        def _():
            load(c + 1, 1 - slot).start()

        load(c, slot).wait()

        @pl.when(c >= 2)
        def _():
            store(c - 2, slot).wait()

        for lo in range(0, 1024, 128):
            dx = dot(wrt[lo : lo + 128, :], dyr[c]) + zbuf[slot, lo : lo + 128, :]
            obuf[slot, lo : lo + 128, :] = (dx * m).astype(BF16)
        store(c, slot).start()

    sp.first_done()
    stages = len(sp.bits)
    for n in range(stages):
        sp.halve(n)
        sp.halved()
    sp.along()
    for i in range(np_):
        lat.arrive(i)
        up.arrive(i)
        down.arrive(i)

        @loop(i * size, (i + 1) * size)
        def _(c):
            slot = lax.rem(c, 2)
            m = mask_of(grp[c])

            @pl.when(c + 1 < nc)
            def _():
                wload(c + 1, 1 - slot).start()

            wload(c, slot).wait()

            @pl.when(c >= 2)
            def _():
                fstore(c - 2, slot).wait()

            for lo in range(0, 512, 128):
                dx = dot(wf[lo : lo + 128, 0:512], dyl[c]) + dot(wf[lo : lo + 128, 512:768], dyq[c])
                dx = dx + wbuf[slot, lo : lo + 128, :]
                fbuf[slot, lo : lo + 128, :] = (dx * m).astype(BF16)
            fstore(c, slot).start()

    sp.summed()
    for n in reversed(range(stages)):
        sp.gather(n)
    sp.last()
    for c in range(max(0, nc - 2), nc):
        store(c, c % 2).wait()
        fstore(c, c % 2).wait()
    lat.sent()
    up.sent()
    down.sent()
    sp.done()


def weights_of(reducer, spatial, expand, lateral, squeeze, narrow, widening):
    eye = jnp.eye(4, dtype=BF16)
    band = jnp.asarray(
        [[[1.0 if e == f + 1 + j else 0.0 for j in range(3)] for e in range(7)] for f in range(4)], BF16
    )
    lat = jnp.transpose(lateral, (1, 0, 2)).reshape(256, 640)
    lat = jnp.pad(lat, ((0, 0), (0, 256)))
    sq = jnp.einsum("fej,jop->foep", band, squeeze).reshape(128, 896)
    wa = jnp.concatenate([lat, sq], axis=0)
    wr = reducer.reshape(768, 1280)
    wrt = jnp.transpose(wr)
    wn = jnp.einsum("fg,koc->fokgc", eye, narrow).reshape(128, 1152)
    wnt = jnp.einsum("fg,koc->fckgo", eye, narrow).reshape(128, 1152)
    ws = jnp.transpose(spatial, (1, 0, 2)).reshape(256, 2304)
    wst = jnp.transpose(spatial, (2, 0, 1)).reshape(256, 2304)
    ww = jnp.einsum("fg,oc->fogc", eye, widening).reshape(512, 128)
    wwt = jnp.transpose(ww)
    back = jnp.asarray(
        [
            [[1.0 if e == (0, 2, 3, 4, 5, 6)[f + 2 - j] else 0.0 for j in range(3)] for e in range(8)]
            for f in range(4)
        ],
        BF16,
    )
    sqb = jnp.einsum("fej,jop->fpeo", back, squeeze).reshape(512, 256)
    late = jnp.asarray(
        [
            [[1.0 if (s, k) in pairs else 0.0 for k in range(5)] for s in range(2)]
            for pairs in (((0, 2),), ((0, 3),), ((0, 4), (1, 0)), ((1, 1),))
        ],
        BF16,
    )
    latb = jnp.einsum("fsk,kop->fpso", late, lateral).reshape(512, 512)
    wf = jnp.concatenate([latb, sqb], axis=1)
    return wa, wr, wrt, wn, wnt, ws, wst, expand, jnp.transpose(expand), ww, wwt, wf


def sds(shape, dtype):
    return jax.ShapeDtypeStruct(shape, dtype)


def build(na, nb):
    def call(body, cid, ins, outs, scratch, args, arw, flops=0):
        spec = {"v": VM, "h": pl.ANY, "s": pltpu.SMEM}
        moved = sum(a.size * a.dtype.itemsize for a in args) + sum(
            o.size * o.dtype.itemsize for o in outs[1]
        )
        return pl.pallas_call(
            functools.partial(body, na, nb),
            name=body.__name__,
            out_shape=tuple(outs[1]),
            in_specs=[pl.BlockSpec(memory_space=spec[k]) for k in ins],
            out_specs=tuple(pl.BlockSpec(memory_space=spec[k]) for k in outs[0]),
            scratch_shapes=scratch + (ar_scratch(na, nb, arw) if arw else []),
            compiler_params=pltpu.CompilerParams(
                collective_id=cid, has_side_effects=True, vmem_limit_bytes=LIMIT
            ),
            cost_estimate=pl.CostEstimate(flops=flops, bytes_accessed=moved, transcendentals=0),
        )(*args)

    def body(
        slow_in, fast_in, clip_group, reducer, spatial, expand, lateral, squeeze, narrow, widening,
        reducer_norm, spatial_norm, expand_norm, lateral_norm, squeeze_norm, narrow_norm, widening_norm,
        slow_cot, fast_cot,
    ):
        nc = slow_in.shape[0]
        dma = pltpu.SemaphoreType.DMA
        grp = clip_group
        slow = slow_in.reshape(nc, 1024, CELLS)
        fast = fast_in.reshape(nc, 512, CELLS)
        scot = slow_cot.reshape(nc, 1024, CELLS)
        fcot = fast_cot.reshape(nc, 512, CELLS)
        wa, wr, wrt, wn, wnt, ws, wst, we, wet, ww, wwt, wf = weights_of(
            reducer, spatial, expand, lateral, squeeze, narrow, widening
        )

        def four(pair):
            return jnp.concatenate([pair] * 4, axis=1)

        par1 = jnp.concatenate([lateral_norm, four(squeeze_norm)], axis=1).astype(F32)
        par2 = jnp.concatenate([reducer_norm, four(narrow_norm)], axis=1).astype(F32)
        par3 = spatial_norm.astype(F32)
        pare = expand_norm.astype(F32)
        parw = four(widening_norm).astype(F32)
        np_ = parts_of(nc)
        sems = [dma((np_,))] * 4

        def act(c, dtype):
            return sds((nc, c, CELLS), dtype)

        def tab(k, c):
            return VM((3, k, c, 128), F32)

        xe, y1, tot1 = call(
            k1, 1, "shv", ("vvv", [act(896, BF16), act(384, F32), sds((8, 384), F32)]),
            [VM((384, 128), F32), dma((np_,))] + sems, (grp, fast, wa), 384,
        )
        half = VM((nc, 256, CELLS), BF16)
        act1, y2, tot2 = call(
            k2, 2, "svvvvvv", ("vvv", [act(384, BF16), act(384, F32), sds((8, 384), F32)]),
            [tab(2, 384), VM((384, 128), F32), VM((1152, CELLS), BF16), half, half, half, half] + sems,
            (grp, y1, tot1, par1, slow, wr, wn), 384,
        )
        act2, y3, tot3 = call(
            k3, 3, "svvvvv", ("vvv", [act(384, BF16), act(256, F32), sds((8, 768), F32)]),
            [tab(2, 384), VM((768, 128), F32), VM((2304, CELLS), BF16)],
            (grp, y2, tot2, par2, ws, ww), 768,
        )
        two = VM((2, 512, CELLS), BF16)
        acts, tot4, fast_out, dzw, accw = call(
            k4, 4, "svvvvvvvvh",
            ("vvhvv", [act(256, BF16), sds((8, 1024), F32), act(512, BF16), act(512, F32), sds((512, 128), F32)]),
            [tab(2, 256), tab(2, 512), VM((1024, 128), F32), two, two, dma((2,)), dma((2,))],
            (grp, y3, tot3, par3, parw, we, ww, act2, xe, fcot), 1024,
        )
        big = VM((2, 1024, CELLS), BF16)
        slow_out, dze, tot5 = call(
            k5, 5, "svvvvvhh", ("hvv", [act(1024, BF16), act(1024, F32), sds((8, 1536), F32)]),
            [tab(2, 1024), VM((1536, 128), F32), big, big, big] + [dma((2,))] * 3,
            (grp, acts, tot4, pare, we, accw, slow, scot), 1536,
        )
        dzs, dzn, tot6, accn, eg, wg, epair, wpair = call(
            k6, 6, "svvvvvv" + "v" * 12,
            (
                "v" * 8,
                [
                    act(256, F32), act(128, F32), sds((8, 256), F32), sds((128, 128), F32),
                    sds((1024, 256), F32), sds((512, 128), F32), sds((2, 1024), F32), sds((2, 128), F32),
                ],
            ),
            [
                tab(3, 1024), tab(2, 256), tab(3, 512), tab(2, 128), VM((256, 128), F32),
                VM((nc, 1024, CELLS), BF16),
            ],
            (grp, acts, act2, y3, y2, dze, dzw, tot5, tot4, tot3, tot2, pare, parw, par3, par2, we, wet, ww, wwt),
            256,
        )
        dzr, dys, tot7, spair = call(
            k7, 7, "s" + "v" * 10,
            ("v" * 4, [act(256, F32), act(256, BF16), sds((8, 384), F32), sds((2, 256), F32)]),
            [tab(3, 256), tab(2, 256), VM((384, 128), F32), VM((2304, CELLS), BF16)],
            (grp, dzs, y3, y2, tot6, tot3, tot2, par3, par2, wst, accn), 384,
        )
        dyr, dz1, tot8, gg, ng, rpair, npair = call(
            k8, 8, "s" + "v" * 15 + "h",
            (
                "v" * 7,
                [
                    act(768, BF16), act(384, F32), sds((8, 384), F32), sds((7168, 256), F32),
                    sds((1152, 128), F32), sds((2, 256), F32), sds((2, 128), F32),
                ],
            ),
            [
                tab(3, 256), tab(3, 128), tab(2, 384), VM((384, 128), F32),
                VM((2304, 2 * CELLS), BF16), VM((1152, CELLS), BF16), VM((2, 2, 1024, CELLS), BF16), dma((2,)),
            ] + sems,
            (grp, dzr, dzn, dys, y2, y1, act1, act2, tot7, tot2, tot1, par2, par1, wrt, wnt, eg, slow), 384,
        )
        slow_grad, fast_grad, out, lpair, qpair = call(
            k9, 9, "svvhvhvvvvvhvvv",
            (
                "hhvvv",
                [
                    act(1024, BF16), act(512, BF16), sds((8192, 256), BF16), sds((2, 256), F32), sds((2, 128), F32),
                ],
            ),
            [
                tab(3, 384), VM((nc, 512, CELLS), BF16), VM((nc, 256, CELLS), BF16),
                VM((2, 1024, CELLS), F32), big, two, VM((2, 896, CELLS), BF16), VM((2, 512, CELLS), F32),
                VM((1024, 256), F32), VM((128, 768), F32), VM((4096, 256), F32),
            ] + [dma((2,))] * 5 + [dma((np_,))] * 2 + sems + spread_scratch(na, nb, 4096, 4),
            (grp, dz1, y1, xe, dyr, dzw, tot8, tot1, par1, wrt, wf, dze, gg, ng, wg), 0,
        )
        reducer_grad = jnp.transpose(out[:3840].reshape(5, 3, 256, 256), (1, 2, 0, 3)).reshape(3, 256, 1280)
        spatial_grad = out[3840:6144].reshape(9, 256, 256)
        expand_grad = out[6144:7168]
        lat6 = jnp.transpose(out[7168:7936].reshape(3, 256, 2, 128), (0, 2, 1, 3)).reshape(6, 256, 128)
        small = out[7936:]
        narrow_grad = jnp.concatenate([small[:, :32], small[:32, 128:160]], axis=0).reshape(9, 32, 32)
        squeeze_grad = small[32:128, 128:].reshape(3, 32, 128)
        widening_grad = small[128:, 128:160]
        grads = tuple(
            v.astype(F32)
            for v in (
                reducer_grad, spatial_grad, expand_grad, lat6[:5], squeeze_grad, narrow_grad, widening_grad,
            )
        )
        return (
            slow_out.reshape(slow_in.shape), fast_out.reshape(fast_in.shape),
            slow_grad.reshape(slow_in.shape), fast_grad.reshape(fast_in.shape),
            *grads,
            rpair, spair, epair, lpair, qpair[:, :32], npair[:, :32], wpair,
        )

    return body


def solution(mesh):
    body = build(mesh.shape["clip"], mesh.shape["tm"])
    big = P("clip", "tm", None, None)
    return jax.shard_map(
        body,
        mesh=mesh,
        in_specs=(big, big, P("clip")) + (P(),) * 14 + (big, big),
        out_specs=(big,) * 4 + (P(),) * 14,
        check_vma=False,
    )
```

```python
import functools

import jax
import jax.numpy as jnp
from jax import lax
from jax.experimental import pallas as pl
from jax.experimental.pallas import tpu as pltpu
from jax.sharding import PartitionSpec as P

MESH = pl.DeviceIdType.MESH
F32, BF16 = jnp.float32, jnp.bfloat16
SIDE = 16
CELLS = SIDE * SIDE
EPS = 1e-05
VM = pltpu.VMEM
LIMIT = 62 * 1024 * 1024


def dot(a, b):
    return lax.dot_general(a, b, (((1,), (0,)), ((), ())), preferred_element_type=F32)


def dot_nt(a, b):
    return lax.dot_general(a, b, (((1,), (1,)), ((), ())), preferred_element_type=F32)


def side_of(g):
    return jnp.where(g == 0, SIDE * 5 // 8, jnp.where(g == 1, SIDE * 7 // 8, SIDE))


def mask_of(g):
    cell = lax.broadcasted_iota(jnp.int32, (1, CELLS), 1)
    side = side_of(g)
    return jnp.where(((cell >> 4) < side) & ((cell & 15) < side), 1.0, 0.0).astype(F32)


def counts_row(grp):
    lane = lax.broadcasted_iota(jnp.int32, (1, 128), 1)
    total = jnp.zeros((1, 128), F32)
    for c in range(grp.shape[0]):
        side = side_of(grp[c])
        total = total + jnp.where(lane == grp[c], (side * side).astype(F32), 0.0)
    return total


def add_stats(acc, lo, rows, first, second, g):
    lane = lax.broadcasted_iota(jnp.int32, (1, 128), 1)
    one = jnp.sum(first[:, :128] + first[:, 128:], axis=1, keepdims=True)
    two = jnp.sum(second[:, :128] + second[:, 128:], axis=1, keepdims=True)
    acc[lo : lo + rows, :] += jnp.where(lane == g, one, 0.0) + jnp.where(lane == g + 3, two, 0.0)


def ar_scratch(na, nb, width):
    dma = pltpu.SemaphoreType.DMA
    return [
        VM((8, width), F32),
        VM((na, 8, width), F32),
        VM((8, width), F32),
        VM((nb, 8, width), F32),
        dma((na - 1,)),
        dma((na - 1,)),
        dma((nb - 1,)),
        dma((nb - 1,)),
    ]


class Peers:
    def __init__(self, na, nb):
        self.na, self.nb = na, nb
        self.a, self.b = lax.axis_index("clip"), lax.axis_index("tm")
        self.along_a = [(lax.rem(self.a + d, na), self.b) for d in range(1, na)]
        self.along_b = [(self.a, lax.rem(self.b + d, nb)) for d in range(1, nb)]
        self.bar = pltpu.get_barrier_semaphore()
        for peer in self.along_a + self.along_b:
            pl.semaphore_signal(self.bar, inc=1, device_id=peer, device_id_type=MESH)

    def greet(self):
        pl.semaphore_wait(self.bar, self.na - 1 + self.nb - 1)


class Sum:
    def __init__(self, peers, refs):
        self.p = peers
        self.mine, self.bufa, self.part, self.bufb, self.sa, self.ra, self.sb, self.rb = refs

    def copies(self, src, buf, slot, ss, rs, peers):
        return [
            pltpu.make_async_remote_copy(
                src, buf.at[slot], ss.at[i], rs.at[i], device_id=peer, device_id_type=MESH
            )
            for i, peer in enumerate(peers)
        ]

    def start(self, acc, counts):
        width = self.mine.shape[1]
        rows = jnp.transpose(acc[0:width, :])[:8, :]
        row = lax.broadcasted_iota(jnp.int32, (8, 128), 0)
        head = jnp.where(row == 6, counts, rows[:, :128])
        value = head if width == 128 else jnp.concatenate([head, rows[:, 128:]], axis=1)
        self.mine[...] = value
        self.bufa[self.p.a] = value
        self.first = self.copies(self.mine, self.bufa, self.p.a, self.sa, self.ra, self.p.along_a)
        for c in self.first:
            c.start()

    def middle(self):
        for c in self.first:
            c.wait()
        total = self.bufa[0]
        for i in range(1, self.p.na):
            total = total + self.bufa[i]
        self.part[...] = total
        self.bufb[self.p.b] = total
        self.second = self.copies(self.part, self.bufb, self.p.b, self.sb, self.rb, self.p.along_b)
        for c in self.second:
            c.start()

    def finish(self):
        for c in self.second:
            c.wait()
        total = self.bufb[0]
        for i in range(1, self.p.nb):
            total = total + self.bufb[i]
        return total


class Halo:
    def __init__(self, peers, step, src, dst, ss, rs):
        self.src, self.dst, self.ss, self.rs = src, dst, ss, rs
        to = peers.b + step
        self.sends = (to >= 0) & (to < peers.nb)
        source = peers.b - step
        self.gets = (source >= 0) & (source < peers.nb)
        self.peer = (peers.a, lax.rem(to + peers.nb, peers.nb))

    def copy(self, c):
        return pltpu.make_async_remote_copy(
            self.src(c), self.dst(c), self.ss.at[c], self.rs.at[c],
            device_id=self.peer, device_id_type=MESH,
        )

    def start(self, c):
        @pl.when(self.sends)
        def _():
            self.copy(c).start()

    def arrive(self, c):
        @pl.when(self.gets)
        def _():
            self.copy(c).wait_recv()

    def sent(self, nc):
        @pl.when(self.sends)
        def _():
            @pl.loop(0, nc)
            def _(c):
                self.copy(c).wait_send()


class Move:
    def __init__(self, src, dst, sem):
        self.src, self.dst, self.sem = src, dst, sem

    def copy(self, c):
        return pltpu.make_async_copy(self.src.at[c], self.dst.at[c], self.sem.at[c])

    def start(self, c):
        self.copy(c).start()

    def wait(self, c):
        self.copy(c).wait()

    def start_all(self, nc):
        @pl.loop(0, nc)
        def _(c):
            self.start(c)

    def wait_all(self, nc):
        @pl.loop(0, nc)
        def _(c):
            self.wait(c)


class Feed:
    def __init__(self, src, buf, sem, nc):
        self.src, self.buf, self.sem, self.nc = src, buf, sem, nc

    def copy(self, c, slot):
        return pltpu.make_async_copy(self.src.at[c], self.buf.at[slot], self.sem.at[slot])

    def prime(self):
        self.copy(0, 0).start()

    def take(self, c):
        slot = lax.rem(c, 2)

        @pl.when(c + 1 < self.nc)
        def _():
            self.copy(c + 1, 1 - slot).start()

        self.copy(c, slot).wait()
        return slot


class Drain:
    def __init__(self, buf, dst, sem, nc):
        self.buf, self.dst, self.sem, self.nc = buf, dst, sem, nc

    def copy(self, c, slot):
        return pltpu.make_async_copy(self.buf.at[slot], self.dst.at[c], self.sem.at[slot])

    def room(self, c):
        slot = lax.rem(c, 2)

        @pl.when(c >= 2)
        def _():
            self.copy(c - 2, slot).wait()

        return slot

    def put(self, c):
        self.copy(c, lax.rem(c, 2)).start()

    def done(self):
        for c in range(max(0, self.nc - 2), self.nc):
            self.copy(c, c % 2).wait()


def fold_frames(total, chans):
    width = total.shape[1]
    if chans < 128:
        out = total
        shift = chans
        while shift < 128:
            out = out + pltpu.roll(out, shift, 1)
            shift *= 2
        return out
    out = total[:, :128]
    for f in range(1, width // 128):
        out = out + total[:, 128 * f : 128 * (f + 1)]
    return jnp.concatenate([out] * (width // 128), axis=1)


def moments(total, counts, frames):
    out = []
    for g in range(3):
        n = counts[6:7, g : g + 1] * float(frames)
        mean = total[g : g + 1, :] / n
        var = total[g + 3 : g + 4, :] / n - mean * mean
        out.append((n, mean, lax.rsqrt(var + EPS)))
    return out


def fill_tables(tab, base, rows_list):
    width = rows_list[0][0].shape[1]
    count = len(rows_list[0])
    rows = [rows_list[g][k] for g in range(3) for k in range(count)]
    rows = rows + [jnp.zeros((1, width), F32)] * (128 - len(rows))
    cols = jnp.transpose(jnp.concatenate(rows, axis=0))
    for g in range(3):
        for k in range(count):
            i = g * count + k
            tab[g, k, base : base + width, :] = jnp.broadcast_to(cols[:, i : i + 1], (width, 128))


def forward_rows(total, counts, frames, pair):
    out = []
    for n, mean, r in moments(total, counts, frames):
        gain = pair[0:1, :] * r
        out.append((gain, pair[1:2, :] - mean * gain))
    return out


def backward_rows(total, grads, counts, frames, pair):
    out, two_all, one_all = [], 0.0, 0.0
    for g, (n, mean, r) in enumerate(moments(total, counts, frames)):
        one = grads[g : g + 1, :]
        two = r * (grads[g + 3 : g + 4, :] - mean * one)
        c0 = pair[0:1, :] * r
        slope = c0 * r * two / n
        out.append((c0, -slope, slope * mean - c0 * one / n))
        two_all, one_all = two_all + two, one_all + one
    return out, jnp.concatenate([two_all, one_all], axis=0)


def wide(v):
    return jnp.concatenate([v, v], axis=1)


def coef(tab, g, k, lo, rows):
    return wide(tab[g, k, lo : lo + rows, :])


def sigmoid(v):
    return 0.5 * jnp.tanh(0.5 * v) + 0.5


def slope_of(v):
    s = sigmoid(v)
    return s * (1.0 + v * (1.0 - s))


def taps(x, dst, rows, sign, at=0):
    cell = lax.broadcasted_iota(jnp.int32, (1, CELLS), 1)
    row, col = cell >> 4, cell & 15
    for k in range(9):
        di, dl = sign * (k // 3 - 1), sign * (k % 3 - 1)
        step = SIDE * di + dl
        if step == 0:
            dst[k * rows : (k + 1) * rows, at : at + CELLS] = x.astype(BF16)
            continue
        moved = pltpu.roll(x, (-step) % CELLS, 1)
        ok = (row + di >= 0) & (row + di < SIDE) & (col + dl >= 0) & (col + dl < SIDE)
        dst[k * rows : (k + 1) * rows, at : at + CELLS] = jnp.where(ok, moved, 0.0).astype(BF16)


def loop(lo, hi):
    return pl.loop(lo, hi)


def spread_lanes(at, lanes):
    row = lax.broadcasted_iota(jnp.int32, (32, lanes), 0)
    lane = lax.broadcasted_iota(jnp.int32, (32, lanes), 1)
    hit = ((lane & 31) == row) if at is None else (lane == row + at)
    return jnp.where(hit, 1.0, 0.0).astype(BF16)


def dot_tn(a, b):
    return lax.dot_general(a, b, (((0,), (0,)), ((), ())), preferred_element_type=F32)


def turned(v):
    return jnp.transpose(v.astype(F32)).astype(BF16)


def four(pair):
    return dot(pair, spread_lanes(None, 128))


def first_weights(lateral, squeeze, wa):
    wa[...] = jnp.zeros_like(wa)
    for k in range(5):
        wa[0:256, 128 * k : 128 * (k + 1)] = lateral[k]
    for f in range(4):
        for j in range(3):
            wa[256 + 32 * f : 288 + 32 * f, 128 * (f + 1 + j) : 128 * (f + 2 + j)] = squeeze[j]


def more_weights(reducer, spatial, expand, lateral, squeeze, narrow, widening, ws, wn, ww, wrt, wst, wet, wwt, wnt, wf):
    lane = lax.broadcasted_iota(jnp.int32, (1, 128), 1) >> 5
    row = lax.broadcasted_iota(jnp.int32, (128, 1), 0) >> 5
    every = spread_lanes(None, 128)
    for k in range(9):
        cols = slice(256 * k, 256 * (k + 1))
        ws[:, cols] = spatial[k]
        wst[:, cols] = turned(spatial[k])
        there, back = dot(narrow[k], every), dot_tn(narrow[k], every)
        for f in range(4):
            at = slice(32 * f, 32 * (f + 1))
            wn[at, 128 * k : 128 * (k + 1)] = jnp.where(lane == f, there, 0.0).astype(BF16)
            wnt[at, 128 * k : 128 * (k + 1)] = jnp.where(lane == f, back, 0.0).astype(BF16)
    wide_w = dot(widening[...], every)
    tall_w = lax.dot_general(every, widening[...], (((0,), (1,)), ((), ())), preferred_element_type=F32)
    for f in range(4):
        ww[128 * f : 128 * (f + 1), :] = jnp.where(lane == f, wide_w, 0.0).astype(BF16)
        wwt[:, 128 * f : 128 * (f + 1)] = jnp.where(row == f, tall_w, 0.0).astype(BF16)
    for q in range(4):
        wet[:, 256 * q : 256 * (q + 1)] = turned(expand[256 * q : 256 * (q + 1), :])
    for j in range(3):
        for q in range(5):
            wrt[256 * q : 256 * (q + 1), 256 * j : 256 * (j + 1)] = turned(
                reducer[256 * j : 256 * (j + 1), 256 * q : 256 * (q + 1)]
            )
    wf[...] = jnp.zeros_like(wf)
    for f, s, k in ((0, 0, 2), (1, 0, 3), (2, 0, 4), (2, 1, 0), (3, 1, 1)):
        wf[128 * f : 128 * (f + 1), 256 * s : 256 * (s + 1)] = turned(lateral[k])
    place = (0, 2, 3, 4, 5, 6)
    for f in range(4):
        wf[128 * f : 128 * (f + 1), 512:768] = sum(
            dot_tn(squeeze[j], spread_lanes(32 * place[f + 2 - j], 256)) for j in range(3)
        ).astype(BF16)


class Spread:
    def __init__(self, na, nb, own, out, refs):
        self.na, self.nb = na, nb
        self.own, self.out = own, out
        (self.stage, self.rc, self.rx, self.cs, self.cr, self.ss, self.sr, self.zs, self.zr,
         self.gs, self.gr, self.hs, self.hr, self.ks, self.kr) = refs
        self.a, self.b = lax.axis_index("clip"), lax.axis_index("tm")
        self.bits = [i for i in range(1, 16) if (1 << i) < na]
        self.order = (self.bits, self.bits[::-1])
        self.half = self.own.shape[0]
        self.h = lax.rem(self.a, 2)

    def peer(self, bit):
        step = 1 << bit
        mine = lax.rem(self.a // step, 2)
        return (self.a + step * (1 - 2 * mine), self.b), mine

    def rows(self, start, count):
        return pl.ds(pl.multiple_of(start, 16), count)

    def copy(self, src, dst, ss, rs, peer):
        return pltpu.make_async_remote_copy(
            src, dst, ss, rs, device_id=peer, device_id_type=MESH
        )

    def first(self, block_of, chunks):
        self.chunks = chunks
        size = self.half // chunks
        peer, _ = self.peer(0)
        self.first_copies = []
        for j in range(chunks):
            rows = slice(j * size, (j + 1) * size)
            for i in range(j * size // 256, (j + 1) * size // 256):
                at = slice(256 * i, 256 * (i + 1))
                for mine in range(2):

                    @pl.when(self.h == mine)
                    def _():
                        self.own[at, :] = block_of(mine, i)
                        self.stage[at, :] = block_of(1 - mine, i).astype(BF16)

            c = self.copy(self.stage.at[rows], self.rc.at[rows], self.cs.at[j], self.cr.at[j], peer)
            c.start()
            self.first_copies.append(c)

    def first_done(self):
        size = self.half // self.chunks
        for j, c in enumerate(self.first_copies):
            c.wait()

            @pl.loop(j * size // 256, (j + 1) * size // 256)
            def _(i):
                at = pl.ds(pl.multiple_of(i * 256, 256), 256)
                self.own[at, :] = self.own[at, :] + self.rc[at, :].astype(F32)

        self.at = [0, self.half // 2]
        self.count = self.half // 2
        self.base = 0

    def cast(self, start, count):
        step = min(count, 256)

        @pl.loop(0, count // step)
        def _(i):
            at = self.rows(start + i * step, step)
            self.rc[at, :] = self.own[at, :].astype(BF16)

    def halve(self, n):
        half = self.count // 2
        self.pending = []
        for p in range(2):
            peer, mine = self.peer(self.order[p][n])
            away = self.at[p] + (1 - mine) * half
            self.at[p] = self.at[p] + mine * half
            self.cast(away, half)
            c = self.copy(
                self.rc.at[self.rows(away, half)], self.rx.at[p, self.base : self.base + half],
                self.ss.at[p, n], self.sr.at[p, n], peer,
            )
            c.start()
            self.pending.append(c)
        self.count = half

    def halved(self):
        half = self.count
        step = min(half, 256)
        for p in range(2):
            self.pending[p].wait()

            @pl.loop(0, half // step)
            def _(i):
                at = self.rows(self.at[p] + i * step, step)
                got = self.rx[p, self.rows(self.base + i * step, step), :]
                self.own[at, :] = self.own[at, :] + got.astype(F32)

        self.base += half

    def along(self):
        self.piece = self.count // self.nb
        self.pending = []
        for p in range(2):
            self.cast(self.at[p], self.count)
            for d in range(1, self.nb):
                to = lax.rem(self.b + d, self.nb)
                c = self.copy(
                    self.rc.at[self.rows(self.at[p] + to * self.piece, self.piece)],
                    self.rx.at[p, self.rows(self.base + self.b * self.piece, self.piece)],
                    self.zs.at[p, d - 1], self.zr.at[p, d - 1], (self.a, to),
                )
                c.start()
                self.pending.append(c)

    def place(self, p, start):
        return self.h * self.half + start

    def summed(self):
        pending, self.pending = self.pending, []
        for p in range(2):
            for c in pending[p * (self.nb - 1) : (p + 1) * (self.nb - 1)]:
                c.wait()
            start = self.at[p] + self.b * self.piece
            total = self.own[self.rows(start, self.piece), :]
            for d in range(1, self.nb):
                source = lax.rem(self.b + d, self.nb)
                total = total + self.rx[
                    p, self.rows(self.base + source * self.piece, self.piece), :
                ].astype(F32)
            at = self.rows(self.place(p, start), self.piece)
            self.out[at, :] = total.astype(BF16)
            for d in range(1, self.nb):
                c = self.copy(
                    self.out.at[at], self.out.at[at], self.gs.at[p, d - 1], self.gr.at[p, d - 1],
                    (self.a, lax.rem(self.b + d, self.nb)),
                )
                c.start()
                self.pending.append(c)

    def gather(self, n):
        for c in self.pending:
            c.wait()
        self.pending = []
        for p in range(2):
            peer, mine = self.peer(self.order[p][n])
            at = self.rows(self.place(p, self.at[p]), self.count)
            c = self.copy(self.out.at[at], self.out.at[at], self.hs.at[p, n], self.hr.at[p, n], peer)
            c.start()
            self.pending.append(c)
            self.at[p] = self.at[p] - mine * self.count
        self.count *= 2

    def last(self):
        pending, self.pending = self.pending, []
        peer, _ = self.peer(0)
        for p in range(2):
            pending[p].wait()
            at = self.rows(self.place(p, self.at[p]), self.count)
            c = self.copy(self.out.at[at], self.out.at[at], self.ks.at[p], self.kr.at[p], peer)
            c.start()
            self.pending.append(c)

    def done(self):
        for c in self.pending:
            c.wait()


def spread_scratch(na, nb, half, chunks):
    dma = pltpu.SemaphoreType.DMA
    stages = max(1, na.bit_length() - 2)
    pairs = [(chunks,), (2, stages), (2, nb - 1), (2, nb - 1), (2, stages), (2,)]
    return [VM((half, 256), BF16), VM((half, 256), BF16), VM((2, half // 2, 256), BF16)] + [
        dma(shape) for shape in pairs for _ in range(2)
    ]


def forward(na, nb, refs):
    r = refs
    grp = r.grp
    nc = r.fast.shape[0]
    p = Peers(na, nb)
    b = p.b
    own = Move(r.fast, r.xe.at[:, 256:768], r.s_own)
    own.start_all(nc)
    raw = [
        pltpu.make_async_copy(src, dst, r.s_raw.at[i])
        for i, (src, dst) in enumerate(((r.reducer, r.wr), (r.spatial, r.sp), (r.expand, r.we)))
    ]
    for c in raw:
        c.start()
    xfeed = Feed(r.slow, r.xbuf, r.s_x, nc)
    xfeed.prime()
    up = Halo(p, 1, lambda c: r.fast.at[c, 256:512], lambda c: r.xe.at[c, 0:256], r.h1us, r.h1ur)
    down = Halo(p, -1, lambda c: r.fast.at[c, 0:128], lambda c: r.xe.at[c, 768:896], r.h1ds, r.h1dr)
    saves = {
        k: Move(getattr(r, k), getattr(r, k + "_o"), getattr(r, "s_" + k))
        for k in ("xe", "y1", "act1", "y2", "act2", "y3", "acts")
    }

    @pl.when(b == 0)
    def _():
        r.xe[:, 0:256, :] = jnp.zeros((nc, 256, CELLS), BF16)
        r.ru[...] = jnp.zeros_like(r.ru)

    @pl.when(b == nb - 1)
    def _():
        r.xe[:, 768:896, :] = jnp.zeros((nc, 128, CELLS), BF16)
        r.rd[...] = jnp.zeros_like(r.rd)

    p.greet()

    @loop(0, nc)
    def _(c):
        up.start(c)
        down.start(c)

    counts = counts_row(grp)
    acc = r.acc
    acc[...] = jnp.zeros_like(acc)
    first_weights(r.lateral, r.squeeze, r.wa)
    for c in raw:
        c.wait()
    more_weights(
        r.wr, r.sp, r.we, r.lateral, r.squeeze, r.narrow, r.widening,
        r.ws, r.wn, r.ww, r.wrt, r.wst, r.wet, r.wwt, r.wnt, r.wf,
    )
    wsaves = [
        pltpu.make_async_copy(getattr(r, k), getattr(r, k + "_o"), r.s_w.at[i])
        for i, k in enumerate(("wrt", "wst", "wet", "wwt", "wnt", "wf", "ww"))
    ]
    for c in wsaves:
        c.start()

    @loop(0, nc)
    def _(c):
        own.wait(c)
        up.arrive(c)
        down.arrive(c)
        saves["xe"].start(c)
        g = grp[c]
        m = mask_of(g)
        for lo in range(0, 384, 128):
            y = dot(r.wa[lo : lo + 128, :], r.xe[c])
            r.y1[c, lo : lo + 128, :] = y
            ym = y * m
            add_stats(acc, lo, 128, ym, ym * y, g)
        saves["y1"].start(c)

    s = Sum(p, r.ar1)
    s.start(acc, counts)
    s.middle()
    up.sent(nc)
    down.sent(nc)
    t1 = s.finish()
    r.tot1[...] = t1

    tab = r.tab
    acc[0:384, :] = jnp.zeros((384, 128), F32)
    fill_tables(tab, 0, forward_rows(t1[:, :256], t1, 1, r.nl[...].astype(F32)))
    fill_tables(tab, 256, forward_rows(fold_frames(t1[:, 256:], 32), t1, 4, four(r.nq[...])))
    up = Halo(p, 1, lambda c: r.su.at[c], lambda c: r.ru.at[c], r.h2us, r.h2ur)
    down = Halo(p, -1, lambda c: r.sd.at[c], lambda c: r.rd.at[c], r.h2ds, r.h2dr)

    @loop(0, nc)
    def _(c):
        g = grp[c]
        m = mask_of(g)
        for lo in range(0, 256, 128):
            u = r.y1[c, lo : lo + 128, :] * coef(tab, g, 0, lo, 128) + coef(tab, g, 1, lo, 128)
            r.act1[c, lo : lo + 128, :] = (u * sigmoid(u) * m).astype(BF16)
        slot = xfeed.take(c)
        for j, dst in enumerate((r.su, r.sd, r.y2)):
            for lo in range(0, 256, 128):
                r0 = 256 * (0, 2, 1)[j] + lo
                v = dot(r.wr[r0 : r0 + 128, :1024], r.xbuf[slot]) + dot(
                    r.wr[r0 : r0 + 128, 1024:], r.act1[c, 0:256, :]
                )
                dst[c, lo : lo + 128, :] = v.astype(dst.dtype)
        up.start(c)
        down.start(c)

    xfeed.prime()

    @loop(0, nc)
    def _(c):
        g = grp[c]
        m = mask_of(g)
        u = r.y1[c, 256:384, :] * coef(tab, g, 0, 256, 128) + coef(tab, g, 1, 256, 128)
        act = u * sigmoid(u) * m
        r.act1[c, 256:384, :] = act.astype(BF16)
        saves["act1"].start(c)
        taps(act, r.x9, 128, 1)
        y = dot(r.wn[...], r.x9[0:1152, :])
        r.y2[c, 256:384, :] = y
        ym = y * m
        add_stats(acc, 256, 128, ym, ym * y, g)

    @loop(0, nc)
    def _(c):
        up.arrive(c)
        down.arrive(c)
        g = grp[c]
        m = mask_of(g)
        for lo in range(0, 256, 128):
            y = (
                r.y2[c, lo : lo + 128, :]
                + r.ru[c, lo : lo + 128, :].astype(F32)
                + r.rd[c, lo : lo + 128, :].astype(F32)
            )
            r.y2[c, lo : lo + 128, :] = y
            ym = y * m
            add_stats(acc, lo, 128, ym, ym * y, g)
        saves["y2"].start(c)

    s = Sum(p, r.ar2)
    s.start(acc, counts)
    s.middle()
    up.sent(nc)
    down.sent(nc)
    t2 = s.finish()
    r.tot2[...] = t2

    acc[0:768, :] = jnp.zeros((768, 128), F32)
    fill_tables(tab, 0, forward_rows(t2[:, :256], t2, 1, r.nr[...].astype(F32)))
    fill_tables(tab, 256, forward_rows(fold_frames(t2[:, 256:], 32), t2, 4, four(r.nn[...])))

    @loop(0, nc)
    def _(c):
        g = grp[c]
        m = mask_of(g)
        u = r.y2[c, 0:256, :] * coef(tab, g, 0, 0, 256) + coef(tab, g, 1, 0, 256)
        act = u * sigmoid(u) * m
        r.act2[c, 0:256, :] = act.astype(BF16)
        taps(act, r.x9, 256, 1)
        u = r.y2[c, 256:384, :] * coef(tab, g, 0, 256, 128) + coef(tab, g, 1, 256, 128)
        r.act2[c, 256:384, :] = (u * sigmoid(u) * m).astype(BF16)
        saves["act2"].start(c)
        for lo in range(0, 512, 128):
            y = dot(r.ww[lo : lo + 128, :], r.act2[c, 256:384, :])
            ym = y * m
            add_stats(acc, 256 + lo, 128, ym, ym * y, g)
        for lo in range(0, 256, 128):
            y = dot(r.ws[lo : lo + 128, :], r.x9[...])
            r.y3[c, lo : lo + 128, :] = y
            ym = y * m
            add_stats(acc, lo, 128, ym, ym * y, g)
        saves["y3"].start(c)

    s = Sum(p, r.ar3)
    s.start(acc, counts)
    s.middle()
    t3 = s.finish()
    r.tot3[...] = t3

    ffeed = Feed(r.fcot, r.fcbuf, r.s_fc, nc)
    ffeed.prime()
    fdrain = Drain(r.fobuf, r.fout, r.s_fo, nc)
    wdrain = Drain(r.dzwb, r.dzw_o, r.s_dzw, nc)
    acc[...] = jnp.zeros_like(acc)
    fill_tables(tab, 0, forward_rows(t3[:, :256], t3, 1, r.ns[...].astype(F32)))
    fill_tables(
        r.tabw, 0,
        forward_rows(fold_frames(t3[:, 256:], 128), t3, 4, jnp.concatenate([r.nw[...].astype(F32)] * 4, axis=1)),
    )

    @loop(0, nc)
    def _(c):
        g = grp[c]
        m = mask_of(g)
        for lo in range(0, 256, 128):
            u = r.y3[c, lo : lo + 128, :] * coef(tab, g, 0, lo, 128) + coef(tab, g, 1, lo, 128)
            r.acts[c, lo : lo + 128, :] = (u * sigmoid(u) * m).astype(BF16)
        saves["acts"].start(c)
        for lo in range(0, 1024, 128):
            y = dot(r.we[lo : lo + 128, :], r.acts[c])
            ym = y * m
            add_stats(acc, lo, 128, ym, ym * y, g)

    def fast_ends(lo_c, hi_c):
        @loop(lo_c, hi_c)
        def _(c):
            g = grp[c]
            m = mask_of(g)
            slot = ffeed.take(c)
            fdrain.room(c)
            wdrain.room(c)
            for lo in range(0, 512, 128):
                y = dot(r.ww[lo : lo + 128, :], r.act2[c, 256:384, :])
                v = y * coef(r.tabw, g, 0, lo, 128) + coef(r.tabw, g, 1, lo, 128)
                v = v + r.xe[c, 256 + lo : 384 + lo, :].astype(F32)
                sg = sigmoid(v)
                r.fobuf[slot, lo : lo + 128, :] = (v * sg * m).astype(BF16)
                dz = r.fcbuf[slot, lo : lo + 128, :].astype(F32) * m * (sg * (1.0 + v * (1.0 - sg)))
                r.dzwb[slot, lo : lo + 128, :] = dz
                add_stats(acc, 1024 + lo, 128, dz, dz * y, g)
            fdrain.put(c)
            wdrain.put(c)

    s = Sum(p, r.ar4)
    s.start(acc, counts)
    fast_ends(0, nc // 2)
    s.middle()
    fast_ends(nc // 2, nc)
    t4 = s.finish()
    r.tot4[...] = t4

    cfeed = Feed(r.scot, r.cbuf, r.s_c, nc)
    cfeed.prime()
    sdrain = Drain(r.obuf, r.sout, r.s_o, nc)
    zdrain = Drain(r.dzeb, r.dze_o, r.s_dze, nc)
    acc[0:1024, :] = jnp.zeros((1024, 128), F32)
    fill_tables(tab, 0, forward_rows(t4, t4, 1, r.ne[...].astype(F32)))

    @loop(0, nc)
    def _(c):
        g = grp[c]
        m = mask_of(g)
        slot = xfeed.take(c)
        cfeed.take(c)
        sdrain.room(c)
        zdrain.room(c)
        for lo in range(0, 1024, 128):
            y = dot(r.we[lo : lo + 128, :], r.acts[c])
            v = y * coef(tab, g, 0, lo, 128) + coef(tab, g, 1, lo, 128)
            v = v + r.xbuf[slot, lo : lo + 128, :].astype(F32)
            sg = sigmoid(v)
            r.obuf[slot, lo : lo + 128, :] = (v * sg * m).astype(BF16)
            dz = r.cbuf[slot, lo : lo + 128, :].astype(F32) * m * (sg * (1.0 + v * (1.0 - sg)))
            r.dzeb[slot, lo : lo + 128, :] = dz
            add_stats(acc, lo, 128, dz, dz * y, g)
        sdrain.put(c)
        zdrain.put(c)

    s = Sum(p, r.ar5)
    s.start(acc, counts)
    for k in saves:
        saves[k].wait_all(nc)
    s.middle()
    for c in wsaves:
        c.wait()
    fdrain.done()
    wdrain.done()
    sdrain.done()
    zdrain.done()
    r.tot5[...] = s.finish()


def back(na, nb, refs):
    r = refs
    grp = r.grp
    nc = r.acts_i.shape[0]
    pairs = nc // 2
    p = Peers(na, nb)
    b = p.b
    zfeed = Feed(r.dze_i, r.zbuf, r.s_z, nc)
    zfeed.prime()
    loads = {
        k: Move(getattr(r, k + "_i"), getattr(r, k), getattr(r, "s_" + k))
        for k in ("acts", "y3", "act2", "y2", "act1", "y1")
    }
    raw = {
        k: pltpu.make_async_copy(
            r.wrt_i.at[1024:1280] if k == "wrl" else getattr(r, k + "_i"), getattr(r, k), r.s_raw.at[i]
        )
        for i, k in enumerate(("wet", "we", "ww", "wwt", "wst", "wrl", "wnt"))
    }
    raw["we"].start()
    raw["wet"].start()
    loads["acts"].start_all(nc)
    loads["y3"].start_all(nc)
    for k in ("ww", "wwt", "wst", "wrl", "wnt"):
        raw[k].start()
    wfeed = Feed(r.dzw_i, r.wbuf, r.s_wb, nc)
    wfeed.prime()
    for k in ("act2", "y2", "act1", "y1"):
        loads[k].start_all(nc)

    def xload(i, slot):
        return pltpu.make_async_copy(r.slow.at[pl.ds(2 * i, 2)], r.xbuf.at[slot], r.s_x.at[slot])

    xload(0, 0).start()
    counts = counts_row(grp)
    acc, tab, tabb = r.acc, r.tab, r.tabb
    acc[...] = jnp.zeros_like(acc)
    t1, t2, t3, t4, t5 = r.tot1[...], r.tot2[...], r.tot3[...], r.tot4[...], r.tot5[...]

    @pl.when(b == 0)
    def _():
        r.dye[:, 512:768, :] = jnp.zeros((nc, 256, CELLS), BF16)

    @pl.when(b == nb - 1)
    def _():
        r.dye[:, 0:256, :] = jnp.zeros((nc, 256, CELLS), BF16)

    rows, pair = backward_rows(t4, t5[:, :1024], t4, 1, r.ne[...].astype(F32))
    fill_tables(tab, 0, rows)
    r.epair[...] = pair
    fill_tables(tabb, 0, forward_rows(t3[:, :256], t3, 1, r.ns[...].astype(F32)))
    raw["we"].wait()
    raw["wet"].wait()
    dye = r.dye2

    @loop(0, nc)
    def _(c):
        g = grp[c]
        m = mask_of(g)
        loads["acts"].wait(c)
        loads["y3"].wait(c)
        slot = zfeed.take(c)
        for lo in range(0, 1024, 128):
            y = dot(r.we[lo : lo + 128, :], r.acts[c])
            dy = r.zbuf[slot, lo : lo + 128, :] * coef(tab, g, 0, lo, 128)
            dy = dy + y * coef(tab, g, 1, lo, 128) + coef(tab, g, 2, lo, 128)
            dye[c, lo : lo + 128, :] = (dy * m).astype(BF16)
        for lo in range(0, 256, 128):
            dx = dot(r.wet[lo : lo + 128, :], dye[c])
            y = r.y3[c, lo : lo + 128, :]
            u = y * coef(tabb, g, 0, lo, 128) + coef(tabb, g, 1, lo, 128)
            dz = m * slope_of(u) * dx
            r.dzs[c, lo : lo + 128, :] = dz
            add_stats(acc, lo, 128, dz, dz * y, g)

    p.greet()
    s = Sum(p, r.ar6)
    s.start(acc, counts)
    rows, pair = backward_rows(
        fold_frames(t3[:, 256:], 128), fold_frames(t5[:, 1024:], 128), t3, 4,
        jnp.concatenate([r.nw[...].astype(F32)] * 4, axis=1),
    )
    fill_tables(tab, 0, rows)
    r.wpair[...] = pair[:, :128]
    fill_tables(tabb, 256, forward_rows(fold_frames(t2[:, 256:], 32), t2, 4, four(r.nn[...])))
    r.wg[...] = jnp.zeros_like(r.wg)
    raw["ww"].wait()
    raw["wwt"].wait()

    def widen_back(lo_c, hi_c):
        @loop(lo_c, hi_c)
        def _(c):
            g = grp[c]
            m = mask_of(g)
            loads["act2"].wait(c)
            loads["y2"].wait(c)
            slot = wfeed.take(c)
            dx = jnp.zeros((128, CELLS), F32)
            act = r.act2[c, 256:384, :]
            for lo in range(0, 512, 128):
                y = dot(r.ww[lo : lo + 128, :], act)
                dy = r.wbuf[slot, lo : lo + 128, :] * coef(tab, g, 0, lo, 128)
                dy = dy + y * coef(tab, g, 1, lo, 128) + coef(tab, g, 2, lo, 128)
                dy = (dy * m).astype(BF16)
                dx = dx + dot(r.wwt[:, lo : lo + 128], dy)
                r.wg[lo : lo + 128, :] += dot_nt(dy, act)
            y = r.y2[c, 256:384, :]
            u = y * coef(tabb, g, 0, 256, 128) + coef(tabb, g, 1, 256, 128)
            dz = m * slope_of(u) * dx
            r.dzn[c] = dz
            add_stats(acc, 256, 128, dz, dz * y, g)

    widen_back(0, nc // 2)
    s.middle()
    widen_back(nc // 2, nc)
    t6 = s.finish()

    acc[0:256, :] = jnp.zeros((256, 128), F32)
    rows, pair = backward_rows(t3[:, :256], t6, t3, 1, r.ns[...].astype(F32))
    fill_tables(tab, 0, rows)
    r.spair[...] = pair
    fill_tables(tabb, 0, forward_rows(t2[:, :256], t2, 1, r.nr[...].astype(F32)))
    raw["wst"].wait()

    @loop(0, nc)
    def _(c):
        g = grp[c]
        m = mask_of(g)
        dy = r.dzs[c] * coef(tab, g, 0, 0, 256) + r.y3[c] * coef(tab, g, 1, 0, 256)
        dy = (dy + coef(tab, g, 2, 0, 256)) * m
        r.dys[c] = dy.astype(BF16)
        taps(dy, r.d9.at[:, 0:256], 256, -1)
        for lo in range(0, 256, 128):
            dx = dot(r.wst[lo : lo + 128, :], r.d9[:, 0:256])
            y = r.y2[c, lo : lo + 128, :]
            u = y * coef(tabb, g, 0, lo, 128) + coef(tabb, g, 1, lo, 128)
            dz = m * slope_of(u) * dx
            r.dzs[c, lo : lo + 128, :] = dz
            add_stats(acc, lo, 128, dz, dz * y, g)

    s = Sum(p, r.ar7)
    s.start(acc, counts)
    gg = r.gg
    gg[...] = jnp.zeros_like(gg)

    def expand_terms(lo_i, hi_i):
        @loop(lo_i, hi_i)
        def _(i):
            act = jnp.concatenate([r.acts[2 * i + h] for h in range(2)], axis=1)
            for lo in range(0, 1024, 256):
                dy = jnp.concatenate([dye[2 * i + h, lo : lo + 256, :] for h in range(2)], axis=1)
                gg[6144 + lo : 6400 + lo, :] += dot_nt(dy, act)

    expand_terms(0, pairs // 2)
    s.middle()
    expand_terms(pairs // 2, pairs)
    t7 = s.finish()

    acc[...] = jnp.zeros_like(acc)
    rows, pair = backward_rows(t2[:, :256], t7[:, :256], t2, 1, r.nr[...].astype(F32))
    fill_tables(tab, 0, rows)
    r.rpair[...] = pair
    dyr = r.dye
    up = Halo(p, 1, lambda c: dyr.at[c, 256:512], lambda c: dyr.at[c, 512:768], r.h3us, r.h3ur)
    down = Halo(p, -1, lambda c: dyr.at[c, 256:512], lambda c: dyr.at[c, 0:256], r.h3ds, r.h3dr)

    @loop(0, nc)
    def _(c):
        g = grp[c]
        m = mask_of(g)
        for lo in range(0, 256, 128):
            dy = r.dzs[c, lo : lo + 128, :] * coef(tab, g, 0, lo, 128)
            dy = dy + r.y2[c, lo : lo + 128, :] * coef(tab, g, 1, lo, 128)
            dy = (dy + coef(tab, g, 2, lo, 128)) * m
            dyr[c, 256 + lo : 384 + lo, :] = dy.astype(BF16)
        up.start(c)
        down.start(c)

    rows, pair = backward_rows(
        fold_frames(t2[:, 256:], 32), fold_frames(t7[:, 256:], 32), t2, 4, four(r.nn[...])
    )
    fill_tables(tab, 0, rows)
    r.npair[...] = pair
    fill_tables(tabb, 0, forward_rows(t1[:, :256], t1, 1, r.nl[...].astype(F32)))
    fill_tables(tabb, 256, forward_rows(fold_frames(t1[:, 256:], 32), t1, 4, four(r.nq[...])))
    r.ng[...] = jnp.zeros_like(r.ng)
    raw["wnt"].wait()
    raw["wrl"].wait()

    @loop(0, pairs)
    def _(i):
        for h in range(2):
            c = 2 * i + h
            g = grp[c]
            m = mask_of(g)
            loads["act1"].wait(c)
            loads["y1"].wait(c)
            dy = r.dzn[c] * coef(tab, g, 0, 0, 128) + r.y2[c, 256:384, :] * coef(tab, g, 1, 0, 128)
            dy = (dy + coef(tab, g, 2, 0, 128)) * m
            taps(dy, r.d9n, 128, -1)
            dx = dot(r.wnt[...], r.d9n[...])
            y = r.y1[c, 256:384, :]
            u = y * coef(tabb, g, 0, 256, 128) + coef(tabb, g, 1, 256, 128)
            dz = m * slope_of(u) * dx
            r.y1[c, 256:384, :] = dz
            add_stats(acc, 256, 128, dz, dz * y, g)
            for lo in range(0, 1152, 384):
                r.ng[lo : lo + 384, :] += dot_nt(r.d9n[lo : lo + 384, :], r.act1[c, 256:384, :])
            taps(r.dys[c].astype(F32), r.d9, 256, -1, h * CELLS)
        act = jnp.concatenate([r.act2[2 * i + h, 0:256, :] for h in range(2)], axis=1)
        for lo in range(0, 2304, 256):
            gg[3840 + lo : 4096 + lo, :] += dot_nt(r.d9[lo : lo + 256, :], act)

    def reducer_terms(taps_of):
        @loop(0, pairs)
        def _(i):
            slot = lax.rem(i, 2)

            @pl.when(i + 1 < pairs)
            def _():
                xload(i + 1, 1 - slot).start()

            xload(i, slot).wait()
            for j in taps_of:
                dy = jnp.concatenate(
                    [dyr[2 * i + h, 256 * j : 256 * (j + 1), :] for h in range(2)], axis=1
                )
                for cb in range(5):
                    if cb < 4:
                        x = [r.xbuf[slot, h, 256 * cb : 256 * (cb + 1), :] for h in range(2)]
                    else:
                        x = [r.act1[2 * i + h, 0:256, :] for h in range(2)]
                    lo = 768 * cb + 256 * j
                    gg[lo : lo + 256, :] += dot_nt(dy, jnp.concatenate(x, axis=1))

    reducer_terms((1,))
    xload(0, 0).start()
    zsave = Move(r.y1, r.dz1_o, r.s_dz1)
    dsave = Move(dyr, r.dyr_o, r.s_dyr)

    @loop(0, nc)
    def _(c):
        up.arrive(c)
        down.arrive(c)
        dsave.start(c)
        g = grp[c]
        m = mask_of(g)
        for lo in range(0, 256, 128):
            dx = dot(r.wrl[lo : lo + 128, :], dyr[c])
            y = r.y1[c, lo : lo + 128, :]
            u = y * coef(tabb, g, 0, lo, 128) + coef(tabb, g, 1, lo, 128)
            dz = m * slope_of(u) * dx
            r.y1[c, lo : lo + 128, :] = dz
            add_stats(acc, lo, 128, dz, dz * y, g)
        zsave.start(c)

    s = Sum(p, r.ar8)
    s.start(acc, counts)
    reducer_terms((0,))
    s.middle()
    xload(0, 0).start()
    reducer_terms((2,))
    gsave = pltpu.make_async_copy(gg, r.gg_o, r.s_gg)
    gsave.start()
    up.sent(nc)
    down.sent(nc)
    r.tot8[...] = s.finish()
    zsave.wait_all(nc)
    dsave.wait_all(nc)
    gsave.wait()


def ends(na, nb, refs):
    r = refs
    grp = r.grp
    nc = r.dz1_i.shape[0]
    p = Peers(na, nb)
    b = p.b
    tab, dyl, dyq, lg, qg = r.tab, r.dyl, r.dyq, r.lg, r.qg
    sp = Spread(na, nb, r.own, r.out, r.sp)
    dfeed = Feed(r.dz1_i, r.dbuf, r.s_d, nc)
    yfeed = Feed(r.y1_i, r.ybuf, r.s_y, nc)
    efeed = Feed(r.xe_i, r.ebuf, r.s_e, nc)
    gfeed = Feed(r.dyr_i, r.gbuf, r.s_g, nc)
    zfeed = Feed(r.dze_i, r.zbuf, r.s_z, nc)
    wfeed = Feed(r.dzw_i, r.wbuf, r.s_wb, nc)
    sdrain = Drain(r.obuf, r.sgrad, r.s_o, nc)
    fdrain = Drain(r.fbuf, r.fgrad, r.s_f, nc)
    for f in (dfeed, yfeed, efeed):
        f.prime()
    gload = pltpu.make_async_copy(r.gg_i, r.gg, r.s_raw.at[0])
    rload = pltpu.make_async_copy(r.wrt_i.at[0:1024], r.wr, r.s_raw.at[1])
    fload = pltpu.make_async_copy(r.wf_i, r.wf, r.s_raw.at[2])
    gload.start()
    for f in (gfeed, zfeed, wfeed):
        f.prime()
    rload.start()
    fload.start()
    t8, t1 = r.tot8[...], r.tot1[...]
    rows, pair = backward_rows(t1[:, :256], t8[:, :256], t1, 1, r.nl[...].astype(F32))
    fill_tables(tab, 0, rows)
    r.lpair[...] = pair
    rows, pair = backward_rows(
        fold_frames(t1[:, 256:], 32), fold_frames(t8[:, 256:], 32), t1, 4, four(r.nq[...])
    )
    fill_tables(tab, 256, rows)
    r.qpair[...] = pair
    lat = Halo(p, -1, lambda c: dyl.at[c, 0:256], lambda c: dyl.at[c, 256:512], r.hls, r.hlr)
    up = Halo(p, 1, lambda c: dyq.at[c, 160:192], lambda c: dyq.at[c, 0:32], r.hus, r.hur)
    down = Halo(p, -1, lambda c: dyq.at[c, 64:96], lambda c: dyq.at[c, 192:224], r.hds, r.hdr)
    dyq[:, 32:64, :] = jnp.zeros((nc, 32, CELLS), BF16)
    dyq[:, 224:256, :] = jnp.zeros((nc, 32, CELLS), BF16)

    @pl.when(b == 0)
    def _():
        dyq[:, 0:32, :] = jnp.zeros((nc, 32, CELLS), BF16)

    @pl.when(b == nb - 1)
    def _():
        dyq[:, 192:224, :] = jnp.zeros((nc, 32, CELLS), BF16)
        dyl[:, 256:512, :] = jnp.zeros((nc, 256, CELLS), BF16)

    lg[...] = jnp.zeros_like(lg)
    qg[...] = jnp.zeros_like(qg)
    p.greet()

    @loop(0, nc)
    def _(c):
        g = grp[c]
        m = mask_of(g)
        slot = dfeed.take(c)
        yfeed.take(c)
        for lo in range(0, 384, 128):
            dy = r.dbuf[slot, lo : lo + 128, :] * coef(tab, g, 0, lo, 128)
            dy = dy + r.ybuf[slot, lo : lo + 128, :] * coef(tab, g, 1, lo, 128)
            dy = ((dy + coef(tab, g, 2, lo, 128)) * m).astype(BF16)
            if lo < 256:
                dyl[c, lo : lo + 128, :] = dy
            else:
                dyq[c, 64:192, :] = dy
        lat.start(c)
        up.start(c)
        down.start(c)
        efeed.take(c)
        dy = dyl[c, 0:256, :]
        lg[0:256, :] += dot_nt(dy, r.ebuf[slot, 0:256, :])
        lg[256:512, :] += dot_nt(dy, r.ebuf[slot, 256:512, :])
        lg[512:768, 0:128] += dot_nt(dy, r.ebuf[slot, 512:640, :])
        qg[...] += dot_nt(dyq[c, 64:192, :], r.ebuf[slot, 128:896, :])

    for j in range(3):
        lg[800 + 32 * j : 832 + 32 * j, 128:256] = sum(
            qg[32 * f : 32 * (f + 1), 128 * (f + j) : 128 * (f + j + 1)] for f in range(4)
        )
    for k in range(9):
        term = sum(
            r.ng[128 * k + 32 * f : 128 * k + 32 * (f + 1), 32 * f : 32 * (f + 1)] for f in range(4)
        )
        if k < 8:
            lg[768 + 32 * k : 800 + 32 * k, 0:32] = term
        else:
            lg[768:800, 128:160] = term
    lg[896:1024, 128:160] = sum(r.wg[128 * f : 128 * (f + 1), 32 * f : 32 * (f + 1)] for f in range(4))
    gload.wait()

    def block_of(half, i):
        if half == 0:
            return r.gg[256 * i : 256 * (i + 1), :]
        if i < 12:
            return r.gg[4096 + 256 * i : 4352 + 256 * i, :]
        return lg[256 * (i - 12) : 256 * (i - 11), :]

    sp.first(block_of, 4)
    rload.wait()

    def slow_ends(lo_c, hi_c):
        @loop(lo_c, hi_c)
        def _(c):
            m = mask_of(grp[c])
            slot = gfeed.take(c)
            zfeed.take(c)
            sdrain.room(c)
            for lo in range(0, 1024, 128):
                dx = dot(r.wr[lo : lo + 128, :], r.gbuf[slot]) + r.zbuf[slot, lo : lo + 128, :]
                r.obuf[slot, lo : lo + 128, :] = (dx * m).astype(BF16)
            sdrain.put(c)

    stages = len(sp.bits)
    cuts = [nc * i // (stages + 1) for i in range(stages + 2)]
    slow_ends(cuts[0], cuts[1])
    sp.first_done()
    for n in range(stages):
        sp.halve(n)
        slow_ends(cuts[n + 1], cuts[n + 2])
        sp.halved()
    sp.along()
    fload.wait()

    @loop(0, nc)
    def _(c):
        lat.arrive(c)
        up.arrive(c)
        down.arrive(c)
        m = mask_of(grp[c])
        slot = wfeed.take(c)
        fdrain.room(c)
        for lo in range(0, 512, 128):
            dx = dot(r.wf[lo : lo + 128, 0:512], dyl[c]) + dot(r.wf[lo : lo + 128, 512:768], dyq[c])
            dx = dx + r.wbuf[slot, lo : lo + 128, :]
            r.fbuf[slot, lo : lo + 128, :] = (dx * m).astype(BF16)
        fdrain.put(c)

    sp.summed()
    for n in reversed(range(stages)):
        sp.gather(n)
    sp.last()
    sdrain.done()
    fdrain.done()
    lat.sent(nc)
    up.sent(nc)
    down.sent(nc)
    sp.done()


def last(out, rp, spr, ep, lp, qp, np_, wp, rg, sg, eg, lg, qg, ng, wg, rpo, spo, epo, lpo, qpo, npo, wpo):
    for cb in range(5):
        for j in range(3):
            lo = 768 * cb + 256 * j
            rg[j, :, 256 * cb : 256 * (cb + 1)] = out[lo : lo + 256, :].astype(F32)
    for k in range(9):
        sg[k] = out[3840 + 256 * k : 4096 + 256 * k, :].astype(F32)
        at = 7936 + 32 * k if k < 8 else 7936
        ng[k] = (out[at : at + 32, 0:32] if k < 8 else out[at : at + 32, 128:160]).astype(F32)
    for q in range(4):
        eg[256 * q : 256 * (q + 1), :] = out[6144 + 256 * q : 6400 + 256 * q, :].astype(F32)
    for k in range(5):
        lo = 7168 + 256 * (k // 2)
        lg[k] = out[lo : lo + 256, 128 * (k % 2) : 128 * (k % 2 + 1)].astype(F32)
    for j in range(3):
        qg[j] = out[7968 + 32 * j : 8000 + 32 * j, 128:256].astype(F32)
    wg[...] = out[8064:8192, 128:160].astype(F32)
    for src, dst in ((rp, rpo), (spr, spo), (ep, epo), (lp, lpo), (wp, wpo)):
        dst[...] = src[...]
    qpo[...] = qp[:, 0:32]
    npo[...] = np_[:, 0:32]


def sds(shape, dtype):
    return jax.ShapeDtypeStruct(shape, dtype)


class Refs:
    pass


SPACE = {"v": VM, "h": pl.ANY, "s": pltpu.SMEM}


def call(body, na, nb, cid, ins, outs, scratch, sums, tail=()):
    tail_name, tail_shapes = tail if tail else (None, [])
    names = [x[0] for x in ins] + [x[0] for x in outs] + [x[0] for x in scratch]
    shapes = [x[1] for x in scratch]
    for _, width in sums:
        shapes += ar_scratch(na, nb, width)
    shapes += list(tail_shapes)

    def kernel(*refs):
        r = Refs()
        for name, ref in zip(names, refs):
            setattr(r, name, ref)
        at = len(names)
        for name, _ in sums:
            setattr(r, name, refs[at : at + 8])
            at += 8
        if tail_name:
            setattr(r, tail_name, refs[at:])
        body(na, nb, r)

    got = pl.pallas_call(
        kernel,
        name=body.__name__,
        out_shape=tuple(x[2] for x in outs),
        in_specs=[pl.BlockSpec(memory_space=SPACE[x[1]]) for x in ins],
        out_specs=tuple(pl.BlockSpec(memory_space=SPACE[x[1]]) for x in outs),
        scratch_shapes=shapes,
        compiler_params=pltpu.CompilerParams(
            collective_id=cid, has_side_effects=True, vmem_limit_bytes=LIMIT
        ),
    )(*[x[2] for x in ins])
    return {x[0]: v for x, v in zip(outs, got)}


def build(na, nb):
    def body(
        slow_in, fast_in, clip_group, reducer, spatial, expand, lateral, squeeze, narrow, widening,
        reducer_norm, spatial_norm, expand_norm, lateral_norm, squeeze_norm, narrow_norm, widening_norm,
        slow_cot, fast_cot,
    ):
        nc = slow_in.shape[0]
        dma = pltpu.SemaphoreType.DMA
        slow = slow_in.reshape(nc, 1024, CELLS)
        norms = [
            ("nl", "v", lateral_norm), ("nq", "v", squeeze_norm), ("nr", "v", reducer_norm),
            ("nn", "v", narrow_norm), ("ns", "v", spatial_norm), ("ne", "v", expand_norm), ("nw", "v", widening_norm),
        ]

        def act(c, dtype):
            return sds((nc, c, CELLS), dtype)

        def vact(c, dtype):
            return VM((nc, c, CELLS), dtype)

        def two(c, dtype):
            return VM((2, c, CELLS), dtype)

        def tab(k, c):
            return VM((3, k, c, 128), F32)

        each, slots = dma((nc,)), dma((2,))
        state = {
            "xe": (896, BF16), "y1": (384, F32), "act1": (384, BF16), "y2": (384, F32),
            "act2": (384, BF16), "y3": (256, F32), "acts": (256, BF16),
        }
        turns = {
            "wrt": (1280, 768), "wst": (256, 2304), "wet": (256, 1024), "wwt": (128, 512),
            "wnt": (128, 1152), "wf": (512, 768), "ww": (512, 128),
        }
        fw = call(
            forward, na, nb, 1,
            [
                ("grp", "s", clip_group), ("fast", "h", fast_in.reshape(nc, 512, CELLS)), ("slow", "h", slow),
                ("scot", "h", slow_cot.reshape(nc, 1024, CELLS)), ("fcot", "h", fast_cot.reshape(nc, 512, CELLS)),
                ("reducer", "h", reducer.reshape(768, 1280)), ("spatial", "h", spatial), ("expand", "h", expand),
                ("lateral", "v", lateral), ("squeeze", "v", squeeze), ("narrow", "v", narrow),
                ("widening", "v", widening),
            ] + norms,
            [("sout", "h", act(1024, BF16)), ("fout", "h", act(512, BF16))]
            + [(k + "_o", "h", act(*v)) for k, v in state.items()]
            + [("dzw_o", "h", act(512, F32)), ("dze_o", "h", act(1024, F32))]
            + [(k + "_o", "h", sds(v, BF16)) for k, v in turns.items()]
            + [("tot%d" % (i + 1), "v", sds((8, w), F32)) for i, w in enumerate((384, 384, 768, 1024, 1536))],
            [(k, vact(*v)) for k, v in state.items()]
            + [(k, VM(v, BF16)) for k, v in turns.items()]
            + [
                ("wr", VM((768, 1280), BF16)), ("sp", VM((9, 256, 256), BF16)), ("we", VM((1024, 256), BF16)),
                ("wa", VM((384, 896), BF16)), ("ws", VM((256, 2304), BF16)), ("wn", VM((128, 1152), BF16)),
                ("su", vact(256, BF16)), ("sd", vact(256, BF16)), ("ru", vact(256, BF16)), ("rd", vact(256, BF16)),
                ("xbuf", two(1024, BF16)), ("cbuf", two(1024, BF16)), ("obuf", two(1024, BF16)),
                ("dzeb", two(1024, F32)), ("fcbuf", two(512, BF16)), ("fobuf", two(512, BF16)), ("dzwb", two(512, F32)),
                ("tab", tab(2, 1024)), ("tabw", tab(2, 512)), ("acc", VM((1536, 128), F32)),
                ("x9", VM((2304, CELLS), BF16)),
            ]
            + [("s_" + k, each) for k in tuple(state) + ("own",)]
            + [(k, each) for k in ("h1us", "h1ur", "h1ds", "h1dr", "h2us", "h2ur", "h2ds", "h2dr")]
            + [("s_" + k, slots) for k in ("x", "c", "o", "dze", "fc", "fo", "dzw")]
            + [("s_raw", dma((3,))), ("s_w", dma((7,)))],
            [("ar%d" % (i + 1), w) for i, w in enumerate((384, 384, 768, 1024, 1536))],
        )
        tots = [("tot%d" % i, "v", fw["tot%d" % i]) for i in range(1, 6)]
        kept = ("acts", "y3", "act2", "y2", "act1", "y1")
        bw = call(
            back, na, nb, 2,
            [("grp", "s", clip_group), ("slow", "h", slow), ("we_i", "h", expand)]
            + [(k + "_i", "h", fw[k + "_o"]) for k in kept + ("dze", "dzw", "wet", "wwt", "wst", "wrt", "wnt", "ww")]
            + tots + norms,
            [
                ("dz1_o", "h", act(384, F32)), ("dyr_o", "h", act(768, BF16)), ("gg_o", "h", sds((7168, 256), F32)),
                ("ng", "v", sds((1152, 128), F32)), ("wg", "v", sds((512, 128), F32)), ("tot8", "v", sds((8, 384), F32)),
                ("epair", "v", sds((2, 1024), F32)), ("spair", "v", sds((2, 256), F32)), ("rpair", "v", sds((2, 256), F32)),
                ("wpair", "v", sds((2, 128), F32)), ("npair", "v", sds((2, 128), F32)),
            ],
            [(k, vact(*state[k])) for k in kept]
            + [
                ("wet", VM((256, 1024), BF16)), ("we", VM((1024, 256), BF16)), ("ww", VM((512, 128), BF16)),
                ("wwt", VM((128, 512), BF16)), ("wst", VM((256, 2304), BF16)), ("wrl", VM((256, 768), BF16)),
                ("wnt", VM((128, 1152), BF16)),
                ("zbuf", two(1024, F32)), ("wbuf", two(512, F32)), ("xbuf", VM((2, 2, 1024, CELLS), BF16)),
                ("dye", vact(768, BF16)), ("dye2", vact(1024, BF16)), ("dzs", vact(256, F32)), ("dzn", vact(128, F32)),
                ("dys", vact(256, BF16)), ("gg", VM((7168, 256), F32)),
                ("tab", tab(3, 1024)), ("tabb", tab(2, 384)), ("acc", VM((384, 128), F32)),
                ("d9", VM((2304, 2 * CELLS), BF16)), ("d9n", VM((1152, CELLS), BF16)),
            ]
            + [("s_" + k, each) for k in kept + ("dz1", "dyr")]
            + [(k, each) for k in ("h3us", "h3ur", "h3ds", "h3dr")]
            + [("s_" + k, slots) for k in ("z", "wb", "x")]
            + [("s_raw", dma((7,))), ("s_gg", dma)],
            [("ar6", 256), ("ar7", 384), ("ar8", 384)],
        )
        half = 4096
        en = call(
            ends, na, nb, 3,
            [("grp", "s", clip_group)]
            + [(k + "_i", "h", bw[k + "_o"]) for k in ("dz1", "dyr", "gg")]
            + [(k + "_i", "h", fw[k + "_o"]) for k in ("y1", "xe", "dze", "dzw", "wrt", "wf")]
            + [("ng", "v", bw["ng"]), ("wg", "v", bw["wg"]), ("tot8", "v", bw["tot8"]), tots[0]] + norms[:2],
            [
                ("sgrad", "h", act(1024, BF16)), ("fgrad", "h", act(512, BF16)), ("out", "v", sds((2 * half, 256), BF16)),
                ("lpair", "v", sds((2, 256), F32)), ("qpair", "v", sds((2, 128), F32)),
            ],
            [
                ("gg", VM((7168, 256), F32)), ("wr", VM((1024, 768), BF16)), ("wf", VM((512, 768), BF16)),
                ("tab", tab(3, 384)), ("dyl", vact(512, BF16)), ("dyq", vact(256, BF16)),
                ("lg", VM((1024, 256), F32)), ("qg", VM((128, 768), F32)), ("own", VM((half, 256), F32)),
                ("dbuf", two(384, F32)), ("ybuf", two(384, F32)), ("ebuf", two(896, BF16)), ("gbuf", two(768, BF16)),
                ("zbuf", two(1024, F32)), ("wbuf", two(512, F32)), ("obuf", two(1024, BF16)), ("fbuf", two(512, BF16)),
            ]
            + [("s_" + k, slots) for k in ("d", "y", "e", "g", "z", "wb", "o", "f")]
            + [("s_raw", dma((3,)))]
            + [(k, each) for k in ("hls", "hlr", "hus", "hur", "hds", "hdr")],
            [],
            ("sp", spread_scratch(na, nb, half, 4)),
        )
        shapes = [
            (3, 256, 1280), (9, 256, 256), (1024, 256), (5, 256, 128), (3, 32, 128), (9, 32, 32), (128, 32),
            (2, 256), (2, 256), (2, 1024), (2, 256), (2, 32), (2, 32), (2, 128),
        ]
        grads = pl.pallas_call(
            last,
            name="last",
            out_shape=tuple(sds(v, F32) for v in shapes),
            in_specs=[pl.BlockSpec(memory_space=VM)] * 8,
            out_specs=tuple([pl.BlockSpec(memory_space=VM)] * len(shapes)),
            compiler_params=pltpu.CompilerParams(vmem_limit_bytes=LIMIT),
        )(
            en["out"], bw["rpair"], bw["spair"], bw["epair"], en["lpair"], en["qpair"], bw["npair"], bw["wpair"]
        )
        return (
            fw["sout"].reshape(slow_in.shape), fw["fout"].reshape(fast_in.shape),
            en["sgrad"].reshape(slow_in.shape), en["fgrad"].reshape(fast_in.shape),
            *grads,
        )

    return body


def solution(mesh):
    body = build(mesh.shape["clip"], mesh.shape["tm"])
    big = P("clip", "tm", None, None)
    return jax.shard_map(
        body,
        mesh=mesh,
        in_specs=(big, big, P("clip")) + (P(),) * 14 + (big, big),
        out_specs=(big,) * 4 + (P(),) * 14,
        check_vma=False,
    )
```

```python
import functools

import jax
import jax.numpy as jnp
from jax import lax
from jax.experimental import pallas as pl
from jax.experimental.pallas import tpu as pltpu
from jax.sharding import PartitionSpec as P

MESH = pl.DeviceIdType.MESH
F32, BF16 = jnp.float32, jnp.bfloat16
SIDE = 16
CELLS = SIDE * SIDE
EPS = 1e-05
VM = pltpu.VMEM
LIMIT = 63 * 1024 * 1024


def dot(a, b):
    return lax.dot_general(a, b, (((1,), (0,)), ((), ())), preferred_element_type=F32)


def dot_nt(a, b):
    return lax.dot_general(a, b, (((1,), (1,)), ((), ())), preferred_element_type=F32)


def side_of(g):
    return jnp.where(g == 0, SIDE * 5 // 8, jnp.where(g == 1, SIDE * 7 // 8, SIDE))


def mask_of(g):
    cell = lax.broadcasted_iota(jnp.int32, (1, CELLS), 1)
    side = side_of(g)
    return jnp.where(((cell >> 4) < side) & ((cell & 15) < side), 1.0, 0.0).astype(F32)


def counts_row(grp):
    lane = lax.broadcasted_iota(jnp.int32, (1, 128), 1)
    total = jnp.zeros((1, 128), F32)
    for c in range(grp.shape[0]):
        side = side_of(grp[c])
        total = total + jnp.where(lane == grp[c], (side * side).astype(F32), 0.0)
    return total


def add_stats(acc, lo, rows, first, second, g):
    lane = lax.broadcasted_iota(jnp.int32, (1, 128), 1)
    one = jnp.sum(first[:, :128] + first[:, 128:], axis=1, keepdims=True)
    two = jnp.sum(second[:, :128] + second[:, 128:], axis=1, keepdims=True)
    acc[lo : lo + rows, :] += jnp.where(lane == g, one, 0.0) + jnp.where(lane == g + 3, two, 0.0)


def add_sums(acc, lo, rows, value, g):
    lane = lax.broadcasted_iota(jnp.int32, (1, 128), 1)
    one = jnp.sum(value[:, :128] + value[:, 128:], axis=1, keepdims=True)
    acc[lo : lo + rows, :] += jnp.where(lane == g, one, 0.0)


def add_gram(gram, act, g):
    term = dot_nt(act, act)
    for k in range(3):
        gram[k] += jnp.where(g == k, term, 0.0)


def wide_sums(acc, gram, tall):
    w = tall.astype(F32)
    exact = dict(precision=lax.Precision.HIGHEST, preferred_element_type=F32)
    one = jnp.dot(rows_of(acc, 256, 384), w, **exact)
    block = lax.broadcasted_iota(jnp.int32, (128, 128), 0) >> 5
    same = block == (lax.broadcasted_iota(jnp.int32, (128, 128), 1) >> 5)
    two = [
        jnp.sum(w * jnp.dot(jnp.where(same, gram[k], 0.0), w, **exact), axis=0, keepdims=True)
        for k in range(3)
    ]
    return jnp.concatenate([one[:3, :]] + two + [jnp.zeros((2, 128), F32)], axis=0)


def ar_scratch(na, nb, width):
    dma = pltpu.SemaphoreType.DMA
    return [
        VM((8, width), F32),
        VM((na, 8, width), F32),
        VM((8, width), F32),
        VM((nb, 8, width), F32),
        dma((na - 1,)),
        dma((na - 1,)),
        dma((nb - 1,)),
        dma((nb - 1,)),
    ]


class Peers:
    def __init__(self, na, nb):
        self.na, self.nb = na, nb
        self.a, self.b = lax.axis_index("clip"), lax.axis_index("tm")
        self.along_a = [(lax.rem(self.a + d, na), self.b) for d in range(1, na)]
        self.along_b = [(self.a, lax.rem(self.b + d, nb)) for d in range(1, nb)]
        self.bar = pltpu.get_barrier_semaphore()
        for peer in self.along_a + self.along_b:
            pl.semaphore_signal(self.bar, inc=1, device_id=peer, device_id_type=MESH)

    def greet(self):
        pl.semaphore_wait(self.bar, self.na - 1 + self.nb - 1)


class Sum:
    def __init__(self, peers, refs):
        self.p = peers
        self.mine, self.bufa, self.part, self.bufb, self.sa, self.ra, self.sb, self.rb = refs

    def copies(self, src, buf, slot, ss, rs, peers):
        return [
            pltpu.make_async_remote_copy(
                src, buf.at[slot], ss.at[i], rs.at[i], device_id=peer, device_id_type=MESH
            )
            for i, peer in enumerate(peers)
        ]

    def start(self, rows, counts):
        row = lax.broadcasted_iota(jnp.int32, (8, 128), 0)
        head = jnp.where(row == 6, counts, rows[:, :128])
        value = jnp.concatenate([head, rows[:, 128:]], axis=1)
        self.mine[...] = value
        self.bufa[self.p.a] = value
        self.first = self.copies(self.mine, self.bufa, self.p.a, self.sa, self.ra, self.p.along_a)
        for c in self.first:
            c.start()

    def middle(self):
        for c in self.first:
            c.wait()
        total = self.bufa[0]
        for i in range(1, self.p.na):
            total = total + self.bufa[i]
        self.part[...] = total
        self.bufb[self.p.b] = total
        self.second = self.copies(self.part, self.bufb, self.p.b, self.sb, self.rb, self.p.along_b)
        for c in self.second:
            c.start()

    def finish(self):
        for c in self.second:
            c.wait()
        total = self.bufb[0]
        for i in range(1, self.p.nb):
            total = total + self.bufb[i]
        return total


def rows_of(acc, lo, hi):
    return jnp.transpose(acc[lo:hi, :])[:8, :]


def folded(rows):
    return sum(rows[:, 128 * f : 128 * (f + 1)] for f in range(rows.shape[1] // 128))


def repeated(rows):
    return jnp.concatenate([rows] * 4, axis=1)


class Halo:
    def __init__(self, peers, step, src, dst, ss, rs):
        self.src, self.dst, self.ss, self.rs = src, dst, ss, rs
        to = peers.b + step
        self.sends = (to >= 0) & (to < peers.nb)
        source = peers.b - step
        self.gets = (source >= 0) & (source < peers.nb)
        self.peer = (peers.a, lax.rem(to + peers.nb, peers.nb))

    def copy(self, c):
        return pltpu.make_async_remote_copy(
            self.src(c), self.dst(c), self.ss.at[c], self.rs.at[c],
            device_id=self.peer, device_id_type=MESH,
        )

    def start(self, c):
        @pl.when(self.sends)
        def _():
            self.copy(c).start()

    def arrive(self, c):
        @pl.when(self.gets)
        def _():
            self.copy(c).wait_recv()

    def sent(self, nc):
        @pl.when(self.sends)
        def _():
            @pl.loop(0, nc)
            def _(c):
                self.copy(c).wait_send()


class Move:
    def __init__(self, src, dst, sem):
        self.src, self.dst, self.sem = src, dst, sem

    def copy(self, c):
        return pltpu.make_async_copy(self.src.at[c], self.dst.at[c], self.sem.at[c])

    def start(self, c):
        self.copy(c).start()

    def wait(self, c):
        self.copy(c).wait()

    def start_all(self, nc):
        @pl.loop(0, nc)
        def _(c):
            self.start(c)

    def wait_all(self, nc):
        @pl.loop(0, nc)
        def _(c):
            self.wait(c)


class Feed:
    def __init__(self, src, buf, sem, nc, rows=0):
        self.src, self.buf, self.sem, self.nc, self.rows = src, buf, sem, nc, rows

    def copy(self, c, slot):
        at = pl.ds(pl.multiple_of(slot * self.rows, 8), self.rows) if self.rows else slot
        return pltpu.make_async_copy(self.src.at[c], self.buf.at[at], self.sem.at[slot])

    def prime(self):
        self.copy(0, 0).start()

    def take(self, c):
        slot = lax.rem(c, 2)

        @pl.when(c + 1 < self.nc)
        def _():
            self.copy(c + 1, 1 - slot).start()

        self.copy(c, slot).wait()
        return slot


class Drain:
    def __init__(self, buf, dst, sem, nc):
        self.buf, self.dst, self.sem, self.nc = buf, dst, sem, nc

    def copy(self, c, slot):
        return pltpu.make_async_copy(self.buf.at[slot], self.dst.at[c], self.sem.at[slot])

    def room(self, c):
        slot = lax.rem(c, 2)

        @pl.when(c >= 2)
        def _():
            self.copy(c - 2, slot).wait()

        return slot

    def put(self, c):
        self.copy(c, lax.rem(c, 2)).start()

    def done(self):
        for c in range(max(0, self.nc - 2), self.nc):
            self.copy(c, c % 2).wait()


def fold_frames(total):
    out = total + pltpu.roll(total, 32, 1)
    return out + pltpu.roll(out, 64, 1)


def moments(total, counts, frames):
    out = []
    for g in range(3):
        n = counts[6:7, g : g + 1] * float(frames)
        mean = total[g : g + 1, :] / n
        var = total[g + 3 : g + 4, :] / n - mean * mean
        out.append((n, mean, lax.rsqrt(var + EPS)))
    return out


def fill_tables(tab, base, rows_list):
    width = rows_list[0][0].shape[1]
    count = len(rows_list[0])
    rows = [rows_list[g][k] for g in range(3) for k in range(count)]
    rows = rows + [jnp.zeros((1, width), F32)] * (128 - len(rows))
    cols = jnp.transpose(jnp.concatenate(rows, axis=0))
    for g in range(3):
        for k in range(count):
            i = g * count + k
            tab[g, k, base : base + width, :] = jnp.broadcast_to(cols[:, i : i + 1], (width, 128))


def forward_rows(total, counts, frames, pair):
    out = []
    for n, mean, r in moments(total, counts, frames):
        gain = 0.5 * (pair[0:1, :] * r)
        out.append((gain, 0.5 * pair[1:2, :] - mean * gain))
    return out


def backward_rows(total, grads, counts, frames, pair):
    out, two_all, one_all = [], 0.0, 0.0
    for g, (n, mean, r) in enumerate(moments(total, counts, frames)):
        one = grads[g : g + 1, :]
        two = r * (grads[g + 3 : g + 4, :] - mean * one)
        c0 = pair[0:1, :] * r
        slope = c0 * r * two / n
        out.append((c0, -slope, slope * mean - c0 * one / n))
        two_all, one_all = two_all + two, one_all + one
    return out, jnp.concatenate([two_all, one_all], axis=0)


def wide(v):
    return jnp.concatenate([v, v], axis=1)


def coef(tab, g, k, lo, rows):
    return wide(tab[g, k, lo : lo + rows, :])


def silu(w):
    return w * (1.0 + jnp.tanh(w))


def silu_and_slope(w):
    p = 1.0 + jnp.tanh(w)
    o = w * p
    return o, p + o * (2.0 - p)


def taps(x, dst, rows, sign, at=0):
    cell = lax.broadcasted_iota(jnp.int32, (1, CELLS), 1)
    row, col = cell >> 4, cell & 15
    for k in range(9):
        di, dl = sign * (k // 3 - 1), sign * (k % 3 - 1)
        step = SIDE * di + dl
        if step == 0:
            dst[k * rows : (k + 1) * rows, at : at + CELLS] = x.astype(BF16)
            continue
        moved = pltpu.roll(x, (-step) % CELLS, 1)
        ok = (row + di >= 0) & (row + di < SIDE) & (col + dl >= 0) & (col + dl < SIDE)
        dst[k * rows : (k + 1) * rows, at : at + CELLS] = jnp.where(ok, moved, 0.0).astype(BF16)


def loop(lo, hi):
    return pl.loop(lo, hi)


def spread_lanes(at, lanes):
    row = lax.broadcasted_iota(jnp.int32, (32, lanes), 0)
    lane = lax.broadcasted_iota(jnp.int32, (32, lanes), 1)
    hit = ((lane & 31) == row) if at is None else (lane == row + at)
    return jnp.where(hit, 1.0, 0.0).astype(BF16)


def dot_tn(a, b):
    return lax.dot_general(a, b, (((0,), (0,)), ((), ())), preferred_element_type=F32)


def turned(v):
    return jnp.transpose(v.astype(F32)).astype(BF16)


def four(pair):
    return dot(pair, spread_lanes(None, 128))


def first_weights(lateral, squeeze, wa):
    wa[...] = jnp.zeros_like(wa)
    for k in range(5):
        wa[0:256, 128 * k : 128 * (k + 1)] = lateral[k]
    for f in range(4):
        for j in range(3):
            wa[256 + 32 * f : 288 + 32 * f, 128 * (f + 1 + j) : 128 * (f + 2 + j)] = squeeze[j]


def more_weights(reducer, spatial, expand, lateral, squeeze, narrow, widening, ws, wn, ww, wrt, wst, wet, wwt, wnt, wf, wp, tall):
    lane = lax.broadcasted_iota(jnp.int32, (1, 128), 1) >> 5
    row = lax.broadcasted_iota(jnp.int32, (128, 1), 0) >> 5
    every = spread_lanes(None, 128)
    for k in range(9):
        cols = slice(256 * k, 256 * (k + 1))
        ws[:, cols] = spatial[k]
        wst[:, cols] = turned(spatial[k])
        there, back = dot(narrow[k], every), dot_tn(narrow[k], every)
        for f in range(4):
            at = slice(32 * f, 32 * (f + 1))
            wn[at, 128 * k : 128 * (k + 1)] = jnp.where(lane == f, there, 0.0).astype(BF16)
            wnt[at, 128 * k : 128 * (k + 1)] = jnp.where(lane == f, back, 0.0).astype(BF16)
    wide_w = dot(widening[...], every)
    tall_w = lax.dot_general(every, widening[...], (((0,), (1,)), ((), ())), preferred_element_type=F32)
    tall[...] = tall_w.astype(BF16)
    for f in range(4):
        ww[128 * f : 128 * (f + 1), :] = jnp.where(lane == f, wide_w, 0.0).astype(BF16)
        wwt[:, 128 * f : 128 * (f + 1)] = jnp.where(row == f, tall_w, 0.0).astype(BF16)
    for q in range(4):
        wet[:, 256 * q : 256 * (q + 1)] = turned(expand[256 * q : 256 * (q + 1), :])
    for j in range(3):
        for q in range(5):
            wrt[256 * q : 256 * (q + 1), 256 * j : 256 * (j + 1)] = turned(
                reducer[256 * j : 256 * (j + 1), 256 * q : 256 * (q + 1)]
            )
    wf[...] = jnp.zeros_like(wf)
    for f, k in ((0, 2), (1, 3), (2, 4)):
        wf[128 * f : 128 * (f + 1), 0:256] = turned(lateral[k])
    place = (0, 2, 3, 4, 5)
    for f in range(4):
        wf[128 * f : 128 * (f + 1), 256:512] = sum(
            dot_tn(squeeze[j], spread_lanes(32 * place[f + 2 - j], 256)) for j in range(3) if f + 2 - j < 5
        ).astype(BF16)
    wp[...] = jnp.zeros_like(wp)
    for f in range(2):
        wp[128 * f : 128 * (f + 1), 0:256] = turned(lateral[f])
    wp[128:256, 256:384] = dot_tn(squeeze[0], spread_lanes(0, 128)).astype(BF16)


class Tree:
    def __init__(self, na, nb, half):
        self.na, self.nb, self.half = na, nb, half
        self.a, self.b = lax.axis_index("clip"), lax.axis_index("tm")
        self.bits = [i for i in range(1, 16) if (1 << i) < na]
        self.order = (self.bits, self.bits[::-1])
        self.h = lax.rem(self.a, 2)
        self.at, self.count, self.pending = [0, half // 2], half // 2, []

    def peer(self, bit):
        step = 1 << bit
        mine = lax.rem(self.a // step, 2)
        return (self.a + step * (1 - 2 * mine), self.b), mine

    def rows(self, start, count):
        return pl.ds(pl.multiple_of(start, 8), count)

    def copy(self, src, dst, ss, rs, peer):
        return pltpu.make_async_remote_copy(
            src, dst, ss, rs, device_id=peer, device_id_type=MESH
        )

    def descend(self):
        for n in range(len(self.bits)):
            self.count //= 2
            for p in range(2):
                self.at[p] = self.at[p] + self.peer(self.order[p][n])[1] * self.count
        self.piece = self.count // self.nb


class Reduce(Tree):
    def __init__(self, na, nb, own, stage, rc, rx, sems):
        super().__init__(na, nb, own.shape[0])
        self.own, self.stage, self.rc, self.rx = own, stage, rc, rx
        self.cs, self.cr, self.ss, self.sr, self.zs, self.zr = sems
        self.first_copies = []

    def first(self, block_of, j, chunks):
        self.chunks = chunks
        size = self.half // chunks
        peer, _ = self.peer(0)
        rows = slice(j * size, (j + 1) * size)
        for i in range(j * size // 256, (j + 1) * size // 256):
            at = slice(256 * i, 256 * (i + 1))
            for mine in range(2):

                @pl.when(self.h == mine)
                def _():
                    self.own[at, :] = block_of(mine, i)
                    self.stage[at, :] = block_of(1 - mine, i).astype(BF16)

        c = self.copy(self.stage.at[rows], self.rc.at[rows], self.cs.at[j], self.cr.at[j], peer)
        c.start()
        self.first_copies.append(c)

    def first_done(self):
        size = self.half // self.chunks
        for j, c in enumerate(self.first_copies):
            c.wait()

            @pl.loop(j * size // 256, (j + 1) * size // 256)
            def _(i):
                at = pl.ds(pl.multiple_of(i * 256, 256), 256)
                self.own[at, :] = self.own[at, :] + self.rc[at, :].astype(F32)

        self.base = 0

    def cast(self, start, count):
        step = min(count, 256)

        @pl.loop(0, count // step)
        def _(i):
            at = self.rows(start + i * step, step)
            self.rc[at, :] = self.own[at, :].astype(BF16)

    def halve(self, n):
        half = self.count // 2
        self.pending = []
        for p in range(2):
            peer, mine = self.peer(self.order[p][n])
            away = self.at[p] + (1 - mine) * half
            self.at[p] = self.at[p] + mine * half
            self.cast(away, half)
            c = self.copy(
                self.rc.at[self.rows(away, half)], self.rx.at[p, self.base : self.base + half],
                self.ss.at[p, n], self.sr.at[p, n], peer,
            )
            c.start()
            self.pending.append(c)
        self.count = half

    def halved(self):
        half = self.count
        step = min(half, 256)
        for p in range(2):
            self.pending[p].wait()

            @pl.loop(0, half // step)
            def _(i):
                at = self.rows(self.at[p] + i * step, step)
                got = self.rx[p, self.rows(self.base + i * step, step), :]
                self.own[at, :] = self.own[at, :] + got.astype(F32)

        self.base += half

    def along(self):
        self.piece = self.count // self.nb
        self.pending = [[], []]
        for p in range(2):
            self.cast(self.at[p], self.count)
            for d in range(1, self.nb):
                to = lax.rem(self.b + d, self.nb)
                c = self.copy(
                    self.rc.at[self.rows(self.at[p] + to * self.piece, self.piece)],
                    self.rx.at[p, self.rows(self.base + self.b * self.piece, self.piece)],
                    self.zs.at[p, d - 1], self.zr.at[p, d - 1], (self.a, to),
                )
                c.start()
                self.pending[p].append(c)

    def summed(self, put):
        for p in range(2):
            for c in self.pending[p]:
                c.wait()
            start = self.at[p] + self.b * self.piece
            total = self.own[self.rows(start, self.piece), :]
            for d in range(1, self.nb):
                source = lax.rem(self.b + d, self.nb)
                total = total + self.rx[
                    p, self.rows(self.base + source * self.piece, self.piece), :
                ].astype(F32)
            put(p, total.astype(BF16))


class Gather(Tree):
    def __init__(self, na, nb, out, sems):
        super().__init__(na, nb, out.shape[0] // 2)
        self.out = out
        self.gs, self.gr, self.hs, self.hr, self.ks, self.kr = sems
        self.descend()

    def place(self, start):
        return self.h * self.half + start

    def put(self, p, piece):
        at = self.rows(self.place(self.at[p] + self.b * self.piece), self.piece)
        self.out[at, :] = piece
        for d in range(1, self.nb):
            c = self.copy(
                self.out.at[at], self.out.at[at], self.gs.at[p, d - 1], self.gr.at[p, d - 1],
                (self.a, lax.rem(self.b + d, self.nb)),
            )
            c.start()
            self.pending.append(c)

    def settle(self):
        pending, self.pending = self.pending, []
        for c in pending:
            c.wait()

    def gather(self, n):
        self.settle()
        for p in range(2):
            peer, mine = self.peer(self.order[p][n])
            at = self.rows(self.place(self.at[p]), self.count)
            c = self.copy(self.out.at[at], self.out.at[at], self.hs.at[p, n], self.hr.at[p, n], peer)
            c.start()
            self.pending.append(c)
            self.at[p] = self.at[p] - mine * self.count
        self.count *= 2

    def final(self):
        pending, self.pending = self.pending, []
        peer, _ = self.peer(0)
        for p in range(2):
            pending[p].wait()
            at = self.rows(self.place(self.at[p]), self.count)
            c = self.copy(self.out.at[at], self.out.at[at], self.ks.at[p], self.kr.at[p], peer)
            c.start()
            self.pending.append(c)


def reduce_sems(na, nb, chunks):
    dma = pltpu.SemaphoreType.DMA
    shapes = [(chunks,), (2, max(1, na.bit_length() - 2)), (2, nb - 1)]
    return [dma(shape) for shape in shapes for _ in range(2)]


def gather_sems(na, nb):
    dma = pltpu.SemaphoreType.DMA
    shapes = [(2, nb - 1), (2, max(1, na.bit_length() - 2)), (2,)]
    return [dma(shape) for shape in shapes for _ in range(2)]


def forward(na, nb, refs):
    r = refs
    grp = r.grp
    nc = r.fast.shape[0]
    pairs = nc // 2
    p = Peers(na, nb)
    b = p.b
    own = Move(r.fast, r.xe.at[:, 256:768], r.s_own)
    own.start_all(nc)
    raw = [
        pltpu.make_async_copy(src, dst, r.s_raw.at[i])
        for i, (src, dst) in enumerate(((r.reducer, r.wr), (r.spatial, r.sp), (r.expand, r.we)))
    ]
    for c in raw:
        c.start()
    xfeed = Feed(r.slow, r.xbuf, r.s_x, nc)
    xfeed.prime()
    up = Halo(p, 1, lambda c: r.fast.at[c, 256:512], lambda c: r.xe.at[c, 0:256], r.h1us, r.h1ur)
    down = Halo(p, -1, lambda c: r.fast.at[c, 0:128], lambda c: r.xe.at[c, 768:896], r.h1ds, r.h1dr)
    saves = {
        k: Move(getattr(r, k), getattr(r, k + "_o"), getattr(r, "s_" + k))
        for k in ("xe", "y1", "act1", "y2", "act2", "y3", "acts")
    }

    @pl.when(b == 0)
    def _():
        r.xe[:, 0:256, :] = jnp.zeros((nc, 256, CELLS), BF16)
        r.ru[...] = jnp.zeros_like(r.ru)

    @pl.when(b == nb - 1)
    def _():
        r.xe[:, 768:896, :] = jnp.zeros((nc, 128, CELLS), BF16)
        r.rd[...] = jnp.zeros_like(r.rd)

    p.greet()

    @loop(0, nc)
    def _(c):
        up.start(c)
        down.start(c)

    counts = counts_row(grp)
    acc = r.acc
    acc[...] = jnp.zeros_like(acc)
    first_weights(r.lateral, r.squeeze, r.wa)
    for c in raw:
        c.wait()
    more_weights(
        r.wr, r.sp, r.we, r.lateral, r.squeeze, r.narrow, r.widening,
        r.ws, r.wn, r.ww, r.wrt, r.wst, r.wet, r.wwt, r.wnt, r.wf, r.wp, r.tall,
    )
    wsaves = [
        pltpu.make_async_copy(getattr(r, k), getattr(r, k + "_o"), r.s_w.at[i])
        for i, k in enumerate(("wrt", "wst", "wet", "wwt", "wnt", "wf", "wp", "ww"))
    ]
    for c in wsaves:
        c.start()

    @loop(0, nc)
    def _(c):
        own.wait(c)
        up.arrive(c)
        down.arrive(c)
        saves["xe"].start(c)
        g = grp[c]
        m = mask_of(g)
        for lo in range(0, 384, 128):
            y = dot(r.wa[lo : lo + 128, :], r.xe[c])
            r.y1[c, lo : lo + 128, :] = y
            ym = y * m
            add_stats(acc, lo, 128, ym, ym * y, g)
        saves["y1"].start(c)

    s = Sum(p, r.ar1)
    s.start(rows_of(acc, 0, 384), counts)
    s.middle()
    up.sent(nc)
    down.sent(nc)
    t1 = s.finish()
    r.tot1[...] = t1

    tab = r.tab
    acc[0:384, :] = jnp.zeros((384, 128), F32)
    fill_tables(tab, 0, forward_rows(t1[:, :256], t1, 1, r.nl[...].astype(F32)))
    fill_tables(tab, 256, forward_rows(fold_frames(t1[:, 256:]), t1, 4, four(r.nq[...])))
    up = Halo(p, 1, lambda c: r.su.at[c], lambda c: r.ru.at[c], r.h2us, r.h2ur)
    down = Halo(p, -1, lambda c: r.sd.at[c], lambda c: r.rd.at[c], r.h2ds, r.h2dr)

    @loop(0, nc)
    def _(c):
        g = grp[c]
        m = mask_of(g)
        for lo in range(0, 256, 128):
            u = r.y1[c, lo : lo + 128, :] * coef(tab, g, 0, lo, 128) + coef(tab, g, 1, lo, 128)
            r.act1[c, lo : lo + 128, :] = (silu(u) * m).astype(BF16)
        slot = xfeed.take(c)
        for j, dst in enumerate((r.su, r.sd, r.y2)):
            for lo in range(0, 256, 128):
                r0 = 256 * (0, 2, 1)[j] + lo
                v = dot(r.wr[r0 : r0 + 128, :1024], r.xbuf[slot]) + dot(
                    r.wr[r0 : r0 + 128, 1024:], r.act1[c, 0:256, :]
                )
                dst[c, lo : lo + 128, :] = v.astype(dst.dtype)
        up.start(c)
        down.start(c)

    @loop(0, nc)
    def _(c):
        g = grp[c]
        m = mask_of(g)
        u = r.y1[c, 256:384, :] * coef(tab, g, 0, 256, 128) + coef(tab, g, 1, 256, 128)
        act = silu(u) * m
        r.act1[c, 256:384, :] = act.astype(BF16)
        saves["act1"].start(c)
        taps(act, r.x9, 128, 1)
        y = dot(r.wn[...], r.x9[0:1152, 0:CELLS])
        r.y2[c, 256:384, :] = y
        ym = y * m
        add_stats(acc, 256, 128, ym, ym * y, g)

    @loop(0, nc)
    def _(c):
        up.arrive(c)
        down.arrive(c)
        g = grp[c]
        m = mask_of(g)
        for lo in range(0, 256, 128):
            y = (
                r.y2[c, lo : lo + 128, :]
                + r.ru[c, lo : lo + 128, :].astype(F32)
                + r.rd[c, lo : lo + 128, :].astype(F32)
            )
            r.y2[c, lo : lo + 128, :] = y
            ym = y * m
            add_stats(acc, lo, 128, ym, ym * y, g)
        saves["y2"].start(c)

    s = Sum(p, r.ar2)
    s.start(rows_of(acc, 0, 384), counts)
    s.middle()
    up.sent(nc)
    down.sent(nc)
    t2 = s.finish()
    r.tot2[...] = t2

    acc[0:384, :] = jnp.zeros((384, 128), F32)
    r.gram[...] = jnp.zeros_like(r.gram)
    fill_tables(tab, 0, forward_rows(t2[:, :256], t2, 1, r.nr[...].astype(F32)))
    fill_tables(tab, 256, forward_rows(fold_frames(t2[:, 256:]), t2, 4, four(r.nn[...])))

    @loop(0, pairs)
    def _(i):
        for h in range(2):
            c = 2 * i + h
            g = grp[c]
            m = mask_of(g)
            u = r.y2[c, 0:256, :] * coef(tab, g, 0, 0, 256) + coef(tab, g, 1, 0, 256)
            act = silu(u) * m
            r.act2[c, 0:256, :] = act.astype(BF16)
            taps(act, r.x9, 256, 1, h * CELLS)
            u = r.y2[c, 256:384, :] * coef(tab, g, 0, 256, 128) + coef(tab, g, 1, 256, 128)
            act = (silu(u) * m).astype(BF16)
            r.act2[c, 256:384, :] = act
            saves["act2"].start(c)
            add_sums(acc, 256, 128, act.astype(F32), g)
            add_gram(r.gram, act, g)
        for lo in range(0, 256, 128):
            both = dot(r.ws[lo : lo + 128, :], r.x9[...])
            for h in range(2):
                c = 2 * i + h
                g = grp[c]
                y = both[:, h * CELLS : (h + 1) * CELLS]
                r.y3[c, lo : lo + 128, :] = y
                ym = y * mask_of(g)
                add_stats(acc, lo, 128, ym, ym * y, g)
        for h in range(2):
            saves["y3"].start(2 * i + h)

    s = Sum(p, r.ar3)
    s.start(jnp.concatenate([rows_of(acc, 0, 256), wide_sums(acc, r.gram, r.tall[...])], axis=1), counts)
    s.middle()
    t3 = s.finish()
    r.tot3[...] = t3

    ffeed = Feed(r.fcot, r.fcbuf, r.s_fc, nc)
    ffeed.prime()
    fdrain = Drain(r.fobuf, r.fout, r.s_fo, nc)
    wdrain = Drain(r.dzwb, r.dzw_o, r.s_dzw, nc)
    acc[...] = jnp.zeros_like(acc)
    fill_tables(tab, 0, forward_rows(t3[:, :256], t3, 1, r.ns[...].astype(F32)))
    fill_tables(
        r.tabw, 0,
        forward_rows(repeated(t3[:, 256:]), t3, 4, jnp.concatenate([r.nw[...].astype(F32)] * 4, axis=1)),
    )

    @loop(0, pairs)
    def _(i):
        for h in range(2):
            c = 2 * i + h
            g = grp[c]
            m = mask_of(g)
            for lo in range(0, 256, 128):
                u = r.y3[c, lo : lo + 128, :] * coef(tab, g, 0, lo, 128) + coef(tab, g, 1, lo, 128)
                r.acts[c, lo : lo + 128, :] = (silu(u) * m).astype(BF16)
            saves["acts"].start(c)
        act = jnp.concatenate([r.acts[2 * i], r.acts[2 * i + 1]], axis=1)
        for lo in range(0, 1024, 128):
            both = dot(r.we[lo : lo + 128, :], act)
            for h in range(2):
                g = grp[2 * i + h]
                y = both[:, h * CELLS : (h + 1) * CELLS]
                ym = y * mask_of(g)
                add_stats(acc, lo, 128, ym, ym * y, g)

    def fast_ends(lo_c, hi_c):
        @loop(lo_c, hi_c)
        def _(c):
            g = grp[c]
            m = mask_of(g)
            slot = ffeed.take(c)
            fdrain.room(c)
            wdrain.room(c)
            for lo in range(0, 512, 128):
                y = dot(r.ww[lo : lo + 128, :], r.act2[c, 256:384, :])
                v = y * coef(r.tabw, g, 0, lo, 128) + coef(r.tabw, g, 1, lo, 128)
                v = v + 0.5 * r.xe[c, 256 + lo : 384 + lo, :].astype(F32)
                o, slope = silu_and_slope(v)
                r.fobuf[slot, lo : lo + 128, :] = (o * m).astype(BF16)
                dz = r.fcbuf[slot, lo : lo + 128, :].astype(F32) * (0.5 * m) * slope
                r.dzwb[slot, lo : lo + 128, :] = dz
                add_stats(acc, 1024 + lo, 128, dz, dz * y, g)
            fdrain.put(c)
            wdrain.put(c)

    s = Sum(p, r.ar4)
    s.start(rows_of(acc, 0, 1024), counts)
    fast_ends(0, nc // 2)
    s.middle()
    fast_ends(nc // 2, nc)
    t4 = s.finish()
    r.tot4[...] = t4

    r.accf[...] = acc[1024:1536, :]
    for k in saves:
        saves[k].wait_all(nc)
    for c in wsaves:
        c.wait()
    fdrain.done()
    wdrain.done()


def middle(grp, acts_i, slow, scot, we, tot4, ne, sout, dze_o, acc, tab, abuf, xbuf, cbuf, obuf, dzeb, s_a, s_x, s_c, s_o, s_z):
    nc = acts_i.shape[0]
    feeds = [Feed(src, buf, sem, nc) for src, buf, sem in ((acts_i, abuf, s_a), (slow, xbuf, s_x), (scot, cbuf, s_c))]
    drains = [Drain(obuf, sout, s_o, nc), Drain(dzeb, dze_o, s_z, nc)]
    for f in feeds:
        f.prime()
    acc[...] = jnp.zeros_like(acc)
    t4 = tot4[...]
    fill_tables(tab, 0, forward_rows(t4, t4, 1, ne[...].astype(F32)))

    @loop(0, nc)
    def _(c):
        g = grp[c]
        m = mask_of(g)
        slot = [f.take(c) for f in feeds][0]
        for d in drains:
            d.room(c)
        for lo in range(0, 1024, 128):
            y = dot(we[lo : lo + 128, :], abuf[slot])
            v = y * coef(tab, g, 0, lo, 128) + coef(tab, g, 1, lo, 128)
            v = v + 0.5 * xbuf[slot, lo : lo + 128, :].astype(F32)
            o, slope = silu_and_slope(v)
            obuf[slot, lo : lo + 128, :] = (o * m).astype(BF16)
            dz = cbuf[slot, lo : lo + 128, :].astype(F32) * (0.5 * m) * slope
            dzeb[slot, lo : lo + 128, :] = dz
            add_stats(acc, lo, 128, dz, dz * y, g)
        for d in drains:
            d.put(c)

    for d in drains:
        d.done()


def back(na, nb, refs):
    r = refs
    grp = r.grp
    nc = r.acts_i.shape[0]
    pairs = nc // 2
    p = Peers(na, nb)
    b = p.b
    zfeed = Feed(r.dze_i, r.zbuf, r.s_z, nc, 1024)
    zfeed.prime()
    loads = {
        k: Move(getattr(r, k + "_i"), getattr(r, k), getattr(r, "s_" + k))
        for k in KEPT
    }
    raw = {
        k: pltpu.make_async_copy(
            r.wrt_i.at[1024:1280] if k == "wrl" else getattr(r, k + "_i"), getattr(r, k), r.s_raw.at[i]
        )
        for i, k in enumerate(("wet", "we", "ww", "wwt", "wst", "wrl", "wnt"))
    }
    raw["we"].start()
    raw["wet"].start()
    loads["acts"].start_all(nc)
    loads["y3"].start_all(nc)
    for k in ("ww", "wwt", "wst", "wrl", "wnt"):
        raw[k].start()
    wfeed = Feed(r.dzw_i, r.wbuf, r.s_wb, nc)
    wfeed.prime()
    for k in ("act2", "y2", "act1", "y1"):
        loads[k].start_all(nc)

    def xload(i, slot):
        return pltpu.make_async_copy(r.slow.at[pl.ds(2 * i, 2)], r.xbuf.at[slot], r.s_x.at[slot])

    xload(0, 0).start()
    counts = counts_row(grp)
    acc, tab, tabb = r.acc, r.tab, r.tabb
    acc[...] = jnp.zeros_like(acc)
    t1, t2, t3, t4 = r.tot1[...], r.tot2[...], r.tot3[...], r.tot4[...]
    p.greet()
    s = Sum(p, r.ar5)
    s.start(jnp.concatenate([rows_of(r.acce, 0, 1024), folded(rows_of(r.accf, 0, 512))], axis=1), counts)

    @pl.when(b == 0)
    def _():
        r.dye[:, 512:768, :] = jnp.zeros((nc, 256, CELLS), BF16)

    @pl.when(b == nb - 1)
    def _():
        r.dye[:, 0:256, :] = jnp.zeros((nc, 256, CELLS), BF16)

    fill_tables(tabb, 0, forward_rows(t3[:, :256], t3, 1, r.ns[...].astype(F32)))
    s.middle()
    raw["we"].wait()
    raw["wet"].wait()
    t5 = s.finish()

    rows, pair = backward_rows(t4, t5[:, :1024], t4, 1, r.ne[...].astype(F32))
    fill_tables(tab, 0, rows)
    r.epair[...] = pair
    dye = r.dye2

    def dye_rows(c, lo, rows):
        return pl.ds(pl.multiple_of(c * 1024 + lo, 8), rows)

    @loop(0, nc)
    def _(c):
        g = grp[c]
        m = mask_of(g)
        loads["acts"].wait(c)
        loads["y3"].wait(c)
        slot = zfeed.take(c)
        for lo in range(0, 1024, 128):
            y = dot(r.we[lo : lo + 128, :], r.acts[c])
            z = r.zbuf[pl.ds(pl.multiple_of(slot * 1024 + lo, 8), 128), :]
            dy = z * coef(tab, g, 0, lo, 128)
            dy = dy + y * coef(tab, g, 1, lo, 128) + coef(tab, g, 2, lo, 128)
            dye[dye_rows(c, lo, 128), :] = (dy * m).astype(BF16)
        for lo in range(0, 256, 128):
            dx = dot(r.wet[lo : lo + 128, :], dye[dye_rows(c, 0, 1024), :])
            y = r.y3[c, lo : lo + 128, :]
            u = y * coef(tabb, g, 0, lo, 128) + coef(tabb, g, 1, lo, 128)
            dz = (0.5 * m) * silu_and_slope(u)[1] * dx
            r.dzs[c, lo : lo + 128, :] = dz
            add_stats(acc, lo, 128, dz, dz * y, g)

    s = Sum(p, r.ar6)
    s.start(rows_of(acc, 0, 256), counts)
    rows, pair = backward_rows(
        repeated(t3[:, 256:]), repeated(t5[:, 1024:]), t3, 4,
        jnp.concatenate([r.nw[...].astype(F32)] * 4, axis=1),
    )
    fill_tables(tab, 0, rows)
    r.wpair[...] = pair[:, :128]
    fill_tables(tabb, 256, forward_rows(fold_frames(t2[:, 256:]), t2, 4, four(r.nn[...])))
    r.wg[...] = jnp.zeros_like(r.wg)
    raw["ww"].wait()
    raw["wwt"].wait()

    def widen_back(lo_c, hi_c):
        @loop(lo_c, hi_c)
        def _(c):
            g = grp[c]
            m = mask_of(g)
            loads["act2"].wait(c)
            loads["y2"].wait(c)
            slot = wfeed.take(c)
            dx = jnp.zeros((128, CELLS), F32)
            act = r.act2[c, 256:384, :]
            for lo in range(0, 512, 128):
                y = dot(r.ww[lo : lo + 128, :], act)
                dy = r.wbuf[slot, lo : lo + 128, :] * coef(tab, g, 0, lo, 128)
                dy = dy + y * coef(tab, g, 1, lo, 128) + coef(tab, g, 2, lo, 128)
                dy = (dy * m).astype(BF16)
                dx = dx + dot(r.wwt[:, lo : lo + 128], dy)
                r.wg[lo : lo + 128, :] += dot_nt(dy, act)
            y = r.y2[c, 256:384, :]
            u = y * coef(tabb, g, 0, 256, 128) + coef(tabb, g, 1, 256, 128)
            dz = (0.5 * m) * silu_and_slope(u)[1] * dx
            r.dzn[c] = dz
            add_stats(acc, 256, 128, dz, dz * y, g)

    gg = r.gg
    gg[...] = jnp.zeros_like(gg)

    @loop(0, pairs)
    def _(i):
        act = jnp.concatenate([r.acts[2 * i + h] for h in range(2)], axis=1)
        for lo in range(0, 1024, 256):
            dy = jnp.concatenate([dye[dye_rows(2 * i + h, lo, 256), :] for h in range(2)], axis=1)
            gg[lo : lo + 256, :] += dot_nt(dy, act)

    s.middle()
    widen_back(0, nc)
    t6 = s.finish()

    acc[0:256, :] = jnp.zeros((256, 128), F32)
    rows, pair = backward_rows(t3[:, :256], t6, t3, 1, r.ns[...].astype(F32))
    fill_tables(tab, 0, rows)
    r.spair[...] = pair
    fill_tables(tabb, 0, forward_rows(t2[:, :256], t2, 1, r.nr[...].astype(F32)))
    raw["wst"].wait()

    @loop(0, pairs)
    def _(i):
        for h in range(2):
            c = 2 * i + h
            g = grp[c]
            m = mask_of(g)
            dy = r.dzs[c] * coef(tab, g, 0, 0, 256) + r.y3[c] * coef(tab, g, 1, 0, 256)
            dy = (dy + coef(tab, g, 2, 0, 256)) * m
            r.dys[c] = dy.astype(BF16)
            taps(dy, r.d9, 256, -1, h * CELLS)
        for lo in range(0, 256, 128):
            both = dot(r.wst[lo : lo + 128, :], r.d9[...])
            for h in range(2):
                c = 2 * i + h
                g = grp[c]
                dx = both[:, h * CELLS : (h + 1) * CELLS]
                y = r.y2[c, lo : lo + 128, :]
                u = y * coef(tabb, g, 0, lo, 128) + coef(tabb, g, 1, lo, 128)
                dz = (0.5 * mask_of(g)) * silu_and_slope(u)[1] * dx
                r.dzs[c, lo : lo + 128, :] = dz
                add_stats(acc, lo, 128, dz, dz * y, g)

    s = Sum(p, r.ar7)
    s.start(rows_of(acc, 0, 384), counts)
    s.middle()
    t7 = s.finish()

    acc[...] = jnp.zeros_like(acc)
    rows, pair = backward_rows(t2[:, :256], t7[:, :256], t2, 1, r.nr[...].astype(F32))
    fill_tables(tab, 0, rows)
    r.rpair[...] = pair
    dyr = r.dye
    up = Halo(p, 1, lambda c: dyr.at[c, 256:512], lambda c: dyr.at[c, 512:768], r.h3us, r.h3ur)
    down = Halo(p, -1, lambda c: dyr.at[c, 256:512], lambda c: dyr.at[c, 0:256], r.h3ds, r.h3dr)

    @loop(0, nc)
    def _(c):
        g = grp[c]
        m = mask_of(g)
        for lo in range(0, 256, 128):
            dy = r.dzs[c, lo : lo + 128, :] * coef(tab, g, 0, lo, 128)
            dy = dy + r.y2[c, lo : lo + 128, :] * coef(tab, g, 1, lo, 128)
            dy = (dy + coef(tab, g, 2, lo, 128)) * m
            dyr[c, 256 + lo : 384 + lo, :] = dy.astype(BF16)
        up.start(c)
        down.start(c)

    rows, pair = backward_rows(
        fold_frames(t2[:, 256:]), fold_frames(t7[:, 256:]), t2, 4, four(r.nn[...])
    )
    fill_tables(tab, 0, rows)
    r.npair[...] = pair
    fill_tables(tabb, 0, forward_rows(t1[:, :256], t1, 1, r.nl[...].astype(F32)))
    fill_tables(tabb, 256, forward_rows(fold_frames(t1[:, 256:]), t1, 4, four(r.nq[...])))
    r.ng[...] = jnp.zeros_like(r.ng)
    raw["wnt"].wait()
    raw["wrl"].wait()

    @loop(0, pairs)
    def _(i):
        for h in range(2):
            c = 2 * i + h
            g = grp[c]
            m = mask_of(g)
            loads["act1"].wait(c)
            loads["y1"].wait(c)
            dy = r.dzn[c] * coef(tab, g, 0, 0, 128) + r.y2[c, 256:384, :] * coef(tab, g, 1, 0, 128)
            dy = (dy + coef(tab, g, 2, 0, 128)) * m
            taps(dy, r.d9n, 128, -1)
            dx = dot(r.wnt[...], r.d9n[...])
            y = r.y1[c, 256:384, :]
            u = y * coef(tabb, g, 0, 256, 128) + coef(tabb, g, 1, 256, 128)
            dz = (0.5 * m) * silu_and_slope(u)[1] * dx
            r.y1[c, 256:384, :] = dz
            add_stats(acc, 256, 128, dz, dz * y, g)
            for lo in range(0, 1152, 384):
                r.ng[lo : lo + 384, :] += dot_nt(r.d9n[lo : lo + 384, :], r.act1[c, 256:384, :])
            taps(r.dys[c].astype(F32), r.d9, 256, -1, h * CELLS)
        act = jnp.concatenate([r.act2[2 * i + h, 0:256, :] for h in range(2)], axis=1)
        for lo in range(0, 2304, 256):
            gg[1024 + lo : 1280 + lo, :] += dot_nt(r.d9[lo : lo + 256, :], act)

    def reducer_terms(taps_of):
        @loop(0, pairs)
        def _(i):
            slot = lax.rem(i, 2)

            @pl.when(i + 1 < pairs)
            def _():
                xload(i + 1, 1 - slot).start()

            xload(i, slot).wait()
            for j in taps_of:
                dy = jnp.concatenate(
                    [dyr[2 * i + h, 256 * j : 256 * (j + 1), :] for h in range(2)], axis=1
                )
                for cb in range(5):
                    if cb < 4:
                        x = [r.xbuf[slot, h, 256 * cb : 256 * (cb + 1), :] for h in range(2)]
                    else:
                        x = [r.act1[2 * i + h, 0:256, :] for h in range(2)]
                    lo = (4608, 3328)[j] + 256 * cb
                    gg[lo : lo + 256, :] += dot_nt(dy, jnp.concatenate(x, axis=1))

    reducer_terms((1,))
    xload(0, 0).start()

    half = r.zbuf.shape[0]
    red = Reduce(
        na, nb, r.zbuf, dye.at[0:half], dye.at[half : 2 * half], r.rx, r.tail
    )
    for j in range(2):
        red.first(lambda mine, i: gg[half * mine + 256 * i : half * mine + 256 * (i + 1), :], j, 2)
    zsave = Move(r.y1, r.dz1_o, r.s_dz1)
    dsave = Move(dyr, r.dyr_o, r.s_dyr)

    def arrivals(lo_c, hi_c):
        @loop(lo_c, hi_c)
        def _(c):
            up.arrive(c)
            down.arrive(c)
            dsave.start(c)
            g = grp[c]
            m = mask_of(g)
            for lo in range(0, 256, 128):
                dx = dot(r.wrl[lo : lo + 128, :], dyr[c])
                y = r.y1[c, lo : lo + 128, :]
                u = y * coef(tabb, g, 0, lo, 128) + coef(tabb, g, 1, lo, 128)
                dz = (0.5 * m) * silu_and_slope(u)[1] * dx
                r.y1[c, lo : lo + 128, :] = dz
                add_stats(acc, lo, 128, dz, dz * y, g)
            zsave.start(c)

    stages = len(red.bits)
    cuts = [nc * (i + 1) // (stages + 2) for i in range(stages + 1)] + [nc]
    arrivals(0, cuts[0])
    red.first_done()
    for n in range(stages):
        red.halve(n)
        arrivals(cuts[n], cuts[n + 1])
        red.halved()
    arrivals(cuts[stages], nc)

    s = Sum(p, r.ar8)
    s.start(rows_of(acc, 0, 384), counts)
    red.along()
    reducer_terms((0,))
    s.middle()
    gsave = pltpu.make_async_copy(gg.at[4096:5888], r.gg_o, r.s_gg)
    gsave.start()

    def keep(q, piece):
        r.piece[q] = piece

    up.sent(nc)
    down.sent(nc)
    r.tot8[...] = s.finish()
    red.summed(keep)
    zsave.wait_all(nc)
    dsave.wait_all(nc)
    gsave.wait()


def ends(na, nb, refs):
    r = refs
    grp = r.grp
    nc = r.dz1_i.shape[0]
    p = Peers(na, nb)
    b = p.b
    tab, dyl, dyq, lg, qg = r.tab, r.dyl, r.dyq, r.lg, r.qg
    red = Reduce(na, nb, r.own, r.stage, r.rc, r.rx, r.tail[0:6])
    early, late = Gather(na, nb, r.oute, r.tail[6:12]), Gather(na, nb, r.outl, r.tail[12:18])
    dfeed = Feed(r.dz1_i, r.dbuf, r.s_d, nc)
    yfeed = Feed(r.y1_i, r.ybuf, r.s_y, nc)
    efeed = Feed(r.xe_i, r.ebuf, r.s_e, nc)
    gfeed = Feed(r.dyr_i, r.gbuf, r.s_g, nc)
    zfeed = Feed(r.dze_i, r.zbuf, r.s_z, nc)
    wfeed = Feed(r.dzw_i, r.wbuf, r.s_wb, nc)
    sdrain = Drain(r.obuf, r.sgrad, r.s_o, nc)
    fdrain = Drain(r.fbuf, r.fgrad, r.s_f, nc)
    for f in (dfeed, yfeed, efeed):
        f.prime()
    gload = pltpu.make_async_copy(r.gg_i, r.gg.at[0:1792], r.s_raw.at[0])
    pairs = nc // 2
    rload = pltpu.make_async_copy(r.wrt_i.at[0:1024], r.wr, r.s_raw.at[1])
    fload = pltpu.make_async_copy(r.wf_i, r.wf, r.s_raw.at[2])
    gload.start()
    xfeed = Feed(r.slow_i, r.xbuf, r.s_x, pairs)
    afeed = Feed(r.act1_i, r.abuf, r.s_a, pairs)
    pfeed = Feed(r.dyr2_i, r.pbuf, r.s_p, pairs)
    for f in (xfeed, afeed, pfeed, gfeed, zfeed, wfeed):
        f.prime()
    rload.start()
    fload.start()
    pload = pltpu.make_async_copy(r.wp_i, r.wp, r.s_raw.at[3])
    pload.start()
    t8, t1 = r.tot8[...], r.tot1[...]
    rows, pair = backward_rows(t1[:, :256], t8[:, :256], t1, 1, r.nl[...].astype(F32))
    fill_tables(tab, 0, rows)
    r.lpair[...] = pair
    rows, pair = backward_rows(
        fold_frames(t1[:, 256:]), fold_frames(t8[:, 256:]), t1, 4, four(r.nq[...])
    )
    fill_tables(tab, 256, rows)
    r.qpair[...] = pair
    lat = Halo(p, -1, lambda c: r.prs.at[c], lambda c: r.prr.at[c], r.hls, r.hlr)
    up = Halo(p, 1, lambda c: dyq.at[c, 160:192], lambda c: dyq.at[c, 0:32], r.hus, r.hur)
    dyq[:, 32:64, :] = jnp.zeros((nc, 32, CELLS), BF16)
    dyq[:, 192:256, :] = jnp.zeros((nc, 64, CELLS), BF16)

    @pl.when(b == 0)
    def _():
        dyq[:, 0:32, :] = jnp.zeros((nc, 32, CELLS), BF16)

    @pl.when(b == nb - 1)
    def _():
        r.prr[...] = jnp.zeros_like(r.prr)

    lg[...] = jnp.zeros_like(lg)
    qg[...] = jnp.zeros_like(qg)
    pload.wait()
    p.greet()
    for q in range(2):
        early.put(q, r.piece[q])

    ahead = nc - nc // 3

    @loop(0, nc)
    def _(c):
        g = grp[c]
        m = mask_of(g)
        slot = dfeed.take(c)
        yfeed.take(c)
        for lo in range(0, 384, 128):
            dy = r.dbuf[slot, lo : lo + 128, :] * coef(tab, g, 0, lo, 128)
            dy = dy + r.ybuf[slot, lo : lo + 128, :] * coef(tab, g, 1, lo, 128)
            dy = ((dy + coef(tab, g, 2, lo, 128)) * m).astype(BF16)
            if lo < 256:
                dyl[c, lo : lo + 128, :] = dy
            else:
                dyq[c, 64:192, :] = dy
        for lo in range(0, 256, 128):
            v = dot(r.wp[lo : lo + 128, 0:256], dyl[c]) + dot(r.wp[lo : lo + 128, 256:384], dyq[c, 64:192, :])
            r.prs[c, lo : lo + 128, :] = v.astype(BF16)

        @pl.when(c < ahead)
        def _():
            lat.start(c)

        up.start(c)
        efeed.take(c)
        dy = dyl[c, 0:256, :]
        lg[0:256, :] += dot_nt(dy, r.ebuf[slot, 0:256, :])
        lg[256:512, :] += dot_nt(dy, r.ebuf[slot, 256:512, :])
        lg[512:768, 0:128] += dot_nt(dy, r.ebuf[slot, 512:640, :])
        qg[...] += dot_nt(dyq[c, 64:192, :], r.ebuf[slot, 128:896, :])

    for j in range(3):
        lg[800 + 32 * j : 832 + 32 * j, 128:256] = sum(
            qg[32 * f : 32 * (f + 1), 128 * (f + j) : 128 * (f + j + 1)] for f in range(4)
        )
    for k in range(9):
        term = sum(
            r.ng[128 * k + 32 * f : 128 * k + 32 * (f + 1), 32 * f : 32 * (f + 1)] for f in range(4)
        )
        if k < 8:
            lg[768 + 32 * k : 800 + 32 * k, 0:32] = term
        else:
            lg[768:800, 128:160] = term
    lg[896:1024, 128:160] = sum(r.wg[128 * f : 128 * (f + 1), 32 * f : 32 * (f + 1)] for f in range(4))
    gload.wait()
    r.gg[1792:3072, :] = jnp.zeros((1280, 256), F32)

    @loop(0, pairs)
    def _(i):
        slot = xfeed.take(i)
        afeed.take(i)
        pfeed.take(i)
        dy = jnp.concatenate([r.pbuf[slot, h, 512:768, :] for h in range(2)], axis=1)
        for cb in range(5):
            if cb < 4:
                x = [r.xbuf[slot, h, 256 * cb : 256 * (cb + 1), :] for h in range(2)]
            else:
                x = [r.abuf[slot, h, 0:256, :] for h in range(2)]
            lo = 1792 + 256 * cb
            r.gg[lo : lo + 256, :] += dot_nt(dy, jnp.concatenate(x, axis=1))

    def block_of(mine, i):
        if mine == 0:
            return r.gg[256 * i : 256 * (i + 1), :]
        if i < 4:
            return r.gg[2048 + 256 * i : 2304 + 256 * i, :]
        return lg[256 * (i - 4) : 256 * (i - 3), :]

    stages = len(red.bits)
    for j in range(2):
        red.first(block_of, j, 2)
    rload.wait()

    def slow_ends(lo_c, hi_c):
        @loop(lo_c, hi_c)
        def _(c):
            m = mask_of(grp[c])
            slot = gfeed.take(c)
            zfeed.take(c)
            sdrain.room(c)
            for lo in range(0, 1024, 128):
                dx = dot(r.wr[lo : lo + 128, :], r.gbuf[slot]) + r.zbuf[slot, lo : lo + 128, :]
                r.obuf[slot, lo : lo + 128, :] = (dx * m).astype(BF16)
            sdrain.put(c)

    cuts = [nc * i // (stages + 1) for i in range(stages + 2)]
    slow_ends(cuts[0], cuts[1])
    red.first_done()
    for n in range(stages):
        red.halve(n)
        slow_ends(cuts[n + 1], cuts[n + 2])
        red.halved()
    red.along()
    fload.wait()

    def fast_ends(lo_c, hi_c):
        @loop(lo_c, hi_c)
        def _(c):
            lat.arrive(c)
            up.arrive(c)
            m = mask_of(grp[c])
            slot = wfeed.take(c)
            fdrain.room(c)
            for lo in range(0, 512, 128):
                dx = dot(r.wf[lo : lo + 128, 0:256], dyl[c]) + dot(r.wf[lo : lo + 128, 256:512], dyq[c])
                dx = dx + r.wbuf[slot, lo : lo + 128, :]
                if lo >= 256:
                    dx = dx + r.prr[c, lo - 256 : lo - 128, :].astype(F32)
                r.fbuf[slot, lo : lo + 128, :] = (dx * m).astype(BF16)
            fdrain.put(c)

    early.gather(stages - 1)
    red.summed(late.put)

    @loop(ahead, nc)
    def _(c):
        lat.start(c)

    cuts = [ahead * i // (2 * stages) for i in range(2 * stages + 1)]
    for n in range(stages):
        fast_ends(cuts[2 * n], cuts[2 * n + 1])
        late.gather(stages - 1 - n)
        fast_ends(cuts[2 * n + 1], cuts[2 * n + 2])
        if n + 1 < stages:
            early.gather(stages - 2 - n)
    early.final()
    late.final()
    fast_ends(ahead, nc)
    sdrain.done()
    fdrain.done()
    lat.sent(nc)
    up.sent(nc)
    early.settle()
    late.settle()


def last(oe_i, ol_i, rp, spr, ep, lp, qp, np_, wp, *refs):
    big, grads, small, big_out = refs[:3], refs[3:10], refs[10:17], refs[17:20]
    bufs, made, (oe, ol, sem_in, sem_out, sem_a, sem_b) = refs[20:23], refs[23:30], refs[30:]
    nc = big[0].shape[0]
    rg, sg, eg, lg, qg, ng, wg = made

    def take(i, c):
        return pltpu.make_async_copy(big[i].at[c], bufs[i].at[c], sem_in.at[i, c])

    def give(i, c):
        return pltpu.make_async_copy(bufs[i].at[c], big_out[i].at[c], sem_out.at[i, c])

    def pass_on(i):
        @loop(0, nc)
        def _(c):
            take(i, c).wait()
            give(i, c).start()

    def hand(i):
        return pltpu.make_async_copy(made[i], grads[i], sem_b.at[i])

    ends_in = [pltpu.make_async_copy(s, d, sem_a.at[i]) for i, (s, d) in enumerate(((oe_i, oe), (ol_i, ol)))]
    for c in ends_in:
        c.start()
    for i in range(3):

        @loop(0, nc)
        def _(c):
            take(i, c).start()

    for c in ends_in:
        c.wait()
    for cb in range(5):
        for j in range(3):
            lo = (512, 3328, 1792)[j] + 256 * cb
            src = ol if j != 1 else oe
            if j == 1 and cb >= 3:
                src, lo = ol, 256 * (cb - 3)
            rg[j, :, 256 * cb : 256 * (cb + 1)] = src[lo : lo + 256, :].astype(F32)
    hand(0).start()
    pass_on(0)
    for k in range(9):
        sg[k] = oe[1024 + 256 * k : 1280 + 256 * k, :].astype(F32)
        at = 3840 + 32 * k if k < 8 else 3840
        ng[k] = (ol[at : at + 32, 0:32] if k < 8 else ol[at : at + 32, 128:160]).astype(F32)
    hand(1).start()
    hand(5).start()
    pass_on(1)
    for q in range(4):
        eg[256 * q : 256 * (q + 1), :] = oe[256 * q : 256 * (q + 1), :].astype(F32)
    for k in range(5):
        lo = 3072 + 256 * (k // 2)
        lg[k] = ol[lo : lo + 256, 128 * (k % 2) : 128 * (k % 2 + 1)].astype(F32)
    for j in range(3):
        qg[j] = ol[3872 + 32 * j : 3904 + 32 * j, 128:256].astype(F32)
    wg[...] = ol[3968:4096, 128:160].astype(F32)
    for i in (2, 3, 4, 6):
        hand(i).start()
    pass_on(2)
    rpo, spo, epo, lpo, qpo, npo, wpo = small
    for src, dst in ((rp, rpo), (spr, spo), (ep, epo), (lp, lpo), (wp, wpo)):
        dst[...] = src[...]
    qpo[...] = qp[:, 0:32]
    npo[...] = np_[:, 0:32]
    for i in range(7):
        hand(i).wait()

    @loop(0, nc)
    def _(c):
        for i in range(3):
            give(i, c).wait()


def sds(shape, dtype):
    return jax.ShapeDtypeStruct(shape, dtype)


class Refs:
    pass


V, H, S = VM, pl.ANY, pltpu.SMEM


def call(body, na, nb, cid, ins, outs, scratch, sums, tail=()):
    names = [*ins, *outs, *scratch]
    shapes = [*scratch.values()]
    for width in sums.values():
        shapes += ar_scratch(na, nb, width)
    shapes += list(tail)

    def kernel(*refs):
        r = Refs()
        for name, ref in zip(names, refs):
            setattr(r, name, ref)
        at = len(names)
        for name in sums:
            setattr(r, name, refs[at : at + 8])
            at += 8
        r.tail = refs[at:]
        body(na, nb, r)

    got = pl.pallas_call(
        kernel,
        name=body.__name__,
        out_shape=tuple(x[1] for x in outs.values()),
        in_specs=[pl.BlockSpec(memory_space=x[0]) for x in ins.values()],
        out_specs=tuple(pl.BlockSpec(memory_space=x[0]) for x in outs.values()),
        scratch_shapes=shapes,
        compiler_params=pltpu.CompilerParams(
            collective_id=cid, has_side_effects=True, vmem_limit_bytes=LIMIT
        ),
    )(*[x[1] for x in ins.values()])
    r = Refs()
    for name, v in zip(outs, got):
        setattr(r, name, v)
    return r


def pick(source, names, end="_o"):
    return {k + "_i": (H, getattr(source, k + end)) for k in names}


def each_of(names, value, start=""):
    return {start + k: value for k in names}


KEPT = ("acts", "y3", "act2", "y2", "act1", "y1")


def build(na, nb):
    def body(
        slow_in, fast_in, clip_group, reducer, spatial, expand, lateral, squeeze, narrow, widening,
        reducer_norm, spatial_norm, expand_norm, lateral_norm, squeeze_norm, narrow_norm, widening_norm,
        slow_cot, fast_cot,
    ):
        nc = slow_in.shape[0]
        dma = pltpu.SemaphoreType.DMA
        slow = slow_in.reshape(nc, 1024, CELLS)
        first_norms = dict(nl=(V, lateral_norm), nq=(V, squeeze_norm))
        norms = first_norms | dict(
            nr=(V, reducer_norm), nn=(V, narrow_norm), ns=(V, spatial_norm), ne=(V, expand_norm), nw=(V, widening_norm)
        )

        def act(c, dtype):
            return sds((nc, c, CELLS), dtype)

        def vact(c, dtype):
            return VM((nc, c, CELLS), dtype)

        def two(c, dtype):
            return VM((2, c, CELLS), dtype)

        def tab(k, c):
            return VM((3, k, c, 128), F32)

        each, slots = dma((nc,)), dma((2,))
        state = dict(
            xe=(896, BF16), y1=(384, F32), act1=(384, BF16), y2=(384, F32), act2=(384, BF16), y3=(256, F32), acts=(256, BF16)
        )
        turns = dict(
            wrt=(1280, 768), wst=(256, 2304), wet=(256, 1024), wwt=(128, 512), wnt=(128, 1152), wf=(512, 512),
            wp=(256, 384), ww=(512, 128),
        )
        fw = call(
            forward, na, nb, 1,
            dict(
                grp=(S, clip_group), fast=(H, fast_in.reshape(nc, 512, CELLS)), slow=(H, slow),
                fcot=(H, fast_cot.reshape(nc, 512, CELLS)),
                reducer=(H, reducer.reshape(768, 1280)), spatial=(H, spatial), expand=(H, expand),
                lateral=(V, lateral), squeeze=(V, squeeze), narrow=(V, narrow), widening=(V, widening),
            ) | norms,
            dict(fout=(H, act(512, BF16)))
            | {k + "_o": (H, act(*v)) for k, v in state.items()}
            | dict(dzw_o=(H, act(512, F32)), accf=(V, sds((512, 128), F32)))
            | {k + "_o": (H, sds(v, BF16)) for k, v in turns.items()}
            | dict(
                tot1=(V, sds((8, 384), F32)), tot2=(V, sds((8, 384), F32)), tot3=(V, sds((8, 384), F32)),
                tot4=(V, sds((8, 1024), F32)),
            ),
            {k: vact(*v) for k, v in state.items()}
            | {k: VM(v, BF16) for k, v in turns.items()}
            | dict(
                wr=VM((768, 1280), BF16), sp=VM((9, 256, 256), BF16), we=VM((1024, 256), BF16),
                wa=VM((384, 896), BF16), tall=VM((128, 128), BF16), gram=VM((3, 128, 128), F32),
                ws=VM((256, 2304), BF16), wn=VM((128, 1152), BF16),
                su=vact(256, BF16), sd=vact(256, BF16), ru=vact(256, BF16), rd=vact(256, BF16),
                xbuf=two(1024, BF16), fcbuf=two(512, BF16), fobuf=two(512, BF16), dzwb=two(512, F32),
                tab=tab(2, 384), tabw=tab(2, 512), acc=VM((1536, 128), F32), x9=VM((2304, 2 * CELLS), BF16),
                s_raw=dma((3,)), s_w=dma((8,)), s_own=each,
            )
            | each_of(("h1us", "h1ur", "h1ds", "h1dr", "h2us", "h2ur", "h2ds", "h2dr"), each)
            | each_of(("x", "fc", "fo", "dzw"), slots, "s_")
            | {"s_" + k: each for k in state},
            dict(ar1=384, ar2=384, ar3=384, ar4=1024),
        )
        hbm, vmem = pl.BlockSpec(memory_space=H), pl.BlockSpec(memory_space=V)
        slow_out, dze, acce = pl.pallas_call(
            middle,
            name="middle",
            out_shape=(act(1024, BF16), act(1024, F32), sds((1024, 128), F32)),
            in_specs=[pl.BlockSpec(memory_space=S)] + [hbm] * 3 + [vmem] * 3,
            out_specs=(hbm, hbm, vmem),
            scratch_shapes=[
                tab(2, 1024), two(256, BF16), two(1024, BF16), two(1024, BF16), two(1024, BF16), two(1024, F32)
            ]
            + [slots] * 5,
            compiler_params=pltpu.CompilerParams(vmem_limit_bytes=LIMIT),
        )(clip_group, fw.acts_o, slow, slow_cot.reshape(nc, 1024, CELLS), expand, fw.tot4, expand_norm)
        half = 2048
        piece = half // (na * nb)
        tots = dict(
            tot1=(V, fw.tot1), tot2=(V, fw.tot2), tot3=(V, fw.tot3), tot4=(V, fw.tot4)
        )
        bw = call(
            back, na, nb, 2,
            dict(
                grp=(S, clip_group), slow=(H, slow), we_i=(H, expand), dze_i=(H, dze), acce=(V, acce), accf=(V, fw.accf)
            )
            | pick(fw, KEPT + ("dzw", "wet", "wwt", "wst", "wrt", "wnt", "ww")) | tots | norms,
            dict(
                dz1_o=(H, act(384, F32)), dyr_o=(H, act(768, BF16)), gg_o=(H, sds((1792, 256), F32)),
                piece=(V, sds((2, piece, 256), BF16)),
                ng=(V, sds((1152, 128), F32)), wg=(V, sds((512, 128), F32)), tot8=(V, sds((8, 384), F32)),
                epair=(V, sds((2, 1024), F32)), spair=(V, sds((2, 256), F32)), rpair=(V, sds((2, 256), F32)),
                wpair=(V, sds((2, 128), F32)), npair=(V, sds((2, 128), F32)),
            ),
            {k: vact(*state[k]) for k in KEPT}
            | dict(
                wet=VM((256, 1024), BF16), we=VM((1024, 256), BF16), ww=VM((512, 128), BF16),
                wwt=VM((128, 512), BF16), wst=VM((256, 2304), BF16), wrl=VM((256, 768), BF16), wnt=VM((128, 1152), BF16),
                zbuf=VM((half, CELLS), F32), wbuf=two(512, F32), xbuf=VM((2, 2, 1024, CELLS), BF16),
                dye=vact(768, BF16), dye2=VM((nc * 1024, CELLS), BF16), rx=VM((2, half // 2, 256), BF16),
                dzs=vact(256, F32), dzn=vact(128, F32), dys=vact(256, BF16), gg=VM((5888, 256), F32),
                tab=tab(3, 1024), tabb=tab(2, 384), acc=VM((384, 128), F32),
                d9=VM((2304, 2 * CELLS), BF16), d9n=VM((1152, CELLS), BF16), s_raw=dma((7,)), s_gg=dma,
            )
            | each_of(KEPT + ("dz1", "dyr"), each, "s_")
            | each_of(("h3us", "h3ur", "h3ds", "h3dr"), each)
            | each_of(("z", "wb", "x"), slots, "s_"),
            dict(ar5=1152, ar6=256, ar7=384, ar8=384),
            reduce_sems(na, nb, 2),
        )
        en = call(
            ends, na, nb, 3,
            dict(
                grp=(S, clip_group), piece=(V, bw.piece), dze_i=(H, dze), slow_i=(H, slow.reshape(nc // 2, 2, 1024, CELLS)),
                act1_i=(H, fw.act1_o.reshape(nc // 2, 2, 384, CELLS)),
                dyr2_i=(H, bw.dyr_o.reshape(nc // 2, 2, 768, CELLS)),
                ng=(V, bw.ng), wg=(V, bw.wg), tot8=(V, bw.tot8), tot1=(V, fw.tot1),
            )
            | pick(bw, ("dz1", "dyr", "gg")) | pick(fw, ("y1", "xe", "dzw", "wrt", "wf", "wp")) | first_norms,
            dict(
                sgrad=(H, act(1024, BF16)), fgrad=(H, act(512, BF16)), oute=(V, sds((2 * half, 256), BF16)),
                outl=(V, sds((2 * half, 256), BF16)), lpair=(V, sds((2, 256), F32)), qpair=(V, sds((2, 128), F32)),
            ),
            dict(
                gg=VM((3072, 256), F32), wr=VM((1024, 768), BF16), wf=VM((512, 512), BF16), wp=VM((256, 384), BF16),
                tab=tab(3, 384), dyl=vact(256, BF16), prs=vact(256, BF16), prr=vact(256, BF16), dyq=vact(256, BF16),
                lg=VM((1024, 256), F32), qg=VM((128, 768), F32), own=VM((half, 256), F32),
                stage=VM((half, 256), BF16), rc=VM((half, 256), BF16), rx=VM((2, half // 2, 256), BF16),
                dbuf=two(384, F32), ybuf=two(384, F32), ebuf=two(896, BF16), gbuf=two(768, BF16),
                zbuf=two(1024, F32), wbuf=two(512, F32), obuf=two(1024, BF16), fbuf=two(512, BF16),
                xbuf=VM((2, 2, 1024, CELLS), BF16), abuf=VM((2, 2, 384, CELLS), BF16), pbuf=VM((2, 2, 768, CELLS), BF16),
                s_raw=dma((4,)),
            )
            | each_of(("d", "y", "e", "g", "z", "wb", "o", "f", "x", "a", "p"), slots, "s_")
            | each_of(("hls", "hlr", "hus", "hur"), each),
            {},
            reduce_sems(na, nb, 2) + gather_sems(na, nb) * 2,
        )
        shapes = [
            (3, 256, 1280), (9, 256, 256), (1024, 256), (5, 256, 128), (3, 32, 128), (9, 32, 32), (128, 32),
            (2, 256), (2, 256), (2, 1024), (2, 256), (2, 32), (2, 32), (2, 128),
        ]
        big = (fw.fout, en.sgrad, en.fgrad)
        got = pl.pallas_call(
            last,
            name="last",
            out_shape=tuple(sds(v, F32) for v in shapes) + tuple(sds(v.shape, BF16) for v in big),
            in_specs=[hbm] * 2 + [vmem] * 7 + [hbm] * 3,
            out_specs=tuple([hbm] * 7 + [vmem] * 7 + [hbm] * 3),
            scratch_shapes=[VM(v.shape, BF16) for v in big]
            + [VM(v, F32) for v in shapes[:7]]
            + [VM((2 * half, 256), BF16), VM((2 * half, 256), BF16)]
            + [dma((3, nc)), dma((3, nc)), dma((2,)), dma((7,))],
            compiler_params=pltpu.CompilerParams(vmem_limit_bytes=LIMIT),
        )(en.oute, en.outl, bw.rpair, bw.spair, bw.epair, en.lpair, en.qpair, bw.npair, bw.wpair, *big)
        fast_out, slow_grad, fast_grad = got[len(shapes) :]
        return (
            slow_out.reshape(slow_in.shape), fast_out.reshape(fast_in.shape),
            slow_grad.reshape(slow_in.shape), fast_grad.reshape(fast_in.shape),
            *got[: len(shapes)],
        )

    return body


def solution(mesh):
    body = build(mesh.shape["clip"], mesh.shape["tm"])
    big = P("clip", "tm", None, None)
    return jax.shard_map(
        body,
        mesh=mesh,
        in_specs=(big, big, P("clip")) + (P(),) * 14 + (big, big),
        out_specs=(big,) * 4 + (P(),) * 14,
        check_vma=False,
    )
```

```python
import functools

import jax
import jax.numpy as jnp
from jax import lax
from jax.experimental import pallas as pl
from jax.experimental.pallas import tpu as pltpu
from jax.sharding import PartitionSpec as P

MESH = pl.DeviceIdType.MESH
F32, BF16 = jnp.float32, jnp.bfloat16
SIDE = 16
CELLS = SIDE * SIDE
EPS = 1e-05
VM = pltpu.VMEM
LIMIT = 63 * 1024 * 1024


def dot(a, b):
    return lax.dot_general(a, b, (((1,), (0,)), ((), ())), preferred_element_type=F32)


def dot_nt(a, b):
    return lax.dot_general(a, b, (((1,), (1,)), ((), ())), preferred_element_type=F32)


def side_of(g):
    return jnp.where(g == 0, SIDE * 5 // 8, jnp.where(g == 1, SIDE * 7 // 8, SIDE))


def mask_of(g):
    cell = lax.broadcasted_iota(jnp.int32, (1, CELLS), 1)
    side = side_of(g)
    return jnp.where(((cell >> 4) < side) & ((cell & 15) < side), 1.0, 0.0).astype(F32)


def counts_row(grp):
    lane = lax.broadcasted_iota(jnp.int32, (1, 128), 1)
    total = jnp.zeros((1, 128), F32)
    for c in range(grp.shape[0]):
        side = side_of(grp[c])
        total = total + jnp.where(lane == grp[c], (side * side).astype(F32), 0.0)
    return total


def add_stats(acc, lo, rows, first, second, g):
    lane = lax.broadcasted_iota(jnp.int32, (1, 128), 1)
    one = jnp.sum(first[:, :128] + first[:, 128:], axis=1, keepdims=True)
    two = jnp.sum(second[:, :128] + second[:, 128:], axis=1, keepdims=True)
    acc[lo : lo + rows, :] += jnp.where(lane == g, one, 0.0) + jnp.where(lane == g + 3, two, 0.0)


def add_sums(acc, lo, rows, value, g):
    lane = lax.broadcasted_iota(jnp.int32, (1, 128), 1)
    one = jnp.sum(value[:, :128] + value[:, 128:], axis=1, keepdims=True)
    acc[lo : lo + rows, :] += jnp.where(lane == g, one, 0.0)


def add_gram(gram, act, g):
    term = dot_nt(act, act)
    for k in range(3):
        gram[k] += jnp.where(g == k, term, 0.0)


def wide_sums(acc, gram, tall):
    w = tall.astype(F32)
    exact = dict(precision=lax.Precision.HIGHEST, preferred_element_type=F32)
    one = jnp.dot(rows_of(acc, 256, 384), w, **exact)
    block = lax.broadcasted_iota(jnp.int32, (128, 128), 0) >> 5
    same = block == (lax.broadcasted_iota(jnp.int32, (128, 128), 1) >> 5)
    two = [
        jnp.sum(w * jnp.dot(jnp.where(same, gram[k], 0.0), w, **exact), axis=0, keepdims=True)
        for k in range(3)
    ]
    return jnp.concatenate([one[:3, :]] + two + [jnp.zeros((2, 128), F32)], axis=0)


def ar_scratch(na, nb, width):
    dma = pltpu.SemaphoreType.DMA
    return [
        VM((8, width), F32),
        VM((na, 8, width), F32),
        VM((8, width), F32),
        VM((nb, 8, width), F32),
        dma((na - 1,)),
        dma((na - 1,)),
        dma((nb - 1,)),
        dma((nb - 1,)),
    ]


class Peers:
    def __init__(self, na, nb):
        self.na, self.nb = na, nb
        self.a, self.b = lax.axis_index("clip"), lax.axis_index("tm")
        self.along_a = [(lax.rem(self.a + d, na), self.b) for d in range(1, na)]
        self.along_b = [(self.a, lax.rem(self.b + d, nb)) for d in range(1, nb)]
        self.bar = pltpu.get_barrier_semaphore()
        for peer in self.along_a + self.along_b:
            pl.semaphore_signal(self.bar, inc=1, device_id=peer, device_id_type=MESH)

    def greet(self):
        pl.semaphore_wait(self.bar, self.na - 1 + self.nb - 1)


class Sum:
    def __init__(self, peers, refs):
        self.p = peers
        self.mine, self.bufa, self.part, self.bufb, self.sa, self.ra, self.sb, self.rb = refs

    def copies(self, src, buf, slot, ss, rs, peers):
        return [
            pltpu.make_async_remote_copy(
                src, buf.at[slot], ss.at[i], rs.at[i], device_id=peer, device_id_type=MESH
            )
            for i, peer in enumerate(peers)
        ]

    def start(self, rows, counts):
        row = lax.broadcasted_iota(jnp.int32, (8, 128), 0)
        head = jnp.where(row == 6, counts, rows[:, :128])
        value = jnp.concatenate([head, rows[:, 128:]], axis=1)
        self.mine[...] = value
        self.bufa[self.p.a] = value
        self.first = self.copies(self.mine, self.bufa, self.p.a, self.sa, self.ra, self.p.along_a)
        for c in self.first:
            c.start()

    def middle(self):
        for c in self.first:
            c.wait()
        total = self.bufa[0]
        for i in range(1, self.p.na):
            total = total + self.bufa[i]
        self.part[...] = total
        self.bufb[self.p.b] = total
        self.second = self.copies(self.part, self.bufb, self.p.b, self.sb, self.rb, self.p.along_b)
        for c in self.second:
            c.start()

    def finish(self):
        for c in self.second:
            c.wait()
        total = self.bufb[0]
        for i in range(1, self.p.nb):
            total = total + self.bufb[i]
        return total


def rows_of(acc, lo, hi):
    return jnp.transpose(acc[lo:hi, :])[:8, :]


def folded(rows):
    return sum(rows[:, 128 * f : 128 * (f + 1)] for f in range(rows.shape[1] // 128))


def repeated(rows):
    return jnp.concatenate([rows] * 4, axis=1)


class Halo:
    def __init__(self, peers, step, src, dst, ss, rs):
        self.src, self.dst, self.ss, self.rs = src, dst, ss, rs
        to = peers.b + step
        self.sends = (to >= 0) & (to < peers.nb)
        source = peers.b - step
        self.gets = (source >= 0) & (source < peers.nb)
        self.peer = (peers.a, lax.rem(to + peers.nb, peers.nb))

    def copy(self, c):
        return pltpu.make_async_remote_copy(
            self.src(c), self.dst(c), self.ss.at[c], self.rs.at[c],
            device_id=self.peer, device_id_type=MESH,
        )

    def start(self, c):
        @pl.when(self.sends)
        def _():
            self.copy(c).start()

    def arrive(self, c):
        @pl.when(self.gets)
        def _():
            self.copy(c).wait_recv()

    def sent(self, nc):
        @pl.when(self.sends)
        def _():
            @pl.loop(0, nc)
            def _(c):
                self.copy(c).wait_send()


class Move:
    def __init__(self, src, dst, sem):
        self.src, self.dst, self.sem = src, dst, sem

    def copy(self, c):
        return pltpu.make_async_copy(self.src.at[c], self.dst.at[c], self.sem.at[c])

    def start(self, c):
        self.copy(c).start()

    def wait(self, c):
        self.copy(c).wait()

    def start_all(self, nc):
        @pl.loop(0, nc)
        def _(c):
            self.start(c)

    def wait_all(self, nc):
        @pl.loop(0, nc)
        def _(c):
            self.wait(c)


class Feed:
    def __init__(self, src, buf, sem, nc, rows=0):
        self.src, self.buf, self.sem, self.nc, self.rows = src, buf, sem, nc, rows

    def copy(self, c, slot):
        at = pl.ds(pl.multiple_of(slot * self.rows, 8), self.rows) if self.rows else slot
        return pltpu.make_async_copy(self.src.at[c], self.buf.at[at], self.sem.at[slot])

    def prime(self):
        self.copy(0, 0).start()

    def take(self, c):
        slot = lax.rem(c, 2)

        @pl.when(c + 1 < self.nc)
        def _():
            self.copy(c + 1, 1 - slot).start()

        self.copy(c, slot).wait()
        return slot


class Drain:
    def __init__(self, buf, dst, sem, nc):
        self.buf, self.dst, self.sem, self.nc = buf, dst, sem, nc

    def copy(self, c, slot):
        return pltpu.make_async_copy(self.buf.at[slot], self.dst.at[c], self.sem.at[slot])

    def room(self, c):
        slot = lax.rem(c, 2)

        @pl.when(c >= 2)
        def _():
            self.copy(c - 2, slot).wait()

        return slot

    def put(self, c):
        self.copy(c, lax.rem(c, 2)).start()

    def done(self):
        for c in range(max(0, self.nc - 2), self.nc):
            self.copy(c, c % 2).wait()


def fold_frames(total):
    out = total + pltpu.roll(total, 32, 1)
    return out + pltpu.roll(out, 64, 1)


def moments(total, counts, frames):
    out = []
    for g in range(3):
        n = counts[6:7, g : g + 1] * float(frames)
        mean = total[g : g + 1, :] / n
        var = total[g + 3 : g + 4, :] / n - mean * mean
        out.append((n, mean, lax.rsqrt(var + EPS)))
    return out


def fill_tables(tab, base, rows_list):
    width = rows_list[0][0].shape[1]
    count = len(rows_list[0])
    rows = [rows_list[g][k] for g in range(3) for k in range(count)]
    rows = rows + [jnp.zeros((1, width), F32)] * (128 - len(rows))
    cols = jnp.transpose(jnp.concatenate(rows, axis=0))
    for g in range(3):
        for k in range(count):
            i = g * count + k
            tab[g, k, base : base + width, :] = jnp.broadcast_to(cols[:, i : i + 1], (width, 128))


def forward_rows(total, counts, frames, pair):
    out = []
    for n, mean, r in moments(total, counts, frames):
        gain = 0.5 * (pair[0:1, :] * r)
        out.append((gain, 0.5 * pair[1:2, :] - mean * gain))
    return out


def backward_rows(total, grads, counts, frames, pair):
    out, two_all, one_all = [], 0.0, 0.0
    for g, (n, mean, r) in enumerate(moments(total, counts, frames)):
        one = grads[g : g + 1, :]
        two = r * (grads[g + 3 : g + 4, :] - mean * one)
        c0 = pair[0:1, :] * r
        slope = c0 * r * two / n
        out.append((c0, -slope, slope * mean - c0 * one / n))
        two_all, one_all = two_all + two, one_all + one
    return out, jnp.concatenate([two_all, one_all], axis=0)


def wide(v):
    return jnp.concatenate([v, v], axis=1)


def coef(tab, g, k, lo, rows):
    return wide(tab[g, k, lo : lo + rows, :])


def silu(w):
    return w * (1.0 + jnp.tanh(w))


def silu_and_slope(w):
    p = 1.0 + jnp.tanh(w)
    o = w * p
    return o, p + o * (2.0 - p)


def taps(x, dst, rows, sign, at=0):
    cell = lax.broadcasted_iota(jnp.int32, (1, CELLS), 1)
    row, col = cell >> 4, cell & 15
    for k in range(9):
        di, dl = sign * (k // 3 - 1), sign * (k % 3 - 1)
        step = SIDE * di + dl
        if step == 0:
            dst[k * rows : (k + 1) * rows, at : at + CELLS] = x.astype(BF16)
            continue
        moved = pltpu.roll(x, (-step) % CELLS, 1)
        ok = (row + di >= 0) & (row + di < SIDE) & (col + dl >= 0) & (col + dl < SIDE)
        dst[k * rows : (k + 1) * rows, at : at + CELLS] = jnp.where(ok, moved, 0.0).astype(BF16)


def loop(lo, hi):
    return pl.loop(lo, hi)


def spread_lanes(at, lanes):
    row = lax.broadcasted_iota(jnp.int32, (32, lanes), 0)
    lane = lax.broadcasted_iota(jnp.int32, (32, lanes), 1)
    hit = ((lane & 31) == row) if at is None else (lane == row + at)
    return jnp.where(hit, 1.0, 0.0).astype(BF16)


def dot_tn(a, b):
    return lax.dot_general(a, b, (((0,), (0,)), ((), ())), preferred_element_type=F32)


def turned(v):
    return jnp.transpose(v.astype(F32)).astype(BF16)


def four(pair):
    return dot(pair, spread_lanes(None, 128))


def first_weights(lateral, squeeze, wa):
    wa[...] = jnp.zeros_like(wa)
    for k in range(5):
        wa[0:256, 128 * k : 128 * (k + 1)] = lateral[k]
    for f in range(4):
        for j in range(3):
            wa[256 + 32 * f : 288 + 32 * f, 128 * (f + 1 + j) : 128 * (f + 2 + j)] = squeeze[j]


def more_weights(reducer, spatial, expand, lateral, squeeze, narrow, widening, ws, wn, ww, wrt, wst, wet, wwt, wnt, wf, wp, tall):
    lane = lax.broadcasted_iota(jnp.int32, (1, 128), 1) >> 5
    row = lax.broadcasted_iota(jnp.int32, (128, 1), 0) >> 5
    every = spread_lanes(None, 128)
    for k in range(9):
        cols = slice(256 * k, 256 * (k + 1))
        ws[:, cols] = spatial[k]
        wst[:, cols] = turned(spatial[k])
        there, back = dot(narrow[k], every), dot_tn(narrow[k], every)
        for f in range(4):
            at = slice(32 * f, 32 * (f + 1))
            wn[at, 128 * k : 128 * (k + 1)] = jnp.where(lane == f, there, 0.0).astype(BF16)
            wnt[at, 128 * k : 128 * (k + 1)] = jnp.where(lane == f, back, 0.0).astype(BF16)
    wide_w = dot_tn(widening[...], every)
    tall_w = dot_tn(every, widening[...])
    tall[...] = tall_w.astype(BF16)
    for f in range(4):
        ww[128 * f : 128 * (f + 1), :] = jnp.where(lane == f, wide_w, 0.0).astype(BF16)
        wwt[:, 128 * f : 128 * (f + 1)] = jnp.where(row == f, tall_w, 0.0).astype(BF16)
    for q in range(4):
        wet[:, 256 * q : 256 * (q + 1)] = turned(expand[256 * q : 256 * (q + 1), :])
    for j in range(3):
        for q in range(5):
            wrt[256 * q : 256 * (q + 1), 256 * j : 256 * (j + 1)] = turned(
                reducer[256 * j : 256 * (j + 1), 256 * q : 256 * (q + 1)]
            )
    wf[...] = jnp.zeros_like(wf)
    for f, k in ((0, 2), (1, 3), (2, 4)):
        wf[128 * f : 128 * (f + 1), 0:256] = turned(lateral[k])
    place = (0, 2, 3, 4, 5)
    for f in range(4):
        wf[128 * f : 128 * (f + 1), 256:512] = sum(
            dot_tn(squeeze[j], spread_lanes(32 * place[f + 2 - j], 256)) for j in range(3) if f + 2 - j < 5
        ).astype(BF16)
    wp[...] = jnp.zeros_like(wp)
    for f in range(2):
        wp[128 * f : 128 * (f + 1), 0:256] = turned(lateral[f])
    wp[128:256, 256:384] = dot_tn(squeeze[0], spread_lanes(0, 128)).astype(BF16)


class Tree:
    def __init__(self, na, nb, half):
        self.na, self.nb, self.half = na, nb, half
        self.a, self.b = lax.axis_index("clip"), lax.axis_index("tm")
        self.bits = [i for i in range(1, 16) if (1 << i) < na]
        self.order = (self.bits, self.bits[::-1])
        self.h = lax.rem(self.a, 2)
        self.at, self.count, self.pending = [0, half // 2], half // 2, []

    def peer(self, bit):
        step = 1 << bit
        mine = lax.rem(self.a // step, 2)
        return (self.a + step * (1 - 2 * mine), self.b), mine

    def rows(self, start, count):
        return pl.ds(pl.multiple_of(start, 8), count)

    def copy(self, src, dst, ss, rs, peer):
        return pltpu.make_async_remote_copy(
            src, dst, ss, rs, device_id=peer, device_id_type=MESH
        )

    def descend(self):
        for n in range(len(self.bits)):
            self.count //= 2
            for p in range(2):
                self.at[p] = self.at[p] + self.peer(self.order[p][n])[1] * self.count
        self.piece = self.count // self.nb


class Reduce(Tree):
    def __init__(self, na, nb, own, stage, rc, rx, sems):
        super().__init__(na, nb, own.shape[0])
        self.own, self.stage, self.rc, self.rx = own, stage, rc, rx
        self.cs, self.cr, self.ss, self.sr, self.zs, self.zr = sems
        self.first_copies = []

    def first(self, block_of, j, chunks):
        self.chunks = chunks
        size = self.half // chunks
        peer, _ = self.peer(0)
        rows = slice(j * size, (j + 1) * size)
        for i in range(j * size // 256, (j + 1) * size // 256):
            at = slice(256 * i, 256 * (i + 1))
            for mine in range(2):

                @pl.when(self.h == mine)
                def _():
                    self.own[at, :] = block_of(mine, i)
                    self.stage[at, :] = block_of(1 - mine, i).astype(BF16)

        c = self.copy(self.stage.at[rows], self.rc.at[rows], self.cs.at[j], self.cr.at[j], peer)
        c.start()
        self.first_copies.append(c)

    def first_done(self):
        size = self.half // self.chunks
        for j, c in enumerate(self.first_copies):
            c.wait()

            @pl.loop(j * size // 256, (j + 1) * size // 256)
            def _(i):
                at = pl.ds(pl.multiple_of(i * 256, 256), 256)
                self.own[at, :] = self.own[at, :] + self.rc[at, :].astype(F32)

        self.base = 0

    def cast(self, start, count):
        step = min(count, 256)

        @pl.loop(0, count // step)
        def _(i):
            at = self.rows(start + i * step, step)
            self.rc[at, :] = self.own[at, :].astype(BF16)

    def halve(self, n):
        half = self.count // 2
        self.pending = []
        for p in range(2):
            peer, mine = self.peer(self.order[p][n])
            away = self.at[p] + (1 - mine) * half
            self.at[p] = self.at[p] + mine * half
            self.cast(away, half)
            c = self.copy(
                self.rc.at[self.rows(away, half)], self.rx.at[p, self.base : self.base + half],
                self.ss.at[p, n], self.sr.at[p, n], peer,
            )
            c.start()
            self.pending.append(c)
        self.count = half

    def halved(self):
        half = self.count
        step = min(half, 256)
        for p in range(2):
            self.pending[p].wait()

            @pl.loop(0, half // step)
            def _(i):
                at = self.rows(self.at[p] + i * step, step)
                got = self.rx[p, self.rows(self.base + i * step, step), :]
                self.own[at, :] = self.own[at, :] + got.astype(F32)

        self.base += half

    def along(self):
        self.piece = self.count // self.nb
        self.pending = [[], []]
        for p in range(2):
            self.cast(self.at[p], self.count)
            for d in range(1, self.nb):
                to = lax.rem(self.b + d, self.nb)
                c = self.copy(
                    self.rc.at[self.rows(self.at[p] + to * self.piece, self.piece)],
                    self.rx.at[p, self.rows(self.base + self.b * self.piece, self.piece)],
                    self.zs.at[p, d - 1], self.zr.at[p, d - 1], (self.a, to),
                )
                c.start()
                self.pending[p].append(c)

    def summed(self, put):
        for p in range(2):
            for c in self.pending[p]:
                c.wait()
            start = self.at[p] + self.b * self.piece
            total = self.own[self.rows(start, self.piece), :]
            for d in range(1, self.nb):
                source = lax.rem(self.b + d, self.nb)
                total = total + self.rx[
                    p, self.rows(self.base + source * self.piece, self.piece), :
                ].astype(F32)
            put(p, total.astype(BF16))


class Gather(Tree):
    def __init__(self, na, nb, out, sems):
        super().__init__(na, nb, out.shape[0] // 2)
        self.out = out
        self.gs, self.gr, self.hs, self.hr, self.ks, self.kr = sems
        self.descend()

    def place(self, start):
        return self.h * self.half + start

    def put(self, p, piece):
        at = self.rows(self.place(self.at[p] + self.b * self.piece), self.piece)
        self.out[at, :] = piece
        for d in range(1, self.nb):
            c = self.copy(
                self.out.at[at], self.out.at[at], self.gs.at[p, d - 1], self.gr.at[p, d - 1],
                (self.a, lax.rem(self.b + d, self.nb)),
            )
            c.start()
            self.pending.append(c)

    def settle(self):
        pending, self.pending = self.pending, []
        for c in pending:
            c.wait()

    def gather(self, n):
        self.settle()
        for p in range(2):
            peer, mine = self.peer(self.order[p][n])
            at = self.rows(self.place(self.at[p]), self.count)
            c = self.copy(self.out.at[at], self.out.at[at], self.hs.at[p, n], self.hr.at[p, n], peer)
            c.start()
            self.pending.append(c)
            self.at[p] = self.at[p] - mine * self.count
        self.count *= 2

    def final(self):
        pending, self.pending = self.pending, []
        peer, _ = self.peer(0)
        for p in range(2):
            pending[p].wait()
            at = self.rows(self.place(self.at[p]), self.count)
            c = self.copy(self.out.at[at], self.out.at[at], self.ks.at[p], self.kr.at[p], peer)
            c.start()
            self.pending.append(c)


def reduce_sems(na, nb, chunks):
    dma = pltpu.SemaphoreType.DMA
    shapes = [(chunks,), (2, max(1, na.bit_length() - 2)), (2, nb - 1)]
    return [dma(shape) for shape in shapes for _ in range(2)]


def gather_sems(na, nb):
    dma = pltpu.SemaphoreType.DMA
    shapes = [(2, nb - 1), (2, max(1, na.bit_length() - 2)), (2,)]
    return [dma(shape) for shape in shapes for _ in range(2)]


def forward(na, nb, refs):
    r = refs
    grp = r.grp
    nc = r.fast.shape[0]
    pairs = nc // 2
    p = Peers(na, nb)
    b = p.b
    own = Move(r.fast, r.xe.at[:, 256:768], r.s_own)
    own.start_all(nc)
    raw = [
        pltpu.make_async_copy(src, dst, r.s_raw.at[i])
        for i, (src, dst) in enumerate(((r.reducer, r.wr), (r.spatial, r.sp), (r.expand, r.we)))
    ]
    for c in raw:
        c.start()
    xfeed = Feed(r.slow, r.xbuf, r.s_x, nc)
    xfeed.prime()
    up = Halo(p, 1, lambda c: r.fast.at[c, 256:512], lambda c: r.xe.at[c, 0:256], r.h1us, r.h1ur)
    down = Halo(p, -1, lambda c: r.fast.at[c, 0:128], lambda c: r.xe.at[c, 768:896], r.h1ds, r.h1dr)
    saves = {
        k: Move(getattr(r, k), getattr(r, k + "_o"), getattr(r, "s_" + k))
        for k in ("xe", "y1", "act1", "y2", "act2", "y3", "acts")
    }

    @pl.when(b == 0)
    def _():
        r.xe[:, 0:256, :] = jnp.zeros((nc, 256, CELLS), BF16)
        r.ru[...] = jnp.zeros_like(r.ru)

    @pl.when(b == nb - 1)
    def _():
        r.xe[:, 768:896, :] = jnp.zeros((nc, 128, CELLS), BF16)
        r.rd[...] = jnp.zeros_like(r.rd)

    p.greet()

    @loop(0, nc)
    def _(c):
        up.start(c)
        down.start(c)

    counts = counts_row(grp)
    acc = r.acc
    acc[...] = jnp.zeros_like(acc)
    first_weights(r.lateral, r.squeeze, r.wa)
    for c in raw:
        c.wait()
    more_weights(
        r.wr, r.sp, r.we, r.lateral, r.squeeze, r.narrow, r.widening,
        r.ws, r.wn, r.ww, r.wrt, r.wst, r.wet, r.wwt, r.wnt, r.wf, r.wp, r.tall,
    )
    wsaves = [
        pltpu.make_async_copy(getattr(r, k), getattr(r, k + "_o"), r.s_w.at[i])
        for i, k in enumerate(("wrt", "wst", "wet", "wwt", "wnt", "wf", "wp", "ww"))
    ]
    for c in wsaves:
        c.start()

    @loop(0, nc)
    def _(c):
        own.wait(c)
        up.arrive(c)
        down.arrive(c)
        saves["xe"].start(c)
        g = grp[c]
        m = mask_of(g)
        for lo in range(0, 384, 128):
            y = dot(r.wa[lo : lo + 128, :], r.xe[c])
            r.y1[c, lo : lo + 128, :] = y
            ym = y * m
            add_stats(acc, lo, 128, ym, ym * y, g)
        saves["y1"].start(c)

    s = Sum(p, r.ar1)
    s.start(rows_of(acc, 0, 384), counts)
    s.middle()
    up.sent(nc)
    down.sent(nc)
    t1 = s.finish()
    r.tot1[...] = t1

    tab = r.tab
    acc[0:384, :] = jnp.zeros((384, 128), F32)
    fill_tables(tab, 0, forward_rows(t1[:, :256], t1, 1, r.nl[...].astype(F32)))
    fill_tables(tab, 256, forward_rows(fold_frames(t1[:, 256:]), t1, 4, four(r.nq[...])))
    up = Halo(p, 1, lambda c: r.su.at[c], lambda c: r.ru.at[c], r.h2us, r.h2ur)
    down = Halo(p, -1, lambda c: r.sd.at[c], lambda c: r.rd.at[c], r.h2ds, r.h2dr)

    @loop(0, nc)
    def _(c):
        g = grp[c]
        m = mask_of(g)
        for lo in range(0, 256, 128):
            u = r.y1[c, lo : lo + 128, :] * coef(tab, g, 0, lo, 128) + coef(tab, g, 1, lo, 128)
            r.act1[c, lo : lo + 128, :] = (silu(u) * m).astype(BF16)
        slot = xfeed.take(c)
        for j, dst in enumerate((r.su, r.sd, r.y2)):
            for lo in range(0, 256, 128):
                r0 = 256 * (0, 2, 1)[j] + lo
                v = dot(r.wr[r0 : r0 + 128, :1024], r.xbuf[slot]) + dot(
                    r.wr[r0 : r0 + 128, 1024:], r.act1[c, 0:256, :]
                )
                dst[c, lo : lo + 128, :] = v.astype(dst.dtype)
        up.start(c)
        down.start(c)

    @loop(0, nc)
    def _(c):
        g = grp[c]
        m = mask_of(g)
        u = r.y1[c, 256:384, :] * coef(tab, g, 0, 256, 128) + coef(tab, g, 1, 256, 128)
        act = silu(u) * m
        r.act1[c, 256:384, :] = act.astype(BF16)
        saves["act1"].start(c)
        taps(act, r.x9, 128, 1)
        y = dot(r.wn[...], r.x9[0:1152, 0:CELLS])
        r.y2[c, 256:384, :] = y
        ym = y * m
        add_stats(acc, 256, 128, ym, ym * y, g)

    @loop(0, nc)
    def _(c):
        up.arrive(c)
        down.arrive(c)
        g = grp[c]
        m = mask_of(g)
        for lo in range(0, 256, 128):
            y = (
                r.y2[c, lo : lo + 128, :]
                + r.ru[c, lo : lo + 128, :].astype(F32)
                + r.rd[c, lo : lo + 128, :].astype(F32)
            )
            r.y2[c, lo : lo + 128, :] = y
            ym = y * m
            add_stats(acc, lo, 128, ym, ym * y, g)
        saves["y2"].start(c)

    s = Sum(p, r.ar2)
    s.start(rows_of(acc, 0, 384), counts)
    s.middle()
    up.sent(nc)
    down.sent(nc)
    t2 = s.finish()
    r.tot2[...] = t2

    acc[0:384, :] = jnp.zeros((384, 128), F32)
    r.gram[...] = jnp.zeros_like(r.gram)
    fill_tables(tab, 0, forward_rows(t2[:, :256], t2, 1, r.nr[...].astype(F32)))
    fill_tables(tab, 256, forward_rows(fold_frames(t2[:, 256:]), t2, 4, four(r.nn[...])))

    @loop(0, pairs)
    def _(i):
        for h in range(2):
            c = 2 * i + h
            g = grp[c]
            m = mask_of(g)
            u = r.y2[c, 0:256, :] * coef(tab, g, 0, 0, 256) + coef(tab, g, 1, 0, 256)
            act = silu(u) * m
            r.act2[c, 0:256, :] = act.astype(BF16)
            taps(act, r.x9, 256, 1, h * CELLS)
            u = r.y2[c, 256:384, :] * coef(tab, g, 0, 256, 128) + coef(tab, g, 1, 256, 128)
            act = (silu(u) * m).astype(BF16)
            r.act2[c, 256:384, :] = act
            saves["act2"].start(c)
            add_sums(acc, 256, 128, act.astype(F32), g)
            add_gram(r.gram, act, g)
        for lo in range(0, 256, 128):
            both = dot(r.ws[lo : lo + 128, :], r.x9[...])
            for h in range(2):
                c = 2 * i + h
                g = grp[c]
                y = both[:, h * CELLS : (h + 1) * CELLS]
                r.y3[c, lo : lo + 128, :] = y
                ym = y * mask_of(g)
                add_stats(acc, lo, 128, ym, ym * y, g)
        for h in range(2):
            saves["y3"].start(2 * i + h)

    s = Sum(p, r.ar3)
    s.start(jnp.concatenate([rows_of(acc, 0, 256), wide_sums(acc, r.gram, r.tall[...])], axis=1), counts)
    s.middle()
    t3 = s.finish()
    r.tot3[...] = t3

    ffeed = Feed(r.fcot, r.fcbuf, r.s_fc, nc)
    ffeed.prime()
    fdrain = Drain(r.fobuf, r.fout, r.s_fo, nc)
    wdrain = Drain(r.dzwb, r.dzw_o, r.s_dzw, nc)
    acc[...] = jnp.zeros_like(acc)
    fill_tables(tab, 0, forward_rows(t3[:, :256], t3, 1, r.ns[...].astype(F32)))
    fill_tables(
        r.tabw, 0,
        forward_rows(repeated(t3[:, 256:]), t3, 4, jnp.concatenate([r.nw[...].astype(F32)] * 4, axis=1)),
    )

    @loop(0, pairs)
    def _(i):
        for h in range(2):
            c = 2 * i + h
            g = grp[c]
            m = mask_of(g)
            for lo in range(0, 256, 128):
                u = r.y3[c, lo : lo + 128, :] * coef(tab, g, 0, lo, 128) + coef(tab, g, 1, lo, 128)
                r.acts[c, lo : lo + 128, :] = (silu(u) * m).astype(BF16)
            saves["acts"].start(c)
        act = jnp.concatenate([r.acts[2 * i], r.acts[2 * i + 1]], axis=1)
        for lo in range(0, 1024, 128):
            both = dot(r.we[lo : lo + 128, :], act)
            for h in range(2):
                g = grp[2 * i + h]
                y = both[:, h * CELLS : (h + 1) * CELLS]
                ym = y * mask_of(g)
                add_stats(acc, lo, 128, ym, ym * y, g)

    def fast_ends(lo_c, hi_c):
        @loop(lo_c, hi_c)
        def _(c):
            g = grp[c]
            m = mask_of(g)
            slot = ffeed.take(c)
            fdrain.room(c)
            wdrain.room(c)
            for lo in range(0, 512, 128):
                y = dot(r.ww[lo : lo + 128, :], r.act2[c, 256:384, :])
                v = y * coef(r.tabw, g, 0, lo, 128) + coef(r.tabw, g, 1, lo, 128)
                v = v + 0.5 * r.xe[c, 256 + lo : 384 + lo, :].astype(F32)
                o, slope = silu_and_slope(v)
                r.fobuf[slot, lo : lo + 128, :] = (o * m).astype(BF16)
                dz = r.fcbuf[slot, lo : lo + 128, :].astype(F32) * (0.5 * m) * slope
                r.dzwb[slot, lo : lo + 128, :] = dz
                add_stats(acc, 1024 + lo, 128, dz, dz * y, g)
            fdrain.put(c)
            wdrain.put(c)

    s = Sum(p, r.ar4)
    s.start(rows_of(acc, 0, 1024), counts)
    fast_ends(0, nc // 2)
    s.middle()
    fast_ends(nc // 2, nc)
    t4 = s.finish()
    r.tot4[...] = t4

    r.accf[...] = acc[1024:1536, :]
    for k in saves:
        saves[k].wait_all(nc)
    for c in wsaves:
        c.wait()
    fdrain.done()
    wdrain.done()


def middle(grp, acts_i, slow, scot, we, tot4, ne, sout, dze_o, acc, tab, abuf, xbuf, cbuf, obuf, dzeb, s_a, s_x, s_c, s_o, s_z):
    nc = acts_i.shape[0]
    feeds = [Feed(src, buf, sem, nc) for src, buf, sem in ((acts_i, abuf, s_a), (slow, xbuf, s_x), (scot, cbuf, s_c))]
    drains = [Drain(obuf, sout, s_o, nc), Drain(dzeb, dze_o, s_z, nc)]
    for f in feeds:
        f.prime()
    acc[...] = jnp.zeros_like(acc)
    t4 = tot4[...]
    fill_tables(tab, 0, forward_rows(t4, t4, 1, ne[...].astype(F32)))

    @loop(0, nc)
    def _(c):
        g = grp[c]
        m = mask_of(g)
        slot = [f.take(c) for f in feeds][0]
        for d in drains:
            d.room(c)
        for lo in range(0, 1024, 128):
            y = dot(we[lo : lo + 128, :], abuf[slot])
            v = y * coef(tab, g, 0, lo, 128) + coef(tab, g, 1, lo, 128)
            v = v + 0.5 * xbuf[slot, lo : lo + 128, :].astype(F32)
            o, slope = silu_and_slope(v)
            obuf[slot, lo : lo + 128, :] = (o * m).astype(BF16)
            dz = cbuf[slot, lo : lo + 128, :].astype(F32) * (0.5 * m) * slope
            dzeb[slot, lo : lo + 128, :] = dz
            add_stats(acc, lo, 128, dz, dz * y, g)
        for d in drains:
            d.put(c)

    for d in drains:
        d.done()


def back(na, nb, refs):
    r = refs
    grp = r.grp
    nc = r.acts_i.shape[0]
    pairs = nc // 2
    p = Peers(na, nb)
    b = p.b
    zfeed = Feed(r.dze_i, r.zbuf, r.s_z, nc, 1024)
    zfeed.prime()
    loads = {
        k: Move(getattr(r, k + "_i"), getattr(r, k), getattr(r, "s_" + k))
        for k in KEPT
    }
    raw = {
        k: pltpu.make_async_copy(
            r.wrt_i.at[1024:1280] if k == "wrl" else getattr(r, k + "_i"), getattr(r, k), r.s_raw.at[i]
        )
        for i, k in enumerate(("wet", "we", "ww", "wwt", "wst", "wrl", "wnt"))
    }
    raw["we"].start()
    raw["wet"].start()
    loads["acts"].start_all(nc)
    loads["y3"].start_all(nc)
    for k in ("ww", "wwt", "wst", "wrl", "wnt"):
        raw[k].start()
    wfeed = Feed(r.dzw_i, r.wbuf, r.s_wb, nc)
    wfeed.prime()
    for k in ("act2", "y2", "act1", "y1"):
        loads[k].start_all(nc)

    def xload(i, slot):
        return pltpu.make_async_copy(r.slow.at[pl.ds(2 * i, 2)], r.xbuf.at[slot], r.s_x.at[slot])

    xload(0, 0).start()
    counts = counts_row(grp)
    acc, tab, tabb = r.acc, r.tab, r.tabb
    acc[...] = jnp.zeros_like(acc)
    t1, t2, t3, t4 = r.tot1[...], r.tot2[...], r.tot3[...], r.tot4[...]
    p.greet()
    s = Sum(p, r.ar5)
    s.start(jnp.concatenate([rows_of(r.acce, 0, 1024), folded(rows_of(r.accf, 0, 512))], axis=1), counts)

    @pl.when(b == 0)
    def _():
        r.dye[:, 512:768, :] = jnp.zeros((nc, 256, CELLS), BF16)

    @pl.when(b == nb - 1)
    def _():
        r.dye[:, 0:256, :] = jnp.zeros((nc, 256, CELLS), BF16)

    fill_tables(tabb, 0, forward_rows(t3[:, :256], t3, 1, r.ns[...].astype(F32)))
    s.middle()
    raw["we"].wait()
    raw["wet"].wait()
    t5 = s.finish()

    rows, pair = backward_rows(t4, t5[:, :1024], t4, 1, r.ne[...].astype(F32))
    fill_tables(tab, 0, rows)
    r.epair[...] = pair
    dye = r.dye2

    def dye_rows(c, lo, rows):
        return pl.ds(pl.multiple_of(c * 1024 + lo, 8), rows)

    @loop(0, nc)
    def _(c):
        g = grp[c]
        m = mask_of(g)
        loads["acts"].wait(c)
        loads["y3"].wait(c)
        slot = zfeed.take(c)
        for lo in range(0, 1024, 128):
            y = dot(r.we[lo : lo + 128, :], r.acts[c])
            z = r.zbuf[pl.ds(pl.multiple_of(slot * 1024 + lo, 8), 128), :]
            dy = z * coef(tab, g, 0, lo, 128)
            dy = dy + y * coef(tab, g, 1, lo, 128) + coef(tab, g, 2, lo, 128)
            dye[dye_rows(c, lo, 128), :] = (dy * m).astype(BF16)
        for lo in range(0, 256, 128):
            dx = dot(r.wet[lo : lo + 128, :], dye[dye_rows(c, 0, 1024), :])
            y = r.y3[c, lo : lo + 128, :]
            u = y * coef(tabb, g, 0, lo, 128) + coef(tabb, g, 1, lo, 128)
            dz = (0.5 * m) * silu_and_slope(u)[1] * dx
            r.dzs[c, lo : lo + 128, :] = dz
            add_stats(acc, lo, 128, dz, dz * y, g)

    s = Sum(p, r.ar6)
    s.start(rows_of(acc, 0, 256), counts)
    rows, pair = backward_rows(
        repeated(t3[:, 256:]), repeated(t5[:, 1024:]), t3, 4,
        jnp.concatenate([r.nw[...].astype(F32)] * 4, axis=1),
    )
    fill_tables(tab, 0, rows)
    r.wpair[...] = pair[:, :128]
    fill_tables(tabb, 256, forward_rows(fold_frames(t2[:, 256:]), t2, 4, four(r.nn[...])))
    r.wg[...] = jnp.zeros_like(r.wg)
    raw["ww"].wait()
    raw["wwt"].wait()

    def widen_back(lo_i, hi_i):
        @loop(lo_i, hi_i)
        def _(i):
            for h in range(2):
                c = 2 * i + h
                g = grp[c]
                m = mask_of(g)
                loads["act2"].wait(c)
                loads["y2"].wait(c)
                slot = wfeed.take(c)
                for lo in range(0, 512, 128):
                    y = dot(r.ww[lo : lo + 128, :], r.act2[c, 256:384, :])
                    dy = r.wbuf[slot, lo : lo + 128, :] * coef(tab, g, 0, lo, 128)
                    dy = dy + y * coef(tab, g, 1, lo, 128) + coef(tab, g, 2, lo, 128)
                    r.d9[lo : lo + 128, h * CELLS : (h + 1) * CELLS] = (dy * m).astype(BF16)
            act = jnp.concatenate([r.act2[2 * i + h, 256:384, :] for h in range(2)], axis=1)
            r.wg[...] += dot_nt(r.d9[0:512, :], act)
            both = dot(r.wwt[...], r.d9[0:512, :])
            for h in range(2):
                c = 2 * i + h
                g = grp[c]
                y = r.y2[c, 256:384, :]
                u = y * coef(tabb, g, 0, 256, 128) + coef(tabb, g, 1, 256, 128)
                dz = (0.5 * mask_of(g)) * silu_and_slope(u)[1] * both[:, h * CELLS : (h + 1) * CELLS]
                r.dzn[c] = dz
                add_stats(acc, 256, 128, dz, dz * y, g)

    gg = r.gg
    gg[...] = jnp.zeros_like(gg)

    widen_back(0, pairs // 2)
    s.middle()
    widen_back(pairs // 2, pairs)
    t6 = s.finish()

    acc[0:256, :] = jnp.zeros((256, 128), F32)
    rows, pair = backward_rows(t3[:, :256], t6, t3, 1, r.ns[...].astype(F32))
    fill_tables(tab, 0, rows)
    r.spair[...] = pair
    fill_tables(tabb, 0, forward_rows(t2[:, :256], t2, 1, r.nr[...].astype(F32)))
    raw["wst"].wait()

    @loop(0, pairs)
    def _(i):
        for h in range(2):
            c = 2 * i + h
            g = grp[c]
            m = mask_of(g)
            dy = r.dzs[c] * coef(tab, g, 0, 0, 256) + r.y3[c] * coef(tab, g, 1, 0, 256)
            dy = (dy + coef(tab, g, 2, 0, 256)) * m
            r.y3[c] = dy
            taps(dy, r.d9, 256, -1, h * CELLS)
        for lo in range(0, 256, 128):
            both = dot(r.wst[lo : lo + 128, :], r.d9[...])
            for h in range(2):
                c = 2 * i + h
                g = grp[c]
                dx = both[:, h * CELLS : (h + 1) * CELLS]
                y = r.y2[c, lo : lo + 128, :]
                u = y * coef(tabb, g, 0, lo, 128) + coef(tabb, g, 1, lo, 128)
                dz = (0.5 * mask_of(g)) * silu_and_slope(u)[1] * dx
                r.dzs[c, lo : lo + 128, :] = dz
                add_stats(acc, lo, 128, dz, dz * y, g)

    s = Sum(p, r.ar7)
    s.start(rows_of(acc, 0, 384), counts)
    @loop(0, pairs)
    def _(i):
        act = jnp.concatenate([r.acts[2 * i + h] for h in range(2)], axis=1)
        for lo in range(0, 1024, 256):
            dy = jnp.concatenate([dye[dye_rows(2 * i + h, lo, 256), :] for h in range(2)], axis=1)
            gg[lo : lo + 256, :] += dot_nt(dy, act)

    s.middle()
    t7 = s.finish()

    acc[...] = jnp.zeros_like(acc)
    rows, pair = backward_rows(t2[:, :256], t7[:, :256], t2, 1, r.nr[...].astype(F32))
    fill_tables(tab, 0, rows)
    r.rpair[...] = pair
    dyr = r.dye
    up = Halo(p, 1, lambda c: dyr.at[c, 256:512], lambda c: dyr.at[c, 512:768], r.h3us, r.h3ur)
    down = Halo(p, -1, lambda c: dyr.at[c, 256:512], lambda c: dyr.at[c, 0:256], r.h3ds, r.h3dr)

    @loop(0, nc)
    def _(c):
        g = grp[c]
        m = mask_of(g)
        for lo in range(0, 256, 128):
            dy = r.dzs[c, lo : lo + 128, :] * coef(tab, g, 0, lo, 128)
            dy = dy + r.y2[c, lo : lo + 128, :] * coef(tab, g, 1, lo, 128)
            dy = (dy + coef(tab, g, 2, lo, 128)) * m
            dyr[c, 256 + lo : 384 + lo, :] = dy.astype(BF16)
        up.start(c)
        down.start(c)

    rows, pair = backward_rows(
        fold_frames(t2[:, 256:]), fold_frames(t7[:, 256:]), t2, 4, four(r.nn[...])
    )
    fill_tables(tab, 0, rows)
    r.npair[...] = pair
    fill_tables(tabb, 0, forward_rows(t1[:, :256], t1, 1, r.nl[...].astype(F32)))
    fill_tables(tabb, 256, forward_rows(fold_frames(t1[:, 256:]), t1, 4, four(r.nq[...])))
    r.ng[...] = jnp.zeros_like(r.ng)
    raw["wnt"].wait()
    raw["wrl"].wait()

    @loop(0, pairs)
    def _(i):
        for h in range(2):
            c = 2 * i + h
            g = grp[c]
            m = mask_of(g)
            loads["act1"].wait(c)
            loads["y1"].wait(c)
            dy = r.dzn[c] * coef(tab, g, 0, 0, 128) + r.y2[c, 256:384, :] * coef(tab, g, 1, 0, 128)
            dy = (dy + coef(tab, g, 2, 0, 128)) * m
            taps(dy, r.d9n, 128, -1)
            dx = dot(r.wnt[...], r.d9n[...])
            y = r.y1[c, 256:384, :]
            u = y * coef(tabb, g, 0, 256, 128) + coef(tabb, g, 1, 256, 128)
            dz = (0.5 * m) * silu_and_slope(u)[1] * dx
            r.y1[c, 256:384, :] = dz
            add_stats(acc, 256, 128, dz, dz * y, g)
            for lo in range(0, 1152, 384):
                r.ng[lo : lo + 384, :] += dot_nt(r.d9n[lo : lo + 384, :], r.act1[c, 256:384, :])
            taps(r.y3[c], r.d9, 256, -1, h * CELLS)
        act = jnp.concatenate([r.act2[2 * i + h, 0:256, :] for h in range(2)], axis=1)
        for lo in range(0, 2304, 256):
            gg[1024 + lo : 1280 + lo, :] += dot_nt(r.d9[lo : lo + 256, :], act)

    def xtake(i):
        slot = lax.rem(i, 2)

        @pl.when(i + 1 < pairs)
        def _():
            xload(i + 1, 1 - slot).start()

        xload(i, slot).wait()
        return slot

    def reducer_terms(i, slot, j):
        dy = jnp.concatenate([dyr[2 * i + h, 256 * j : 256 * (j + 1), :] for h in range(2)], axis=1)
        for cb in range(5):
            if cb < 4:
                x = [r.xbuf[slot, h, 256 * cb : 256 * (cb + 1), :] for h in range(2)]
            else:
                x = [r.act1[2 * i + h, 0:256, :] for h in range(2)]
            lo = (4608, 3328, 5888)[j] + 256 * cb
            gg[lo : lo + 256, :] += dot_nt(dy, jnp.concatenate(x, axis=1))

    @loop(0, pairs)
    def _(i):
        reducer_terms(i, xtake(i), 1)

    xload(0, 0).start()

    half = r.zbuf.shape[0]
    red = Reduce(
        na, nb, r.zbuf, dye.at[0:half], r.rc, r.rx, r.tail
    )
    for j in range(2):
        red.first(lambda mine, i: gg[half * mine + 256 * i : half * mine + 256 * (i + 1), :], j, 2)
    zsave = Move(r.y1, r.dz1_o, r.s_dz1)
    dsave = Move(dyr, r.dyr_o, r.s_dyr)

    def arrive(c):
        up.arrive(c)
        down.arrive(c)
        dsave.start(c)
        g = grp[c]
        m = mask_of(g)
        for lo in range(0, 256, 128):
            dx = dot(r.wrl[lo : lo + 128, :], dyr[c])
            y = r.y1[c, lo : lo + 128, :]
            u = y * coef(tabb, g, 0, lo, 128) + coef(tabb, g, 1, lo, 128)
            dz = (0.5 * m) * silu_and_slope(u)[1] * dx
            r.y1[c, lo : lo + 128, :] = dz
            add_stats(acc, lo, 128, dz, dz * y, g)
        zsave.start(c)

    def arrivals(lo_i, hi_i):
        @loop(lo_i, hi_i)
        def _(i):
            @loop(2 * i, 2 * i + 2)
            def _(c):
                arrive(c)

            slot = xtake(i)
            for j in (0, 2):
                reducer_terms(i, slot, j)

    stages = len(red.bits)
    cuts = [(pairs - 1) * (i + 1) // (stages + 1) for i in range(stages + 1)]
    arrivals(0, cuts[0])
    red.first_done()
    for n in range(stages):
        red.halve(n)
        arrivals(cuts[n], cuts[n + 1])
        red.halved()

    @loop(nc - 2, nc)
    def _(c):
        arrive(c)

    s = Sum(p, r.ar8)
    s.start(rows_of(acc, 0, 384), counts)
    red.along()
    slot = xtake(pairs - 1)
    for j in (0, 2):
        reducer_terms(pairs - 1, slot, j)
    s.middle()
    gsave = pltpu.make_async_copy(gg.at[4096:7168], r.gg_o, r.s_gg)
    gsave.start()

    def keep(q, piece):
        r.piece[q] = piece

    up.sent(nc)
    down.sent(nc)
    r.tot8[...] = s.finish()
    red.summed(keep)
    zsave.wait_all(nc)
    dsave.wait_all(nc)
    gsave.wait()


def ends(na, nb, refs):
    r = refs
    grp = r.grp
    nc = r.dz1_i.shape[0]
    p = Peers(na, nb)
    b = p.b
    tab, dyl, dyq, lg, qg = r.tab, r.dyl, r.dyq, r.lg, r.qg
    red = Reduce(na, nb, r.own, r.stage, r.rc, r.rx, r.tail[0:6])
    early, late = Gather(na, nb, r.oute, r.tail[6:12]), Gather(na, nb, r.outl, r.tail[12:18])
    dfeed = Feed(r.dz1_i, r.dbuf, r.s_d, nc)
    yfeed = Feed(r.y1_i, r.ybuf, r.s_y, nc)
    efeed = Feed(r.xe_i, r.ebuf, r.s_e, nc)
    gfeed = Feed(r.dyr_i, r.gbuf, r.s_g, nc)
    zfeed = Feed(r.dze_i, r.zbuf, r.s_z, nc)
    wfeed = Feed(r.dzw_i, r.wbuf, r.s_wb, nc)
    sdrain = Drain(r.obuf, r.sgrad, r.s_o, nc)
    fdrain = Drain(r.fbuf, r.fgrad, r.s_f, nc)
    for f in (dfeed, yfeed, efeed):
        f.prime()
    gload = pltpu.make_async_copy(r.gg_i, r.gg, r.s_raw.at[0])
    rload = pltpu.make_async_copy(r.wrt_i.at[0:1024], r.wr, r.s_raw.at[1])
    fload = pltpu.make_async_copy(r.wf_i, r.wf, r.s_raw.at[2])
    gload.start()
    for f in (gfeed, zfeed, wfeed):
        f.prime()
    rload.start()
    fload.start()
    pload = pltpu.make_async_copy(r.wp_i, r.wp, r.s_raw.at[3])
    pload.start()
    t8, t1 = r.tot8[...], r.tot1[...]
    rows, pair = backward_rows(t1[:, :256], t8[:, :256], t1, 1, r.nl[...].astype(F32))
    fill_tables(tab, 0, rows)
    r.lpair[...] = pair
    rows, pair = backward_rows(
        fold_frames(t1[:, 256:]), fold_frames(t8[:, 256:]), t1, 4, four(r.nq[...])
    )
    fill_tables(tab, 256, rows)
    r.qpair[...] = pair
    lat = Halo(p, -1, lambda c: r.prs.at[c], lambda c: r.prr.at[c], r.hls, r.hlr)
    up = Halo(p, 1, lambda c: dyq.at[c, 160:192], lambda c: dyq.at[c, 0:32], r.hus, r.hur)
    dyq[:, 32:64, :] = jnp.zeros((nc, 32, CELLS), BF16)
    dyq[:, 192:256, :] = jnp.zeros((nc, 64, CELLS), BF16)

    @pl.when(b == 0)
    def _():
        dyq[:, 0:32, :] = jnp.zeros((nc, 32, CELLS), BF16)

    @pl.when(b == nb - 1)
    def _():
        r.prr[...] = jnp.zeros_like(r.prr)

    lg[...] = jnp.zeros_like(lg)
    qg[...] = jnp.zeros_like(qg)
    pload.wait()
    p.greet()
    for q in range(2):
        early.put(q, r.piece[q])

    ahead = nc - nc // 3

    def lateral_back(lo_c, hi_c):
        @loop(lo_c, hi_c)
        def _(c):
            lateral_clip(c)

    def lateral_clip(c):
        g = grp[c]
        m = mask_of(g)
        slot = dfeed.take(c)
        yfeed.take(c)
        for lo in range(0, 384, 128):
            dy = r.dbuf[slot, lo : lo + 128, :] * coef(tab, g, 0, lo, 128)
            dy = dy + r.ybuf[slot, lo : lo + 128, :] * coef(tab, g, 1, lo, 128)
            dy = ((dy + coef(tab, g, 2, lo, 128)) * m).astype(BF16)
            if lo < 256:
                dyl[c, lo : lo + 128, :] = dy
            else:
                dyq[c, 64:192, :] = dy
        for lo in range(0, 256, 128):
            v = dot(r.wp[lo : lo + 128, 0:256], dyl[c]) + dot(r.wp[lo : lo + 128, 256:384], dyq[c, 64:192, :])
            r.prs[c, lo : lo + 128, :] = v.astype(BF16)

        @pl.when(c < ahead)
        def _():
            lat.start(c)

        up.start(c)
        efeed.take(c)
        dy = dyl[c, 0:256, :]
        lg[0:256, :] += dot_nt(dy, r.ebuf[slot, 0:256, :])
        lg[256:512, :] += dot_nt(dy, r.ebuf[slot, 256:512, :])
        lg[512:768, 0:128] += dot_nt(dy, r.ebuf[slot, 512:640, :])
        qg[...] += dot_nt(dyq[c, 64:192, :], r.ebuf[slot, 128:896, :])

    def block_of(mine, i):
        if mine == 0:
            return r.gg[256 * i : 256 * (i + 1), :]
        if i < 4:
            return r.gg[2048 + 256 * i : 2304 + 256 * i, :]
        return lg[256 * (i - 4) : 256 * (i - 3), :]

    stages = len(red.bits)
    lateral_back(0, nc // 4)
    gload.wait()
    red.first(block_of, 0, 2)
    lateral_back(nc // 4, nc)
    for j in range(3):
        lg[800 + 32 * j : 832 + 32 * j, 128:256] = sum(
            qg[32 * f : 32 * (f + 1), 128 * (f + j) : 128 * (f + j + 1)] for f in range(4)
        )
    for k in range(9):
        term = sum(
            r.ng[128 * k + 32 * f : 128 * k + 32 * (f + 1), 32 * f : 32 * (f + 1)] for f in range(4)
        )
        if k < 8:
            lg[768 + 32 * k : 800 + 32 * k, 0:32] = term
        else:
            lg[768:800, 128:160] = term
    lg[896:1024, 128:160] = sum(r.wg[128 * f : 128 * (f + 1), 32 * f : 32 * (f + 1)] for f in range(4))
    red.first(block_of, 1, 2)
    rload.wait()

    def slow_ends(lo_c, hi_c):
        @loop(lo_c, hi_c)
        def _(c):
            m = mask_of(grp[c])
            slot = gfeed.take(c)
            zfeed.take(c)
            sdrain.room(c)
            for lo in range(0, 1024, 128):
                dx = dot(r.wr[lo : lo + 128, :], r.gbuf[slot]) + r.zbuf[slot, lo : lo + 128, :]
                r.obuf[slot, lo : lo + 128, :] = (dx * m).astype(BF16)
            sdrain.put(c)

    cuts = [nc * i // (stages + 1) for i in range(stages + 2)]
    slow_ends(cuts[0], cuts[1])
    red.first_done()
    for n in range(stages):
        red.halve(n)
        slow_ends(cuts[n + 1], cuts[n + 2])
        red.halved()
    red.along()
    fload.wait()

    def fast_ends(lo_c, hi_c):
        @loop(lo_c, hi_c)
        def _(c):
            lat.arrive(c)
            up.arrive(c)
            m = mask_of(grp[c])
            slot = wfeed.take(c)
            fdrain.room(c)
            for lo in range(0, 512, 128):
                dx = dot(r.wf[lo : lo + 128, 0:256], dyl[c]) + dot(r.wf[lo : lo + 128, 256:512], dyq[c])
                dx = dx + r.wbuf[slot, lo : lo + 128, :]
                if lo >= 256:
                    dx = dx + r.prr[c, lo - 256 : lo - 128, :].astype(F32)
                r.fbuf[slot, lo : lo + 128, :] = (dx * m).astype(BF16)
            fdrain.put(c)

    early.gather(stages - 1)
    red.summed(late.put)

    @loop(ahead, nc)
    def _(c):
        lat.start(c)

    cuts = [ahead * i // (2 * stages) for i in range(2 * stages + 1)]
    for n in range(stages):
        fast_ends(cuts[2 * n], cuts[2 * n + 1])
        late.gather(stages - 1 - n)
        fast_ends(cuts[2 * n + 1], cuts[2 * n + 2])
        if n + 1 < stages:
            early.gather(stages - 2 - n)
    early.final()
    late.final()
    fast_ends(ahead, nc)
    sdrain.done()
    fdrain.done()
    lat.sent(nc)
    up.sent(nc)
    early.settle()
    late.settle()


def last(oe_i, ol_i, rp, spr, ep, lp, qp, np_, wp, *refs):
    big, grads, small, big_out = refs[:3], refs[3:10], refs[10:17], refs[17:20]
    bufs, made, (oe, ol, sem_in, sem_out, sem_a, sem_b) = refs[20:23], refs[23:30], refs[30:]
    nc = big[0].shape[0]
    rg, sg, eg, lg, qg, ng, wg = made

    def take(i, c):
        return pltpu.make_async_copy(big[i].at[c], bufs[i].at[c], sem_in.at[i, c])

    def give(i, c):
        return pltpu.make_async_copy(bufs[i].at[c], big_out[i].at[c], sem_out.at[i, c])

    def pass_on(i):
        @loop(0, nc)
        def _(c):
            take(i, c).wait()
            give(i, c).start()

    def hand(i):
        return pltpu.make_async_copy(made[i], grads[i], sem_b.at[i])

    ends_in = [pltpu.make_async_copy(s, d, sem_a.at[i]) for i, (s, d) in enumerate(((oe_i, oe), (ol_i, ol)))]
    for c in ends_in:
        c.start()
    for i in range(3):

        @loop(0, nc)
        def _(c):
            take(i, c).start()

    for c in ends_in:
        c.wait()
    for cb in range(5):
        for j in range(3):
            lo = (512, 3328, 1792)[j] + 256 * cb
            src = ol if j != 1 else oe
            if j == 1 and cb >= 3:
                src, lo = ol, 256 * (cb - 3)
            rg[j, :, 256 * cb : 256 * (cb + 1)] = src[lo : lo + 256, :].astype(F32)
    hand(0).start()
    pass_on(0)
    for k in range(9):
        sg[k] = oe[1024 + 256 * k : 1280 + 256 * k, :].astype(F32)
        at = 3840 + 32 * k if k < 8 else 3840
        ng[k] = (ol[at : at + 32, 0:32] if k < 8 else ol[at : at + 32, 128:160]).astype(F32)
    hand(1).start()
    hand(5).start()
    pass_on(1)
    for q in range(4):
        eg[256 * q : 256 * (q + 1), :] = oe[256 * q : 256 * (q + 1), :].astype(F32)
    for k in range(5):
        lo = 3072 + 256 * (k // 2)
        lg[k] = ol[lo : lo + 256, 128 * (k % 2) : 128 * (k % 2 + 1)].astype(F32)
    for j in range(3):
        qg[j] = ol[3872 + 32 * j : 3904 + 32 * j, 128:256].astype(F32)
    wg[...] = jnp.transpose(ol[3968:4096, 128:256].astype(F32))[0:32, :]
    for i in (2, 3, 4, 6):
        hand(i).start()
    pass_on(2)
    rpo, spo, epo, lpo, qpo, npo, wpo = small
    for src, dst in ((rp, rpo), (spr, spo), (ep, epo), (lp, lpo), (wp, wpo)):
        dst[...] = src[...]
    qpo[...] = qp[:, 0:32]
    npo[...] = np_[:, 0:32]
    for i in range(7):
        hand(i).wait()

    @loop(0, nc)
    def _(c):
        for i in range(3):
            give(i, c).wait()


def sds(shape, dtype):
    return jax.ShapeDtypeStruct(shape, dtype)


class Refs:
    pass


V, H, S = VM, pl.ANY, pltpu.SMEM


def call(body, na, nb, cid, ins, outs, scratch, sums, tail=()):
    names = [*ins, *outs, *scratch]
    shapes = [*scratch.values()]
    for width in sums.values():
        shapes += ar_scratch(na, nb, width)
    shapes += list(tail)

    def kernel(*refs):
        r = Refs()
        for name, ref in zip(names, refs):
            setattr(r, name, ref)
        at = len(names)
        for name in sums:
            setattr(r, name, refs[at : at + 8])
            at += 8
        r.tail = refs[at:]
        body(na, nb, r)

    got = pl.pallas_call(
        kernel,
        name=body.__name__,
        out_shape=tuple(x[1] for x in outs.values()),
        in_specs=[pl.BlockSpec(memory_space=x[0]) for x in ins.values()],
        out_specs=tuple(pl.BlockSpec(memory_space=x[0]) for x in outs.values()),
        scratch_shapes=shapes,
        compiler_params=pltpu.CompilerParams(
            collective_id=cid, has_side_effects=True, vmem_limit_bytes=LIMIT
        ),
    )(*[x[1] for x in ins.values()])
    r = Refs()
    for name, v in zip(outs, got):
        setattr(r, name, v)
    return r


def pick(source, names, end="_o"):
    return {k + "_i": (H, getattr(source, k + end)) for k in names}


def each_of(names, value, start=""):
    return {start + k: value for k in names}


KEPT = ("acts", "y3", "act2", "y2", "act1", "y1")


def build(na, nb):
    def body(
        slow_in, fast_in, clip_group, reducer, spatial, expand, lateral, squeeze, narrow, widening,
        reducer_norm, spatial_norm, expand_norm, lateral_norm, squeeze_norm, narrow_norm, widening_norm,
        slow_cot, fast_cot,
    ):
        nc = slow_in.shape[0]
        dma = pltpu.SemaphoreType.DMA
        slow = slow_in.reshape(nc, 1024, CELLS)
        first_norms = dict(nl=(V, lateral_norm), nq=(V, squeeze_norm))
        norms = first_norms | dict(
            nr=(V, reducer_norm), nn=(V, narrow_norm), ns=(V, spatial_norm), ne=(V, expand_norm), nw=(V, widening_norm)
        )

        def act(c, dtype):
            return sds((nc, c, CELLS), dtype)

        def vact(c, dtype):
            return VM((nc, c, CELLS), dtype)

        def two(c, dtype):
            return VM((2, c, CELLS), dtype)

        def tab(k, c):
            return VM((3, k, c, 128), F32)

        each, slots = dma((nc,)), dma((2,))
        state = dict(
            xe=(896, BF16), y1=(384, F32), act1=(384, BF16), y2=(384, F32), act2=(384, BF16), y3=(256, F32), acts=(256, BF16)
        )
        turns = dict(
            wrt=(1280, 768), wst=(256, 2304), wet=(256, 1024), wwt=(128, 512), wnt=(128, 1152), wf=(512, 512),
            wp=(256, 384), ww=(512, 128),
        )
        fw = call(
            forward, na, nb, 1,
            dict(
                grp=(S, clip_group), fast=(H, fast_in.reshape(nc, 512, CELLS)), slow=(H, slow),
                fcot=(H, fast_cot.reshape(nc, 512, CELLS)),
                reducer=(H, reducer.reshape(768, 1280)), spatial=(H, spatial), expand=(H, expand),
                lateral=(V, lateral), squeeze=(V, squeeze), narrow=(V, narrow), widening=(V, jnp.transpose(widening)),
            ) | norms,
            dict(fout=(H, act(512, BF16)))
            | {k + "_o": (H, act(*v)) for k, v in state.items()}
            | dict(dzw_o=(H, act(512, F32)), accf=(V, sds((512, 128), F32)))
            | {k + "_o": (H, sds(v, BF16)) for k, v in turns.items()}
            | dict(
                tot1=(V, sds((8, 384), F32)), tot2=(V, sds((8, 384), F32)), tot3=(V, sds((8, 384), F32)),
                tot4=(V, sds((8, 1024), F32)),
            ),
            {k: vact(*v) for k, v in state.items()}
            | {k: VM(v, BF16) for k, v in turns.items()}
            | dict(
                wr=VM((768, 1280), BF16), sp=VM((9, 256, 256), BF16), we=VM((1024, 256), BF16),
                wa=VM((384, 896), BF16), tall=VM((128, 128), BF16), gram=VM((3, 128, 128), F32),
                ws=VM((256, 2304), BF16), wn=VM((128, 1152), BF16),
                su=vact(256, BF16), sd=vact(256, BF16), ru=vact(256, BF16), rd=vact(256, BF16),
                xbuf=two(1024, BF16), fcbuf=two(512, BF16), fobuf=two(512, BF16), dzwb=two(512, F32),
                tab=tab(2, 384), tabw=tab(2, 512), acc=VM((1536, 128), F32), x9=VM((2304, 2 * CELLS), BF16),
                s_raw=dma((3,)), s_w=dma((8,)), s_own=each,
            )
            | each_of(("h1us", "h1ur", "h1ds", "h1dr", "h2us", "h2ur", "h2ds", "h2dr"), each)
            | each_of(("x", "fc", "fo", "dzw"), slots, "s_")
            | {"s_" + k: each for k in state},
            dict(ar1=384, ar2=384, ar3=384, ar4=1024),
        )
        hbm, vmem = pl.BlockSpec(memory_space=H), pl.BlockSpec(memory_space=V)
        slow_out, dze, acce = pl.pallas_call(
            middle,
            name="middle",
            out_shape=(act(1024, BF16), act(1024, F32), sds((1024, 128), F32)),
            in_specs=[pl.BlockSpec(memory_space=S)] + [hbm] * 3 + [vmem] * 3,
            out_specs=(hbm, hbm, vmem),
            scratch_shapes=[
                tab(2, 1024), two(256, BF16), two(1024, BF16), two(1024, BF16), two(1024, BF16), two(1024, F32)
            ]
            + [slots] * 5,
            compiler_params=pltpu.CompilerParams(vmem_limit_bytes=LIMIT),
        )(clip_group, fw.acts_o, slow, slow_cot.reshape(nc, 1024, CELLS), expand, fw.tot4, expand_norm)
        half = 2048
        piece = half // (na * nb)
        tots = dict(
            tot1=(V, fw.tot1), tot2=(V, fw.tot2), tot3=(V, fw.tot3), tot4=(V, fw.tot4)
        )
        bw = call(
            back, na, nb, 2,
            dict(
                grp=(S, clip_group), slow=(H, slow), we_i=(H, expand), dze_i=(H, dze), acce=(V, acce), accf=(V, fw.accf)
            )
            | pick(fw, KEPT + ("dzw", "wet", "wwt", "wst", "wrt", "wnt", "ww")) | tots | norms,
            dict(
                dz1_o=(H, act(384, F32)), dyr_o=(H, act(768, BF16)), gg_o=(H, sds((3072, 256), F32)),
                piece=(V, sds((2, piece, 256), BF16)),
                ng=(V, sds((1152, 128), F32)), wg=(V, sds((512, 128), F32)), tot8=(V, sds((8, 384), F32)),
                epair=(V, sds((2, 1024), F32)), spair=(V, sds((2, 256), F32)), rpair=(V, sds((2, 256), F32)),
                wpair=(V, sds((2, 128), F32)), npair=(V, sds((2, 128), F32)),
            ),
            {k: vact(*state[k]) for k in KEPT}
            | dict(
                wet=VM((256, 1024), BF16), we=VM((1024, 256), BF16), ww=VM((512, 128), BF16),
                wwt=VM((128, 512), BF16), wst=VM((256, 2304), BF16), wrl=VM((256, 768), BF16), wnt=VM((128, 1152), BF16),
                zbuf=VM((half, CELLS), F32), wbuf=two(512, F32), xbuf=VM((2, 2, 1024, CELLS), BF16),
                dye=vact(768, BF16), dye2=VM((nc * 1024, CELLS), BF16), rx=VM((2, half // 2, 256), BF16), rc=VM((half, 256), BF16),
                dzs=vact(256, F32), dzn=vact(128, F32), gg=VM((7168, 256), F32),
                tab=tab(3, 1024), tabb=tab(2, 384), acc=VM((384, 128), F32),
                d9=VM((2304, 2 * CELLS), BF16), d9n=VM((1152, CELLS), BF16), s_raw=dma((7,)), s_gg=dma,
            )
            | each_of(KEPT + ("dz1", "dyr"), each, "s_")
            | each_of(("h3us", "h3ur", "h3ds", "h3dr"), each)
            | each_of(("z", "wb", "x"), slots, "s_"),
            dict(ar5=1152, ar6=256, ar7=384, ar8=384),
            reduce_sems(na, nb, 2),
        )
        en = call(
            ends, na, nb, 3,
            dict(
                grp=(S, clip_group), piece=(V, bw.piece), dze_i=(H, dze),
                ng=(V, bw.ng), wg=(V, bw.wg), tot8=(V, bw.tot8), tot1=(V, fw.tot1),
            )
            | pick(bw, ("dz1", "dyr", "gg")) | pick(fw, ("y1", "xe", "dzw", "wrt", "wf", "wp")) | first_norms,
            dict(
                sgrad=(H, act(1024, BF16)), fgrad=(H, act(512, BF16)), oute=(V, sds((2 * half, 256), BF16)),
                outl=(V, sds((2 * half, 256), BF16)), lpair=(V, sds((2, 256), F32)), qpair=(V, sds((2, 128), F32)),
            ),
            dict(
                gg=VM((3072, 256), F32), wr=VM((1024, 768), BF16), wf=VM((512, 512), BF16), wp=VM((256, 384), BF16),
                tab=tab(3, 384), dyl=vact(256, BF16), prs=vact(256, BF16), prr=vact(256, BF16), dyq=vact(256, BF16),
                lg=VM((1024, 256), F32), qg=VM((128, 768), F32), own=VM((half, 256), F32),
                stage=VM((half, 256), BF16), rc=VM((half, 256), BF16), rx=VM((2, half // 2, 256), BF16),
                dbuf=two(384, F32), ybuf=two(384, F32), ebuf=two(896, BF16), gbuf=two(768, BF16),
                zbuf=two(1024, F32), wbuf=two(512, F32), obuf=two(1024, BF16), fbuf=two(512, BF16),
                s_raw=dma((4,)),
            )
            | each_of(("d", "y", "e", "g", "z", "wb", "o", "f"), slots, "s_")
            | each_of(("hls", "hlr", "hus", "hur"), each),
            {},
            reduce_sems(na, nb, 2) + gather_sems(na, nb) * 2,
        )
        shapes = [
            (3, 256, 1280), (9, 256, 256), (1024, 256), (5, 256, 128), (3, 32, 128), (9, 32, 32), (32, 128),
            (2, 256), (2, 256), (2, 1024), (2, 256), (2, 32), (2, 32), (2, 128),
        ]
        big = (fw.fout, en.sgrad, en.fgrad)
        got = pl.pallas_call(
            last,
            name="last",
            out_shape=tuple(sds(v, F32) for v in shapes) + tuple(sds(v.shape, BF16) for v in big),
            in_specs=[hbm] * 2 + [vmem] * 7 + [hbm] * 3,
            out_specs=tuple([hbm] * 7 + [vmem] * 7 + [hbm] * 3),
            scratch_shapes=[VM(v.shape, BF16) for v in big]
            + [VM(v, F32) for v in shapes[:7]]
            + [VM((2 * half, 256), BF16), VM((2 * half, 256), BF16)]
            + [dma((3, nc)), dma((3, nc)), dma((2,)), dma((7,))],
            compiler_params=pltpu.CompilerParams(vmem_limit_bytes=LIMIT),
        )(en.oute, en.outl, bw.rpair, bw.spair, bw.epair, en.lpair, en.qpair, bw.npair, bw.wpair, *big)
        fast_out, slow_grad, fast_grad = got[len(shapes) :]
        return (
            slow_out.reshape(slow_in.shape), fast_out.reshape(fast_in.shape),
            slow_grad.reshape(slow_in.shape), fast_grad.reshape(fast_in.shape),
            *got[:6], jnp.transpose(got[6]), *got[7 : len(shapes)],
        )

    return body


def solution(mesh):
    body = build(mesh.shape["clip"], mesh.shape["tm"])
    big = P("clip", "tm", None, None)
    return jax.shard_map(
        body,
        mesh=mesh,
        in_specs=(big, big, P("clip")) + (P(),) * 14 + (big, big),
        out_specs=(big,) * 4 + (P(),) * 14,
        check_vma=False,
    )
```

```python
import functools

import jax
import jax.numpy as jnp
from jax import lax
from jax.experimental import pallas as pl
from jax.experimental.pallas import tpu as pltpu
from jax.sharding import PartitionSpec as P

MESH = pl.DeviceIdType.MESH
F32, BF16 = jnp.float32, jnp.bfloat16
SIDE = 16
CELLS = SIDE * SIDE
EPS = 1e-05
VM = pltpu.VMEM
LIMIT = 63 * 1024 * 1024 + 256 * 1024


def dot(a, b):
    return lax.dot_general(a, b, (((1,), (0,)), ((), ())), preferred_element_type=F32)


def dot_nt(a, b):
    return lax.dot_general(a, b, (((1,), (1,)), ((), ())), preferred_element_type=F32)


def side_of(g):
    return jnp.where(g == 0, SIDE * 5 // 8, jnp.where(g == 1, SIDE * 7 // 8, SIDE))


def mask_of(g):
    cell = lax.broadcasted_iota(jnp.int32, (1, CELLS), 1)
    side = side_of(g)
    return jnp.where(((cell >> 4) < side) & ((cell & 15) < side), 1.0, 0.0).astype(F32)


def counts_row(grp):
    lane = lax.broadcasted_iota(jnp.int32, (1, 128), 1)
    total = jnp.zeros((1, 128), F32)
    for c in range(grp.shape[0]):
        side = side_of(grp[c])
        total = total + jnp.where(lane == grp[c], (side * side).astype(F32), 0.0)
    return total


def add_stats(acc, lo, rows, first, second, g):
    lane = lax.broadcasted_iota(jnp.int32, (1, 128), 1)
    one = jnp.sum(first[:, :128] + first[:, 128:], axis=1, keepdims=True)
    two = jnp.sum(second[:, :128] + second[:, 128:], axis=1, keepdims=True)
    acc[lo : lo + rows, :] += jnp.where(lane == g, one, 0.0) + jnp.where(lane == g + 3, two, 0.0)


def add_sums(acc, lo, rows, value, g):
    lane = lax.broadcasted_iota(jnp.int32, (1, 128), 1)
    one = jnp.sum(value[:, :128] + value[:, 128:], axis=1, keepdims=True)
    acc[lo : lo + rows, :] += jnp.where(lane == g, one, 0.0)


def add_gram(gram, act, g):
    term = dot_nt(act, act)
    for k in range(3):
        gram[k] += jnp.where(g == k, term, 0.0)


def wide_sums(acc, gram, tall):
    w = tall.astype(F32)
    exact = dict(precision=lax.Precision.HIGHEST, preferred_element_type=F32)
    one = jnp.dot(rows_of(acc, 256, 384), w, **exact)
    block = lax.broadcasted_iota(jnp.int32, (128, 128), 0) >> 5
    same = block == (lax.broadcasted_iota(jnp.int32, (128, 128), 1) >> 5)
    two = [
        jnp.sum(w * jnp.dot(jnp.where(same, gram[k], 0.0), w, **exact), axis=0, keepdims=True)
        for k in range(3)
    ]
    return jnp.concatenate([one[:3, :]] + two + [jnp.zeros((2, 128), F32)], axis=0)


def ar_scratch(na, nb, width):
    dma = pltpu.SemaphoreType.DMA
    return [
        VM((8, width), F32),
        VM((na, 8, width), F32),
        VM((8, width), F32),
        VM((nb, 8, width), F32),
        dma((na - 1,)),
        dma((na - 1,)),
        dma((nb - 1,)),
        dma((nb - 1,)),
    ]


class Peers:
    def __init__(self, na, nb):
        self.na, self.nb = na, nb
        self.a, self.b = lax.axis_index("clip"), lax.axis_index("tm")
        self.along_a = [(lax.rem(self.a + d, na), self.b) for d in range(1, na)]
        self.along_b = [(self.a, lax.rem(self.b + d, nb)) for d in range(1, nb)]
        self.bar = pltpu.get_barrier_semaphore()
        for peer in self.along_a + self.along_b:
            pl.semaphore_signal(self.bar, inc=1, device_id=peer, device_id_type=MESH)

    def greet(self):
        pl.semaphore_wait(self.bar, self.na - 1 + self.nb - 1)


class Sum:
    def __init__(self, peers, refs):
        self.p = peers
        self.mine, self.bufa, self.part, self.bufb, self.sa, self.ra, self.sb, self.rb = refs

    def copies(self, src, buf, slot, ss, rs, peers):
        return [
            pltpu.make_async_remote_copy(
                src, buf.at[slot], ss.at[i], rs.at[i], device_id=peer, device_id_type=MESH
            )
            for i, peer in enumerate(peers)
        ]

    def start(self, rows, counts):
        row = lax.broadcasted_iota(jnp.int32, (8, 128), 0)
        head = jnp.where(row == 6, counts, rows[:, :128])
        value = jnp.concatenate([head, rows[:, 128:]], axis=1)
        self.mine[...] = value
        self.bufa[self.p.a] = value
        self.first = self.copies(self.mine, self.bufa, self.p.a, self.sa, self.ra, self.p.along_a)
        for c in self.first:
            c.start()

    def middle(self):
        for c in self.first:
            c.wait()
        total = self.bufa[0]
        for i in range(1, self.p.na):
            total = total + self.bufa[i]
        self.part[...] = total
        self.bufb[self.p.b] = total
        self.second = self.copies(self.part, self.bufb, self.p.b, self.sb, self.rb, self.p.along_b)
        for c in self.second:
            c.start()

    def finish(self):
        for c in self.second:
            c.wait()
        total = self.bufb[0]
        for i in range(1, self.p.nb):
            total = total + self.bufb[i]
        return total


def rows_of(acc, lo, hi):
    return jnp.transpose(acc[lo:hi, :])[:8, :]


def folded(rows):
    return sum(rows[:, 128 * f : 128 * (f + 1)] for f in range(rows.shape[1] // 128))


def repeated(rows):
    return jnp.concatenate([rows] * 4, axis=1)


class Halo:
    def __init__(self, peers, step, src, dst, ss, rs):
        self.src, self.dst, self.ss, self.rs = src, dst, ss, rs
        to = peers.b + step
        self.sends = (to >= 0) & (to < peers.nb)
        source = peers.b - step
        self.gets = (source >= 0) & (source < peers.nb)
        self.peer = (peers.a, lax.rem(to + peers.nb, peers.nb))

    def copy(self, c):
        return pltpu.make_async_remote_copy(
            self.src(c), self.dst(c), self.ss.at[c], self.rs.at[c],
            device_id=self.peer, device_id_type=MESH,
        )

    def start(self, c):
        @pl.when(self.sends)
        def _():
            self.copy(c).start()

    def arrive(self, c):
        @pl.when(self.gets)
        def _():
            self.copy(c).wait_recv()

    def sent(self, nc):
        @pl.when(self.sends)
        def _():
            @pl.loop(0, nc)
            def _(c):
                self.copy(c).wait_send()


class Move:
    def __init__(self, src, dst, sem):
        self.src, self.dst, self.sem = src, dst, sem

    def copy(self, c):
        return pltpu.make_async_copy(self.src.at[c], self.dst.at[c], self.sem.at[c])

    def start(self, c):
        self.copy(c).start()

    def wait(self, c):
        self.copy(c).wait()

    def start_all(self, nc):
        @pl.loop(0, nc)
        def _(c):
            self.start(c)

    def wait_all(self, nc):
        @pl.loop(0, nc)
        def _(c):
            self.wait(c)


class Feed:
    def __init__(self, src, buf, sem, nc, rows=0, slots=2):
        self.src, self.buf, self.sem, self.nc, self.rows, self.slots = src, buf, sem, nc, rows, slots

    def copy(self, c, slot):
        at = pl.ds(pl.multiple_of(slot * self.rows, 8), self.rows) if self.rows else slot
        return pltpu.make_async_copy(self.src.at[c], self.buf.at[at], self.sem.at[slot])

    def prime(self):
        for c in range(self.slots - 1):
            self.copy(c, c).start()

    def take(self, c):
        slot = lax.rem(c, self.slots)
        ahead = self.slots - 1

        @pl.when(c + ahead < self.nc)
        def _():
            self.copy(c + ahead, lax.rem(c + ahead, self.slots)).start()

        self.copy(c, slot).wait()
        return slot


class Drain:
    def __init__(self, buf, dst, sem, nc, slots=2):
        self.buf, self.dst, self.sem, self.nc, self.slots = buf, dst, sem, nc, slots

    def copy(self, c, slot):
        return pltpu.make_async_copy(self.buf.at[slot], self.dst.at[c], self.sem.at[slot])

    def room(self, c):
        slot = lax.rem(c, self.slots)

        @pl.when(c >= self.slots)
        def _():
            self.copy(c - self.slots, slot).wait()

        return slot

    def put(self, c):
        self.copy(c, lax.rem(c, self.slots)).start()

    def done(self):
        for c in range(max(0, self.nc - self.slots), self.nc):
            self.copy(c, c % self.slots).wait()


def fold_frames(total):
    out = total + pltpu.roll(total, 32, 1)
    return out + pltpu.roll(out, 64, 1)


def moments(total, counts, frames):
    out = []
    for g in range(3):
        n = counts[6:7, g : g + 1] * float(frames)
        mean = total[g : g + 1, :] / n
        var = total[g + 3 : g + 4, :] / n - mean * mean
        out.append((n, mean, lax.rsqrt(var + EPS)))
    return out


def fill_tables(tab, base, rows_list):
    width = rows_list[0][0].shape[1]
    count = len(rows_list[0])
    rows = [rows_list[g][k] for g in range(3) for k in range(count)]
    rows = rows + [jnp.zeros((1, width), F32)] * (128 - len(rows))
    cols = jnp.transpose(jnp.concatenate(rows, axis=0))
    for g in range(3):
        for k in range(count):
            i = g * count + k
            tab[g, k, base : base + width, :] = jnp.broadcast_to(cols[:, i : i + 1], (width, 128))


def forward_rows(total, counts, frames, pair):
    out = []
    for n, mean, r in moments(total, counts, frames):
        gain = 0.5 * (pair[0:1, :] * r)
        out.append((gain, 0.5 * pair[1:2, :] - mean * gain))
    return out


def backward_rows(total, grads, counts, frames, pair):
    out, two_all, one_all = [], 0.0, 0.0
    for g, (n, mean, r) in enumerate(moments(total, counts, frames)):
        one = grads[g : g + 1, :]
        two = r * (grads[g + 3 : g + 4, :] - mean * one)
        c0 = pair[0:1, :] * r
        slope = c0 * r * two / n
        out.append((c0, -slope, slope * mean - c0 * one / n))
        two_all, one_all = two_all + two, one_all + one
    return out, jnp.concatenate([two_all, one_all], axis=0)


def wide(v):
    return jnp.concatenate([v, v], axis=1)


def coef(tab, g, k, lo, rows):
    return wide(tab[g, k, lo : lo + rows, :])


def silu(w):
    return w * (1.0 + jnp.tanh(w))


def silu_and_slope(w):
    p = 1.0 + jnp.tanh(w)
    o = w * p
    return o, p + o * (2.0 - p)


def taps(x, dst, rows, sign, at=0):
    cell = lax.broadcasted_iota(jnp.int32, (1, CELLS), 1)
    row, col = cell >> 4, cell & 15
    for k in range(9):
        di, dl = sign * (k // 3 - 1), sign * (k % 3 - 1)
        step = SIDE * di + dl
        if step == 0:
            dst[k * rows : (k + 1) * rows, at : at + CELLS] = x.astype(BF16)
            continue
        moved = pltpu.roll(x, (-step) % CELLS, 1)
        ok = (row + di >= 0) & (row + di < SIDE) & (col + dl >= 0) & (col + dl < SIDE)
        dst[k * rows : (k + 1) * rows, at : at + CELLS] = jnp.where(ok, moved, 0.0).astype(BF16)


def column_taps(x, dst, sign, at):
    col = lax.broadcasted_iota(jnp.int32, (1, CELLS), 1) & 15
    rows = x.shape[0]
    for b in range(3):
        dl = sign * (b - 1)
        moved = x
        if dl:
            moved = jnp.where((col + dl >= 0) & (col + dl < SIDE), pltpu.roll(x, (-dl) % CELLS, 1), 0.0)
        dst[rows * b : rows * (b + 1), at : at + CELLS] = moved.astype(BF16)


def row_taps(terms, sign):
    row = lax.broadcasted_iota(jnp.int32, (1, CELLS), 1) >> 4
    total = terms[1]
    for a in (0, 2):
        di = sign * (a - 1)
        moved = pltpu.roll(terms[a], (-SIDE * di) % CELLS, 1)
        total = total + jnp.where((row + di >= 0) & (row + di < SIDE), moved, 0.0)
    return total


def loop(lo, hi):
    return pl.loop(lo, hi)


def spread_lanes(at, lanes):
    row = lax.broadcasted_iota(jnp.int32, (32, lanes), 0)
    lane = lax.broadcasted_iota(jnp.int32, (32, lanes), 1)
    hit = ((lane & 31) == row) if at is None else (lane == row + at)
    return jnp.where(hit, 1.0, 0.0).astype(BF16)


def dot_tn(a, b):
    return lax.dot_general(a, b, (((0,), (0,)), ((), ())), preferred_element_type=F32)


def turned(v):
    return jnp.transpose(v.astype(F32)).astype(BF16)


def four(pair):
    return dot(pair, spread_lanes(None, 128))


def first_weights(lateral, squeeze, wa):
    wa[...] = jnp.zeros_like(wa)
    for k in range(5):
        wa[0:256, 128 * k : 128 * (k + 1)] = lateral[k]
    for f in range(4):
        for j in range(3):
            wa[256 + 32 * f : 288 + 32 * f, 128 * (f + 1 + j) : 128 * (f + 2 + j)] = squeeze[j]


def more_weights(reducer, spatial, expand, lateral, squeeze, narrow, widening, ws, wn, ww, wrt, wst, wet, wwt, wnt, wf, wp, tall):
    lane = lax.broadcasted_iota(jnp.int32, (1, 128), 1) >> 5
    row = lax.broadcasted_iota(jnp.int32, (128, 1), 0) >> 5
    every = spread_lanes(None, 128)
    for k in range(9):
        a, b = 256 * (k // 3), 256 * (k % 3)
        ws[a : a + 256, b : b + 256] = spatial[k]
        wst[a : a + 256, b : b + 256] = turned(spatial[k])
        there, back = dot(narrow[k], every), dot_tn(narrow[k], every)
        for f in range(4):
            at = slice(32 * f, 32 * (f + 1))
            wn[at, 128 * k : 128 * (k + 1)] = jnp.where(lane == f, there, 0.0).astype(BF16)
            wnt[at, 128 * k : 128 * (k + 1)] = jnp.where(lane == f, back, 0.0).astype(BF16)
    wide_w = dot_tn(widening[...], every)
    tall_w = dot_tn(every, widening[...])
    tall[...] = tall_w.astype(BF16)
    for f in range(4):
        ww[128 * f : 128 * (f + 1), :] = jnp.where(lane == f, wide_w, 0.0).astype(BF16)
        wwt[:, 128 * f : 128 * (f + 1)] = jnp.where(row == f, tall_w, 0.0).astype(BF16)
    for q in range(4):
        wet[:, 256 * q : 256 * (q + 1)] = turned(expand[256 * q : 256 * (q + 1), :])
    for j in range(3):
        for q in range(5):
            wrt[256 * q : 256 * (q + 1), 256 * j : 256 * (j + 1)] = turned(
                reducer[256 * j : 256 * (j + 1), 256 * q : 256 * (q + 1)]
            )
    wf[...] = jnp.zeros_like(wf)
    for f, k in ((0, 2), (1, 3), (2, 4)):
        wf[128 * f : 128 * (f + 1), 0:256] = turned(lateral[k])
    place = (0, 2, 3, 4, 5)
    for f in range(4):
        wf[128 * f : 128 * (f + 1), 256:512] = sum(
            dot_tn(squeeze[j], spread_lanes(32 * place[f + 2 - j], 256)) for j in range(3) if f + 2 - j < 5
        ).astype(BF16)
    wp[...] = jnp.zeros_like(wp)
    for f in range(2):
        wp[128 * f : 128 * (f + 1), 0:256] = turned(lateral[f])
    wp[128:256, 256:384] = dot_tn(squeeze[0], spread_lanes(0, 128)).astype(BF16)


class Tree:
    def __init__(self, na, nb, half):
        self.na, self.nb, self.half = na, nb, half
        self.a, self.b = lax.axis_index("clip"), lax.axis_index("tm")
        self.bits = [i for i in range(1, 16) if (1 << i) < na]
        self.order = (self.bits, self.bits[::-1])
        self.h = lax.rem(self.a, 2)
        self.at, self.count, self.pending = [0, half // 2], half // 2, []

    def peer(self, bit):
        step = 1 << bit
        mine = lax.rem(self.a // step, 2)
        return (self.a + step * (1 - 2 * mine), self.b), mine

    def rows(self, start, count):
        return pl.ds(pl.multiple_of(start, 8), count)

    def copy(self, src, dst, ss, rs, peer):
        return pltpu.make_async_remote_copy(
            src, dst, ss, rs, device_id=peer, device_id_type=MESH
        )

    def descend(self):
        for n in range(len(self.bits)):
            self.count //= 2
            for p in range(2):
                self.at[p] = self.at[p] + self.peer(self.order[p][n])[1] * self.count
        self.piece = self.count // self.nb


class Reduce(Tree):
    def __init__(self, na, nb, own, stage, rc, rx, sems):
        super().__init__(na, nb, own.shape[0])
        self.own, self.stage, self.rc, self.rx = own, stage, rc, rx
        self.cs, self.cr, self.ss, self.sr, self.zs, self.zr = sems
        self.first_copies = []

    def first(self, block_of, j, chunks):
        self.chunks = chunks
        size = self.half // chunks
        peer, _ = self.peer(0)
        rows = slice(j * size, (j + 1) * size)
        for i in range(j * size // 256, (j + 1) * size // 256):
            at = slice(256 * i, 256 * (i + 1))
            for mine in range(2):

                @pl.when(self.h == mine)
                def _():
                    self.own[at, :] = block_of(mine, i)
                    self.stage[at, :] = block_of(1 - mine, i).astype(BF16)

        c = self.copy(self.stage.at[rows], self.rc.at[rows], self.cs.at[j], self.cr.at[j], peer)
        c.start()
        self.first_copies.append(c)

    def first_done(self):
        size = self.half // self.chunks
        for j, c in enumerate(self.first_copies):
            c.wait()

            @pl.loop(j * size // 256, (j + 1) * size // 256)
            def _(i):
                at = pl.ds(pl.multiple_of(i * 256, 256), 256)
                self.own[at, :] = self.own[at, :] + self.rc[at, :].astype(F32)

        self.base = 0

    def cast(self, start, count):
        step = min(count, 256)

        @pl.loop(0, count // step)
        def _(i):
            at = self.rows(start + i * step, step)
            self.rc[at, :] = self.own[at, :].astype(BF16)

    def halve(self, n):
        half = self.count // 2
        self.pending = []
        for p in range(2):
            peer, mine = self.peer(self.order[p][n])
            away = self.at[p] + (1 - mine) * half
            self.at[p] = self.at[p] + mine * half
            self.cast(away, half)
            c = self.copy(
                self.rc.at[self.rows(away, half)], self.rx.at[p, self.base : self.base + half],
                self.ss.at[p, n], self.sr.at[p, n], peer,
            )
            c.start()
            self.pending.append(c)
        self.count = half

    def halved(self):
        half = self.count
        step = min(half, 256)
        for p in range(2):
            self.pending[p].wait()

            @pl.loop(0, half // step)
            def _(i):
                at = self.rows(self.at[p] + i * step, step)
                got = self.rx[p, self.rows(self.base + i * step, step), :]
                self.own[at, :] = self.own[at, :] + got.astype(F32)

        self.base += half

    def along(self):
        self.piece = self.count // self.nb
        self.pending = [[], []]
        for p in range(2):
            self.cast(self.at[p], self.count)
            for d in range(1, self.nb):
                to = lax.rem(self.b + d, self.nb)
                c = self.copy(
                    self.rc.at[self.rows(self.at[p] + to * self.piece, self.piece)],
                    self.rx.at[p, self.rows(self.base + self.b * self.piece, self.piece)],
                    self.zs.at[p, d - 1], self.zr.at[p, d - 1], (self.a, to),
                )
                c.start()
                self.pending[p].append(c)

    def summed(self, put):
        for p in range(2):
            for c in self.pending[p]:
                c.wait()
            start = self.at[p] + self.b * self.piece
            total = self.own[self.rows(start, self.piece), :]
            for d in range(1, self.nb):
                source = lax.rem(self.b + d, self.nb)
                total = total + self.rx[
                    p, self.rows(self.base + source * self.piece, self.piece), :
                ].astype(F32)
            put(p, total.astype(BF16))


class Gather(Tree):
    def __init__(self, na, nb, out, sems):
        super().__init__(na, nb, out.shape[0] // 2)
        self.out = out
        self.gs, self.gr, self.hs, self.hr, self.ks, self.kr = sems
        self.descend()

    def place(self, start):
        return self.h * self.half + start

    def put(self, p, piece):
        at = self.rows(self.place(self.at[p] + self.b * self.piece), self.piece)
        self.out[at, :] = piece
        for d in range(1, self.nb):
            c = self.copy(
                self.out.at[at], self.out.at[at], self.gs.at[p, d - 1], self.gr.at[p, d - 1],
                (self.a, lax.rem(self.b + d, self.nb)),
            )
            c.start()
            self.pending.append(c)

    def settle(self):
        pending, self.pending = self.pending, []
        for c in pending:
            c.wait()

    def gather(self, n):
        self.settle()
        for p in range(2):
            peer, mine = self.peer(self.order[p][n])
            at = self.rows(self.place(self.at[p]), self.count)
            c = self.copy(self.out.at[at], self.out.at[at], self.hs.at[p, n], self.hr.at[p, n], peer)
            c.start()
            self.pending.append(c)
            self.at[p] = self.at[p] - mine * self.count
        self.count *= 2

    def final(self):
        pending, self.pending = self.pending, []
        peer, _ = self.peer(0)
        for p in range(2):
            pending[p].wait()
            at = self.rows(self.place(self.at[p]), self.count)
            c = self.copy(self.out.at[at], self.out.at[at], self.ks.at[p], self.kr.at[p], peer)
            c.start()
            self.pending.append(c)


def reduce_sems(na, nb, chunks):
    dma = pltpu.SemaphoreType.DMA
    shapes = [(chunks,), (2, max(1, na.bit_length() - 2)), (2, nb - 1)]
    return [dma(shape) for shape in shapes for _ in range(2)]


def gather_sems(na, nb):
    dma = pltpu.SemaphoreType.DMA
    shapes = [(2, nb - 1), (2, max(1, na.bit_length() - 2)), (2,)]
    return [dma(shape) for shape in shapes for _ in range(2)]


def forward(na, nb, refs):
    r = refs
    grp = r.grp
    nc = r.fast.shape[0]
    pairs = nc // 2
    p = Peers(na, nb)
    b = p.b
    own = Move(r.fast, r.xe.at[:, 256:768], r.s_own)
    own.start_all(nc)
    raw = [
        pltpu.make_async_copy(src, dst, r.s_raw.at[i])
        for i, (src, dst) in enumerate(((r.reducer, r.wr), (r.spatial, r.sp), (r.expand, r.we)))
    ]
    for c in raw:
        c.start()
    xfeed = Feed(r.slow, r.xbuf, r.s_x, nc)
    xfeed.prime()
    up = Halo(p, 1, lambda c: r.fast.at[c, 256:512], lambda c: r.xe.at[c, 0:256], r.h1us, r.h1ur)
    down = Halo(p, -1, lambda c: r.fast.at[c, 0:128], lambda c: r.xe.at[c, 768:896], r.h1ds, r.h1dr)
    saves = {
        k: Move(getattr(r, k), getattr(r, k + "_o"), getattr(r, "s_" + k))
        for k in ("xe", "y1", "act1", "y2", "act2", "y3", "acts")
    }

    @pl.when(b == 0)
    def _():
        r.xe[:, 0:256, :] = jnp.zeros((nc, 256, CELLS), BF16)
        r.ru[...] = jnp.zeros_like(r.ru)

    @pl.when(b == nb - 1)
    def _():
        r.xe[:, 768:896, :] = jnp.zeros((nc, 128, CELLS), BF16)
        r.rd[...] = jnp.zeros_like(r.rd)

    p.greet()

    @loop(0, nc)
    def _(c):
        up.start(c)
        down.start(c)

    counts = counts_row(grp)
    acc = r.acc
    acc[...] = jnp.zeros_like(acc)
    first_weights(r.lateral, r.squeeze, r.wa)
    for c in raw:
        c.wait()
    more_weights(
        r.wr, r.sp, r.we, r.lateral, r.squeeze, r.narrow, r.widening,
        r.ws, r.wn, r.ww, r.wrt, r.wst, r.wet, r.wwt, r.wnt, r.wf, r.wp, r.tall,
    )
    wsaves = [
        pltpu.make_async_copy(getattr(r, k), getattr(r, k + "_o"), r.s_w.at[i])
        for i, k in enumerate(("wrt", "wst", "wet", "wwt", "wnt", "wf", "wp", "ww"))
    ]
    for c in wsaves:
        c.start()

    @loop(0, nc)
    def _(c):
        own.wait(c)
        up.arrive(c)
        down.arrive(c)
        saves["xe"].start(c)
        g = grp[c]
        m = mask_of(g)
        for lo in range(0, 384, 128):
            y = dot(r.wa[lo : lo + 128, :], r.xe[c])
            r.y1[c, lo : lo + 128, :] = y
            ym = y * m
            add_stats(acc, lo, 128, ym, ym * y, g)
        saves["y1"].start(c)

    s = Sum(p, r.ar1)
    s.start(rows_of(acc, 0, 384), counts)
    s.middle()
    up.sent(nc)
    down.sent(nc)
    t1 = s.finish()
    r.tot1[...] = t1

    tab = r.tab
    acc[0:384, :] = jnp.zeros((384, 128), F32)
    fill_tables(tab, 0, forward_rows(t1[:, :256], t1, 1, r.nl[...].astype(F32)))
    fill_tables(tab, 256, forward_rows(fold_frames(t1[:, 256:]), t1, 4, four(r.nq[...])))
    up = Halo(p, 1, lambda c: r.su.at[c], lambda c: r.ru.at[c], r.h2us, r.h2ur)
    down = Halo(p, -1, lambda c: r.sd.at[c], lambda c: r.rd.at[c], r.h2ds, r.h2dr)

    @loop(0, nc)
    def _(c):
        g = grp[c]
        m = mask_of(g)
        for lo in range(0, 256, 128):
            u = r.y1[c, lo : lo + 128, :] * coef(tab, g, 0, lo, 128) + coef(tab, g, 1, lo, 128)
            r.act1[c, lo : lo + 128, :] = (silu(u) * m).astype(BF16)
        slot = xfeed.take(c)
        for j, dst in enumerate((r.su, r.sd, r.y2)):
            for lo in range(0, 256, 128):
                r0 = 256 * (0, 2, 1)[j] + lo
                v = dot(r.wr[r0 : r0 + 128, :1024], r.xbuf[slot]) + dot(
                    r.wr[r0 : r0 + 128, 1024:], r.act1[c, 0:256, :]
                )
                dst[c, lo : lo + 128, :] = v.astype(dst.dtype)
        up.start(c)
        down.start(c)

    @loop(0, nc)
    def _(c):
        g = grp[c]
        m = mask_of(g)
        u = r.y1[c, 256:384, :] * coef(tab, g, 0, 256, 128) + coef(tab, g, 1, 256, 128)
        act = silu(u) * m
        r.act1[c, 256:384, :] = act.astype(BF16)
        saves["act1"].start(c)
        taps(act, r.x9, 128, 1)
        y = dot(r.wn[...], r.x9[0:1152, 0:CELLS])
        r.y2[c, 256:384, :] = y
        ym = y * m
        add_stats(acc, 256, 128, ym, ym * y, g)

    @loop(0, nc)
    def _(c):
        up.arrive(c)
        down.arrive(c)
        g = grp[c]
        m = mask_of(g)
        for lo in range(0, 256, 128):
            y = (
                r.y2[c, lo : lo + 128, :]
                + r.ru[c, lo : lo + 128, :].astype(F32)
                + r.rd[c, lo : lo + 128, :].astype(F32)
            )
            r.y2[c, lo : lo + 128, :] = y
            ym = y * m
            add_stats(acc, lo, 128, ym, ym * y, g)
        saves["y2"].start(c)

    s = Sum(p, r.ar2)
    s.start(rows_of(acc, 0, 384), counts)
    s.middle()
    up.sent(nc)
    down.sent(nc)
    t2 = s.finish()
    r.tot2[...] = t2

    acc[0:384, :] = jnp.zeros((384, 128), F32)
    r.gram[...] = jnp.zeros_like(r.gram)
    fill_tables(tab, 0, forward_rows(t2[:, :256], t2, 1, r.nr[...].astype(F32)))
    fill_tables(tab, 256, forward_rows(fold_frames(t2[:, 256:]), t2, 4, four(r.nn[...])))

    @loop(0, pairs)
    def _(i):
        for h in range(2):
            c = 2 * i + h
            g = grp[c]
            m = mask_of(g)
            u = r.y2[c, 0:256, :] * coef(tab, g, 0, 0, 256) + coef(tab, g, 1, 0, 256)
            act = silu(u) * m
            r.act2[c, 0:256, :] = act.astype(BF16)
            column_taps(act, r.x9, 1, h * CELLS)
            u = r.y2[c, 256:384, :] * coef(tab, g, 0, 256, 128) + coef(tab, g, 1, 256, 128)
            act = (silu(u) * m).astype(BF16)
            r.act2[c, 256:384, :] = act
            saves["act2"].start(c)
            add_sums(acc, 256, 128, act.astype(F32), g)
            add_gram(r.gram, act, g)
        for a in range(3):
            r.tt[256 * a : 256 * (a + 1), :] = dot(r.ws[256 * a : 256 * (a + 1), :], r.x9[0:768, :])
        for lo in range(0, 256, 128):
            for h in range(2):
                c = 2 * i + h
                g = grp[c]
                y = row_taps(
                    [r.tt[256 * a + lo : 256 * a + lo + 128, h * CELLS : (h + 1) * CELLS] for a in range(3)], 1
                )
                r.y3[c, lo : lo + 128, :] = y
                ym = y * mask_of(g)
                add_stats(acc, lo, 128, ym, ym * y, g)
        for h in range(2):
            saves["y3"].start(2 * i + h)

    s = Sum(p, r.ar3)
    s.start(jnp.concatenate([rows_of(acc, 0, 256), wide_sums(acc, r.gram, r.tall[...])], axis=1), counts)
    s.middle()
    t3 = s.finish()
    r.tot3[...] = t3

    ffeed = Feed(r.fcot, r.fcbuf, r.s_fc, nc, 0, 3)
    ffeed.prime()
    fdrain = Drain(r.fobuf, r.fout, r.s_fo, nc, 3)
    wdrain = Drain(r.dzwb, r.dzw_o, r.s_dzw, nc, 3)
    acc[...] = jnp.zeros_like(acc)
    fill_tables(tab, 0, forward_rows(t3[:, :256], t3, 1, r.ns[...].astype(F32)))
    fill_tables(
        r.tabw, 0,
        forward_rows(repeated(t3[:, 256:]), t3, 4, jnp.concatenate([r.nw[...].astype(F32)] * 4, axis=1)),
    )

    @loop(0, pairs)
    def _(i):
        for h in range(2):
            c = 2 * i + h
            g = grp[c]
            m = mask_of(g)
            for lo in range(0, 256, 128):
                u = r.y3[c, lo : lo + 128, :] * coef(tab, g, 0, lo, 128) + coef(tab, g, 1, lo, 128)
                r.acts[c, lo : lo + 128, :] = (silu(u) * m).astype(BF16)
            saves["acts"].start(c)
        act = jnp.concatenate([r.acts[2 * i], r.acts[2 * i + 1]], axis=1)
        for lo in range(0, 1024, 128):
            both = dot(r.we[lo : lo + 128, :], act)
            for h in range(2):
                g = grp[2 * i + h]
                y = both[:, h * CELLS : (h + 1) * CELLS]
                ym = y * mask_of(g)
                add_stats(acc, lo, 128, ym, ym * y, g)

    def fast_ends(lo_c, hi_c):
        @loop(lo_c, hi_c)
        def _(c):
            g = grp[c]
            m = mask_of(g)
            slot = ffeed.take(c)
            fdrain.room(c)
            wdrain.room(c)
            for lo in range(0, 512, 128):
                y = dot(r.ww[lo : lo + 128, :], r.act2[c, 256:384, :])
                v = y * coef(r.tabw, g, 0, lo, 128) + coef(r.tabw, g, 1, lo, 128)
                v = v + 0.5 * r.xe[c, 256 + lo : 384 + lo, :].astype(F32)
                o, slope = silu_and_slope(v)
                r.fobuf[slot, lo : lo + 128, :] = (o * m).astype(BF16)
                dz = r.fcbuf[slot, lo : lo + 128, :].astype(F32) * (0.5 * m) * slope
                r.dzwb[slot, lo : lo + 128, :] = dz
                add_stats(acc, 1024 + lo, 128, dz, dz * y, g)
            fdrain.put(c)
            wdrain.put(c)

    s = Sum(p, r.ar4)
    s.start(rows_of(acc, 0, 1024), counts)
    fast_ends(0, nc // 2)
    s.middle()
    fast_ends(nc // 2, nc)
    t4 = s.finish()
    r.tot4[...] = t4

    r.accf[...] = folded(rows_of(acc, 1024, 1536))
    for k in saves:
        saves[k].wait_all(nc)
    for c in wsaves:
        c.wait()
    fdrain.done()
    wdrain.done()


def middle(grp, acts_i, slow, scot, we, tot4, ne, sout, dze_o, rows_o, acc, tab, abuf, xbuf, cbuf, obuf, dzeb, s_a, s_x, s_c, s_o, s_z):
    nc = acts_i.shape[0]
    feeds = [Feed(src, buf, sem, nc, 0, 3) for src, buf, sem in ((acts_i, abuf, s_a), (slow, xbuf, s_x), (scot, cbuf, s_c))]
    drains = [Drain(obuf, sout, s_o, nc, 3), Drain(dzeb, dze_o, s_z, nc, 3)]
    for f in feeds:
        f.prime()
    acc[...] = jnp.zeros_like(acc)
    t4 = tot4[...]
    fill_tables(tab, 0, forward_rows(t4, t4, 1, ne[...].astype(F32)))

    @loop(0, nc)
    def _(c):
        g = grp[c]
        m = mask_of(g)
        slot = [f.take(c) for f in feeds][0]
        for d in drains:
            d.room(c)
        for lo in range(0, 1024, 128):
            y = dot(we[lo : lo + 128, :], abuf[slot])
            v = y * coef(tab, g, 0, lo, 128) + coef(tab, g, 1, lo, 128)
            v = v + 0.5 * xbuf[slot, lo : lo + 128, :].astype(F32)
            o, slope = silu_and_slope(v)
            obuf[slot, lo : lo + 128, :] = (o * m).astype(BF16)
            dz = cbuf[slot, lo : lo + 128, :].astype(F32) * (0.5 * m) * slope
            dzeb[slot, lo : lo + 128, :] = dz
            add_stats(acc, lo, 128, dz, dz * y, g)
        for d in drains:
            d.put(c)

    rows_o[...] = rows_of(acc, 0, 1024)
    for d in drains:
        d.done()


def back(na, nb, refs):
    r = refs
    grp = r.grp
    nc = r.acts_i.shape[0]
    pairs = nc // 2
    p = Peers(na, nb)
    b = p.b
    zfeed = Feed(r.dze_i, r.zbuf, r.s_z, nc, 1024, 3)
    zfeed.prime()
    loads = {
        k: Move(getattr(r, k + "_i"), getattr(r, k), getattr(r, "s_" + k))
        for k in KEPT
    }
    raw = {
        k: pltpu.make_async_copy(
            r.wrt_i.at[1024:1280] if k == "wrl" else getattr(r, k + "_i"), getattr(r, k), r.s_raw.at[i]
        )
        for i, k in enumerate(("wet", "we", "ww", "wwt", "wst", "wrl", "wnt"))
    }
    raw["we"].start()
    raw["wet"].start()
    loads["acts"].start_all(nc)
    loads["y3"].start_all(nc)
    for k in ("ww", "wwt", "wst", "wrl", "wnt"):
        raw[k].start()
    wfeed = Feed(r.dzw_i, r.wbuf, r.s_wb, nc)
    wfeed.prime()
    for k in ("act2", "y2", "act1", "y1"):
        loads[k].start_all(nc)

    def xload(i, slot):
        return pltpu.make_async_copy(r.slow.at[pl.ds(2 * i, 2)], r.xbuf.at[slot], r.s_x.at[slot])

    xload(0, 0).start()
    counts = counts_row(grp)
    acc, tab, tabb = r.acc, r.tab, r.tabb
    acc[...] = jnp.zeros_like(acc)
    t1, t2, t3, t4 = r.tot1[...], r.tot2[...], r.tot3[...], r.tot4[...]
    p.greet()
    s = Sum(p, r.ar5)
    s.start(jnp.concatenate([r.acce[...], r.accf[...]], axis=1), counts)

    @pl.when(b == 0)
    def _():
        r.dye[:, 512:768, :] = jnp.zeros((nc, 256, CELLS), BF16)

    @pl.when(b == nb - 1)
    def _():
        r.dye[:, 0:256, :] = jnp.zeros((nc, 256, CELLS), BF16)

    fill_tables(tabb, 0, forward_rows(t3[:, :256], t3, 1, r.ns[...].astype(F32)))
    s.middle()
    raw["we"].wait()
    raw["wet"].wait()
    t5 = s.finish()

    rows, pair = backward_rows(t4, t5[:, :1024], t4, 1, r.ne[...].astype(F32))
    fill_tables(tab, 0, rows)
    r.epair[...] = pair
    dye = r.dye2

    def dye_rows(c, lo, rows):
        return pl.ds(pl.multiple_of(c * 1024 + lo, 8), rows)

    @loop(0, nc)
    def _(c):
        g = grp[c]
        m = mask_of(g)
        loads["acts"].wait(c)
        loads["y3"].wait(c)
        slot = zfeed.take(c)
        for lo in range(0, 1024, 128):
            y = dot(r.we[lo : lo + 128, :], r.acts[c])
            z = r.zbuf[pl.ds(pl.multiple_of(slot * 1024 + lo, 8), 128), :]
            dy = z * coef(tab, g, 0, lo, 128)
            dy = dy + y * coef(tab, g, 1, lo, 128) + coef(tab, g, 2, lo, 128)
            dye[dye_rows(c, lo, 128), :] = (dy * m).astype(BF16)
        for lo in range(0, 256, 128):
            dx = dot(r.wet[lo : lo + 128, :], dye[dye_rows(c, 0, 1024), :])
            y = r.y3[c, lo : lo + 128, :]
            u = y * coef(tabb, g, 0, lo, 128) + coef(tabb, g, 1, lo, 128)
            dz = (0.5 * m) * silu_and_slope(u)[1] * dx
            r.dzs[c, lo : lo + 128, :] = dz
            add_stats(acc, lo, 128, dz, dz * y, g)

    s = Sum(p, r.ar6)
    s.start(rows_of(acc, 0, 256), counts)
    rows, pair = backward_rows(
        repeated(t3[:, 256:]), repeated(t5[:, 1024:]), t3, 4,
        jnp.concatenate([r.nw[...].astype(F32)] * 4, axis=1),
    )
    fill_tables(tab, 0, rows)
    r.wpair[...] = pair[:, :128]
    fill_tables(tabb, 256, forward_rows(fold_frames(t2[:, 256:]), t2, 4, four(r.nn[...])))
    r.wg[...] = jnp.zeros_like(r.wg)
    raw["ww"].wait()
    raw["wwt"].wait()

    def widen_back(lo_i, hi_i):
        @loop(lo_i, hi_i)
        def _(i):
            for h in range(2):
                c = 2 * i + h
                g = grp[c]
                m = mask_of(g)
                loads["act2"].wait(c)
                loads["y2"].wait(c)
                slot = wfeed.take(c)
                for lo in range(0, 512, 128):
                    y = dot(r.ww[lo : lo + 128, :], r.act2[c, 256:384, :])
                    dy = r.wbuf[slot, lo : lo + 128, :] * coef(tab, g, 0, lo, 128)
                    dy = dy + y * coef(tab, g, 1, lo, 128) + coef(tab, g, 2, lo, 128)
                    r.d9[lo : lo + 128, h * CELLS : (h + 1) * CELLS] = (dy * m).astype(BF16)
            act = jnp.concatenate([r.act2[2 * i + h, 256:384, :] for h in range(2)], axis=1)
            r.wg[...] += dot_nt(r.d9[0:512, :], act)
            both = dot(r.wwt[...], r.d9[0:512, :])
            for h in range(2):
                c = 2 * i + h
                g = grp[c]
                y = r.y2[c, 256:384, :]
                u = y * coef(tabb, g, 0, 256, 128) + coef(tabb, g, 1, 256, 128)
                dz = (0.5 * mask_of(g)) * silu_and_slope(u)[1] * both[:, h * CELLS : (h + 1) * CELLS]
                r.dzn[c] = dz
                add_stats(acc, 256, 128, dz, dz * y, g)

    gg = r.gg

    widen_back(0, pairs // 2)
    s.middle()
    widen_back(pairs // 2, pairs)
    t6 = s.finish()

    acc[0:256, :] = jnp.zeros((256, 128), F32)
    rows, pair = backward_rows(t3[:, :256], t6, t3, 1, r.ns[...].astype(F32))
    fill_tables(tab, 0, rows)
    r.spair[...] = pair
    fill_tables(tabb, 0, forward_rows(t2[:, :256], t2, 1, r.nr[...].astype(F32)))
    raw["wst"].wait()

    @loop(0, pairs)
    def _(i):
        for h in range(2):
            c = 2 * i + h
            g = grp[c]
            m = mask_of(g)
            dy = r.dzs[c] * coef(tab, g, 0, 0, 256) + r.y3[c] * coef(tab, g, 1, 0, 256)
            dy = (dy + coef(tab, g, 2, 0, 256)) * m
            r.y3[c] = dy
            column_taps(dy, r.d9, -1, h * CELLS)
        for a in range(3):
            both = dot(r.wst[256 * a : 256 * (a + 1), :], r.d9[0:768, :])
            for h in range(2):
                gg[768 * h + 256 * a : 768 * h + 256 * (a + 1), :] = both[:, h * CELLS : (h + 1) * CELLS]
        for lo in range(0, 256, 128):
            for h in range(2):
                c = 2 * i + h
                g = grp[c]
                dx = row_taps([gg[768 * h + 256 * a + lo : 768 * h + 256 * a + lo + 128, :] for a in range(3)], -1)
                y = r.y2[c, lo : lo + 128, :]
                u = y * coef(tabb, g, 0, lo, 128) + coef(tabb, g, 1, lo, 128)
                dz = (0.5 * mask_of(g)) * silu_and_slope(u)[1] * dx
                r.dzs[c, lo : lo + 128, :] = dz
                add_stats(acc, lo, 128, dz, dz * y, g)

    s = Sum(p, r.ar7)
    s.start(rows_of(acc, 0, 384), counts)
    gg[...] = jnp.zeros_like(gg)
    @loop(0, pairs)
    def _(i):
        act = jnp.concatenate([r.acts[2 * i + h] for h in range(2)], axis=1)
        for lo in range(0, 1024, 256):
            dy = jnp.concatenate([dye[dye_rows(2 * i + h, lo, 256), :] for h in range(2)], axis=1)
            gg[lo : lo + 256, :] += dot_nt(dy, act)

    s.middle()
    t7 = s.finish()

    acc[...] = jnp.zeros_like(acc)
    rows, pair = backward_rows(t2[:, :256], t7[:, :256], t2, 1, r.nr[...].astype(F32))
    fill_tables(tab, 0, rows)
    r.rpair[...] = pair
    dyr = r.dye
    up = Halo(p, 1, lambda c: dyr.at[c, 256:512], lambda c: dyr.at[c, 512:768], r.h3us, r.h3ur)
    down = Halo(p, -1, lambda c: dyr.at[c, 256:512], lambda c: dyr.at[c, 0:256], r.h3ds, r.h3dr)

    @loop(0, nc)
    def _(c):
        g = grp[c]
        m = mask_of(g)
        for lo in range(0, 256, 128):
            dy = r.dzs[c, lo : lo + 128, :] * coef(tab, g, 0, lo, 128)
            dy = dy + r.y2[c, lo : lo + 128, :] * coef(tab, g, 1, lo, 128)
            dy = (dy + coef(tab, g, 2, lo, 128)) * m
            dyr[c, 256 + lo : 384 + lo, :] = dy.astype(BF16)
        up.start(c)
        down.start(c)

    rows, pair = backward_rows(
        fold_frames(t2[:, 256:]), fold_frames(t7[:, 256:]), t2, 4, four(r.nn[...])
    )
    fill_tables(tab, 0, rows)
    r.npair[...] = pair
    fill_tables(tabb, 0, forward_rows(t1[:, :256], t1, 1, r.nl[...].astype(F32)))
    fill_tables(tabb, 256, forward_rows(fold_frames(t1[:, 256:]), t1, 4, four(r.nq[...])))
    r.ng[...] = jnp.zeros_like(r.ng)
    raw["wnt"].wait()
    raw["wrl"].wait()

    @loop(0, pairs)
    def _(i):
        for h in range(2):
            c = 2 * i + h
            g = grp[c]
            m = mask_of(g)
            loads["act1"].wait(c)
            loads["y1"].wait(c)
            dy = r.dzn[c] * coef(tab, g, 0, 0, 128) + r.y2[c, 256:384, :] * coef(tab, g, 1, 0, 128)
            dy = (dy + coef(tab, g, 2, 0, 128)) * m
            taps(dy, r.d9n, 128, -1)
            dx = dot(r.wnt[...], r.d9n[...])
            y = r.y1[c, 256:384, :]
            u = y * coef(tabb, g, 0, 256, 128) + coef(tabb, g, 1, 256, 128)
            dz = (0.5 * m) * silu_and_slope(u)[1] * dx
            r.y1[c, 256:384, :] = dz
            add_stats(acc, 256, 128, dz, dz * y, g)
            for lo in range(0, 1152, 384):
                r.ng[lo : lo + 384, :] += dot_nt(r.d9n[lo : lo + 384, :], r.act1[c, 256:384, :])
            taps(r.y3[c], r.d9, 256, -1, h * CELLS)
        act = jnp.concatenate([r.act2[2 * i + h, 0:256, :] for h in range(2)], axis=1)
        for lo in range(0, 2304, 256):
            gg[1024 + lo : 1280 + lo, :] += dot_nt(r.d9[lo : lo + 256, :], act)

    def xtake(i):
        slot = lax.rem(i, 2)

        @pl.when(i + 1 < pairs)
        def _():
            xload(i + 1, 1 - slot).start()

        xload(i, slot).wait()
        return slot

    def reducer_terms(i, slot, j):
        dy = jnp.concatenate([dyr[2 * i + h, 256 * j : 256 * (j + 1), :] for h in range(2)], axis=1)
        for cb in range(5):
            if cb < 4:
                x = [r.xbuf[slot, h, 256 * cb : 256 * (cb + 1), :] for h in range(2)]
            else:
                x = [r.act1[2 * i + h, 0:256, :] for h in range(2)]
            lo = (4608, 3328, 5888)[j] + 256 * cb
            gg[lo : lo + 256, :] += dot_nt(dy, jnp.concatenate(x, axis=1))

    @loop(0, pairs)
    def _(i):
        reducer_terms(i, xtake(i), 1)

    xload(0, 0).start()

    half = r.rc.shape[0]
    red = Reduce(
        na, nb, r.zbuf.at[0:half], dye.at[0:half], r.rc, r.rx, r.tail
    )
    for j in range(2):
        red.first(lambda mine, i: gg[half * mine + 256 * i : half * mine + 256 * (i + 1), :], j, 2)
    zsave = Move(r.y1, r.dz1_o, r.s_dz1)
    dsave = Move(dyr, r.dyr_o, r.s_dyr)

    def arrive(c):
        up.arrive(c)
        down.arrive(c)
        dsave.start(c)
        g = grp[c]
        m = mask_of(g)
        for lo in range(0, 256, 128):
            dx = dot(r.wrl[lo : lo + 128, :], dyr[c])
            y = r.y1[c, lo : lo + 128, :]
            u = y * coef(tabb, g, 0, lo, 128) + coef(tabb, g, 1, lo, 128)
            dz = (0.5 * m) * silu_and_slope(u)[1] * dx
            r.y1[c, lo : lo + 128, :] = dz
            add_stats(acc, lo, 128, dz, dz * y, g)
        zsave.start(c)

    def arrivals(lo_i, hi_i):
        @loop(lo_i, hi_i)
        def _(i):
            @loop(2 * i, 2 * i + 2)
            def _(c):
                arrive(c)

            slot = xtake(i)
            for j in (0, 2):
                reducer_terms(i, slot, j)

    stages = len(red.bits)
    cuts = [(pairs - 1) * (i + 1) // (stages + 1) for i in range(stages + 1)]
    arrivals(0, cuts[0])
    red.first_done()
    for n in range(stages):
        red.halve(n)
        arrivals(cuts[n], cuts[n + 1])
        red.halved()

    @loop(nc - 2, nc)
    def _(c):
        arrive(c)

    s = Sum(p, r.ar8)
    s.start(rows_of(acc, 0, 384), counts)
    red.along()
    slot = xtake(pairs - 1)
    for j in (0, 2):
        reducer_terms(pairs - 1, slot, j)
    s.middle()
    gsave = pltpu.make_async_copy(gg.at[4096:7168], r.gg_o, r.s_gg)
    gsave.start()

    def keep(q, piece):
        r.piece[q] = piece

    up.sent(nc)
    down.sent(nc)
    r.tot8[...] = s.finish()
    red.summed(keep)
    zsave.wait_all(nc)
    dsave.wait_all(nc)
    gsave.wait()


def ends(na, nb, refs):
    r = refs
    grp = r.grp
    nc = r.dz1_i.shape[0]
    p = Peers(na, nb)
    b = p.b
    tab, dyl, dyq, lg, qg = r.tab, r.dyl, r.dyq, r.lg, r.qg
    red = Reduce(na, nb, r.own, r.stage, r.rc, r.rx, r.tail[0:6])
    early, late = Gather(na, nb, r.oute, r.tail[6:12]), Gather(na, nb, r.outl, r.tail[12:18])
    dfeed = Feed(r.dz1_i, r.dbuf, r.s_d, nc, 0, 3)
    yfeed = Feed(r.y1_i, r.ybuf, r.s_y, nc, 0, 3)
    efeed = Feed(r.xe_i, r.ebuf, r.s_e, nc, 0, 3)
    gfeed = Feed(r.dyr_i, r.gbuf, r.s_g, nc, 0, 3)
    zfeed = Feed(r.dze_i, r.zbuf, r.s_z, nc, 0, 3)
    wfeed = Feed(r.dzw_i, r.wbuf, r.s_wb, nc, 0, 3)
    sdrain = Drain(r.obuf, r.sgrad, r.s_o, nc, 3)
    fdrain = Drain(r.fbuf, r.fgrad, r.s_f, nc, 3)
    for f in (dfeed, yfeed, efeed):
        f.prime()
    gload = pltpu.make_async_copy(r.gg_i, r.gg, r.s_raw.at[0])
    rload = pltpu.make_async_copy(r.wrt_i.at[0:1024], r.wr, r.s_raw.at[1])
    fload = pltpu.make_async_copy(r.wf_i, r.wf, r.s_raw.at[2])
    gload.start()
    for f in (gfeed, zfeed, wfeed):
        f.prime()
    rload.start()
    fload.start()
    pload = pltpu.make_async_copy(r.wp_i, r.wp, r.s_raw.at[3])
    pload.start()
    t8, t1 = r.tot8[...], r.tot1[...]
    rows, pair = backward_rows(t1[:, :256], t8[:, :256], t1, 1, r.nl[...].astype(F32))
    fill_tables(tab, 0, rows)
    r.lpair[...] = pair
    rows, pair = backward_rows(
        fold_frames(t1[:, 256:]), fold_frames(t8[:, 256:]), t1, 4, four(r.nq[...])
    )
    fill_tables(tab, 256, rows)
    r.qpair[...] = pair
    lat = Halo(p, -1, lambda c: r.prs.at[c], lambda c: r.prr.at[c], r.hls, r.hlr)
    up = Halo(p, 1, lambda c: dyq.at[c, 160:192], lambda c: dyq.at[c, 0:32], r.hus, r.hur)
    dyq[:, 32:64, :] = jnp.zeros((nc, 32, CELLS), BF16)
    dyq[:, 192:256, :] = jnp.zeros((nc, 64, CELLS), BF16)

    @pl.when(b == 0)
    def _():
        dyq[:, 0:32, :] = jnp.zeros((nc, 32, CELLS), BF16)

    @pl.when(b == nb - 1)
    def _():
        r.prr[...] = jnp.zeros_like(r.prr)

    lg[...] = jnp.zeros_like(lg)
    qg[...] = jnp.zeros_like(qg)
    pload.wait()
    p.greet()
    for q in range(2):
        early.put(q, r.piece[q])

    ahead = nc - nc // 3

    def lateral_back(lo_c, hi_c):
        @loop(lo_c, hi_c)
        def _(c):
            lateral_clip(c)

    def lateral_clip(c):
        g = grp[c]
        m = mask_of(g)
        slot = dfeed.take(c)
        yfeed.take(c)
        for lo in range(0, 384, 128):
            dy = r.dbuf[slot, lo : lo + 128, :] * coef(tab, g, 0, lo, 128)
            dy = dy + r.ybuf[slot, lo : lo + 128, :] * coef(tab, g, 1, lo, 128)
            dy = ((dy + coef(tab, g, 2, lo, 128)) * m).astype(BF16)
            if lo < 256:
                dyl[c, lo : lo + 128, :] = dy
            else:
                dyq[c, 64:192, :] = dy
        for lo in range(0, 256, 128):
            v = dot(r.wp[lo : lo + 128, 0:256], dyl[c]) + dot(r.wp[lo : lo + 128, 256:384], dyq[c, 64:192, :])
            r.prs[c, lo : lo + 128, :] = v.astype(BF16)

        @pl.when(c < ahead)
        def _():
            lat.start(c)

        up.start(c)
        efeed.take(c)
        dy = dyl[c, 0:256, :]
        lg[0:256, :] += dot_nt(dy, r.ebuf[slot, 0:256, :])
        lg[256:512, :] += dot_nt(dy, r.ebuf[slot, 256:512, :])
        lg[512:768, 0:128] += dot_nt(dy, r.ebuf[slot, 512:640, :])
        qg[...] += dot_nt(dyq[c, 64:192, :], r.ebuf[slot, 128:896, :])

    def block_of(mine, i):
        if mine == 0:
            return r.gg[256 * i : 256 * (i + 1), :]
        if i < 4:
            return r.gg[2048 + 256 * i : 2304 + 256 * i, :]
        return lg[256 * (i - 4) : 256 * (i - 3), :]

    stages = len(red.bits)
    lateral_back(0, nc // 4)
    gload.wait()
    red.first(block_of, 0, 2)
    lateral_back(nc // 4, nc)
    for j in range(3):
        lg[800 + 32 * j : 832 + 32 * j, 128:256] = sum(
            qg[32 * f : 32 * (f + 1), 128 * (f + j) : 128 * (f + j + 1)] for f in range(4)
        )
    for k in range(9):
        term = sum(
            r.ng[128 * k + 32 * f : 128 * k + 32 * (f + 1), 32 * f : 32 * (f + 1)] for f in range(4)
        )
        if k < 8:
            lg[768 + 32 * k : 800 + 32 * k, 0:32] = term
        else:
            lg[768:800, 128:160] = term
    lg[896:1024, 128:160] = sum(r.wg[128 * f : 128 * (f + 1), 32 * f : 32 * (f + 1)] for f in range(4))
    red.first(block_of, 1, 2)
    rload.wait()

    def slow_ends(lo_c, hi_c):
        @loop(lo_c, hi_c)
        def _(c):
            m = mask_of(grp[c])
            slot = gfeed.take(c)
            zfeed.take(c)
            sdrain.room(c)
            for lo in range(0, 1024, 128):
                dx = dot(r.wr[lo : lo + 128, :], r.gbuf[slot]) + r.zbuf[slot, lo : lo + 128, :]
                r.obuf[slot, lo : lo + 128, :] = (dx * m).astype(BF16)
            sdrain.put(c)

    cuts = [nc * i // (stages + 1) for i in range(stages + 2)]
    slow_ends(cuts[0], cuts[1])
    red.first_done()
    for n in range(stages):
        red.halve(n)
        slow_ends(cuts[n + 1], cuts[n + 2])
        red.halved()
    red.along()
    fload.wait()

    def fast_ends(lo_c, hi_c):
        @loop(lo_c, hi_c)
        def _(c):
            lat.arrive(c)
            up.arrive(c)
            m = mask_of(grp[c])
            slot = wfeed.take(c)
            fdrain.room(c)
            for lo in range(0, 512, 128):
                dx = dot(r.wf[lo : lo + 128, 0:256], dyl[c]) + dot(r.wf[lo : lo + 128, 256:512], dyq[c])
                dx = dx + r.wbuf[slot, lo : lo + 128, :]
                if lo >= 256:
                    dx = dx + r.prr[c, lo - 256 : lo - 128, :].astype(F32)
                r.fbuf[slot, lo : lo + 128, :] = (dx * m).astype(BF16)
            fdrain.put(c)

    early.gather(stages - 1)
    red.summed(late.put)

    @loop(ahead, nc)
    def _(c):
        lat.start(c)

    cuts = [ahead * i // (2 * stages) for i in range(2 * stages + 1)]
    for n in range(stages):
        fast_ends(cuts[2 * n], cuts[2 * n + 1])
        late.gather(stages - 1 - n)
        fast_ends(cuts[2 * n + 1], cuts[2 * n + 2])
        if n + 1 < stages:
            early.gather(stages - 2 - n)
    early.final()
    late.final()
    fast_ends(ahead, nc)
    sdrain.done()
    fdrain.done()
    lat.sent(nc)
    up.sent(nc)
    early.settle()
    late.settle()


def last(oe_i, ol_i, rp, spr, ep, lp, qp, np_, wp, *refs):
    big, grads, small, big_out = refs[:3], refs[3:10], refs[10:17], refs[17:20]
    bufs, made, (oe, ol, sem_in, sem_out, sem_a, sem_b) = refs[20:23], refs[23:30], refs[30:]
    nc = big[0].shape[0]
    rg, sg, eg, lg, qg, ng, wg = made

    def take(i, c):
        return pltpu.make_async_copy(big[i].at[c], bufs[i].at[c], sem_in.at[i, c])

    def give(i, c):
        return pltpu.make_async_copy(bufs[i].at[c], big_out[i].at[c], sem_out.at[i, c])

    def pass_on(i):
        @loop(0, nc)
        def _(c):
            take(i, c).wait()
            give(i, c).start()

    def hand(i):
        return pltpu.make_async_copy(made[i], grads[i], sem_b.at[i])

    ends_in = [pltpu.make_async_copy(s, d, sem_a.at[i]) for i, (s, d) in enumerate(((oe_i, oe), (ol_i, ol)))]
    for c in ends_in:
        c.start()
    for i in range(3):

        @loop(0, nc)
        def _(c):
            take(i, c).start()

    for c in ends_in:
        c.wait()
    for cb in range(5):
        for j in range(3):
            lo = (512, 3328, 1792)[j] + 256 * cb
            src = ol if j != 1 else oe
            if j == 1 and cb >= 3:
                src, lo = ol, 256 * (cb - 3)
            rg[j, :, 256 * cb : 256 * (cb + 1)] = src[lo : lo + 256, :].astype(F32)
    hand(0).start()
    pass_on(0)
    for k in range(9):
        sg[k] = oe[1024 + 256 * k : 1280 + 256 * k, :].astype(F32)
        at = 3840 + 32 * k if k < 8 else 3840
        ng[k] = (ol[at : at + 32, 0:32] if k < 8 else ol[at : at + 32, 128:160]).astype(F32)
    hand(1).start()
    hand(5).start()
    pass_on(1)
    for q in range(4):
        eg[256 * q : 256 * (q + 1), :] = oe[256 * q : 256 * (q + 1), :].astype(F32)
    for k in range(5):
        lo = 3072 + 256 * (k // 2)
        lg[k] = ol[lo : lo + 256, 128 * (k % 2) : 128 * (k % 2 + 1)].astype(F32)
    for j in range(3):
        qg[j] = ol[3872 + 32 * j : 3904 + 32 * j, 128:256].astype(F32)
    wg[...] = jnp.transpose(ol[3968:4096, 128:256].astype(F32))[0:32, :]
    for i in (2, 3, 4, 6):
        hand(i).start()
    pass_on(2)
    rpo, spo, epo, lpo, qpo, npo, wpo = small
    for src, dst in ((rp, rpo), (spr, spo), (ep, epo), (lp, lpo), (wp, wpo)):
        dst[...] = src[...]
    qpo[...] = qp[:, 0:32]
    npo[...] = np_[:, 0:32]
    for i in range(7):
        hand(i).wait()

    @loop(0, nc)
    def _(c):
        for i in range(3):
            give(i, c).wait()


def sds(shape, dtype):
    return jax.ShapeDtypeStruct(shape, dtype)


class Refs:
    pass


V, H, S = VM, pl.ANY, pltpu.SMEM


def call(body, na, nb, cid, ins, outs, scratch, sums, tail=()):
    names = [*ins, *outs, *scratch]
    shapes = [*scratch.values()]
    for width in sums.values():
        shapes += ar_scratch(na, nb, width)
    shapes += list(tail)

    def kernel(*refs):
        r = Refs()
        for name, ref in zip(names, refs):
            setattr(r, name, ref)
        at = len(names)
        for name in sums:
            setattr(r, name, refs[at : at + 8])
            at += 8
        r.tail = refs[at:]
        body(na, nb, r)

    got = pl.pallas_call(
        kernel,
        name=body.__name__,
        out_shape=tuple(x[1] for x in outs.values()),
        in_specs=[pl.BlockSpec(memory_space=x[0]) for x in ins.values()],
        out_specs=tuple(pl.BlockSpec(memory_space=x[0]) for x in outs.values()),
        scratch_shapes=shapes,
        compiler_params=pltpu.CompilerParams(
            collective_id=cid, has_side_effects=True, vmem_limit_bytes=LIMIT
        ),
    )(*[x[1] for x in ins.values()])
    r = Refs()
    for name, v in zip(outs, got):
        setattr(r, name, v)
    return r


def pick(source, names, end="_o"):
    return {k + "_i": (H, getattr(source, k + end)) for k in names}


def each_of(names, value, start=""):
    return {start + k: value for k in names}


KEPT = ("acts", "y3", "act2", "y2", "act1", "y1")


def build(na, nb):
    def body(
        slow_in, fast_in, clip_group, reducer, spatial, expand, lateral, squeeze, narrow, widening,
        reducer_norm, spatial_norm, expand_norm, lateral_norm, squeeze_norm, narrow_norm, widening_norm,
        slow_cot, fast_cot,
    ):
        nc = slow_in.shape[0]
        dma = pltpu.SemaphoreType.DMA
        slow = slow_in.reshape(nc, 1024, CELLS)
        first_norms = dict(nl=(V, lateral_norm), nq=(V, squeeze_norm))
        norms = first_norms | dict(
            nr=(V, reducer_norm), nn=(V, narrow_norm), ns=(V, spatial_norm), ne=(V, expand_norm), nw=(V, widening_norm)
        )

        def act(c, dtype):
            return sds((nc, c, CELLS), dtype)

        def vact(c, dtype):
            return VM((nc, c, CELLS), dtype)

        def two(c, dtype):
            return VM((2, c, CELLS), dtype)

        def three(c, dtype):
            return VM((3, c, CELLS), dtype)

        def tab(k, c):
            return VM((3, k, c, 128), F32)

        each, slots = dma((nc,)), dma((2,))
        state = dict(
            xe=(896, BF16), y1=(384, F32), act1=(384, BF16), y2=(384, F32), act2=(384, BF16), y3=(256, F32), acts=(256, BF16)
        )
        turns = dict(
            wrt=(1280, 768), wst=(768, 768), wet=(256, 1024), wwt=(128, 512), wnt=(128, 1152), wf=(512, 512),
            wp=(256, 384), ww=(512, 128),
        )
        fw = call(
            forward, na, nb, 1,
            dict(
                grp=(S, clip_group), fast=(H, fast_in.reshape(nc, 512, CELLS)), slow=(H, slow),
                fcot=(H, fast_cot.reshape(nc, 512, CELLS)),
                reducer=(H, reducer.reshape(768, 1280)), spatial=(H, spatial), expand=(H, expand),
                lateral=(V, lateral), squeeze=(V, squeeze), narrow=(V, narrow), widening=(V, jnp.transpose(widening)),
            ) | norms,
            dict(fout=(H, act(512, BF16)))
            | {k + "_o": (H, act(*v)) for k, v in state.items()}
            | dict(dzw_o=(H, act(512, F32)), accf=(V, sds((8, 128), F32)))
            | {k + "_o": (H, sds(v, BF16)) for k, v in turns.items()}
            | dict(
                tot1=(V, sds((8, 384), F32)), tot2=(V, sds((8, 384), F32)), tot3=(V, sds((8, 384), F32)),
                tot4=(V, sds((8, 1024), F32)),
            ),
            {k: vact(*v) for k, v in state.items()}
            | {k: VM(v, BF16) for k, v in turns.items()}
            | dict(
                wr=VM((768, 1280), BF16), sp=VM((9, 256, 256), BF16), we=VM((1024, 256), BF16),
                wa=VM((384, 896), BF16), tall=VM((128, 128), BF16), gram=VM((3, 128, 128), F32),
                ws=VM((768, 768), BF16), tt=VM((768, 2 * CELLS), F32), wn=VM((128, 1152), BF16),
                su=vact(256, BF16), sd=vact(256, BF16), ru=vact(256, BF16), rd=vact(256, BF16),
                xbuf=two(1024, BF16), fcbuf=three(512, BF16), fobuf=three(512, BF16), dzwb=three(512, F32),
                tab=tab(2, 384), tabw=tab(2, 512), acc=VM((1536, 128), F32), x9=VM((1152, 2 * CELLS), BF16),
                s_raw=dma((3,)), s_w=dma((8,)), s_own=each,
            )
            | each_of(("h1us", "h1ur", "h1ds", "h1dr", "h2us", "h2ur", "h2ds", "h2dr"), each)
            | dict(s_x=slots) | each_of(("fc", "fo", "dzw"), dma((3,)), "s_")
            | {"s_" + k: each for k in state},
            dict(ar1=384, ar2=384, ar3=384, ar4=1024),
        )
        hbm, vmem = pl.BlockSpec(memory_space=H), pl.BlockSpec(memory_space=V)
        slow_out, dze, acce = pl.pallas_call(
            middle,
            name="middle",
            out_shape=(act(1024, BF16), act(1024, F32), sds((8, 1024), F32)),
            in_specs=[pl.BlockSpec(memory_space=S)] + [hbm] * 3 + [vmem] * 3,
            out_specs=(hbm, hbm, vmem),
            scratch_shapes=[VM((1024, 128), F32), tab(2, 1024)]
            + [three(c, d) for c, d in ((256, BF16), (1024, BF16), (1024, BF16), (1024, BF16), (1024, F32))]
            + [dma((3,))] * 5,
            compiler_params=pltpu.CompilerParams(vmem_limit_bytes=LIMIT),
        )(clip_group, fw.acts_o, slow, slow_cot.reshape(nc, 1024, CELLS), expand, fw.tot4, expand_norm)
        half = 2048
        piece = half // (na * nb)
        tots = dict(
            tot1=(V, fw.tot1), tot2=(V, fw.tot2), tot3=(V, fw.tot3), tot4=(V, fw.tot4)
        )
        bw = call(
            back, na, nb, 2,
            dict(
                grp=(S, clip_group), slow=(H, slow), we_i=(H, expand), dze_i=(H, dze), acce=(V, acce), accf=(V, fw.accf)
            )
            | pick(fw, KEPT + ("dzw", "wet", "wwt", "wst", "wrt", "wnt", "ww")) | tots | norms,
            dict(
                dz1_o=(H, act(384, F32)), dyr_o=(H, act(768, BF16)), gg_o=(H, sds((3072, 256), F32)),
                piece=(V, sds((2, piece, 256), BF16)),
                ng=(V, sds((1152, 128), F32)), wg=(V, sds((512, 128), F32)), tot8=(V, sds((8, 384), F32)),
                epair=(V, sds((2, 1024), F32)), spair=(V, sds((2, 256), F32)), rpair=(V, sds((2, 256), F32)),
                wpair=(V, sds((2, 128), F32)), npair=(V, sds((2, 128), F32)),
            ),
            {k: vact(*state[k]) for k in KEPT}
            | dict(
                wet=VM((256, 1024), BF16), we=VM((1024, 256), BF16), ww=VM((512, 128), BF16),
                wwt=VM((128, 512), BF16), wst=VM((768, 768), BF16), wrl=VM((256, 768), BF16), wnt=VM((128, 1152), BF16),
                zbuf=VM((3 * 1024, CELLS), F32), wbuf=two(512, F32), xbuf=VM((2, 2, 1024, CELLS), BF16),
                dye=vact(768, BF16), dye2=VM((nc * 1024, CELLS), BF16), rx=VM((2, half // 2, 256), BF16), rc=VM((half, 256), BF16),
                dzs=vact(256, F32), dzn=vact(128, F32), gg=VM((7168, 256), F32),
                tab=tab(3, 1024), tabb=tab(2, 384), acc=VM((384, 128), F32),
                d9=VM((2304, 2 * CELLS), BF16), d9n=VM((1152, CELLS), BF16), s_raw=dma((7,)), s_gg=dma,
            )
            | each_of(KEPT + ("dz1", "dyr"), each, "s_")
            | each_of(("h3us", "h3ur", "h3ds", "h3dr"), each)
            | each_of(("wb", "x"), slots, "s_")
            | dict(s_z=dma((3,))),
            dict(ar5=1152, ar6=256, ar7=384, ar8=384),
            reduce_sems(na, nb, 2),
        )
        en = call(
            ends, na, nb, 3,
            dict(
                grp=(S, clip_group), piece=(V, bw.piece), dze_i=(H, dze),
                ng=(V, bw.ng), wg=(V, bw.wg), tot8=(V, bw.tot8), tot1=(V, fw.tot1),
            )
            | pick(bw, ("dz1", "dyr", "gg")) | pick(fw, ("y1", "xe", "dzw", "wrt", "wf", "wp")) | first_norms,
            dict(
                sgrad=(H, act(1024, BF16)), fgrad=(H, act(512, BF16)), oute=(V, sds((2 * half, 256), BF16)),
                outl=(V, sds((2 * half, 256), BF16)), lpair=(V, sds((2, 256), F32)), qpair=(V, sds((2, 128), F32)),
            ),
            dict(
                gg=VM((3072, 256), F32), wr=VM((1024, 768), BF16), wf=VM((512, 512), BF16), wp=VM((256, 384), BF16),
                tab=tab(3, 384), dyl=vact(256, BF16), prs=vact(256, BF16), prr=vact(256, BF16), dyq=vact(256, BF16),
                lg=VM((1024, 256), F32), qg=VM((128, 768), F32), own=VM((half, 256), F32),
                stage=VM((half, 256), BF16), rc=VM((half, 256), BF16), rx=VM((2, half // 2, 256), BF16),
                dbuf=three(384, F32), ybuf=three(384, F32), ebuf=three(896, BF16), gbuf=three(768, BF16),
                zbuf=three(1024, F32), wbuf=three(512, F32), obuf=three(1024, BF16), fbuf=three(512, BF16),
                s_raw=dma((4,)),
            )
            | each_of(("d", "y", "e", "g", "z", "wb", "o", "f"), dma((3,)), "s_")
            | each_of(("hls", "hlr", "hus", "hur"), each),
            {},
            reduce_sems(na, nb, 2) + gather_sems(na, nb) * 2,
        )
        shapes = [
            (3, 256, 1280), (9, 256, 256), (1024, 256), (5, 256, 128), (3, 32, 128), (9, 32, 32), (32, 128),
            (2, 256), (2, 256), (2, 1024), (2, 256), (2, 32), (2, 32), (2, 128),
        ]
        big = (fw.fout, en.sgrad, en.fgrad)
        got = pl.pallas_call(
            last,
            name="last",
            out_shape=tuple(sds(v, F32) for v in shapes) + tuple(sds(v.shape, BF16) for v in big),
            in_specs=[hbm] * 2 + [vmem] * 7 + [hbm] * 3,
            out_specs=tuple([hbm] * 7 + [vmem] * 7 + [hbm] * 3),
            scratch_shapes=[VM(v.shape, BF16) for v in big]
            + [VM(v, F32) for v in shapes[:7]]
            + [VM((2 * half, 256), BF16), VM((2 * half, 256), BF16)]
            + [dma((3, nc)), dma((3, nc)), dma((2,)), dma((7,))],
            compiler_params=pltpu.CompilerParams(vmem_limit_bytes=LIMIT),
        )(en.oute, en.outl, bw.rpair, bw.spair, bw.epair, en.lpair, en.qpair, bw.npair, bw.wpair, *big)
        fast_out, slow_grad, fast_grad = got[len(shapes) :]
        return (
            slow_out.reshape(slow_in.shape), fast_out.reshape(fast_in.shape),
            slow_grad.reshape(slow_in.shape), fast_grad.reshape(fast_in.shape),
            *got[:6], jnp.transpose(got[6]), *got[7 : len(shapes)],
        )

    return body


def solution(mesh):
    body = build(mesh.shape["clip"], mesh.shape["tm"])
    big = P("clip", "tm", None, None)
    return jax.shard_map(
        body,
        mesh=mesh,
        in_specs=(big, big, P("clip")) + (P(),) * 14 + (big, big),
        out_specs=(big,) * 4 + (P(),) * 14,
        check_vma=False,
    )
```

```python
import functools

import jax
import jax.numpy as jnp
from jax import lax
from jax.experimental import pallas as pl
from jax.experimental.pallas import tpu as pltpu
from jax.sharding import PartitionSpec as P

MESH = pl.DeviceIdType.MESH
F32, BF16 = jnp.float32, jnp.bfloat16
SIDE = 16
CELLS = SIDE * SIDE
EPS = 1e-05
VM = pltpu.VMEM
LIMIT = 63 * 1024 * 1024 + 256 * 1024


def dot(a, b):
    return lax.dot_general(a, b, (((1,), (0,)), ((), ())), preferred_element_type=F32)


def dot_nt(a, b):
    return lax.dot_general(a, b, (((1,), (1,)), ((), ())), preferred_element_type=F32)


def side_of(g):
    return jnp.where(g == 0, SIDE * 5 // 8, jnp.where(g == 1, SIDE * 7 // 8, SIDE))


def mask_of(g):
    cell = lax.broadcasted_iota(jnp.int32, (1, CELLS), 1)
    side = side_of(g)
    return jnp.where(((cell >> 4) < side) & ((cell & 15) < side), 1.0, 0.0).astype(F32)


def counts_row(grp):
    lane = lax.broadcasted_iota(jnp.int32, (1, 128), 1)
    total = jnp.zeros((1, 128), F32)
    for c in range(grp.shape[0]):
        side = side_of(grp[c])
        total = total + jnp.where(lane == grp[c], (side * side).astype(F32), 0.0)
    return total


def add_stats(acc, lo, rows, first, second, g):
    lane = lax.broadcasted_iota(jnp.int32, (1, 128), 1)
    one = jnp.sum(first[:, :128] + first[:, 128:], axis=1, keepdims=True)
    two = jnp.sum(second[:, :128] + second[:, 128:], axis=1, keepdims=True)
    acc[lo : lo + rows, :] += jnp.where(lane == g, one, 0.0) + jnp.where(lane == g + 3, two, 0.0)


def add_sums(acc, lo, rows, value, g):
    lane = lax.broadcasted_iota(jnp.int32, (1, 128), 1)
    one = jnp.sum(value[:, :128] + value[:, 128:], axis=1, keepdims=True)
    acc[lo : lo + rows, :] += jnp.where(lane == g, one, 0.0)


def add_gram(gram, act, g):
    term = dot_nt(act, act)
    for k in range(3):
        gram[k] += jnp.where(g == k, term, 0.0)


def wide_sums(acc, gram, tall):
    w = tall.astype(F32)
    exact = dict(precision=lax.Precision.HIGHEST, preferred_element_type=F32)
    one = jnp.dot(rows_of(acc, 256, 384), w, **exact)
    block = lax.broadcasted_iota(jnp.int32, (128, 128), 0) >> 5
    same = block == (lax.broadcasted_iota(jnp.int32, (128, 128), 1) >> 5)
    two = [
        jnp.sum(w * jnp.dot(jnp.where(same, gram[k], 0.0), w, **exact), axis=0, keepdims=True)
        for k in range(3)
    ]
    return jnp.concatenate([one[:3, :]] + two + [jnp.zeros((2, 128), F32)], axis=0)


def ar_scratch(na, nb, width):
    dma = pltpu.SemaphoreType.DMA
    return [
        VM((8, width), F32),
        VM((na, 8, width), F32),
        VM((8, width), F32),
        VM((nb, 8, width), F32),
        dma((na - 1,)),
        dma((na - 1,)),
        dma((nb - 1,)),
        dma((nb - 1,)),
    ]


class Peers:
    def __init__(self, na, nb):
        self.na, self.nb = na, nb
        self.a, self.b = lax.axis_index("clip"), lax.axis_index("tm")
        self.along_a = [(lax.rem(self.a + d, na), self.b) for d in range(1, na)]
        self.along_b = [(self.a, lax.rem(self.b + d, nb)) for d in range(1, nb)]
        self.bar = pltpu.get_barrier_semaphore()
        for peer in self.along_a + self.along_b:
            pl.semaphore_signal(self.bar, inc=1, device_id=peer, device_id_type=MESH)

    def greet(self):
        pl.semaphore_wait(self.bar, self.na - 1 + self.nb - 1)


class Sum:
    def __init__(self, peers, refs):
        self.p = peers
        self.mine, self.bufa, self.part, self.bufb, self.sa, self.ra, self.sb, self.rb = refs

    def copies(self, src, buf, slot, ss, rs, peers):
        return [
            pltpu.make_async_remote_copy(
                src, buf.at[slot], ss.at[i], rs.at[i], device_id=peer, device_id_type=MESH
            )
            for i, peer in enumerate(peers)
        ]

    def start(self, rows, counts):
        row = lax.broadcasted_iota(jnp.int32, (8, 128), 0)
        head = jnp.where(row == 6, counts, rows[:, :128])
        value = jnp.concatenate([head, rows[:, 128:]], axis=1)
        self.mine[...] = value
        self.bufa[self.p.a] = value
        self.first = self.copies(self.mine, self.bufa, self.p.a, self.sa, self.ra, self.p.along_a)
        for c in self.first:
            c.start()

    def middle(self):
        for c in self.first:
            c.wait()
        total = self.bufa[0]
        for i in range(1, self.p.na):
            total = total + self.bufa[i]
        self.part[...] = total
        self.bufb[self.p.b] = total
        self.second = self.copies(self.part, self.bufb, self.p.b, self.sb, self.rb, self.p.along_b)
        for c in self.second:
            c.start()

    def finish(self):
        for c in self.second:
            c.wait()
        total = self.bufb[0]
        for i in range(1, self.p.nb):
            total = total + self.bufb[i]
        return total


def rows_of(acc, lo, hi):
    return jnp.transpose(acc[lo:hi, :])[:8, :]


def folded(rows):
    return sum(rows[:, 128 * f : 128 * (f + 1)] for f in range(rows.shape[1] // 128))


def repeated(rows):
    return jnp.concatenate([rows] * 4, axis=1)


class Halo:
    def __init__(self, peers, step, src, dst, ss, rs):
        self.src, self.dst, self.ss, self.rs = src, dst, ss, rs
        to = peers.b + step
        self.sends = (to >= 0) & (to < peers.nb)
        source = peers.b - step
        self.gets = (source >= 0) & (source < peers.nb)
        self.peer = (peers.a, lax.rem(to + peers.nb, peers.nb))

    def copy(self, c):
        return pltpu.make_async_remote_copy(
            self.src(c), self.dst(c), self.ss.at[c], self.rs.at[c],
            device_id=self.peer, device_id_type=MESH,
        )

    def start(self, c):
        @pl.when(self.sends)
        def _():
            self.copy(c).start()

    def arrive(self, c):
        @pl.when(self.gets)
        def _():
            self.copy(c).wait_recv()

    def sent(self, nc):
        @pl.when(self.sends)
        def _():
            @pl.loop(0, nc)
            def _(c):
                self.copy(c).wait_send()


class Move:
    def __init__(self, src, dst, sem):
        self.src, self.dst, self.sem = src, dst, sem

    def copy(self, c):
        return pltpu.make_async_copy(self.src.at[c], self.dst.at[c], self.sem.at[c])

    def start(self, c):
        self.copy(c).start()

    def wait(self, c):
        self.copy(c).wait()

    def start_all(self, nc):
        @pl.loop(0, nc)
        def _(c):
            self.start(c)

    def wait_all(self, nc):
        @pl.loop(0, nc)
        def _(c):
            self.wait(c)


class Feed:
    def __init__(self, src, buf, sem, nc, rows=0, slots=2):
        self.src, self.buf, self.sem, self.nc, self.rows, self.slots = src, buf, sem, nc, rows, slots

    def copy(self, c, slot):
        at = pl.ds(pl.multiple_of(slot * self.rows, 8), self.rows) if self.rows else slot
        return pltpu.make_async_copy(self.src.at[c], self.buf.at[at], self.sem.at[slot])

    def prime(self):
        for c in range(self.slots - 1):
            self.copy(c, c).start()

    def take(self, c):
        slot = lax.rem(c, self.slots)
        ahead = self.slots - 1

        @pl.when(c + ahead < self.nc)
        def _():
            self.copy(c + ahead, lax.rem(c + ahead, self.slots)).start()

        self.copy(c, slot).wait()
        return slot


class Drain:
    def __init__(self, buf, dst, sem, nc, slots=2):
        self.buf, self.dst, self.sem, self.nc, self.slots = buf, dst, sem, nc, slots

    def copy(self, c, slot):
        return pltpu.make_async_copy(self.buf.at[slot], self.dst.at[c], self.sem.at[slot])

    def room(self, c):
        slot = lax.rem(c, self.slots)

        @pl.when(c >= self.slots)
        def _():
            self.copy(c - self.slots, slot).wait()

        return slot

    def put(self, c):
        self.copy(c, lax.rem(c, self.slots)).start()

    def done(self):
        for c in range(max(0, self.nc - self.slots), self.nc):
            self.copy(c, c % self.slots).wait()


def fold_frames(total):
    out = total + pltpu.roll(total, 32, 1)
    return out + pltpu.roll(out, 64, 1)


def moments(total, counts, frames):
    out = []
    for g in range(3):
        n = counts[6:7, g : g + 1] * float(frames)
        mean = total[g : g + 1, :] / n
        var = total[g + 3 : g + 4, :] / n - mean * mean
        out.append((n, mean, lax.rsqrt(var + EPS)))
    return out


def fill_tables(tab, base, rows_list):
    width = rows_list[0][0].shape[1]
    count = len(rows_list[0])
    rows = [rows_list[g][k] for g in range(3) for k in range(count)]
    rows = rows + [jnp.zeros((1, width), F32)] * (128 - len(rows))
    cols = jnp.transpose(jnp.concatenate(rows, axis=0))
    for g in range(3):
        for k in range(count):
            i = g * count + k
            tab[g, k, base : base + width, :] = jnp.broadcast_to(cols[:, i : i + 1], (width, 128))


def forward_rows(total, counts, frames, pair):
    out = []
    for n, mean, r in moments(total, counts, frames):
        gain = 0.5 * (pair[0:1, :] * r)
        out.append((gain, 0.5 * pair[1:2, :] - mean * gain))
    return out


def backward_rows(total, grads, counts, frames, pair):
    out, two_all, one_all = [], 0.0, 0.0
    for g, (n, mean, r) in enumerate(moments(total, counts, frames)):
        one = grads[g : g + 1, :]
        two = r * (grads[g + 3 : g + 4, :] - mean * one)
        c0 = pair[0:1, :] * r
        slope = c0 * r * two / n
        out.append((c0, -slope, slope * mean - c0 * one / n))
        two_all, one_all = two_all + two, one_all + one
    return out, jnp.concatenate([two_all, one_all], axis=0)


def wide(v):
    return jnp.concatenate([v, v], axis=1)


def coef(tab, g, k, lo, rows):
    return wide(tab[g, k, lo : lo + rows, :])


def silu(w):
    return w * (1.0 + jnp.tanh(w))


def silu_and_slope(w):
    p = 1.0 + jnp.tanh(w)
    o = w * p
    return o, p + o * (2.0 - p)


def taps(x, dst, rows, sign, at=0):
    cell = lax.broadcasted_iota(jnp.int32, (1, CELLS), 1)
    row, col = cell >> 4, cell & 15
    for k in range(9):
        di, dl = sign * (k // 3 - 1), sign * (k % 3 - 1)
        step = SIDE * di + dl
        if step == 0:
            dst[k * rows : (k + 1) * rows, at : at + CELLS] = x.astype(BF16)
            continue
        moved = pltpu.roll(x, (-step) % CELLS, 1)
        ok = (row + di >= 0) & (row + di < SIDE) & (col + dl >= 0) & (col + dl < SIDE)
        dst[k * rows : (k + 1) * rows, at : at + CELLS] = jnp.where(ok, moved, 0.0).astype(BF16)


def column_taps(x, dst, sign, at):
    col = lax.broadcasted_iota(jnp.int32, (1, CELLS), 1) & 15
    rows = x.shape[0]
    for b in range(3):
        dl = sign * (b - 1)
        moved = x
        if dl:
            moved = jnp.where((col + dl >= 0) & (col + dl < SIDE), pltpu.roll(x, (-dl) % CELLS, 1), 0.0)
        dst[rows * b : rows * (b + 1), at : at + CELLS] = moved.astype(BF16)


def row_taps(terms, sign):
    row = lax.broadcasted_iota(jnp.int32, (1, CELLS), 1) >> 4
    total = terms[1]
    for a in (0, 2):
        di = sign * (a - 1)
        moved = pltpu.roll(terms[a], (-SIDE * di) % CELLS, 1)
        total = total + jnp.where((row + di >= 0) & (row + di < SIDE), moved, 0.0)
    return total


def loop(lo, hi):
    return pl.loop(lo, hi)


def spread_lanes(at, lanes):
    row = lax.broadcasted_iota(jnp.int32, (32, lanes), 0)
    lane = lax.broadcasted_iota(jnp.int32, (32, lanes), 1)
    hit = ((lane & 31) == row) if at is None else (lane == row + at)
    return jnp.where(hit, 1.0, 0.0).astype(BF16)


def dot_tn(a, b):
    return lax.dot_general(a, b, (((0,), (0,)), ((), ())), preferred_element_type=F32)


def turned(v):
    return jnp.transpose(v.astype(F32)).astype(BF16)


def four(pair):
    return dot(pair, spread_lanes(None, 128))


def first_weights(lateral, squeeze, wa):
    wa[...] = jnp.zeros_like(wa)
    for k in range(5):
        wa[0:256, 128 * k : 128 * (k + 1)] = lateral[k]
    for f in range(4):
        for j in range(3):
            wa[256 + 32 * f : 288 + 32 * f, 128 * (f + 1 + j) : 128 * (f + 2 + j)] = squeeze[j]


def more_weights(reducer, spatial, expand, lateral, squeeze, narrow, widening, ws, wn, ww, wrt, wst, wet, wwt, wnt, wf, wp, tall):
    lane = lax.broadcasted_iota(jnp.int32, (1, 128), 1) >> 5
    row = lax.broadcasted_iota(jnp.int32, (128, 1), 0) >> 5
    every = spread_lanes(None, 128)
    for k in range(9):
        a, b = 256 * (k // 3), 256 * (k % 3)
        ws[a : a + 256, b : b + 256] = spatial[k]
        wst[a : a + 256, b : b + 256] = turned(spatial[k])
        there, back = dot(narrow[k], every), dot_tn(narrow[k], every)
        for f in range(4):
            at = slice(32 * f, 32 * (f + 1))
            wn[at, 128 * k : 128 * (k + 1)] = jnp.where(lane == f, there, 0.0).astype(BF16)
            wnt[at, 128 * k : 128 * (k + 1)] = jnp.where(lane == f, back, 0.0).astype(BF16)
    wide_w = dot_tn(widening[...], every)
    tall_w = dot_tn(every, widening[...])
    tall[...] = tall_w.astype(BF16)
    for f in range(4):
        ww[128 * f : 128 * (f + 1), :] = jnp.where(lane == f, wide_w, 0.0).astype(BF16)
        wwt[:, 128 * f : 128 * (f + 1)] = jnp.where(row == f, tall_w, 0.0).astype(BF16)
    for q in range(4):
        wet[:, 256 * q : 256 * (q + 1)] = turned(expand[256 * q : 256 * (q + 1), :])
    for j in range(3):
        for q in range(5):
            wrt[256 * q : 256 * (q + 1), 256 * j : 256 * (j + 1)] = turned(
                reducer[256 * j : 256 * (j + 1), 256 * q : 256 * (q + 1)]
            )
    wf[...] = jnp.zeros_like(wf)
    for f, k in ((0, 2), (1, 3), (2, 4)):
        wf[128 * f : 128 * (f + 1), 0:256] = turned(lateral[k])
    place = (0, 2, 3, 4, 5)
    for f in range(4):
        wf[128 * f : 128 * (f + 1), 256:512] = sum(
            dot_tn(squeeze[j], spread_lanes(32 * place[f + 2 - j], 256)) for j in range(3) if f + 2 - j < 5
        ).astype(BF16)
    wp[...] = jnp.zeros_like(wp)
    for f in range(2):
        wp[128 * f : 128 * (f + 1), 0:256] = turned(lateral[f])
    wp[128:256, 256:384] = dot_tn(squeeze[0], spread_lanes(0, 128)).astype(BF16)


class Tree:
    def __init__(self, na, nb, half):
        self.na, self.nb, self.half = na, nb, half
        self.a, self.b = lax.axis_index("clip"), lax.axis_index("tm")
        self.bits = [i for i in range(1, 16) if (1 << i) < na]
        self.order = (self.bits, self.bits[::-1])
        self.h = lax.rem(self.a, 2)
        self.at, self.count, self.pending = [0, half // 2], half // 2, []

    def peer(self, bit):
        step = 1 << bit
        mine = lax.rem(self.a // step, 2)
        return (self.a + step * (1 - 2 * mine), self.b), mine

    def rows(self, start, count):
        return pl.ds(pl.multiple_of(start, 8), count)

    def copy(self, src, dst, ss, rs, peer):
        return pltpu.make_async_remote_copy(
            src, dst, ss, rs, device_id=peer, device_id_type=MESH
        )

    def descend(self):
        for n in range(len(self.bits)):
            self.count //= 2
            for p in range(2):
                self.at[p] = self.at[p] + self.peer(self.order[p][n])[1] * self.count
        self.piece = self.count // self.nb


class Reduce(Tree):
    def __init__(self, na, nb, own, stage, rc, rx, sems):
        super().__init__(na, nb, own.shape[0])
        self.own, self.stage, self.rc, self.rx = own, stage, rc, rx
        self.cs, self.cr, self.ss, self.sr, self.zs, self.zr = sems
        self.first_copies = []

    def first(self, block_of, j, chunks):
        self.chunks = chunks
        size = self.half // chunks
        peer, _ = self.peer(0)
        rows = slice(j * size, (j + 1) * size)
        for i in range(j * size // 256, (j + 1) * size // 256):
            at = slice(256 * i, 256 * (i + 1))
            for mine in range(2):

                @pl.when(self.h == mine)
                def _():
                    self.own[at, :] = block_of(mine, i)
                    self.stage[at, :] = block_of(1 - mine, i).astype(BF16)

        c = self.copy(self.stage.at[rows], self.rc.at[rows], self.cs.at[j], self.cr.at[j], peer)
        c.start()
        self.first_copies.append(c)

    def first_done(self):
        size = self.half // self.chunks
        for j, c in enumerate(self.first_copies):
            c.wait()

            @pl.loop(j * size // 256, (j + 1) * size // 256)
            def _(i):
                at = pl.ds(pl.multiple_of(i * 256, 256), 256)
                self.own[at, :] = self.own[at, :] + self.rc[at, :].astype(F32)

        self.base = 0

    def cast(self, start, count):
        step = min(count, 256)

        @pl.loop(0, count // step)
        def _(i):
            at = self.rows(start + i * step, step)
            self.rc[at, :] = self.own[at, :].astype(BF16)

    def halve(self, n):
        half = self.count // 2
        self.pending = []
        for p in range(2):
            peer, mine = self.peer(self.order[p][n])
            away = self.at[p] + (1 - mine) * half
            self.at[p] = self.at[p] + mine * half
            self.cast(away, half)
            c = self.copy(
                self.rc.at[self.rows(away, half)], self.rx.at[p, self.base : self.base + half],
                self.ss.at[p, n], self.sr.at[p, n], peer,
            )
            c.start()
            self.pending.append(c)
        self.count = half

    def halved(self):
        half = self.count
        step = min(half, 256)
        for p in range(2):
            self.pending[p].wait()

            @pl.loop(0, half // step)
            def _(i):
                at = self.rows(self.at[p] + i * step, step)
                got = self.rx[p, self.rows(self.base + i * step, step), :]
                self.own[at, :] = self.own[at, :] + got.astype(F32)

        self.base += half

    def along(self):
        self.piece = self.count // self.nb
        self.pending = [[], []]
        for p in range(2):
            self.cast(self.at[p], self.count)
            for d in range(1, self.nb):
                to = lax.rem(self.b + d, self.nb)
                c = self.copy(
                    self.rc.at[self.rows(self.at[p] + to * self.piece, self.piece)],
                    self.rx.at[p, self.rows(self.base + self.b * self.piece, self.piece)],
                    self.zs.at[p, d - 1], self.zr.at[p, d - 1], (self.a, to),
                )
                c.start()
                self.pending[p].append(c)

    def summed(self, put):
        for p in range(2):
            for c in self.pending[p]:
                c.wait()
            start = self.at[p] + self.b * self.piece
            total = self.own[self.rows(start, self.piece), :]
            for d in range(1, self.nb):
                source = lax.rem(self.b + d, self.nb)
                total = total + self.rx[
                    p, self.rows(self.base + source * self.piece, self.piece), :
                ].astype(F32)
            put(p, total.astype(BF16))


class Gather(Tree):
    def __init__(self, na, nb, out, sems):
        super().__init__(na, nb, out.shape[0] // 2)
        self.out = out
        self.gs, self.gr, self.hs, self.hr, self.ks, self.kr = sems
        self.descend()

    def place(self, start):
        return self.h * self.half + start

    def put(self, p, piece):
        at = self.rows(self.place(self.at[p] + self.b * self.piece), self.piece)
        self.out[at, :] = piece
        for d in range(1, self.nb):
            c = self.copy(
                self.out.at[at], self.out.at[at], self.gs.at[p, d - 1], self.gr.at[p, d - 1],
                (self.a, lax.rem(self.b + d, self.nb)),
            )
            c.start()
            self.pending.append(c)

    def settle(self):
        pending, self.pending = self.pending, []
        for c in pending:
            c.wait()

    def gather(self, n):
        self.settle()
        for p in range(2):
            peer, mine = self.peer(self.order[p][n])
            at = self.rows(self.place(self.at[p]), self.count)
            c = self.copy(self.out.at[at], self.out.at[at], self.hs.at[p, n], self.hr.at[p, n], peer)
            c.start()
            self.pending.append(c)
            self.at[p] = self.at[p] - mine * self.count
        self.count *= 2

    def final(self):
        pending, self.pending = self.pending, []
        peer, _ = self.peer(0)
        for p in range(2):
            pending[p].wait()
            at = self.rows(self.place(self.at[p]), self.count)
            c = self.copy(self.out.at[at], self.out.at[at], self.ks.at[p], self.kr.at[p], peer)
            c.start()
            self.pending.append(c)


def reduce_sems(na, nb, chunks):
    dma = pltpu.SemaphoreType.DMA
    shapes = [(chunks,), (2, max(1, na.bit_length() - 2)), (2, nb - 1)]
    return [dma(shape) for shape in shapes for _ in range(2)]


def gather_sems(na, nb):
    dma = pltpu.SemaphoreType.DMA
    shapes = [(2, nb - 1), (2, max(1, na.bit_length() - 2)), (2,)]
    return [dma(shape) for shape in shapes for _ in range(2)]


def forward(na, nb, refs):
    r = refs
    grp = r.grp
    nc = r.fast.shape[0]
    pairs = nc // 2
    p = Peers(na, nb)
    b = p.b
    own = Move(r.fast, r.xe.at[:, 256:768], r.s_own)
    own.start_all(nc)
    raw = [
        pltpu.make_async_copy(src, dst, r.s_raw.at[i])
        for i, (src, dst) in enumerate(((r.reducer, r.wr), (r.spatial, r.sp), (r.expand, r.we)))
    ]
    for c in raw:
        c.start()
    xfeed = Feed(r.slow, r.xbuf, r.s_x, nc)
    xfeed.prime()
    up = Halo(p, 1, lambda c: r.fast.at[c, 256:512], lambda c: r.xe.at[c, 0:256], r.h1us, r.h1ur)
    down = Halo(p, -1, lambda c: r.fast.at[c, 0:128], lambda c: r.xe.at[c, 768:896], r.h1ds, r.h1dr)
    saves = {
        k: Move(getattr(r, k), getattr(r, k + "_o"), getattr(r, "s_" + k))
        for k in ("xe", "y1", "act1", "y2", "act2", "y3", "acts")
    }

    @pl.when(b == 0)
    def _():
        r.xe[:, 0:256, :] = jnp.zeros((nc, 256, CELLS), BF16)
        r.ru[...] = jnp.zeros_like(r.ru)

    @pl.when(b == nb - 1)
    def _():
        r.xe[:, 768:896, :] = jnp.zeros((nc, 128, CELLS), BF16)
        r.rd[...] = jnp.zeros_like(r.rd)

    p.greet()

    @loop(0, nc)
    def _(c):
        up.start(c)
        down.start(c)

    counts = counts_row(grp)
    acc = r.acc
    acc[...] = jnp.zeros_like(acc)
    first_weights(r.lateral, r.squeeze, r.wa)
    for c in raw:
        c.wait()
    more_weights(
        r.wr, r.sp, r.we, r.lateral, r.squeeze, r.narrow, r.widening,
        r.ws, r.wn, r.ww, r.wrt, r.wst, r.wet, r.wwt, r.wnt, r.wf, r.wp, r.tall,
    )
    wsaves = [
        pltpu.make_async_copy(getattr(r, k), getattr(r, k + "_o"), r.s_w.at[i])
        for i, k in enumerate(("wrt", "wst", "wet", "wwt", "wnt", "wf", "wp", "ww"))
    ]
    for c in wsaves:
        c.start()

    @loop(0, nc)
    def _(c):
        own.wait(c)
        up.arrive(c)
        down.arrive(c)
        saves["xe"].start(c)
        g = grp[c]
        m = mask_of(g)
        for lo in range(0, 384, 128):
            y = dot(r.wa[lo : lo + 128, :], r.xe[c])
            r.y1[c, lo : lo + 128, :] = y
            ym = y * m
            add_stats(acc, lo, 128, ym, ym * y, g)
        saves["y1"].start(c)

    s = Sum(p, r.ar1)
    s.start(rows_of(acc, 0, 384), counts)
    s.middle()
    up.sent(nc)
    down.sent(nc)
    t1 = s.finish()
    r.tot1[...] = t1

    tab = r.tab
    acc[0:384, :] = jnp.zeros((384, 128), F32)
    fill_tables(tab, 0, forward_rows(t1[:, :256], t1, 1, r.nl[...].astype(F32)))
    fill_tables(tab, 256, forward_rows(fold_frames(t1[:, 256:]), t1, 4, four(r.nq[...])))
    up = Halo(p, 1, lambda c: r.su.at[c], lambda c: r.ru.at[c], r.h2us, r.h2ur)
    down = Halo(p, -1, lambda c: r.sd.at[c], lambda c: r.rd.at[c], r.h2ds, r.h2dr)

    @loop(0, nc)
    def _(c):
        g = grp[c]
        m = mask_of(g)
        for lo in range(0, 256, 128):
            u = r.y1[c, lo : lo + 128, :] * coef(tab, g, 0, lo, 128) + coef(tab, g, 1, lo, 128)
            r.act1[c, lo : lo + 128, :] = (silu(u) * m).astype(BF16)
        slot = xfeed.take(c)
        for j, dst in enumerate((r.su, r.sd, r.y2)):
            for lo in range(0, 256, 128):
                r0 = 256 * (0, 2, 1)[j] + lo
                v = dot(r.wr[r0 : r0 + 128, :1024], r.xbuf[slot]) + dot(
                    r.wr[r0 : r0 + 128, 1024:], r.act1[c, 0:256, :]
                )
                dst[c, lo : lo + 128, :] = v.astype(dst.dtype)
        up.start(c)
        down.start(c)

    @loop(0, nc)
    def _(c):
        g = grp[c]
        m = mask_of(g)
        u = r.y1[c, 256:384, :] * coef(tab, g, 0, 256, 128) + coef(tab, g, 1, 256, 128)
        act = silu(u) * m
        r.act1[c, 256:384, :] = act.astype(BF16)
        saves["act1"].start(c)
        taps(act, r.x9, 128, 1)
        y = dot(r.wn[...], r.x9[0:1152, 0:CELLS])
        r.y2[c, 256:384, :] = y
        ym = y * m
        add_stats(acc, 256, 128, ym, ym * y, g)

    @loop(0, nc)
    def _(c):
        up.arrive(c)
        down.arrive(c)
        g = grp[c]
        m = mask_of(g)
        for lo in range(0, 256, 128):
            y = (
                r.y2[c, lo : lo + 128, :]
                + r.ru[c, lo : lo + 128, :].astype(F32)
                + r.rd[c, lo : lo + 128, :].astype(F32)
            )
            r.y2[c, lo : lo + 128, :] = y
            ym = y * m
            add_stats(acc, lo, 128, ym, ym * y, g)
        saves["y2"].start(c)

    s = Sum(p, r.ar2)
    s.start(rows_of(acc, 0, 384), counts)
    s.middle()
    up.sent(nc)
    down.sent(nc)
    t2 = s.finish()
    r.tot2[...] = t2

    acc[0:384, :] = jnp.zeros((384, 128), F32)
    r.gram[...] = jnp.zeros_like(r.gram)
    fill_tables(tab, 0, forward_rows(t2[:, :256], t2, 1, r.nr[...].astype(F32)))
    fill_tables(tab, 256, forward_rows(fold_frames(t2[:, 256:]), t2, 4, four(r.nn[...])))

    @loop(0, pairs)
    def _(i):
        for h in range(2):
            c = 2 * i + h
            g = grp[c]
            m = mask_of(g)
            u = r.y2[c, 0:256, :] * coef(tab, g, 0, 0, 256) + coef(tab, g, 1, 0, 256)
            act = silu(u) * m
            r.act2[c, 0:256, :] = act.astype(BF16)
            column_taps(act, r.x9, 1, h * CELLS)
            u = r.y2[c, 256:384, :] * coef(tab, g, 0, 256, 128) + coef(tab, g, 1, 256, 128)
            act = (silu(u) * m).astype(BF16)
            r.act2[c, 256:384, :] = act
            saves["act2"].start(c)
            add_sums(acc, 256, 128, act.astype(F32), g)
            add_gram(r.gram, act, g)
        for a in range(3):
            r.tt[256 * a : 256 * (a + 1), :] = dot(r.ws[256 * a : 256 * (a + 1), :], r.x9[0:768, :])
        for lo in range(0, 256, 128):
            for h in range(2):
                c = 2 * i + h
                g = grp[c]
                y = row_taps(
                    [r.tt[256 * a + lo : 256 * a + lo + 128, h * CELLS : (h + 1) * CELLS] for a in range(3)], 1
                )
                r.y3[c, lo : lo + 128, :] = y
                ym = y * mask_of(g)
                add_stats(acc, lo, 128, ym, ym * y, g)
        for h in range(2):
            saves["y3"].start(2 * i + h)

    s = Sum(p, r.ar3)
    s.start(jnp.concatenate([rows_of(acc, 0, 256), wide_sums(acc, r.gram, r.tall[...])], axis=1), counts)
    s.middle()
    t3 = s.finish()
    r.tot3[...] = t3

    ffeed = Feed(r.fcot, r.fcbuf, r.s_fc, nc, 0, 3)
    ffeed.prime()
    fdrain = Drain(r.fobuf, r.fout, r.s_fo, nc, 3)
    wdrain = Drain(r.dzwb, r.dzw_o, r.s_dzw, nc, 3)
    acc[...] = jnp.zeros_like(acc)
    fill_tables(tab, 0, forward_rows(t3[:, :256], t3, 1, r.ns[...].astype(F32)))
    fill_tables(
        r.tabw, 0,
        forward_rows(repeated(t3[:, 256:]), t3, 4, jnp.concatenate([r.nw[...].astype(F32)] * 4, axis=1)),
    )

    @loop(0, pairs)
    def _(i):
        for h in range(2):
            c = 2 * i + h
            g = grp[c]
            m = mask_of(g)
            for lo in range(0, 256, 128):
                u = r.y3[c, lo : lo + 128, :] * coef(tab, g, 0, lo, 128) + coef(tab, g, 1, lo, 128)
                r.acts[c, lo : lo + 128, :] = (silu(u) * m).astype(BF16)
            saves["acts"].start(c)
        act = jnp.concatenate([r.acts[2 * i], r.acts[2 * i + 1]], axis=1)
        for lo in range(0, 1024, 128):
            both = dot(r.we[lo : lo + 128, :], act)
            for h in range(2):
                g = grp[2 * i + h]
                y = both[:, h * CELLS : (h + 1) * CELLS]
                ym = y * mask_of(g)
                add_stats(acc, lo, 128, ym, ym * y, g)

    def fast_ends(lo_c, hi_c):
        @loop(lo_c, hi_c)
        def _(c):
            g = grp[c]
            m = mask_of(g)
            slot = ffeed.take(c)
            fdrain.room(c)
            wdrain.room(c)
            for lo in range(0, 512, 128):
                y = dot(r.ww[lo : lo + 128, :], r.act2[c, 256:384, :])
                v = y * coef(r.tabw, g, 0, lo, 128) + coef(r.tabw, g, 1, lo, 128)
                v = v + 0.5 * r.xe[c, 256 + lo : 384 + lo, :].astype(F32)
                o, slope = silu_and_slope(v)
                r.fobuf[slot, lo : lo + 128, :] = (o * m).astype(BF16)
                dz = r.fcbuf[slot, lo : lo + 128, :].astype(F32) * (0.5 * m) * slope
                r.dzwb[slot, lo : lo + 128, :] = dz
                add_stats(acc, 1024 + lo, 128, dz, dz * y, g)
            fdrain.put(c)
            wdrain.put(c)

    s = Sum(p, r.ar4)
    s.start(rows_of(acc, 0, 1024), counts)
    fast_ends(0, nc // 2)
    s.middle()
    fast_ends(nc // 2, nc)
    t4 = s.finish()
    r.tot4[...] = t4

    r.accf[...] = folded(rows_of(acc, 1024, 1536))
    for k in saves:
        saves[k].wait_all(nc)
    for c in wsaves:
        c.wait()
    fdrain.done()
    wdrain.done()


def middle(grp, acts_i, slow, scot, we, tot4, ne, sout, dze_o, rows_o, acc, tab, abuf, xbuf, cbuf, obuf, dzeb, s_a, s_x, s_c, s_o, s_z):
    nc = acts_i.shape[0]
    feeds = [Feed(src, buf, sem, nc, 0, 3) for src, buf, sem in ((acts_i, abuf, s_a), (slow, xbuf, s_x), (scot, cbuf, s_c))]
    drains = [Drain(obuf, sout, s_o, nc, 3), Drain(dzeb, dze_o, s_z, nc, 3)]
    for f in feeds:
        f.prime()
    acc[...] = jnp.zeros_like(acc)
    t4 = tot4[...]
    fill_tables(tab, 0, forward_rows(t4, t4, 1, ne[...].astype(F32)))

    @loop(0, nc)
    def _(c):
        g = grp[c]
        m = mask_of(g)
        slot = [f.take(c) for f in feeds][0]
        for d in drains:
            d.room(c)
        for lo in range(0, 1024, 128):
            y = dot(we[lo : lo + 128, :], abuf[slot])
            v = y * coef(tab, g, 0, lo, 128) + coef(tab, g, 1, lo, 128)
            v = v + 0.5 * xbuf[slot, lo : lo + 128, :].astype(F32)
            o, slope = silu_and_slope(v)
            obuf[slot, lo : lo + 128, :] = (o * m).astype(BF16)
            dz = cbuf[slot, lo : lo + 128, :].astype(F32) * (0.5 * m) * slope
            dzeb[slot, lo : lo + 128, :] = dz
            add_stats(acc, lo, 128, dz, dz * y, g)
        for d in drains:
            d.put(c)

    rows_o[...] = rows_of(acc, 0, 1024)
    for d in drains:
        d.done()


def back(na, nb, refs):
    r = refs
    grp = r.grp
    nc = r.acts_i.shape[0]
    pairs = nc // 2
    p = Peers(na, nb)
    b = p.b
    zfeed = Feed(r.dze_i, r.zbuf, r.s_z, nc, 1024, 3)
    zfeed.prime()
    loads = {
        k: Move(getattr(r, k + "_i"), getattr(r, k), getattr(r, "s_" + k))
        for k in KEPT
    }
    raw = {
        k: pltpu.make_async_copy(
            r.wrt_i.at[1024:1280] if k == "wrl" else getattr(r, k + "_i"), getattr(r, k), r.s_raw.at[i]
        )
        for i, k in enumerate(("wet", "we", "ww", "wwt", "wst", "wrl", "wnt"))
    }
    raw["we"].start()
    raw["wet"].start()
    loads["acts"].start_all(nc)
    loads["y3"].start_all(nc)
    for k in ("ww", "wwt", "wst", "wrl", "wnt"):
        raw[k].start()
    wfeed = Feed(r.dzw_i, r.wbuf, r.s_wb, nc)
    wfeed.prime()
    for k in ("act2", "y2", "act1", "y1"):
        loads[k].start_all(nc)

    def xload(i, slot):
        return pltpu.make_async_copy(r.slow.at[pl.ds(2 * i, 2)], r.xbuf.at[slot], r.s_x.at[slot])

    xload(0, 0).start()
    counts = counts_row(grp)
    acc, tab, tabb = r.acc, r.tab, r.tabb
    acc[...] = jnp.zeros_like(acc)
    t1, t2, t3, t4 = r.tot1[...], r.tot2[...], r.tot3[...], r.tot4[...]
    p.greet()
    s = Sum(p, r.ar5)
    s.start(jnp.concatenate([r.acce[...], r.accf[...]], axis=1), counts)

    @pl.when(b == 0)
    def _():
        r.dye[:, 512:768, :] = jnp.zeros((nc, 256, CELLS), BF16)

    @pl.when(b == nb - 1)
    def _():
        r.dye[:, 0:256, :] = jnp.zeros((nc, 256, CELLS), BF16)

    fill_tables(tabb, 0, forward_rows(t3[:, :256], t3, 1, r.ns[...].astype(F32)))
    s.middle()
    raw["we"].wait()
    raw["wet"].wait()
    t5 = s.finish()

    rows, pair = backward_rows(t4, t5[:, :1024], t4, 1, r.ne[...].astype(F32))
    fill_tables(tab, 0, rows)
    r.epair[...] = pair
    dye = r.dye2

    def dye_rows(c, lo, rows):
        return pl.ds(pl.multiple_of(c * 1024 + lo, 8), rows)

    @loop(0, nc)
    def _(c):
        g = grp[c]
        m = mask_of(g)
        loads["acts"].wait(c)
        loads["y3"].wait(c)
        slot = zfeed.take(c)
        for lo in range(0, 1024, 128):
            y = dot(r.we[lo : lo + 128, :], r.acts[c])
            z = r.zbuf[pl.ds(pl.multiple_of(slot * 1024 + lo, 8), 128), :]
            dy = z * coef(tab, g, 0, lo, 128)
            dy = dy + y * coef(tab, g, 1, lo, 128) + coef(tab, g, 2, lo, 128)
            dye[dye_rows(c, lo, 128), :] = (dy * m).astype(BF16)
        for lo in range(0, 256, 128):
            dx = dot(r.wet[lo : lo + 128, :], dye[dye_rows(c, 0, 1024), :])
            y = r.y3[c, lo : lo + 128, :]
            u = y * coef(tabb, g, 0, lo, 128) + coef(tabb, g, 1, lo, 128)
            dz = (0.5 * m) * silu_and_slope(u)[1] * dx
            r.dzs[c, lo : lo + 128, :] = dz
            add_stats(acc, lo, 128, dz, dz * y, g)

    s = Sum(p, r.ar6)
    s.start(rows_of(acc, 0, 256), counts)
    rows, pair = backward_rows(
        repeated(t3[:, 256:]), repeated(t5[:, 1024:]), t3, 4,
        jnp.concatenate([r.nw[...].astype(F32)] * 4, axis=1),
    )
    fill_tables(tab, 0, rows)
    r.wpair[...] = pair[:, :128]
    fill_tables(tabb, 256, forward_rows(fold_frames(t2[:, 256:]), t2, 4, four(r.nn[...])))
    r.wg[...] = jnp.zeros_like(r.wg)
    raw["ww"].wait()
    raw["wwt"].wait()

    def widen_back(lo_i, hi_i):
        @loop(lo_i, hi_i)
        def _(i):
            for h in range(2):
                c = 2 * i + h
                g = grp[c]
                m = mask_of(g)
                loads["act2"].wait(c)
                loads["y2"].wait(c)
                slot = wfeed.take(c)
                for lo in range(0, 512, 128):
                    y = dot(r.ww[lo : lo + 128, :], r.act2[c, 256:384, :])
                    dy = r.wbuf[slot, lo : lo + 128, :] * coef(tab, g, 0, lo, 128)
                    dy = dy + y * coef(tab, g, 1, lo, 128) + coef(tab, g, 2, lo, 128)
                    r.d9[lo : lo + 128, h * CELLS : (h + 1) * CELLS] = (dy * m).astype(BF16)
            act = jnp.concatenate([r.act2[2 * i + h, 256:384, :] for h in range(2)], axis=1)
            r.wg[...] += dot_nt(r.d9[0:512, :], act)
            both = dot(r.wwt[...], r.d9[0:512, :])
            for h in range(2):
                c = 2 * i + h
                g = grp[c]
                y = r.y2[c, 256:384, :]
                u = y * coef(tabb, g, 0, 256, 128) + coef(tabb, g, 1, 256, 128)
                dz = (0.5 * mask_of(g)) * silu_and_slope(u)[1] * both[:, h * CELLS : (h + 1) * CELLS]
                r.dzn[c] = dz
                add_stats(acc, 256, 128, dz, dz * y, g)

    gg = r.gg

    widen_back(0, pairs // 2)
    s.middle()
    widen_back(pairs // 2, pairs)
    t6 = s.finish()

    acc[0:256, :] = jnp.zeros((256, 128), F32)
    rows, pair = backward_rows(t3[:, :256], t6, t3, 1, r.ns[...].astype(F32))
    fill_tables(tab, 0, rows)
    r.spair[...] = pair
    fill_tables(tabb, 0, forward_rows(t2[:, :256], t2, 1, r.nr[...].astype(F32)))
    raw["wst"].wait()

    @loop(0, pairs)
    def _(i):
        for h in range(2):
            c = 2 * i + h
            g = grp[c]
            m = mask_of(g)
            dy = r.dzs[c] * coef(tab, g, 0, 0, 256) + r.y3[c] * coef(tab, g, 1, 0, 256)
            dy = (dy + coef(tab, g, 2, 0, 256)) * m
            r.y3[c] = dy
            column_taps(dy, r.d9, -1, h * CELLS)
        for a in range(3):
            both = dot(r.wst[256 * a : 256 * (a + 1), :], r.d9[0:768, :])
            for h in range(2):
                gg[768 * h + 256 * a : 768 * h + 256 * (a + 1), :] = both[:, h * CELLS : (h + 1) * CELLS]
        for lo in range(0, 256, 128):
            for h in range(2):
                c = 2 * i + h
                g = grp[c]
                dx = row_taps([gg[768 * h + 256 * a + lo : 768 * h + 256 * a + lo + 128, :] for a in range(3)], -1)
                y = r.y2[c, lo : lo + 128, :]
                u = y * coef(tabb, g, 0, lo, 128) + coef(tabb, g, 1, lo, 128)
                dz = (0.5 * mask_of(g)) * silu_and_slope(u)[1] * dx
                r.dzs[c, lo : lo + 128, :] = dz
                add_stats(acc, lo, 128, dz, dz * y, g)

    s = Sum(p, r.ar7)
    s.start(rows_of(acc, 0, 384), counts)
    gg[...] = jnp.zeros_like(gg)
    @loop(0, pairs)
    def _(i):
        act = jnp.concatenate([r.acts[2 * i + h] for h in range(2)], axis=1)
        for lo in range(0, 1024, 256):
            dy = jnp.concatenate([dye[dye_rows(2 * i + h, lo, 256), :] for h in range(2)], axis=1)
            gg[lo : lo + 256, :] += dot_nt(dy, act)

    s.middle()
    t7 = s.finish()

    acc[...] = jnp.zeros_like(acc)
    rows, pair = backward_rows(t2[:, :256], t7[:, :256], t2, 1, r.nr[...].astype(F32))
    fill_tables(tab, 0, rows)
    r.rpair[...] = pair
    dyr = r.dye
    up = Halo(p, 1, lambda c: dyr.at[c, 256:512], lambda c: dyr.at[c, 512:768], r.h3us, r.h3ur)
    down = Halo(p, -1, lambda c: dyr.at[c, 256:512], lambda c: dyr.at[c, 0:256], r.h3ds, r.h3dr)

    @loop(0, nc)
    def _(c):
        g = grp[c]
        m = mask_of(g)
        for lo in range(0, 256, 128):
            dy = r.dzs[c, lo : lo + 128, :] * coef(tab, g, 0, lo, 128)
            dy = dy + r.y2[c, lo : lo + 128, :] * coef(tab, g, 1, lo, 128)
            dy = (dy + coef(tab, g, 2, lo, 128)) * m
            dyr[c, 256 + lo : 384 + lo, :] = dy.astype(BF16)
        up.start(c)
        down.start(c)

    rows, pair = backward_rows(
        fold_frames(t2[:, 256:]), fold_frames(t7[:, 256:]), t2, 4, four(r.nn[...])
    )
    fill_tables(tab, 0, rows)
    r.npair[...] = pair
    fill_tables(tabb, 0, forward_rows(t1[:, :256], t1, 1, r.nl[...].astype(F32)))
    fill_tables(tabb, 256, forward_rows(fold_frames(t1[:, 256:]), t1, 4, four(r.nq[...])))
    r.ng[...] = jnp.zeros_like(r.ng)
    raw["wnt"].wait()
    raw["wrl"].wait()

    @loop(0, pairs)
    def _(i):
        for h in range(2):
            c = 2 * i + h
            g = grp[c]
            m = mask_of(g)
            loads["act1"].wait(c)
            loads["y1"].wait(c)
            dy = r.dzn[c] * coef(tab, g, 0, 0, 128) + r.y2[c, 256:384, :] * coef(tab, g, 1, 0, 128)
            dy = (dy + coef(tab, g, 2, 0, 128)) * m
            taps(dy, r.d9n, 128, -1)
            dx = dot(r.wnt[...], r.d9n[...])
            y = r.y1[c, 256:384, :]
            u = y * coef(tabb, g, 0, 256, 128) + coef(tabb, g, 1, 256, 128)
            dz = (0.5 * m) * silu_and_slope(u)[1] * dx
            r.y1[c, 256:384, :] = dz
            add_stats(acc, 256, 128, dz, dz * y, g)
            for lo in range(0, 1152, 384):
                r.ng[lo : lo + 384, :] += dot_nt(r.d9n[lo : lo + 384, :], r.act1[c, 256:384, :])
            taps(r.y3[c], r.d9, 256, -1, h * CELLS)
        act = jnp.concatenate([r.act2[2 * i + h, 0:256, :] for h in range(2)], axis=1)
        for lo in range(0, 2304, 256):
            gg[1024 + lo : 1280 + lo, :] += dot_nt(r.d9[lo : lo + 256, :], act)

    def xtake(i):
        slot = lax.rem(i, 2)

        @pl.when(i + 1 < pairs)
        def _():
            xload(i + 1, 1 - slot).start()

        xload(i, slot).wait()
        return slot

    def reducer_terms(i, slot, j):
        dy = jnp.concatenate([dyr[2 * i + h, 256 * j : 256 * (j + 1), :] for h in range(2)], axis=1)
        for cb in range(5):
            if cb < 4:
                x = [r.xbuf[slot, h, 256 * cb : 256 * (cb + 1), :] for h in range(2)]
            else:
                x = [r.act1[2 * i + h, 0:256, :] for h in range(2)]
            lo = (4608, 3328, 5888)[j] + 256 * cb
            gg[lo : lo + 256, :] += dot_nt(dy, jnp.concatenate(x, axis=1))

    @loop(0, pairs)
    def _(i):
        reducer_terms(i, xtake(i), 1)

    xload(0, 0).start()

    half = r.rc.shape[0]
    red = Reduce(
        na, nb, r.zbuf.at[0:half], dye.at[0:half], r.rc, r.rx, r.tail
    )
    for j in range(2):
        red.first(lambda mine, i: gg[half * mine + 256 * i : half * mine + 256 * (i + 1), :], j, 2)
    zsave = Move(r.y1, r.dz1_o, r.s_dz1)
    dsave = Move(dyr, r.dyr_o, r.s_dyr)

    def arrive(c):
        up.arrive(c)
        down.arrive(c)
        dsave.start(c)
        g = grp[c]
        m = mask_of(g)
        for lo in range(0, 256, 128):
            dx = dot(r.wrl[lo : lo + 128, :], dyr[c])
            y = r.y1[c, lo : lo + 128, :]
            u = y * coef(tabb, g, 0, lo, 128) + coef(tabb, g, 1, lo, 128)
            dz = (0.5 * m) * silu_and_slope(u)[1] * dx
            r.y1[c, lo : lo + 128, :] = dz
            add_stats(acc, lo, 128, dz, dz * y, g)
        zsave.start(c)

    def arrivals(lo_i, hi_i):
        @loop(lo_i, hi_i)
        def _(i):
            @loop(2 * i, 2 * i + 2)
            def _(c):
                arrive(c)

            slot = xtake(i)
            for j in (0, 2):
                reducer_terms(i, slot, j)

    stages = len(red.bits)
    cuts = [(pairs - 1) * (i + 1) // (stages + 1) for i in range(stages + 1)]
    arrivals(0, cuts[0])
    red.first_done()
    for n in range(stages):
        red.halve(n)
        arrivals(cuts[n], cuts[n + 1])
        red.halved()

    @loop(nc - 2, nc)
    def _(c):
        arrive(c)

    s = Sum(p, r.ar8)
    s.start(rows_of(acc, 0, 384), counts)
    red.along()
    slot = xtake(pairs - 1)
    for j in (0, 2):
        reducer_terms(pairs - 1, slot, j)
    s.middle()
    gsave = pltpu.make_async_copy(gg.at[4096:7168], r.gg_o, r.s_gg)
    gsave.start()

    def keep(q, piece):
        r.piece[q] = piece

    up.sent(nc)
    down.sent(nc)
    r.tot8[...] = s.finish()
    red.summed(keep)
    zsave.wait_all(nc)
    dsave.wait_all(nc)
    gsave.wait()


def ends(na, nb, refs):
    r = refs
    grp = r.grp
    nc = r.dz1_i.shape[0]
    p = Peers(na, nb)
    b = p.b
    tab, dyl, dyq, lg, qg = r.tab, r.dyl, r.dyq, r.lg, r.qg
    red = Reduce(na, nb, r.own, r.stage, r.rc, r.rx, r.tail[0:6])
    early, late = Gather(na, nb, r.oute, r.tail[6:12]), Gather(na, nb, r.outl, r.tail[12:18])
    dfeed = Feed(r.dz1_i, r.dbuf, r.s_d, nc, 0, 3)
    yfeed = Feed(r.y1_i, r.ybuf, r.s_y, nc, 0, 3)
    efeed = Feed(r.xe_i, r.ebuf, r.s_e, nc, 0, 3)
    gfeed = Feed(r.dyr_i, r.gbuf, r.s_g, nc, 0, 3)
    zfeed = Feed(r.dze_i, r.zbuf, r.s_z, nc, 0, 3)
    wfeed = Feed(r.dzw_i, r.wbuf, r.s_wb, nc, 0, 3)
    sdrain = Drain(r.obuf, r.sgrad, r.s_o, nc, 3)
    fdrain = Drain(r.fbuf, r.fgrad, r.s_f, nc, 3)
    for f in (dfeed, yfeed, efeed):
        f.prime()
    gload = pltpu.make_async_copy(r.gg_i, r.gg, r.s_raw.at[0])
    rload = pltpu.make_async_copy(r.wrt_i.at[0:1024], r.wr, r.s_raw.at[1])
    fload = pltpu.make_async_copy(r.wf_i, r.wf, r.s_raw.at[2])
    gload.start()
    for f in (gfeed, zfeed, wfeed):
        f.prime()
    rload.start()
    fload.start()
    pload = pltpu.make_async_copy(r.wp_i, r.wp, r.s_raw.at[3])
    pload.start()
    t8, t1 = r.tot8[...], r.tot1[...]
    rows, pair = backward_rows(t1[:, :256], t8[:, :256], t1, 1, r.nl[...].astype(F32))
    fill_tables(tab, 0, rows)
    r.lpair[...] = pair
    rows, pair = backward_rows(
        fold_frames(t1[:, 256:]), fold_frames(t8[:, 256:]), t1, 4, four(r.nq[...])
    )
    fill_tables(tab, 256, rows)
    r.qpair[...] = pair
    lat = Halo(p, -1, lambda c: r.prs.at[c], lambda c: r.prr.at[c], r.hls, r.hlr)
    up = Halo(p, 1, lambda c: dyq.at[c, 160:192], lambda c: dyq.at[c, 0:32], r.hus, r.hur)
    dyq[:, 32:64, :] = jnp.zeros((nc, 32, CELLS), BF16)
    dyq[:, 192:256, :] = jnp.zeros((nc, 64, CELLS), BF16)

    @pl.when(b == 0)
    def _():
        dyq[:, 0:32, :] = jnp.zeros((nc, 32, CELLS), BF16)

    @pl.when(b == nb - 1)
    def _():
        r.prr[...] = jnp.zeros_like(r.prr)

    lg[...] = jnp.zeros_like(lg)
    qg[...] = jnp.zeros_like(qg)
    pload.wait()
    p.greet()
    for q in range(2):
        early.put(q, r.piece[q])

    ahead = nc // 2

    def lateral_back(lo_c, hi_c):
        @loop(lo_c, hi_c)
        def _(c):
            lateral_clip(c)

    def lateral_clip(c):
        g = grp[c]
        m = mask_of(g)
        slot = dfeed.take(c)
        yfeed.take(c)
        for lo in range(0, 384, 128):
            dy = r.dbuf[slot, lo : lo + 128, :] * coef(tab, g, 0, lo, 128)
            dy = dy + r.ybuf[slot, lo : lo + 128, :] * coef(tab, g, 1, lo, 128)
            dy = ((dy + coef(tab, g, 2, lo, 128)) * m).astype(BF16)
            if lo < 256:
                dyl[c, lo : lo + 128, :] = dy
            else:
                dyq[c, 64:192, :] = dy
        for lo in range(0, 256, 128):
            v = dot(r.wp[lo : lo + 128, 0:256], dyl[c]) + dot(r.wp[lo : lo + 128, 256:384], dyq[c, 64:192, :])
            r.prs[c, lo : lo + 128, :] = v.astype(BF16)

        @pl.when(c < ahead)
        def _():
            lat.start(c)

        up.start(c)
        efeed.take(c)
        dy = dyl[c, 0:256, :]
        lg[0:256, :] += dot_nt(dy, r.ebuf[slot, 0:256, :])
        lg[256:512, :] += dot_nt(dy, r.ebuf[slot, 256:512, :])
        lg[512:768, 0:128] += dot_nt(dy, r.ebuf[slot, 512:640, :])
        qg[...] += dot_nt(dyq[c, 64:192, :], r.ebuf[slot, 128:896, :])

    def block_of(mine, i):
        if mine == 0:
            return r.gg[256 * i : 256 * (i + 1), :]
        if i < 4:
            return r.gg[2048 + 256 * i : 2304 + 256 * i, :]
        return lg[256 * (i - 4) : 256 * (i - 3), :]

    stages = len(red.bits)
    lateral_back(0, nc // 6)
    gload.wait()
    red.first(block_of, 0, 2)
    lateral_back(nc // 6, nc)
    for j in range(3):
        lg[800 + 32 * j : 832 + 32 * j, 128:256] = sum(
            qg[32 * f : 32 * (f + 1), 128 * (f + j) : 128 * (f + j + 1)] for f in range(4)
        )
    for k in range(9):
        term = sum(
            r.ng[128 * k + 32 * f : 128 * k + 32 * (f + 1), 32 * f : 32 * (f + 1)] for f in range(4)
        )
        if k < 8:
            lg[768 + 32 * k : 800 + 32 * k, 0:32] = term
        else:
            lg[768:800, 128:160] = term
    lg[896:1024, 128:160] = sum(r.wg[128 * f : 128 * (f + 1), 32 * f : 32 * (f + 1)] for f in range(4))
    red.first(block_of, 1, 2)
    rload.wait()

    def slow_ends(lo_c, hi_c):
        @loop(lo_c, hi_c)
        def _(c):
            m = mask_of(grp[c])
            slot = gfeed.take(c)
            zfeed.take(c)
            sdrain.room(c)
            for lo in range(0, 1024, 128):
                dx = dot(r.wr[lo : lo + 128, :], r.gbuf[slot]) + r.zbuf[slot, lo : lo + 128, :]
                r.obuf[slot, lo : lo + 128, :] = (dx * m).astype(BF16)
            sdrain.put(c)

    cuts = [nc * i // (stages + 1) for i in range(stages + 2)]
    slow_ends(cuts[0], cuts[1])
    red.first_done()
    for n in range(stages):
        red.halve(n)
        slow_ends(cuts[n + 1], cuts[n + 2])
        red.halved()
    red.along()
    fload.wait()

    def fast_ends(lo_c, hi_c):
        @loop(lo_c, hi_c)
        def _(c):
            lat.arrive(c)
            up.arrive(c)
            m = mask_of(grp[c])
            slot = wfeed.take(c)
            fdrain.room(c)
            for lo in range(0, 512, 128):
                dx = dot(r.wf[lo : lo + 128, 0:256], dyl[c]) + dot(r.wf[lo : lo + 128, 256:512], dyq[c])
                dx = dx + r.wbuf[slot, lo : lo + 128, :]
                if lo >= 256:
                    dx = dx + r.prr[c, lo - 256 : lo - 128, :].astype(F32)
                r.fbuf[slot, lo : lo + 128, :] = (dx * m).astype(BF16)
            fdrain.put(c)

    early.gather(stages - 1)
    red.summed(late.put)

    @loop(ahead, nc)
    def _(c):
        lat.start(c)

    cuts = [ahead * i // (2 * stages) for i in range(2 * stages + 1)]
    for n in range(stages):
        fast_ends(cuts[2 * n], cuts[2 * n + 1])
        late.gather(stages - 1 - n)
        fast_ends(cuts[2 * n + 1], cuts[2 * n + 2])
        if n + 1 < stages:
            early.gather(stages - 2 - n)
    early.final()
    late.final()
    fast_ends(ahead, nc)
    sdrain.done()
    fdrain.done()
    lat.sent(nc)
    up.sent(nc)
    early.settle()
    late.settle()


def last(oe_i, ol_i, rp, spr, ep, lp, qp, np_, wp, *refs):
    big, grads, small, big_out = refs[:3], refs[3:10], refs[10:17], refs[17:20]
    bufs, made, (oe, ol, sem_in, sem_out, sem_a, sem_b) = refs[20:23], refs[23:30], refs[30:]
    nc = big[0].shape[0]
    rg, sg, eg, lg, qg, ng, wg = made

    def take(i, c):
        return pltpu.make_async_copy(big[i].at[c], bufs[i].at[c], sem_in.at[i, c])

    def give(i, c):
        return pltpu.make_async_copy(bufs[i].at[c], big_out[i].at[c], sem_out.at[i, c])

    def pass_on(i):
        @loop(0, nc)
        def _(c):
            take(i, c).wait()
            give(i, c).start()

    def hand(i):
        return pltpu.make_async_copy(made[i], grads[i], sem_b.at[i])

    ends_in = [pltpu.make_async_copy(s, d, sem_a.at[i]) for i, (s, d) in enumerate(((oe_i, oe), (ol_i, ol)))]
    for c in ends_in:
        c.start()
    for i in range(3):

        @loop(0, nc)
        def _(c):
            take(i, c).start()

    for c in ends_in:
        c.wait()
    for cb in range(5):
        for j in range(3):
            lo = (512, 3328, 1792)[j] + 256 * cb
            src = ol if j != 1 else oe
            if j == 1 and cb >= 3:
                src, lo = ol, 256 * (cb - 3)
            rg[j, :, 256 * cb : 256 * (cb + 1)] = src[lo : lo + 256, :].astype(F32)
    hand(0).start()
    pass_on(0)
    for k in range(9):
        sg[k] = oe[1024 + 256 * k : 1280 + 256 * k, :].astype(F32)
        at = 3840 + 32 * k if k < 8 else 3840
        ng[k] = (ol[at : at + 32, 0:32] if k < 8 else ol[at : at + 32, 128:160]).astype(F32)
    hand(1).start()
    hand(5).start()
    pass_on(1)
    for q in range(4):
        eg[256 * q : 256 * (q + 1), :] = oe[256 * q : 256 * (q + 1), :].astype(F32)
    for k in range(5):
        lo = 3072 + 256 * (k // 2)
        lg[k] = ol[lo : lo + 256, 128 * (k % 2) : 128 * (k % 2 + 1)].astype(F32)
    for j in range(3):
        qg[j] = ol[3872 + 32 * j : 3904 + 32 * j, 128:256].astype(F32)
    wg[...] = jnp.transpose(ol[3968:4096, 128:256].astype(F32))[0:32, :]
    for i in (2, 3, 4, 6):
        hand(i).start()
    pass_on(2)
    rpo, spo, epo, lpo, qpo, npo, wpo = small
    for src, dst in ((rp, rpo), (spr, spo), (ep, epo), (lp, lpo), (wp, wpo)):
        dst[...] = src[...]
    qpo[...] = qp[:, 0:32]
    npo[...] = np_[:, 0:32]
    for i in range(7):
        hand(i).wait()

    @loop(0, nc)
    def _(c):
        for i in range(3):
            give(i, c).wait()


def sds(shape, dtype):
    return jax.ShapeDtypeStruct(shape, dtype)


class Refs:
    pass


V, H, S = VM, pl.ANY, pltpu.SMEM


def call(body, na, nb, cid, ins, outs, scratch, sums, tail=()):
    names = [*ins, *outs, *scratch]
    shapes = [*scratch.values()]
    for width in sums.values():
        shapes += ar_scratch(na, nb, width)
    shapes += list(tail)

    def kernel(*refs):
        r = Refs()
        for name, ref in zip(names, refs):
            setattr(r, name, ref)
        at = len(names)
        for name in sums:
            setattr(r, name, refs[at : at + 8])
            at += 8
        r.tail = refs[at:]
        body(na, nb, r)

    got = pl.pallas_call(
        kernel,
        name=body.__name__,
        out_shape=tuple(x[1] for x in outs.values()),
        in_specs=[pl.BlockSpec(memory_space=x[0]) for x in ins.values()],
        out_specs=tuple(pl.BlockSpec(memory_space=x[0]) for x in outs.values()),
        scratch_shapes=shapes,
        compiler_params=pltpu.CompilerParams(
            collective_id=cid, has_side_effects=True, vmem_limit_bytes=LIMIT
        ),
    )(*[x[1] for x in ins.values()])
    r = Refs()
    for name, v in zip(outs, got):
        setattr(r, name, v)
    return r


def pick(source, names, end="_o"):
    return {k + "_i": (H, getattr(source, k + end)) for k in names}


def each_of(names, value, start=""):
    return {start + k: value for k in names}


KEPT = ("acts", "y3", "act2", "y2", "act1", "y1")


def build(na, nb):
    def body(
        slow_in, fast_in, clip_group, reducer, spatial, expand, lateral, squeeze, narrow, widening,
        reducer_norm, spatial_norm, expand_norm, lateral_norm, squeeze_norm, narrow_norm, widening_norm,
        slow_cot, fast_cot,
    ):
        nc = slow_in.shape[0]
        dma = pltpu.SemaphoreType.DMA
        slow = slow_in.reshape(nc, 1024, CELLS)
        first_norms = dict(nl=(V, lateral_norm), nq=(V, squeeze_norm))
        norms = first_norms | dict(
            nr=(V, reducer_norm), nn=(V, narrow_norm), ns=(V, spatial_norm), ne=(V, expand_norm), nw=(V, widening_norm)
        )

        def act(c, dtype):
            return sds((nc, c, CELLS), dtype)

        def vact(c, dtype):
            return VM((nc, c, CELLS), dtype)

        def two(c, dtype):
            return VM((2, c, CELLS), dtype)

        def three(c, dtype):
            return VM((3, c, CELLS), dtype)

        def tab(k, c):
            return VM((3, k, c, 128), F32)

        each, slots = dma((nc,)), dma((2,))
        state = dict(
            xe=(896, BF16), y1=(384, F32), act1=(384, BF16), y2=(384, F32), act2=(384, BF16), y3=(256, F32), acts=(256, BF16)
        )
        turns = dict(
            wrt=(1280, 768), wst=(768, 768), wet=(256, 1024), wwt=(128, 512), wnt=(128, 1152), wf=(512, 512),
            wp=(256, 384), ww=(512, 128),
        )
        fw = call(
            forward, na, nb, 1,
            dict(
                grp=(S, clip_group), fast=(H, fast_in.reshape(nc, 512, CELLS)), slow=(H, slow),
                fcot=(H, fast_cot.reshape(nc, 512, CELLS)),
                reducer=(H, reducer.reshape(768, 1280)), spatial=(H, spatial), expand=(H, expand),
                lateral=(V, lateral), squeeze=(V, squeeze), narrow=(V, narrow), widening=(V, jnp.transpose(widening)),
            ) | norms,
            dict(fout=(H, act(512, BF16)))
            | {k + "_o": (H, act(*v)) for k, v in state.items()}
            | dict(dzw_o=(H, act(512, F32)), accf=(V, sds((8, 128), F32)))
            | {k + "_o": (H, sds(v, BF16)) for k, v in turns.items()}
            | dict(
                tot1=(V, sds((8, 384), F32)), tot2=(V, sds((8, 384), F32)), tot3=(V, sds((8, 384), F32)),
                tot4=(V, sds((8, 1024), F32)),
            ),
            {k: vact(*v) for k, v in state.items()}
            | {k: VM(v, BF16) for k, v in turns.items()}
            | dict(
                wr=VM((768, 1280), BF16), sp=VM((9, 256, 256), BF16), we=VM((1024, 256), BF16),
                wa=VM((384, 896), BF16), tall=VM((128, 128), BF16), gram=VM((3, 128, 128), F32),
                ws=VM((768, 768), BF16), tt=VM((768, 2 * CELLS), F32), wn=VM((128, 1152), BF16),
                su=vact(256, BF16), sd=vact(256, BF16), ru=vact(256, BF16), rd=vact(256, BF16),
                xbuf=two(1024, BF16), fcbuf=three(512, BF16), fobuf=three(512, BF16), dzwb=three(512, F32),
                tab=tab(2, 384), tabw=tab(2, 512), acc=VM((1536, 128), F32), x9=VM((1152, 2 * CELLS), BF16),
                s_raw=dma((3,)), s_w=dma((8,)), s_own=each,
            )
            | each_of(("h1us", "h1ur", "h1ds", "h1dr", "h2us", "h2ur", "h2ds", "h2dr"), each)
            | dict(s_x=slots) | each_of(("fc", "fo", "dzw"), dma((3,)), "s_")
            | {"s_" + k: each for k in state},
            dict(ar1=384, ar2=384, ar3=384, ar4=1024),
        )
        hbm, vmem = pl.BlockSpec(memory_space=H), pl.BlockSpec(memory_space=V)
        slow_out, dze, acce = pl.pallas_call(
            middle,
            name="middle",
            out_shape=(act(1024, BF16), act(1024, F32), sds((8, 1024), F32)),
            in_specs=[pl.BlockSpec(memory_space=S)] + [hbm] * 3 + [vmem] * 3,
            out_specs=(hbm, hbm, vmem),
            scratch_shapes=[VM((1024, 128), F32), tab(2, 1024)]
            + [three(c, d) for c, d in ((256, BF16), (1024, BF16), (1024, BF16), (1024, BF16), (1024, F32))]
            + [dma((3,))] * 5,
            compiler_params=pltpu.CompilerParams(vmem_limit_bytes=LIMIT),
        )(clip_group, fw.acts_o, slow, slow_cot.reshape(nc, 1024, CELLS), expand, fw.tot4, expand_norm)
        half = 2048
        piece = half // (na * nb)
        tots = dict(
            tot1=(V, fw.tot1), tot2=(V, fw.tot2), tot3=(V, fw.tot3), tot4=(V, fw.tot4)
        )
        bw = call(
            back, na, nb, 2,
            dict(
                grp=(S, clip_group), slow=(H, slow), we_i=(H, expand), dze_i=(H, dze), acce=(V, acce), accf=(V, fw.accf)
            )
            | pick(fw, KEPT + ("dzw", "wet", "wwt", "wst", "wrt", "wnt", "ww")) | tots | norms,
            dict(
                dz1_o=(H, act(384, F32)), dyr_o=(H, act(768, BF16)), gg_o=(H, sds((3072, 256), F32)),
                piece=(V, sds((2, piece, 256), BF16)),
                ng=(V, sds((1152, 128), F32)), wg=(V, sds((512, 128), F32)), tot8=(V, sds((8, 384), F32)),
                epair=(V, sds((2, 1024), F32)), spair=(V, sds((2, 256), F32)), rpair=(V, sds((2, 256), F32)),
                wpair=(V, sds((2, 128), F32)), npair=(V, sds((2, 128), F32)),
            ),
            {k: vact(*state[k]) for k in KEPT}
            | dict(
                wet=VM((256, 1024), BF16), we=VM((1024, 256), BF16), ww=VM((512, 128), BF16),
                wwt=VM((128, 512), BF16), wst=VM((768, 768), BF16), wrl=VM((256, 768), BF16), wnt=VM((128, 1152), BF16),
                zbuf=VM((3 * 1024, CELLS), F32), wbuf=two(512, F32), xbuf=VM((2, 2, 1024, CELLS), BF16),
                dye=vact(768, BF16), dye2=VM((nc * 1024, CELLS), BF16), rx=VM((2, half // 2, 256), BF16), rc=VM((half, 256), BF16),
                dzs=vact(256, F32), dzn=vact(128, F32), gg=VM((7168, 256), F32),
                tab=tab(3, 1024), tabb=tab(2, 384), acc=VM((384, 128), F32),
                d9=VM((2304, 2 * CELLS), BF16), d9n=VM((1152, CELLS), BF16), s_raw=dma((7,)), s_gg=dma,
            )
            | each_of(KEPT + ("dz1", "dyr"), each, "s_")
            | each_of(("h3us", "h3ur", "h3ds", "h3dr"), each)
            | each_of(("wb", "x"), slots, "s_")
            | dict(s_z=dma((3,))),
            dict(ar5=1152, ar6=256, ar7=384, ar8=384),
            reduce_sems(na, nb, 2),
        )
        en = call(
            ends, na, nb, 3,
            dict(
                grp=(S, clip_group), piece=(V, bw.piece), dze_i=(H, dze),
                ng=(V, bw.ng), wg=(V, bw.wg), tot8=(V, bw.tot8), tot1=(V, fw.tot1),
            )
            | pick(bw, ("dz1", "dyr", "gg")) | pick(fw, ("y1", "xe", "dzw", "wrt", "wf", "wp")) | first_norms,
            dict(
                sgrad=(H, act(1024, BF16)), fgrad=(H, act(512, BF16)), oute=(V, sds((2 * half, 256), BF16)),
                outl=(V, sds((2 * half, 256), BF16)), lpair=(V, sds((2, 256), F32)), qpair=(V, sds((2, 128), F32)),
            ),
            dict(
                gg=VM((3072, 256), F32), wr=VM((1024, 768), BF16), wf=VM((512, 512), BF16), wp=VM((256, 384), BF16),
                tab=tab(3, 384), dyl=vact(256, BF16), prs=vact(256, BF16), prr=vact(256, BF16), dyq=vact(256, BF16),
                lg=VM((1024, 256), F32), qg=VM((128, 768), F32), own=VM((half, 256), F32),
                stage=VM((half, 256), BF16), rc=VM((half, 256), BF16), rx=VM((2, half // 2, 256), BF16),
                dbuf=three(384, F32), ybuf=three(384, F32), ebuf=three(896, BF16), gbuf=three(768, BF16),
                zbuf=three(1024, F32), wbuf=three(512, F32), obuf=three(1024, BF16), fbuf=three(512, BF16),
                s_raw=dma((4,)),
            )
            | each_of(("d", "y", "e", "g", "z", "wb", "o", "f"), dma((3,)), "s_")
            | each_of(("hls", "hlr", "hus", "hur"), each),
            {},
            reduce_sems(na, nb, 2) + gather_sems(na, nb) * 2,
        )
        shapes = [
            (3, 256, 1280), (9, 256, 256), (1024, 256), (5, 256, 128), (3, 32, 128), (9, 32, 32), (32, 128),
            (2, 256), (2, 256), (2, 1024), (2, 256), (2, 32), (2, 32), (2, 128),
        ]
        big = (fw.fout, en.sgrad, en.fgrad)
        got = pl.pallas_call(
            last,
            name="last",
            out_shape=tuple(sds(v, F32) for v in shapes) + tuple(sds(v.shape, BF16) for v in big),
            in_specs=[hbm] * 2 + [vmem] * 7 + [hbm] * 3,
            out_specs=tuple([hbm] * 7 + [vmem] * 7 + [hbm] * 3),
            scratch_shapes=[VM(v.shape, BF16) for v in big]
            + [VM(v, F32) for v in shapes[:7]]
            + [VM((2 * half, 256), BF16), VM((2 * half, 256), BF16)]
            + [dma((3, nc)), dma((3, nc)), dma((2,)), dma((7,))],
            compiler_params=pltpu.CompilerParams(vmem_limit_bytes=LIMIT),
        )(en.oute, en.outl, bw.rpair, bw.spair, bw.epair, en.lpair, en.qpair, bw.npair, bw.wpair, *big)
        fast_out, slow_grad, fast_grad = got[len(shapes) :]
        return (
            slow_out.reshape(slow_in.shape), fast_out.reshape(fast_in.shape),
            slow_grad.reshape(slow_in.shape), fast_grad.reshape(fast_in.shape),
            *got[:6], jnp.transpose(got[6]), *got[7 : len(shapes)],
        )

    return body


def solution(mesh):
    body = build(mesh.shape["clip"], mesh.shape["tm"])
    big = P("clip", "tm", None, None)
    return jax.shard_map(
        body,
        mesh=mesh,
        in_specs=(big, big, P("clip")) + (P(),) * 14 + (big, big),
        out_specs=(big,) * 4 + (P(),) * 14,
        check_vma=False,
    )
```
